32 devices in a mesh: dp: 2 (over x), ctx: 4 (over y, core), tp: 4 (over z).
Axes of the slice: x: 2, y: 2, z: 4, core: 2. Of those that a mesh axis runs over, the one named last changes fastest.
Arguments:
- tokens: bfloat16 [16384, 768], P(('dp', 'ctx', 'tp')), may hold values from -6 to 6
- first_gain: bfloat16 [768], replicated, may hold values from 0.5 to 1.5
- first_bias: bfloat16 [768], replicated, may hold values from -0.4375 to 0.4375
- mixer_weight: bfloat16 [768, 3, 768], P(None, None, 'tp'), may hold values from -0.21875 to 0.21875
- mixer_bias: bfloat16 [3, 768], P(None, 'tp'), may hold values from -0.3125 to 0.3125
- feature_weight: bfloat16 [2, 12, 64, 64], P(None, 'tp'), may hold values from -1.5 to 1.5
- feature_bias: bfloat16 [2, 12, 64], P(None, 'tp'), may hold values from -6 to 6
- output_weight: bfloat16 [768, 768], P('tp'), may hold values from -6 to 6
- output_bias: bfloat16 [768], replicated, may hold values from -4 to 4
- second_gain: bfloat16 [768], replicated, may hold values from 0.5 to 1.5
- second_bias: bfloat16 [768], replicated, may hold values from -4 to 4
- inner_weight: bfloat16 [768, 3072], P(None, 'tp'), may hold values from -0.21875 to 0.21875
- inner_bias: bfloat16 [3072], P('tp'), may hold values from -4 to 4
- outer_weight: bfloat16 [3072, 768], P('tp'), may hold values from -0.109375 to 0.109375
- outer_bias: bfloat16 [768], replicated, may hold values from -4 to 4
- block_owner: int32 [2, 32], P('dp'), may hold values from 0 to 0, as said below
- cotangent: bfloat16 [16384, 768], P(('dp', 'ctx', 'tp')), may hold values from -6 to 6
Outputs:
- result: bfloat16 [16384, 768], P(('dp', 'ctx', 'tp'))
- tokens_gradient: float32 [16384, 768], P(('dp', 'ctx', 'tp'))
- first_gain_gradient: float32 [768], replicated
- first_bias_gradient: float32 [768], replicated
- mixer_weight_gradient: float32 [768, 3, 768], P(None, None, 'tp')
- mixer_bias_gradient: float32 [3, 768], P(None, 'tp')
- feature_weight_gradient: float32 [2, 12, 64, 64], P(None, 'tp')
- feature_bias_gradient: float32 [2, 12, 64], P(None, 'tp')
- output_weight_gradient: float32 [768, 768], P('tp')
- output_bias_gradient: float32 [768], replicated
- second_gain_gradient: float32 [768], replicated
- second_bias_gradient: float32 [768], replicated
- inner_weight_gradient: float32 [768, 3072], P(None, 'tp')
- inner_bias_gradient: float32 [3072], P('tp')
- outer_weight_gradient: float32 [3072, 768], P('tp')
- outer_bias_gradient: float32 [768], replicated
The draws below stay inside these ranges and needn't reach their ends.
Inputs may be any that keep to these rules, and one draw needn't show every extreme that they name: `block_owner`: all blocks of one sequence carry one number, and pieces of a data group share the same blocks. A sequence covers 8192 // 256 or twice that many consecutive blocks of every piece, so it has 8192 or 16384 tokens; its number is the index of its last 8192-token unit, so numbers rise along a row, differ between sequences, and the last block of every row carries 1 - 1.
All inputs are finite; a program needn't handle non-finite values.
Results may differ from the reference program's by a relative error of at most 0.015.
Values may be sent and summed in bfloat16 or wider, within the bound.
A program may use at most 128 MiB of HBM per device.

```python
import jax
import jax.numpy as jnp
from jax import lax

D = 768
HEADS = 12
HD = 64
FF = 3072
BLOCK = 64
PIECE = 2048
GROUPS = 2
BLOCKS = 32
UNITS = 1
TOKENS = 16384
N_DP = 2
N_CTX = 4


def draw_block_owner(key, part):
    flips = jax.random.randint(key, (UNITS, GROUPS), 0, 2).astype(jnp.int32)

    def advance(previous, coin):
        joined = coin * (1 - previous)
        return (joined, joined)
    first_unit = jnp.ones((GROUPS,), jnp.int32)
    final_carry, joined = lax.scan(advance, first_unit, flips)
    following = jnp.concatenate([joined[1:], jnp.zeros((1, GROUPS), jnp.int32)], axis=0)
    unit_owner = jnp.arange(UNITS, dtype=jnp.int32)[:, None] + following
    return jnp.repeat(unit_owner.T, BLOCKS // UNITS, axis=1).astype(jnp.int32)


def steps_of(rng, dims, shards, smallest, high):
    gain = 1.0
    for position, parts in shards:
        draws = jax.random.uniform(jax.random.fold_in(jax.random.fold_in(rng, 6), position), (parts,), jnp.float32, smallest / len(shards), high / len(shards))
        gain = gain * jnp.repeat(jnp.exp(draws), dims[position] // parts).reshape((-1,) + (1,) * (len(dims) - 1 - position))
    return gain


def scatter_about(key, extent, deviation, most, pieces=(), kind=jnp.bfloat16):
    values = jax.random.normal(key, extent, jnp.float32) * deviation
    if len(pieces) > 0:
        values = steps_of(key, extent, pieces, -0.22, 0.18) * values
    return jnp.clip(values, min=-most, max=most).astype(kind)


def setup_inputs(seed: int = 0) -> dict:
    keys = jax.random.split(jax.random.key(seed), 18)
    return {
        "tokens": scatter_about(keys[0], (TOKENS, D), 1.0, 6.0, ((0, 32),)),
        "first_gain": jnp.clip(1.0 + 0.1 * jax.random.normal(keys[1], (D,), jnp.float32), 0.5, 1.5).astype(jnp.bfloat16),
        "first_bias": scatter_about(keys[2], (D,), 0.03, 0.4375),
        "mixer_weight": scatter_about(keys[3], (D, 3, D), D ** -0.5, 0.21875, ((2, 4),)),
        "mixer_bias": scatter_about(keys[4], (3, D), 0.02, 0.3125, ((1, 4),)),
        "feature_weight": scatter_about(keys[5], (2, HEADS, HD, HD), (HD // 4) ** -0.5, 1.5, ((1, 4),)),
        "feature_bias": scatter_about(keys[6], (2, HEADS, HD), 1.0, 6.0, ((1, 4),)),
        "output_weight": scatter_about(keys[7], (D, D), (max(1, D // 512)) ** -0.5, 6.0, ((0, 4),)),
        "output_bias": scatter_about(keys[8], (D,), 0.3, 4.0),
        "second_gain": jnp.clip(1.0 + 0.1 * jax.random.normal(keys[9], (D,), jnp.float32), 0.5, 1.5).astype(jnp.bfloat16),
        "second_bias": scatter_about(keys[10], (D,), 0.3, 4.0),
        "inner_weight": scatter_about(keys[11], (D, FF), D ** -0.5, 0.21875, ((1, 4),)),
        "inner_bias": scatter_about(keys[12], (FF,), 0.3, 4.0, ((0, 4),)),
        "outer_weight": scatter_about(keys[13], (FF, D), FF ** -0.5, 0.109375, ((0, 4),)),
        "outer_bias": scatter_about(keys[14], (D,), 0.3, 4.0),
        "block_owner": draw_block_owner(jax.random.fold_in(keys[17], 71), 0),
        "cotangent": scatter_about(keys[16], (TOKENS, D), 1.0, 6.0, ((0, 32),)),
    }


EPSILON = 1e-05
HIGHEST = lax.Precision.HIGHEST

@jax.custom_vjp
def low(v):
    return lax.optimization_barrier(v.astype(jnp.bfloat16)).astype(jnp.float32)

@jax.custom_vjp
def low_back(v):
    return v

def low_keep(v):
    return (low(v), None)

def low_pass(kept, grad):
    return (grad,)

def back_keep(v):
    return (v, None)

def back_low(kept, grad):
    return (low(grad),)
low.defvjp(low_keep, low_pass)
low_back.defvjp(back_keep, back_low)

def layer_norm(values, norm_gain, norm_offset):
    average = lax.optimization_barrier(jnp.mean(values, axis=-1, keepdims=True))
    centered = values - average
    variance = lax.optimization_barrier(jnp.mean(centered * centered, axis=-1, keepdims=True))
    return centered * lax.rsqrt(variance + EPSILON) * norm_gain + norm_offset

def gaussian_unit(values):
    return 0.5 * values * (1.0 + jnp.tanh(0.7978845608028654 * (values + 0.044715 * values * values * values)))

def feature_map(inputs, weight, offset):
    logits = jnp.einsum('thd,hde->the', inputs, weight, precision=HIGHEST) + offset
    return jnp.concatenate([jax.nn.softmax(logits, axis=-1), jax.nn.softmax(-logits, axis=-1)], axis=-1)

def piece_forward(params, inputs, owners, carried):
    first_gain, first_bias, mixer_weight, mixer_bias, feature_weight, feature_bias, output_weight, output_bias, second_gain, second_bias, inner_weight, inner_bias, outer_weight, outer_bias = params
    state_in, norm_in = carried
    first_low = low(layer_norm(inputs, first_gain, first_bias))
    mixed_rows = jnp.dot(first_low, mixer_weight.reshape(D, 3 * D), precision=HIGHEST) + mixer_bias.reshape(3 * D)
    mixed_rows = low(low_back(mixed_rows)).reshape(PIECE, 3, HEADS, HD)
    query_rows = mixed_rows[:, 0]
    key_rows = mixed_rows[:, 1]
    value_rows = mixed_rows[:, 2]
    query_lifted = low(low_back(feature_map(query_rows, feature_weight[0], feature_bias[0])))
    key_lifted = low(low_back(feature_map(key_rows, feature_weight[1], feature_bias[1])))
    query_blocks = query_lifted.reshape(BLOCKS, BLOCK, HEADS, 2 * HD)
    key_blocks = key_lifted.reshape(BLOCKS, BLOCK, HEADS, 2 * HD)
    value_blocks = value_rows.reshape(BLOCKS, BLOCK, HEADS, HD)
    block_state = jnp.einsum('jthe,jthf->jhef', value_blocks, key_blocks, precision=HIGHEST)
    block_norm = lax.optimization_barrier(jnp.sum(key_blocks, axis=1))
    block_index = jnp.arange(BLOCKS)
    member = (owners[:, None] == jnp.arange(UNITS)[None, :]).astype(jnp.float32)
    earlier = ((owners[:, None] == owners[None, :]) & (block_index[:, None] > block_index[None, :])).astype(jnp.float32)
    causal = jnp.arange(BLOCK)[:, None] >= jnp.arange(BLOCK)[None, :]
    state_before = jnp.einsum('ji,ihef->jhef', earlier, block_state, precision=HIGHEST) + jnp.einsum('js,shef->jhef', member, state_in, precision=HIGHEST)
    norm_before = jnp.einsum('ji,ihf->jhf', earlier, block_norm, precision=HIGHEST) + jnp.einsum('js,shf->jhf', member, norm_in, precision=HIGHEST)
    numerator = jnp.einsum('jthf,jhef->jthe', query_blocks, state_before, precision=HIGHEST)
    denominator = jnp.einsum('jthf,jhf->jth', query_blocks, norm_before, precision=HIGHEST)
    scores = jnp.einsum('jthf,jshf->jhts', query_blocks, key_blocks, precision=HIGHEST)
    scores = low(low_back(jnp.where(causal, scores, 0.0)))
    numerator = numerator + jnp.einsum('jhts,jshe->jthe', scores, value_blocks, precision=HIGHEST)
    denominator = denominator + jnp.swapaxes(lax.optimization_barrier(jnp.sum(scores, axis=-1)), 1, 2)
    attended = low(low_back(numerator / denominator[..., None])).reshape(PIECE, D)
    branch = low_back(jnp.dot(attended, output_weight, precision=HIGHEST))
    middle = inputs + branch + output_bias
    second_low = low(layer_norm(middle, second_gain, second_bias))
    hidden_input = low_back(jnp.dot(second_low, inner_weight, precision=HIGHEST) + inner_bias)
    activated = low(gaussian_unit(hidden_input))
    result = middle + low_back(jnp.dot(activated, outer_weight, precision=HIGHEST)) + outer_bias
    carried_out = (state_in + jnp.einsum('js,jhef->shef', member, block_state, precision=HIGHEST), norm_in + jnp.einsum('js,jhf->shf', member, block_norm, precision=HIGHEST))
    return (result, carried_out)

def forward(inputs, owners, params):

    def group_pass(group_data):
        group_inputs, group_owner = group_data
        initial_state = (jnp.zeros((UNITS, HEADS, HD, 2 * HD), jnp.float32), jnp.zeros((UNITS, HEADS, 2 * HD), jnp.float32))

        def piece_step(carried, piece_inputs):
            result, carried = jax.checkpoint(piece_forward)(params, piece_inputs, group_owner, carried)
            return (carried, result)
        final_state, results = lax.scan(piece_step, initial_state, group_inputs)
        return results
    return lax.map(group_pass, (inputs, owners))

def reference(tokens, first_gain, first_bias, mixer_weight, mixer_bias, feature_weight, feature_bias, output_weight, output_bias, second_gain, second_bias, inner_weight, inner_bias, outer_weight, outer_bias, block_owner, cotangent):
    params = tuple((weight_arg.astype(jnp.float32) for weight_arg in (first_gain, first_bias, mixer_weight, mixer_bias, feature_weight, feature_bias, output_weight, output_bias, second_gain, second_bias, inner_weight, inner_bias, outer_weight, outer_bias)))
    inputs = tokens.astype(jnp.float32).reshape(N_DP, N_CTX, PIECE, D)
    owners = block_owner.astype(jnp.int32)
    result, pullback = jax.vjp(lambda inner_inputs, inner_params: forward(inner_inputs, owners, inner_params), inputs, params)
    tokens_delta, param_deltas = pullback(cotangent.astype(jnp.float32).reshape(N_DP, N_CTX, PIECE, D))
    return (result.reshape(TOKENS, D).astype(jnp.bfloat16), tokens_delta.reshape(TOKENS, D), param_deltas[0], param_deltas[1], param_deltas[2], param_deltas[3], param_deltas[4], param_deltas[5], param_deltas[6], param_deltas[7], param_deltas[8], param_deltas[9], param_deltas[10], param_deltas[11], param_deltas[12], param_deltas[13])
```

```python
import jax
import jax.numpy as jnp
from jax import lax
from jax.sharding import PartitionSpec as P

HD = 64
BLOCK = 64
CHUNK = 256
EPSILON = 1e-05
F32 = jnp.float32
BF16 = jnp.bfloat16
ALL = ("dp", "ctx", "tp")


def ein(spec, a, b):
    return jnp.einsum(spec, a, b, preferred_element_type=F32)


def layer_norm(v, gain, offset):
    c = v - jnp.mean(v, axis=-1, keepdims=True)
    r = lax.rsqrt(jnp.mean(c * c, axis=-1, keepdims=True) + EPSILON)
    n = c * r
    return n * gain + offset, n, r


def layer_norm_back(e, n, r, gain):
    m = e * gain
    back = r * (
        m - jnp.mean(m, axis=-1, keepdims=True) - n * jnp.mean(m * n, axis=-1, keepdims=True)
    )
    return back, jnp.sum(e * n, axis=0), jnp.sum(e, axis=0)


def gelu_parts(s):
    t = jnp.tanh(0.7978845608028654 * (s + 0.044715 * s * s * s))
    slope = 0.7978845608028654 * (1.0 + 3.0 * 0.044715 * s * s)
    return 0.5 * s * (1.0 + t), 0.5 * (1.0 + t) + 0.5 * s * (1.0 - t * t) * slope


def feature_map(q, weight, offset):
    u = ein("thd,hde->the", q, weight) + offset
    up, down = jax.nn.softmax(u, axis=-1), jax.nn.softmax(-u, axis=-1)
    return up, down, jnp.concatenate([up, down], axis=-1).astype(BF16)


def feature_back(delta, up, down, q, weight):
    d, dd = delta[..., :HD], delta[..., HD:]
    du = up * (d - jnp.sum(up * d, axis=-1, keepdims=True)) - down * (
        dd - jnp.sum(down * dd, axis=-1, keepdims=True)
    )
    low = du.astype(BF16)
    return ein("the,hde->thd", low, weight), ein("thd,the->hde", q, low), jnp.sum(du, axis=0)


def merge_heads(gathered):
    tp, rows, three, width = gathered.shape
    return gathered.transpose(1, 2, 0, 3).reshape(rows, three, tp * width)


def shards(
    tokens,
    first_gain,
    first_bias,
    mixer_weight,
    mixer_bias,
    feature_weight,
    feature_bias,
    output_weight,
    output_bias,
    second_gain,
    second_bias,
    inner_weight,
    inner_bias,
    outer_weight,
    outer_bias,
    block_owner,
    cotangent,
):
    rows, width = tokens.shape
    n_tp, n_ctx = lax.axis_size("tp"), lax.axis_size("ctx")
    n_plane = lax.axis_size("dp") * n_ctx
    plane = lax.axis_index("dp") * n_ctx + lax.axis_index("ctx")
    heads_here = mixer_weight.shape[2] // HD
    heads = heads_here * n_tp
    mine = lax.axis_index("ctx") * n_tp + lax.axis_index("tp")

    mixer_t = mixer_weight.transpose(1, 2, 0).reshape(-1, width)
    sizes = [w.shape[0] for w in (mixer_t, output_weight, inner_weight, outer_weight)]
    pack = jnp.concatenate([mixer_t, output_weight, inner_weight, outer_weight], axis=0)
    part = pack.shape[0] // n_plane
    piece = lax.dynamic_slice_in_dim(pack, plane * part, part, 0)
    full = lax.all_gather(piece, ALL, axis=0, tiled=True)
    full = full.reshape(n_plane, n_tp, part, width).transpose(1, 0, 2, 3).reshape(n_tp, -1, width)
    cuts = [0]
    for s in sizes:
        cuts.append(cuts[-1] + s)
    mixer_all, output_all, inner_all, outer_all = [
        full[:, a:b] for a, b in zip(cuts[:-1], cuts[1:])
    ]
    small = jnp.concatenate(
        [feature_weight.reshape(-1), mixer_bias.reshape(-1), feature_bias.reshape(-1), inner_bias]
    )
    small = lax.all_gather(small, "tp")
    cut = feature_weight.size
    feature_all = (
        small[:, :cut].reshape(n_tp, 2, heads_here, HD, HD).transpose(1, 0, 2, 3, 4)
    ).reshape(2, heads, HD, HD)
    mixer_bias_all = small[:, cut : cut + mixer_bias.size].astype(F32).reshape(n_tp, -1)
    cut += mixer_bias.size
    feature_bias_all = (
        small[:, cut : cut + feature_bias.size]
        .astype(F32)
        .reshape(n_tp, 2, heads_here, HD)
        .transpose(1, 0, 2, 3)
        .reshape(2, heads, HD)
    )
    cut += feature_bias.size
    inner_bias_all = small[:, cut:].astype(F32)

    x = tokens.astype(F32)
    gain1, gain2 = first_gain.astype(F32), second_gain.astype(F32)
    h1, n1, r1 = layer_norm(x, gain1, first_bias.astype(F32))
    h1 = h1.astype(BF16)
    mix = ein("td,skd->tsk", h1, mixer_all) + mixer_bias_all
    mix = mix.astype(BF16).reshape(rows, n_tp, 3, heads_here, HD).transpose(2, 0, 1, 3, 4)
    mix = mix.reshape(3, rows, heads, HD)
    q, k, v = mix[0], mix[1], mix[2]
    q_up, q_down, phi_q = feature_map(q, feature_all[0], feature_bias_all[0])
    k_up, k_down, phi_k = feature_map(k, feature_all[1], feature_bias_all[1])

    chunk = min(CHUNK, rows)
    chunks = rows // chunk
    pq = phi_q.reshape(chunks, chunk, heads, 2 * HD)
    pk = phi_k.reshape(chunks, chunk, heads, 2 * HD)
    vc = v.reshape(chunks, chunk, heads, HD)
    causal = jnp.arange(chunk)[:, None] >= jnp.arange(chunk)[None, :]
    state = ein("jthe,jthf->jhef", vc, pk)
    norm = jnp.sum(pk.astype(F32), axis=1)
    both = jnp.concatenate([state, norm[:, :, None]], axis=2)
    owners = block_owner[0].reshape(n_tp, -1)[:, 0]
    order = jnp.arange(n_ctx * n_tp)
    same = jnp.tile(owners, n_ctx) == jnp.tile(owners, n_ctx)[mine]

    def prefix(totals, reach):
        everything = lax.all_gather(totals.astype(BF16), ("ctx", "tp")).astype(F32)
        return jnp.einsum("s,shef->hef", reach.astype(F32), everything, precision="highest")

    def running(blocks, start, reverse):
        out = [None] * chunks
        acc = start
        for j in reversed(range(chunks)) if reverse else range(chunks):
            out[j] = acc
            acc = acc + blocks[j]
        return jnp.stack(out)

    before = running(both, prefix(jnp.sum(both, axis=0), same & (order < mine)), False)
    before = before.astype(BF16)
    scores = ein("jthf,jshf->jhts", pq, pk)
    a_low = jnp.where(causal, scores, 0.0).astype(BF16)
    v_one = jnp.concatenate([vc, jnp.ones(vc.shape[:-1] + (1,), BF16)], axis=-1)
    num = ein("jthf,jhef->jthe", pq, before) + ein("jhts,jshe->jthe", a_low, v_one)
    num, den = num[..., :HD], num[..., HD:]
    o = num / den
    o_low = o.astype(BF16)
    o_flat = o_low.reshape(rows, n_tp, heads_here * HD)
    x2 = x + ein("tsk,skd->td", o_flat, output_all) + output_bias.astype(F32)
    h2, n2, r2 = layer_norm(x2, gain2, second_bias.astype(F32))
    h2 = h2.astype(BF16)
    f = ein("td,sdf->tsf", h2, inner_all) + inner_bias_all
    a, slope = gelu_parts(f)
    a = a.astype(BF16)
    result = (x2 + ein("tsf,sfd->td", a, outer_all) + outer_bias.astype(F32)).astype(BF16)

    g = cotangent.astype(F32)
    d_outer = ein("tsf,td->sfd", a, cotangent)
    df = (ein("td,sfd->tsf", cotangent, outer_all) * slope).astype(BF16)
    d_inner_bias = jnp.sum(df.astype(F32), axis=0)
    d_inner = ein("td,tsf->sdf", h2, df)
    e2 = ein("tsf,sdf->td", df, inner_all)
    back2, d_gain2, d_bias2 = layer_norm_back(e2, n2, r2, gain2)
    dx2 = g + back2
    big_g = dx2.astype(BF16)
    d_output = ein("tsk,td->skd", o_flat, big_g)
    do = ein("td,skd->tsk", big_g, output_all).astype(BF16).astype(F32)
    do = do.reshape(chunks, chunk, heads, HD)
    dnum = do / den
    dden = -jnp.sum(do * o, axis=-1, keepdims=True) / den
    dne = jnp.concatenate([dnum, dden], axis=-1).astype(BF16)
    da = ein("jthe,jshe->jhts", dne, v_one)
    da_low = jnp.where(causal, da, 0.0).astype(BF16)
    d_both = ein("jthe,jthf->jhef", dne, pq)
    after = running(d_both, prefix(jnp.sum(d_both, axis=0), same & (order > mine)), True)
    after = after.astype(BF16)
    dphi_q = ein("jhts,jshf->jthf", da_low, pk) + ein("jthe,jhef->jthf", dne, before)
    dphi_k = ein("jhts,jthf->jshf", da_low, pq) + ein("jthe,jhef->jthf", v_one, after)
    dv = ein("jhts,jthe->jshe", a_low, dne[..., :HD]) + ein("jthf,jhef->jthe", pk, after[:, :, :HD])
    dphi_q = dphi_q.reshape(rows, heads, 2 * HD)
    dphi_k = dphi_k.reshape(rows, heads, 2 * HD)
    dq, d_fq, d_fbq = feature_back(dphi_q, q_up, q_down, q, feature_all[0])
    dk, d_fk, d_fbk = feature_back(dphi_k, k_up, k_down, k, feature_all[1])
    dmix = jnp.stack([dq, dk, dv.reshape(rows, heads, HD)], axis=1).astype(BF16)
    dmix = dmix.reshape(rows, 3, n_tp, heads_here * HD).transpose(0, 2, 1, 3)
    dmix = dmix.reshape(rows, n_tp, -1)
    d_mixer_bias = jnp.sum(dmix.astype(F32), axis=0)
    d_mixer = ein("tsk,td->skd", dmix, h1)
    e1 = ein("tsk,skd->td", dmix, mixer_all)
    back1, d_gain1, d_bias1 = layer_norm_back(e1, n1, r1, gain1)
    tokens_gradient = dx2 + back1

    big = jnp.concatenate([d_mixer, d_output, d_inner, d_outer], axis=1).astype(BF16)
    big = big.reshape(n_tp, n_plane, part, width).transpose(1, 0, 2, 3).reshape(-1, width)
    big = lax.psum_scatter(big, ("dp", "ctx"), scatter_dimension=0, tiled=True)
    big = lax.psum_scatter(big, "tp", scatter_dimension=0, tiled=True)
    big = lax.all_gather(big, ("dp", "ctx"), axis=0, tiled=True).astype(F32)
    d_mixer, d_output, d_inner, d_outer = [big[a:b] for a, b in zip(cuts[:-1], cuts[1:])]
    d_mixer = d_mixer.reshape(3, heads_here * HD, width).transpose(2, 0, 1)
    per_tp = jnp.concatenate(
        [
            jnp.stack([d_fq, d_fk]).reshape(2, n_tp, -1).transpose(1, 0, 2).reshape(n_tp, -1),
            d_mixer_bias,
            jnp.stack([d_fbq, d_fbk]).reshape(2, n_tp, -1).transpose(1, 0, 2).reshape(n_tp, -1),
            d_inner_bias,
        ],
        axis=1,
    )
    shared = jnp.stack(
        [d_gain1, d_bias1, jnp.sum(dx2, axis=0), d_gain2, d_bias2, jnp.sum(g, axis=0)]
    )
    total = lax.psum(jnp.concatenate([per_tp.reshape(-1), shared.reshape(-1)]), ALL)
    shared = total[per_tp.size :].reshape(6, width)
    own = lax.dynamic_slice_in_dim(
        total[: per_tp.size].reshape(n_tp, -1), lax.axis_index("tp"), 1, 0
    )[0]
    cut = feature_weight.size
    d_feature = own[:cut].reshape(feature_weight.shape)
    d_mixer_bias = own[cut : cut + mixer_bias.size].reshape(mixer_bias.shape)
    cut += mixer_bias.size
    d_feature_bias = own[cut : cut + feature_bias.size].reshape(feature_bias.shape)
    d_inner_bias = own[cut + feature_bias.size :]
    return (
        result,
        tokens_gradient,
        shared[0],
        shared[1],
        d_mixer,
        d_mixer_bias,
        d_feature,
        d_feature_bias,
        d_output,
        shared[2],
        shared[3],
        shared[4],
        d_inner,
        d_inner_bias,
        d_outer,
        shared[5],
    )


def solution(mesh):
    in_specs = (
        P(("dp", "ctx", "tp"), None),
        P(),
        P(),
        P(None, None, "tp"),
        P(None, "tp"),
        P(None, "tp", None, None),
        P(None, "tp", None),
        P("tp", None),
        P(),
        P(),
        P(),
        P(None, "tp"),
        P("tp"),
        P("tp", None),
        P(),
        P("dp", None),
        P(("dp", "ctx", "tp"), None),
    )
    out_specs = (
        P(("dp", "ctx", "tp"), None),
        P(("dp", "ctx", "tp"), None),
        P(),
        P(),
        P(None, None, "tp"),
        P(None, "tp"),
        P(None, "tp", None, None),
        P(None, "tp", None),
        P("tp", None),
        P(),
        P(),
        P(),
        P(None, "tp"),
        P("tp"),
        P("tp", None),
        P(),
    )
    return jax.shard_map(shards, mesh=mesh, in_specs=in_specs, out_specs=out_specs, check_vma=False)
```

```python
import functools

import jax
import jax.numpy as jnp
from jax import lax
from jax.experimental import pallas as pl
from jax.experimental.pallas import tpu as pltpu
from jax.sharding import PartitionSpec as P

MESH = pl.DeviceIdType.MESH

HD = 64
BLOCK = 64
CHUNK = 256
EPSILON = 1e-05
F32 = jnp.float32
BF16 = jnp.bfloat16
ALL = ("dp", "ctx", "tp")


def ein(spec, a, b):
    return jnp.einsum(spec, a, b, preferred_element_type=F32)


def layer_norm(v, gain, offset):
    c = v - jnp.mean(v, axis=-1, keepdims=True)
    r = lax.rsqrt(jnp.mean(c * c, axis=-1, keepdims=True) + EPSILON)
    n = c * r
    return n * gain + offset, n, r


def layer_norm_back(e, n, r, gain):
    m = e * gain
    back = r * (
        m - jnp.mean(m, axis=-1, keepdims=True) - n * jnp.mean(m * n, axis=-1, keepdims=True)
    )
    return back, jnp.sum(e * n, axis=0), jnp.sum(e, axis=0)


def gelu_parts(s):
    t = jnp.tanh(0.7978845608028654 * (s + 0.044715 * s * s * s))
    slope = 0.7978845608028654 * (1.0 + 3.0 * 0.044715 * s * s)
    return 0.5 * s * (1.0 + t), 0.5 * (1.0 + t) + 0.5 * s * (1.0 - t * t) * slope


def feature_map(q, weight, offset):
    u = ein("thd,hde->the", q, weight) + offset
    up, down = jax.nn.softmax(u, axis=-1), jax.nn.softmax(-u, axis=-1)
    return up, down, jnp.concatenate([up, down], axis=-1).astype(BF16)


def feature_back(delta, up, down, q, weight):
    d, dd = delta[..., :HD], delta[..., HD:]
    du = up * (d - jnp.sum(up * d, axis=-1, keepdims=True)) - down * (
        dd - jnp.sum(down * dd, axis=-1, keepdims=True)
    )
    low = du.astype(BF16)
    return ein("the,hde->thd", low, weight), ein("thd,the->hde", q, low), jnp.sum(du, axis=0)


def place():
    d, c, t = lax.axis_index("dp"), lax.axis_index("ctx"), lax.axis_index("tp")
    y, core = c // 2, lax.rem(c, 2)
    return dict(d=d, c=c, t=t, y=y, core=core, q=d * 2 + y,
        x_nb=(1 - d, c, t), y_nb=(d, (1 - y) * 2 + core, t), core_nb=(d, y * 2 + 1 - core, t),
        qx=(1 - d) * 2 + y, qy=d * 2 + 1 - y, qd=(1 - d) * 2 + 1 - y)

def greet(p):
    bar = pltpu.get_barrier_semaphore()
    peers = [p["x_nb"], p["y_nb"], p["core_nb"]] + [(p["d"], p["c"], lax.rem(p["t"] + k, 4)) for k in (1, 2, 3)]
    for peer in peers:
        pl.semaphore_signal(bar, inc=1, device_id=peer, device_id_type=MESH)
    pl.semaphore_wait(bar, len(peers))

def nearest(t):
    return [
        jnp.where(t < 2, 1, 3),
        jnp.where(t == 0, 2, jnp.where(t == 1, 3, jnp.where(t == 2, 1, 2))),
        jnp.where(t == 0, 3, jnp.where(t == 3, 1, 2)),
    ]


class Gather:
    def __init__(self, p, buf, sems, index):
        self.p, self.buf, self.sems, self.i = p, buf, sems, index
        self.rows = buf.shape[1]
        self.piece = self.rows // 8
        self.half = self.piece // 2
        self.sent = []
    def at(self, t, q, core, half=None):
        start = q * (2 * self.piece) + core * self.piece
        size = self.piece
        if half is not None:
            start, size = start + half * self.half, self.half
        return self.buf.at[t, pl.ds(pl.multiple_of(start, 16), size)]
    def shard(self, k): return lax.rem(self.p["t"] + k, 4)
    def copy(self, ref, kind, k, peer):
        s = self.sems[kind]
        return pltpu.make_async_remote_copy(ref, ref, s.at[0, self.i, k - 1], s.at[1, self.i, k - 1], device_id=peer, device_id_type=MESH)
    def go(self, *a):
        c = self.copy(*a); c.start(); self.sent.append(c)
    def first(self):
        p = self.p
        for k in (1, 2, 3):
            ref = self.at(p["t"], p["q"], p["core"])
            s = self.sems["z"]
            c = pltpu.make_async_remote_copy(ref, ref, s.at[0, self.i, k - 1], s.at[1, self.i, 3 - k], device_id=(p["d"], p["c"], lax.rem(p["t"] + k, 4)), device_id_type=MESH)
            c.start(); self.sent.append(c)
    def z(self, k):
        p, t = self.p, self.shard(k)
        ref = self.at(t, p["q"], p["core"])
        self.copy(ref, "z", k, p["x_nb"]).wait_recv()
        self.go(ref, "x", k, p["x_nb"]); self.go(ref, "y", k, p["y_nb"])
    def hop(self, ref, ok, up, k_there):
        p = self.p; s = self.sems["z"]
        i = self.nz; self.nz += 1
        c = pltpu.make_async_remote_copy(ref, ref, s.at[0, self.i, i], s.at[1, self.i, k_there - 1],
            device_id=(p["d"], p["c"], jnp.where(up, p["t"] + 1, p["t"] - 1)), device_id_type=MESH)
        @pl.when(ok)
        def _(): c.start()
        self.cond.append((ok, c))
    def first_hop(self):
        p = self.p; self.nz = 0; self.cond = []
        ref = self.at(p["t"], p["q"], p["core"])
        self.hop(ref, p["t"] < 3, True, 3)
        self.hop(ref, p["t"] > 0, False, 1)
    def zf(self, k):
        p, t = self.p, self.shard(k)
        ref = self.at(t, p["q"], p["core"])
        self.copy(ref, "z", k, p["x_nb"]).wait_recv()
        up = t < p["t"]
        self.hop(ref, jnp.where(up, p["t"] < 3, p["t"] > 0), up, jnp.where(up, k - 1, k + 1))
        self.go(ref, "x", k, p["x_nb"]); self.go(ref, "y", k, p["y_nb"])
    def drain_hops(self):
        for ok, c in self.cond:
            @pl.when(ok)
            def _(): c.wait_send()
    def xy(self, k):
        p, t = self.p, self.shard(k)
        self.copy(self.at(t, p["qx"], p["core"]), "x", k, p["x_nb"]).wait_recv()
        self.go(self.at(t, p["qx"], p["core"], 0), "fy", k, p["y_nb"])
        self.copy(self.at(t, p["qy"], p["core"]), "y", k, p["y_nb"]).wait_recv()
        self.go(self.at(t, p["qy"], p["core"], 1), "fx", k, p["x_nb"])
    def diag(self, k):
        p, t = self.p, self.shard(k)
        self.copy(self.at(t, p["qd"], p["core"], 0), "fy", k, p["y_nb"]).wait_recv()
        self.copy(self.at(t, p["qd"], p["core"], 1), "fx", k, p["x_nb"]).wait_recv()
        for q in range(4):
            self.go(self.at(t, q, p["core"]), "c", k, p["core_nb"])
    def done(self, k):
        p, t = self.p, self.shard(k)
        ref = self.buf.at[t, pl.ds(0, 4 * self.piece)]
        s = self.sems["c"]
        pltpu.make_async_remote_copy(ref, ref, s.at[0, self.i, k - 1], s.at[1, self.i, k - 1], device_id=p["core_nb"], device_id_type=MESH).wait_recv()
    def drain(self):
        for c in self.sent:
            c.wait_send()
def ag_kernel(wm, wo, w1, w2, sm, WA, W1, W2, S, ld, z, x, y, fx, fy, c):
    p = place(); sems = dict(z=z, x=x, y=y, fx=fx, fy=fy, c=c)
    t = p["t"]
    loads = [pltpu.make_async_copy(sm, S.at[t], ld.at[0]), pltpu.make_async_copy(wm, WA.at[t, pl.ds(0, 576)], ld.at[1]),
             pltpu.make_async_copy(wo, WA.at[t, pl.ds(576, 192)], ld.at[2]), pltpu.make_async_copy(w1, W1.at[t], ld.at[3]), pltpu.make_async_copy(w2, W2.at[t], ld.at[4])]
    for l in loads: l.start()
    greet(p)
    gs = [Gather(p, b, sems, i) for i, b in enumerate((S, WA, W1, W2))]
    waits=[[0],[1,2],[3],[4]]
    for n, (g, ws) in enumerate(zip(gs, waits)):
        for i in ws: loads[i].wait()
        g.first() if n == 0 else g.first_hop()
    K = nearest(t)
    a, b, c1, c2 = gs
    for k in K: a.z(k); b.zf(k)
    for k in K: a.xy(k); b.xy(k)
    for k in K: c1.zf(k)
    for k in K: a.diag(k); b.diag(k)
    for k in K: c1.xy(k)
    for k in K: c2.zf(k)
    for k in K: c1.diag(k)
    for k in K: c2.xy(k)
    for k in K: c2.diag(k)
    for g in gs:
        for k in K: g.done(k)
    for n, g in enumerate(gs):
        g.drain()
        if n: g.drain_hops()

def gather_call(wm, wo, w1, w2, sm):
    V = pl.BlockSpec(memory_space=pltpu.VMEM); A = pl.BlockSpec(memory_space=pl.ANY)
    sem = pltpu.SemaphoreType.DMA((2, 4, 5))
    return pl.pallas_call(ag_kernel, out_shape=[jax.ShapeDtypeStruct((4, 768, 768), BF16)] * 3 + [jax.ShapeDtypeStruct((4, 256, 128), BF16)],
        in_specs=[A] * 5, out_specs=[V] * 4, scratch_shapes=[pltpu.SemaphoreType.DMA((5,))] + [sem] * 6,
        compiler_params=pltpu.CompilerParams(collective_id=0, has_side_effects=True, vmem_limit_bytes=60 << 20), name="gather")(wm, wo, w1, w2, sm)


class Reduce:
    def __init__(self, p, i, G, X1, Y1, X2, Y2, Z, OUT, sems):
        self.p, self.i, self.G, self.OUT, self.sems = p, i, G, OUT, sems
        self.X1, self.Y1, self.X2, self.Y2, self.Z = X1, Y1, X2, Y2, Z
        self.half = G.shape[1]; self.qr = self.half // 4; self.hr = self.qr // 2
        self.sent = []
    def t(self, k): return lax.rem(self.p["t"] + k, 4)
    def rows(self, q, h): return pl.ds(pl.multiple_of(q * self.qr + h * self.hr, 16), self.hr)
    def rdma(self, src, dst, kind, k, peer, k_there=None):
        s = self.sems[kind]
        return pltpu.make_async_remote_copy(src, dst, s.at[0, self.i, k], s.at[1, self.i, k if k_there is None else k_there], device_id=peer, device_id_type=MESH)
    def go(self, *a):
        c = self.rdma(*a); c.start(); self.sent.append(c)
    def got(self, ref, kind, k):
        self.rdma(ref, ref, kind, k, self.p["x_nb"]).wait_recv()
    def one(self, k):
        p, t = self.p, self.t(k)
        for j in range(2):
            self.go(self.G.at[t, self.rows((1 - p["d"]) * 2 + j, 0)], self.X1.at[k, j], "x1", k, p["x_nb"])
            self.go(self.G.at[t, self.rows(j * 2 + 1 - p["y"], 1)], self.Y1.at[k, j], "y1", k, p["y_nb"])
    def two(self, k):
        p, t, G = self.p, self.t(k), self.G
        self.got(self.X1.at[k], "x1", k)
        for j in range(2):
            r = self.rows(p["d"] * 2 + j, 0)
            G[t, r] = G[t, r] + self.X1[k, j]
        self.go(G.at[t, self.rows(p["qy"], 0)], self.Y2.at[k], "y2", k, p["y_nb"])
        self.got(self.Y1.at[k], "y1", k)
        for j in range(2):
            r = self.rows(j * 2 + p["y"], 1)
            G[t, r] = G[t, r] + self.Y1[k, j]
        self.go(G.at[t, self.rows(p["qx"], 1)], self.X2.at[k], "x2", k, p["x_nb"])
    def three(self, k):
        p, t, G = self.p, self.t(k), self.G
        for h, (kind, R) in enumerate((("y2", self.Y2), ("x2", self.X2))):
            self.got(R.at[k], kind, k)
            r = self.rows(p["q"], h)
            G[t, r] = G[t, r] + R[k]
        if k:
            whole = pl.ds(pl.multiple_of(p["q"] * self.qr, 16), self.qr)
            self.go(G.at[t, whole], self.Z.at[3 - k], "z", k - 1, (p["d"], p["c"], t), 3 - k)
    def piece(self, q, core, h=None):
        start, size = core * self.half + q * self.qr, self.qr
        if h is not None: start, size = start + h * self.hr, self.hr
        return self.OUT.at[pl.ds(pl.multiple_of(start, 16), size)]
    def final(self):
        p = self.p
        whole = pl.ds(pl.multiple_of(p["q"] * self.qr, 16), self.qr)
        total = self.G[p["t"], whole].astype(F32)
        for k in range(3):
            self.got(self.Z.at[k], "z", k)
            total = total + self.Z[k].astype(F32)
        ref = self.piece(p["q"], p["core"])
        ref[...] = total.astype(BF16)
        self.go(ref, ref, "f", 0, p["x_nb"]); self.go(ref, ref, "f", 1, p["y_nb"])
    def spread(self):
        p = self.p
        ref = self.piece(p["qx"], p["core"]); self.got(ref, "f", 0)
        ref = self.piece(p["qx"], p["core"], 0); self.go(ref, ref, "f", 2, p["y_nb"])
        ref = self.piece(p["qy"], p["core"]); self.got(ref, "f", 1)
        ref = self.piece(p["qy"], p["core"], 1); self.go(ref, ref, "f", 3, p["x_nb"])
    def corner(self):
        p = self.p
        self.got(self.piece(p["qd"], p["core"], 0), "f", 2); self.got(self.piece(p["qd"], p["core"], 1), "f", 3)
        ref = self.OUT.at[pl.ds(pl.multiple_of(p["core"] * self.half, 16), self.half)]
        self.go(ref, ref, "f", 4, p["core_nb"])
    def end(self):
        p = self.p
        ref = self.OUT.at[pl.ds(pl.multiple_of((1 - p["core"]) * self.half, 16), self.half)]
        self.got(ref, "f", 4)
        for c in self.sent: c.wait_send()
def scratch(rows, lanes):
    h = rows // 2; q = h // 4; r = q // 2
    return [pltpu.VMEM((4, h, lanes), BF16), pltpu.VMEM((4, 2, r, lanes), BF16), pltpu.VMEM((4, 2, r, lanes), BF16),
            pltpu.VMEM((4, r, lanes), BF16), pltpu.VMEM((4, r, lanes), BF16), pltpu.VMEM((3, q, lanes), BF16)]
SEMS = ("x1", "y1", "x2", "y2", "z", "f")
KO = (2, 1, 3, 0)
def rs_kernel(*refs):
    ins, outs, rest = refs[:4], refs[4:8], refs[8:]
    bufs = [rest[6 * i:6 * i + 6] for i in range(4)]; rest = rest[24:]
    cbuf = rest[:4]; rest = rest[4:]
    sems = dict(zip(SEMS, rest[:6])); ld, cs = rest[6], rest[7]
    p = place()
    loads = []
    for i in range(4):
        half = ins[i].shape[1] // 2
        mine = pl.ds(pl.multiple_of(p["core"] * half, 16), half)
        for k in KO:
            t = lax.rem(p["t"] + k, 4)
            c = pltpu.make_async_copy(ins[i].at[t, mine], bufs[i][0].at[t], ld.at[i, k]); c.start(); loads.append(c)
    greet(p)
    sent = []
    for i in range(4):
        half = ins[i].shape[1] // 2
        theirs = pl.ds(pl.multiple_of((1 - p["core"]) * half, 16), half)
        for k in KO:
            t = lax.rem(p["t"] + k, 4)
            c = pltpu.make_async_remote_copy(ins[i].at[t, theirs], cbuf[i].at[t], cs.at[0, i, k], cs.at[1, i, k], device_id=p["core_nb"], device_id_type=MESH)
            c.start(); sent.append(c)
    R = [Reduce(p, i, *bufs[i], outs[i], sems) for i in range(4)]
    units = [(i, k) for i in range(4) for k in KO]
    def start(n):
        i, k = units[n]
        t = lax.rem(p["t"] + k, 4)
        loads[n].wait(); sent[n].wait_recv()
        G, C = bufs[i][0], cbuf[i]
        def add(j, _):
            r = pl.ds(pl.multiple_of(j * 64, 64), 64)
            G[t, r] = G[t, r] + C[t, r]; return 0
        lax.fori_loop(0, G.shape[1] // 64, add, 0)
        R[i].one(k)
    LAG = 2
    N = len(units)
    events = []
    for n in range(N + 2 * LAG):
        if n < N: start(n)
        if 0 <= n - LAG < N: i, k = units[n - LAG]; R[i].two(k)
        if 0 <= n - 2 * LAG < N:
            i, k = units[n - 2 * LAG]; R[i].three(k)
            m = n - 2 * LAG
            if m >= 5 and m % 4 == 1: R[m // 4 - 1].final()
            if m >= 5 and m % 4 == 2: R[m // 4 - 1].spread()
            if m >= 5 and m % 4 == 3: R[m // 4 - 1].corner()
    R[3].final(); R[3].spread(); R[3].corner()
    for r in R: r.end()
    for c in sent: c.wait_send()
def reduce_call(*gs):
    V = pl.BlockSpec(memory_space=pltpu.VMEM); A = pl.BlockSpec(memory_space=pl.ANY)
    sem = pltpu.SemaphoreType.DMA((2, 4, 5))
    scr = [s for g in gs for s in scratch(g.shape[1], g.shape[2])] + [pltpu.VMEM((4, g.shape[1] // 2, g.shape[2]), BF16) for g in gs]
    return pl.pallas_call(rs_kernel, out_shape=[jax.ShapeDtypeStruct(g.shape[1:], BF16) for g in gs],
        in_specs=[A] * 4, out_specs=[V] * 4, scratch_shapes=scr + [sem] * 6 + [pltpu.SemaphoreType.DMA((4, 4)), pltpu.SemaphoreType.DMA((2, 4, 4))],
        compiler_params=pltpu.CompilerParams(collective_id=1, has_side_effects=True, vmem_limit_bytes=60 << 20), name="reduce")(*gs)


def small_pack(feature_weight, mixer_bias, feature_bias, inner_bias):
    weights = feature_weight.transpose(1, 2, 0, 3).reshape(192, 128)
    left = jnp.pad(mixer_bias.reshape(9, HD), ((0, 7), (0, 0)))
    right = jnp.pad(feature_bias.reshape(6, HD), ((0, 10), (0, 0)))
    rows = jnp.concatenate([left, right], axis=1)
    return jnp.concatenate([weights, rows, jnp.pad(inner_bias.reshape(6, 128), ((0, 42), (0, 0)))])


def small_unpack(small):
    n = small.shape[0]
    weights = small[:, :192].reshape(n, 3, HD, 2, HD).transpose(0, 3, 1, 2, 4)
    mixer_bias = small[:, 192:201, :HD].reshape(n, 3, 3 * HD)
    feature_bias = small[:, 192:198, HD:].reshape(n, 2, 3, HD)
    return weights, mixer_bias, feature_bias, small[:, 208:214].reshape(n, 768)


def shards(
    fast,
    tokens,
    first_gain,
    first_bias,
    mixer_weight,
    mixer_bias,
    feature_weight,
    feature_bias,
    output_weight,
    output_bias,
    second_gain,
    second_bias,
    inner_weight,
    inner_bias,
    outer_weight,
    outer_bias,
    block_owner,
    cotangent,
):
    rows, width = tokens.shape
    n_tp, n_ctx = lax.axis_size("tp"), lax.axis_size("ctx")
    n_plane = lax.axis_size("dp") * n_ctx
    plane = lax.axis_index("dp") * n_ctx + lax.axis_index("ctx")
    heads_here = mixer_weight.shape[2] // HD
    heads = heads_here * n_tp
    mine = lax.axis_index("ctx") * n_tp + lax.axis_index("tp")

    mixer_t = mixer_weight.transpose(1, 2, 0).reshape(-1, width)
    if fast:
        mixed_pack, inner_all, outer_all, small = gather_call(
            mixer_t, output_weight, inner_weight, outer_weight, small_pack(
                feature_weight, mixer_bias, feature_bias, inner_bias
            )
        )
        mixer_all, output_all = mixed_pack[:, :576], mixed_pack[:, 576:]
        feature_all, mixer_bias_all, feature_bias_all, inner_bias_all = small_unpack(small)
        feature_all = feature_all.transpose(1, 0, 2, 3, 4).reshape(2, heads, HD, HD)
        feature_bias_all = feature_bias_all.astype(F32).transpose(1, 0, 2, 3).reshape(2, heads, HD)
        mixer_bias_all = mixer_bias_all.astype(F32).reshape(n_tp, -1)
        inner_bias_all = inner_bias_all.astype(F32)
    else:
        sizes = [w.shape[0] for w in (mixer_t, output_weight, inner_weight, outer_weight)]
        pack = jnp.concatenate([mixer_t, output_weight, inner_weight, outer_weight], axis=0)
        part = pack.shape[0] // n_plane
        piece = lax.dynamic_slice_in_dim(pack, plane * part, part, 0)
        full = lax.all_gather(piece, ALL, axis=0, tiled=True)
        full = full.reshape(n_plane, n_tp, part, width).transpose(1, 0, 2, 3).reshape(n_tp, -1, width)
        cuts = [0]
        for s in sizes:
            cuts.append(cuts[-1] + s)
        mixer_all, output_all, inner_all, outer_all = [
            full[:, a:b] for a, b in zip(cuts[:-1], cuts[1:])
        ]
        small = jnp.concatenate(
            [feature_weight.reshape(-1), mixer_bias.reshape(-1), feature_bias.reshape(-1), inner_bias]
        )
        small = lax.all_gather(small, "tp")
        cut = feature_weight.size
        feature_all = (
            small[:, :cut].reshape(n_tp, 2, heads_here, HD, HD).transpose(1, 0, 2, 3, 4)
        ).reshape(2, heads, HD, HD)
        mixer_bias_all = small[:, cut : cut + mixer_bias.size].astype(F32).reshape(n_tp, -1)
        cut += mixer_bias.size
        feature_bias_all = (
            small[:, cut : cut + feature_bias.size]
            .astype(F32)
            .reshape(n_tp, 2, heads_here, HD)
            .transpose(1, 0, 2, 3)
            .reshape(2, heads, HD)
        )
        cut += feature_bias.size
        inner_bias_all = small[:, cut:].astype(F32)

    x = tokens.astype(F32)
    gain1, gain2 = first_gain.astype(F32), second_gain.astype(F32)
    h1, n1, r1 = layer_norm(x, gain1, first_bias.astype(F32))
    h1 = h1.astype(BF16)
    mix = ein("td,skd->tsk", h1, mixer_all) + mixer_bias_all
    mix = mix.astype(BF16).reshape(rows, n_tp, 3, heads_here, HD).transpose(2, 0, 1, 3, 4)
    mix = mix.reshape(3, rows, heads, HD)
    q, k, v = mix[0], mix[1], mix[2]
    q_up, q_down, phi_q = feature_map(q, feature_all[0], feature_bias_all[0])
    k_up, k_down, phi_k = feature_map(k, feature_all[1], feature_bias_all[1])

    chunk = min(CHUNK, rows)
    chunks = rows // chunk
    pq = phi_q.reshape(chunks, chunk, heads, 2 * HD)
    pk = phi_k.reshape(chunks, chunk, heads, 2 * HD)
    vc = v.reshape(chunks, chunk, heads, HD)
    causal = jnp.arange(chunk)[:, None] >= jnp.arange(chunk)[None, :]
    state = ein("jthe,jthf->jhef", vc, pk)
    norm = jnp.sum(pk.astype(F32), axis=1)
    both = jnp.concatenate([state, norm[:, :, None]], axis=2)
    owners = block_owner[0].reshape(n_tp, -1)[:, 0]
    order = jnp.arange(n_ctx * n_tp)
    same = jnp.tile(owners, n_ctx) == jnp.tile(owners, n_ctx)[mine]

    def prefix(totals, reach):
        everything = lax.all_gather(totals.astype(BF16), ("ctx", "tp")).astype(F32)
        return jnp.einsum("s,shef->hef", reach.astype(F32), everything, precision="highest")

    def running(blocks, start, reverse):
        out = [None] * chunks
        acc = start
        for j in reversed(range(chunks)) if reverse else range(chunks):
            out[j] = acc
            acc = acc + blocks[j]
        return jnp.stack(out)

    before = running(both, prefix(jnp.sum(both, axis=0), same & (order < mine)), False)
    before = before.astype(BF16)
    scores = ein("jthf,jshf->jhts", pq, pk)
    a_low = jnp.where(causal, scores, 0.0).astype(BF16)
    v_one = jnp.concatenate([vc, jnp.ones(vc.shape[:-1] + (1,), BF16)], axis=-1)
    num = ein("jthf,jhef->jthe", pq, before) + ein("jhts,jshe->jthe", a_low, v_one)
    num, den = num[..., :HD], num[..., HD:]
    o = num / den
    o_low = o.astype(BF16)
    o_flat = o_low.reshape(rows, n_tp, heads_here * HD)
    x2 = x + ein("tsk,skd->td", o_flat, output_all) + output_bias.astype(F32)
    h2, n2, r2 = layer_norm(x2, gain2, second_bias.astype(F32))
    h2 = h2.astype(BF16)
    f = ein("td,sdf->tsf", h2, inner_all) + inner_bias_all
    a, slope = gelu_parts(f)
    a = a.astype(BF16)
    result = (x2 + ein("tsf,sfd->td", a, outer_all) + outer_bias.astype(F32)).astype(BF16)

    g = cotangent.astype(F32)
    d_outer = ein("tsf,td->sfd", a, cotangent)
    df = (ein("td,sfd->tsf", cotangent, outer_all) * slope).astype(BF16)
    d_inner_bias = jnp.sum(df.astype(F32), axis=0)
    d_inner = ein("td,tsf->sdf", h2, df)
    e2 = ein("tsf,sdf->td", df, inner_all)
    back2, d_gain2, d_bias2 = layer_norm_back(e2, n2, r2, gain2)
    dx2 = g + back2
    big_g = dx2.astype(BF16)
    d_output = ein("tsk,td->skd", o_flat, big_g)
    do = ein("td,skd->tsk", big_g, output_all).astype(BF16).astype(F32)
    do = do.reshape(chunks, chunk, heads, HD)
    dnum = do / den
    dden = -jnp.sum(do * o, axis=-1, keepdims=True) / den
    dne = jnp.concatenate([dnum, dden], axis=-1).astype(BF16)
    da = ein("jthe,jshe->jhts", dne, v_one)
    da_low = jnp.where(causal, da, 0.0).astype(BF16)
    d_both = ein("jthe,jthf->jhef", dne, pq)
    after = running(d_both, prefix(jnp.sum(d_both, axis=0), same & (order > mine)), True)
    after = after.astype(BF16)
    dphi_q = ein("jhts,jshf->jthf", da_low, pk) + ein("jthe,jhef->jthf", dne, before)
    dphi_k = ein("jhts,jthf->jshf", da_low, pq) + ein("jthe,jhef->jthf", v_one, after)
    dv = ein("jhts,jthe->jshe", a_low, dne[..., :HD]) + ein("jthf,jhef->jthe", pk, after[:, :, :HD])
    dphi_q = dphi_q.reshape(rows, heads, 2 * HD)
    dphi_k = dphi_k.reshape(rows, heads, 2 * HD)
    dq, d_fq, d_fbq = feature_back(dphi_q, q_up, q_down, q, feature_all[0])
    dk, d_fk, d_fbk = feature_back(dphi_k, k_up, k_down, k, feature_all[1])
    dmix = jnp.stack([dq, dk, dv.reshape(rows, heads, HD)], axis=1).astype(BF16)
    dmix = dmix.reshape(rows, 3, n_tp, heads_here * HD).transpose(0, 2, 1, 3)
    dmix = dmix.reshape(rows, n_tp, -1)
    d_mixer_bias = jnp.sum(dmix.astype(F32), axis=0)
    d_mixer = ein("tsk,td->skd", dmix, h1)
    e1 = ein("tsk,skd->td", dmix, mixer_all)
    back1, d_gain1, d_bias1 = layer_norm_back(e1, n1, r1, gain1)
    tokens_gradient = dx2 + back1

    if fast:
        shared = jnp.stack(
            [d_gain1, d_bias1, jnp.sum(dx2, axis=0), d_gain2, d_bias2, jnp.sum(g, axis=0)]
        )
        small = jax.vmap(small_pack)(
            jnp.stack([d_fq, d_fk]).reshape(2, n_tp, heads_here, HD, HD).transpose(1, 0, 2, 3, 4),
            d_mixer_bias.reshape(n_tp, 3, -1),
            jnp.stack([d_fbq, d_fbk]).reshape(2, n_tp, heads_here, HD).transpose(1, 0, 2, 3),
            d_inner_bias,
        )
        small = small + jnp.pad(shared.reshape(36, 128), ((216, 4), (0, 0)))
        d_outer, d_inner, mixed_pack, small = reduce_call(
            d_outer.astype(BF16),
            d_inner.astype(BF16),
            jnp.concatenate([d_mixer, d_output], axis=1).astype(BF16),
            small.astype(BF16),
        )
        d_outer, d_inner, mixed_pack = [v.astype(F32) for v in (d_outer, d_inner, mixed_pack)]
        small = small.astype(F32)
        d_mixer, d_output = mixed_pack[:576], mixed_pack[576:]
        d_mixer = d_mixer.reshape(3, heads_here * HD, width).transpose(2, 0, 1)
        d_feature, d_mixer_bias, d_feature_bias, d_inner_bias = [
            v[0] for v in small_unpack(small[None])
        ]
        shared = small[216:252].reshape(6, width)
    else:
        big = jnp.concatenate([d_mixer, d_output, d_inner, d_outer], axis=1).astype(BF16)
        big = big.reshape(n_tp, n_plane, part, width).transpose(1, 0, 2, 3).reshape(-1, width)
        big = lax.psum_scatter(big, ("dp", "ctx"), scatter_dimension=0, tiled=True)
        big = lax.psum_scatter(big, "tp", scatter_dimension=0, tiled=True)
        big = lax.all_gather(big, ("dp", "ctx"), axis=0, tiled=True).astype(F32)
        d_mixer, d_output, d_inner, d_outer = [big[a:b] for a, b in zip(cuts[:-1], cuts[1:])]
        d_mixer = d_mixer.reshape(3, heads_here * HD, width).transpose(2, 0, 1)
        per_tp = jnp.concatenate(
            [
                jnp.stack([d_fq, d_fk]).reshape(2, n_tp, -1).transpose(1, 0, 2).reshape(n_tp, -1),
                d_mixer_bias,
                jnp.stack([d_fbq, d_fbk]).reshape(2, n_tp, -1).transpose(1, 0, 2).reshape(n_tp, -1),
                d_inner_bias,
            ],
            axis=1,
        )
        shared = jnp.stack(
            [d_gain1, d_bias1, jnp.sum(dx2, axis=0), d_gain2, d_bias2, jnp.sum(g, axis=0)]
        )
        total = lax.psum(jnp.concatenate([per_tp.reshape(-1), shared.reshape(-1)]), ALL)
        shared = total[per_tp.size :].reshape(6, width)
        own = lax.dynamic_slice_in_dim(
            total[: per_tp.size].reshape(n_tp, -1), lax.axis_index("tp"), 1, 0
        )[0]
        cut = feature_weight.size
        d_feature = own[:cut].reshape(feature_weight.shape)
        d_mixer_bias = own[cut : cut + mixer_bias.size].reshape(mixer_bias.shape)
        cut += mixer_bias.size
        d_feature_bias = own[cut : cut + feature_bias.size].reshape(feature_bias.shape)
        d_inner_bias = own[cut + feature_bias.size :]

    return (
        result,
        tokens_gradient,
        shared[0],
        shared[1],
        d_mixer,
        d_mixer_bias,
        d_feature,
        d_feature_bias,
        d_output,
        shared[2],
        shared[3],
        shared[4],
        d_inner,
        d_inner_bias,
        d_outer,
        shared[5],
    )


def solution(mesh):
    in_specs = (
        P(("dp", "ctx", "tp"), None),
        P(),
        P(),
        P(None, None, "tp"),
        P(None, "tp"),
        P(None, "tp", None, None),
        P(None, "tp", None),
        P("tp", None),
        P(),
        P(),
        P(),
        P(None, "tp"),
        P("tp"),
        P("tp", None),
        P(),
        P("dp", None),
        P(("dp", "ctx", "tp"), None),
    )
    out_specs = (
        P(("dp", "ctx", "tp"), None),
        P(("dp", "ctx", "tp"), None),
        P(),
        P(),
        P(None, None, "tp"),
        P(None, "tp"),
        P(None, "tp", None, None),
        P(None, "tp", None),
        P("tp", None),
        P(),
        P(),
        P(),
        P(None, "tp"),
        P("tp"),
        P("tp", None),
        P(),
    )
    fast = (mesh.shape["dp"], mesh.shape["ctx"], mesh.shape["tp"]) == (2, 4, 4)
    return jax.shard_map(functools.partial(shards, fast), mesh=mesh, in_specs=in_specs, out_specs=out_specs, check_vma=False)
```

```python
import functools
from types import SimpleNamespace

import jax
import jax.numpy as jnp
from jax import lax
from jax.experimental import pallas as pl
from jax.experimental.pallas import tpu as pltpu
from jax.sharding import PartitionSpec as P

MESH = pl.DeviceIdType.MESH

HD = 64
BLOCK = 64
CHUNK = 256
EPSILON = 1e-05
F32 = jnp.float32
BF16 = jnp.bfloat16
ALL = ("dp", "ctx", "tp")


def ein(spec, a, b):
    return jnp.einsum(spec, a, b, preferred_element_type=F32)


def layer_norm(v, gain, offset):
    c = v - jnp.mean(v, axis=-1, keepdims=True)
    r = lax.rsqrt(jnp.mean(c * c, axis=-1, keepdims=True) + EPSILON)
    n = c * r
    return n * gain + offset, n, r


def layer_norm_back(e, n, r, gain):
    m = e * gain
    back = r * (
        m - jnp.mean(m, axis=-1, keepdims=True) - n * jnp.mean(m * n, axis=-1, keepdims=True)
    )
    return back, jnp.sum(e * n, axis=0), jnp.sum(e, axis=0)


def gelu_parts(s):
    t = jnp.tanh(0.7978845608028654 * (s + 0.044715 * s * s * s))
    slope = 0.7978845608028654 * (1.0 + 3.0 * 0.044715 * s * s)
    return 0.5 * s * (1.0 + t), 0.5 * (1.0 + t) + 0.5 * s * (1.0 - t * t) * slope


def feature_map(q, weight, offset):
    u = ein("thd,hde->the", q, weight) + offset
    up, down = jax.nn.softmax(u, axis=-1), jax.nn.softmax(-u, axis=-1)
    return up, down, jnp.concatenate([up, down], axis=-1).astype(BF16)


def feature_back(delta, up, down, q, weight):
    d, dd = delta[..., :HD], delta[..., HD:]
    du = up * (d - jnp.sum(up * d, axis=-1, keepdims=True)) - down * (
        dd - jnp.sum(down * dd, axis=-1, keepdims=True)
    )
    low = du.astype(BF16)
    return ein("the,hde->thd", low, weight), ein("thd,the->hde", q, low), jnp.sum(du, axis=0)


HD = 64
BLOCK = 64
CHUNK = 256
EPSILON = 1e-05
F32 = jnp.float32
BF16 = jnp.bfloat16
ALL = ("dp", "ctx", "tp")


def ein(spec, a, b):
    return jnp.einsum(spec, a, b, preferred_element_type=F32)


def layer_norm(v, gain, offset):
    c = v - jnp.mean(v, axis=-1, keepdims=True)
    r = lax.rsqrt(jnp.mean(c * c, axis=-1, keepdims=True) + EPSILON)
    n = c * r
    return n * gain + offset, n, r


def layer_norm_back(e, n, r, gain):
    m = e * gain
    back = r * (
        m - jnp.mean(m, axis=-1, keepdims=True) - n * jnp.mean(m * n, axis=-1, keepdims=True)
    )
    return back, jnp.sum(e * n, axis=0), jnp.sum(e, axis=0)


def gelu_parts(s):
    t = jnp.tanh(0.7978845608028654 * (s + 0.044715 * s * s * s))
    slope = 0.7978845608028654 * (1.0 + 3.0 * 0.044715 * s * s)
    return 0.5 * s * (1.0 + t), 0.5 * (1.0 + t) + 0.5 * s * (1.0 - t * t) * slope


def feature_map(q, weight, offset):
    u = ein("thd,hde->the", q, weight) + offset
    up, down = jax.nn.softmax(u, axis=-1), jax.nn.softmax(-u, axis=-1)
    return up, down, jnp.concatenate([up, down], axis=-1).astype(BF16)


def feature_back(delta, up, down, q, weight):
    d, dd = delta[..., :HD], delta[..., HD:]
    du = up * (d - jnp.sum(up * d, axis=-1, keepdims=True)) - down * (
        dd - jnp.sum(down * dd, axis=-1, keepdims=True)
    )
    low = du.astype(BF16)
    return ein("the,hde->thd", low, weight), ein("thd,the->hde", q, low), jnp.sum(du, axis=0)


def place():
    d, c, t = lax.axis_index("dp"), lax.axis_index("ctx"), lax.axis_index("tp")
    y, core = c // 2, lax.rem(c, 2)
    return SimpleNamespace(d=d, c=c, t=t, y=y, core=core, q=d * 2 + y,
        x_nb=(1 - d, c, t), y_nb=(d, (1 - y) * 2 + core, t), core_nb=(d, y * 2 + 1 - core, t),
        qx=(1 - d) * 2 + y, qy=d * 2 + 1 - y, qd=(1 - d) * 2 + 1 - y)

def greet(p):
    bar = pltpu.get_barrier_semaphore()
    peers = [p.x_nb, p.y_nb, p.core_nb] + [(p.d, p.c, lax.rem(p.t + k, 4)) for k in (1, 2, 3)]
    for peer in peers:
        pl.semaphore_signal(bar, inc=1, device_id=peer, device_id_type=MESH)
    pl.semaphore_wait(bar, len(peers))

def nearest(t):
    return [
        jnp.where(t < 2, 1, 3),
        jnp.where(t == 0, 2, jnp.where(t == 1, 3, jnp.where(t == 2, 1, 2))),
        jnp.where(t == 0, 3, jnp.where(t == 3, 1, 2)),
    ]


class Gather:
    def __init__(self, p, buf, sems, index):
        self.p, self.buf, self.sems, self.i = p, buf, sems, index
        self.rows = buf.shape[1]
        self.piece = self.rows // 8
        self.half = self.piece // 2
        self.sent = []
    def at(self, t, q, core, half=None):
        start = q * (2 * self.piece) + core * self.piece
        size = self.piece
        if half is not None:
            start, size = start + half * self.half, self.half
        return self.buf.at[t, pl.ds(pl.multiple_of(start, 16), size)]
    def shard(self, k): return lax.rem(self.p.t + k, 4)
    def copy(self, ref, kind, k, peer):
        s = self.sems[kind]
        return pltpu.make_async_remote_copy(ref, ref, s.at[0, self.i, k - 1], s.at[1, self.i, k - 1], device_id=peer, device_id_type=MESH)
    def go(self, *a):
        c = self.copy(*a); c.start(); self.sent.append(c)
    def first(self):
        p = self.p
        for k in (1, 2, 3):
            ref = self.at(p.t, p.q, p.core)
            s = self.sems["z"]
            c = pltpu.make_async_remote_copy(ref, ref, s.at[0, self.i, k - 1], s.at[1, self.i, 3 - k], device_id=(p.d, p.c, lax.rem(p.t + k, 4)), device_id_type=MESH)
            c.start(); self.sent.append(c)
    def z(self, k):
        p, t = self.p, self.shard(k)
        ref = self.at(t, p.q, p.core)
        self.copy(ref, "z", k, p.x_nb).wait_recv()
        self.go(ref, "x", k, p.x_nb); self.go(ref, "y", k, p.y_nb)
    def hop(self, ref, ok, up, k_there):
        p = self.p; s = self.sems["z"]
        i = self.nz; self.nz += 1
        c = pltpu.make_async_remote_copy(ref, ref, s.at[0, self.i, i], s.at[1, self.i, k_there - 1],
            device_id=(p.d, p.c, jnp.where(up, p.t + 1, p.t - 1)), device_id_type=MESH)
        @pl.when(ok)
        def _(): c.start()
        self.cond.append((ok, c))
    def first_hop(self):
        p = self.p; self.nz = 0; self.cond = []
        ref = self.at(p.t, p.q, p.core)
        self.hop(ref, p.t < 3, True, 3)
        self.hop(ref, p.t > 0, False, 1)
    def zf(self, k):
        p, t = self.p, self.shard(k)
        ref = self.at(t, p.q, p.core)
        self.copy(ref, "z", k, p.x_nb).wait_recv()
        up = t < p.t
        self.hop(ref, jnp.where(up, p.t < 3, p.t > 0), up, jnp.where(up, k - 1, k + 1))
        self.go(ref, "x", k, p.x_nb); self.go(ref, "y", k, p.y_nb)
    def drain_hops(self):
        for ok, c in self.cond:
            @pl.when(ok)
            def _(): c.wait_send()
    def xy(self, k):
        p, t = self.p, self.shard(k)
        self.copy(self.at(t, p.qx, p.core), "x", k, p.x_nb).wait_recv()
        self.go(self.at(t, p.qx, p.core, 0), "fy", k, p.y_nb)
        self.copy(self.at(t, p.qy, p.core), "y", k, p.y_nb).wait_recv()
        self.go(self.at(t, p.qy, p.core, 1), "fx", k, p.x_nb)
    def diag(self, k):
        p, t = self.p, self.shard(k)
        self.copy(self.at(t, p.qd, p.core, 0), "fy", k, p.y_nb).wait_recv()
        self.copy(self.at(t, p.qd, p.core, 1), "fx", k, p.x_nb).wait_recv()
        for q in range(4):
            self.go(self.at(t, q, p.core), "c", k, p.core_nb)
    def done(self, k):
        p, t = self.p, self.shard(k)
        ref = self.buf.at[t, pl.ds(0, 4 * self.piece)]
        s = self.sems["c"]
        pltpu.make_async_remote_copy(ref, ref, s.at[0, self.i, k - 1], s.at[1, self.i, k - 1], device_id=p.core_nb, device_id_type=MESH).wait_recv()
    def drain(self):
        for c in self.sent:
            c.wait_send()


class Reduce:
    def __init__(self, p, i, G, X1, Y1, X2, Y2, Z, F, OUT, sems, own):
        self.p, self.i, self.G, self.OUT, self.sems = p, i, G, OUT, sems
        self.X1, self.Y1, self.X2, self.Y2, self.Z = X1, Y1, X2, Y2, Z
        self.half = G.shape[1]; self.qr = self.half // 4; self.hr = self.qr // 2
        self.sent = []
        self.F, self.own = F, own
    def t(self, k): return lax.rem(self.p.t + k, 4)
    def rows(self, q, h): return pl.ds(pl.multiple_of(q * self.qr + h * self.hr, 16), self.hr)
    def rdma(self, src, dst, kind, k, peer, k_there=None):
        s = self.sems[kind]
        return pltpu.make_async_remote_copy(src, dst, s.at[0, self.i, k], s.at[1, self.i, k if k_there is None else k_there], device_id=peer, device_id_type=MESH)
    def go(self, *a):
        c = self.rdma(*a); c.start(); self.sent.append(c)
    def got(self, ref, kind, k):
        self.rdma(ref, ref, kind, k, self.p.x_nb).wait_recv()
    def one(self, k):
        p, t = self.p, self.t(k)
        for j in range(2):
            self.go(self.G.at[t, self.rows((1 - p.d) * 2 + j, 0)], self.X1.at[k, j], "x1", k, p.x_nb)
            self.go(self.G.at[t, self.rows(j * 2 + 1 - p.y, 1)], self.Y1.at[k, j], "y1", k, p.y_nb)
    def two(self, k):
        p, t, G = self.p, self.t(k), self.G
        self.got(self.X1.at[k], "x1", k)
        for j in range(2):
            r = self.rows(p.d * 2 + j, 0)
            G[t, r] = G[t, r] + self.X1[k, j]
        self.go(G.at[t, self.rows(p.qy, 0)], self.Y2.at[k], "y2", k, p.y_nb)
        self.got(self.Y1.at[k], "y1", k)
        for j in range(2):
            r = self.rows(j * 2 + p.y, 1)
            G[t, r] = G[t, r] + self.Y1[k, j]
        self.go(G.at[t, self.rows(p.qx, 1)], self.X2.at[k], "x2", k, p.x_nb)
    def three(self, k):
        p, t, G = self.p, self.t(k), self.G
        for h, (kind, R) in enumerate((("y2", self.Y2), ("x2", self.X2))):
            self.got(R.at[k], kind, k)
            r = self.rows(p.q, h)
            G[t, r] = G[t, r] + R[k]
        if not isinstance(k, int):
            whole = pl.ds(pl.multiple_of(p.q * self.qr, 16), self.qr)
            self.go(G.at[t, whole], self.Z.at[3 - k], "z", k - 1, (p.d, p.c, t), 3 - k)
    def piece(self, q, core, h=None):
        start, size = core * self.half + q * self.qr, self.qr
        if h is not None: start, size = start + h * self.hr, self.hr
        return self.OUT.at[pl.ds(pl.multiple_of(start, 16), size)]
    def final(self):
        p = self.p
        whole = pl.ds(pl.multiple_of(p.q * self.qr, 16), self.qr)
        total = self.G[p.t, whole].astype(F32)
        for k in range(3):
            self.got(self.Z.at[k], "z", k)
            total = total + self.Z[k].astype(F32)
        ref = self.piece(p.q, p.core)
        self.F[...] = total.astype(BF16)
        self.go(self.F, ref, "f", 0, p.x_nb)
        self.go(self.F, ref, "f", 1, p.y_nb)
        pltpu.make_async_copy(self.F, ref, self.own.at[self.i]).start()

    def spread(self):
        p = self.p
        ref = self.piece(p.qx, p.core); self.got(ref, "f", 0)
        ref = self.piece(p.qx, p.core, 0); self.go(ref, ref, "f", 2, p.y_nb)
        ref = self.piece(p.qy, p.core); self.got(ref, "f", 1)
        ref = self.piece(p.qy, p.core, 1); self.go(ref, ref, "f", 3, p.x_nb)
    def corner(self):
        p = self.p
        pltpu.make_async_copy(self.F, self.piece(p.q, p.core), self.own.at[self.i]).wait()
        self.got(self.piece(p.qd, p.core, 0), "f", 2); self.got(self.piece(p.qd, p.core, 1), "f", 3)
        ref = self.OUT.at[pl.ds(pl.multiple_of(p.core * self.half, 16), self.half)]
        self.go(ref, ref, "f", 4, p.core_nb)
    def end(self):
        p = self.p
        ref = self.OUT.at[pl.ds(pl.multiple_of((1 - p.core) * self.half, 16), self.half)]
        self.got(ref, "f", 4)
        for c in self.sent: c.wait_send()


GATHER_SEMS = ("z", "x", "y", "fx", "fy", "c")
SEMS = ("x1", "y1", "x2", "y2", "z", "f")


def dot(a, b, ca, cb):
    return lax.dot_general(a, b, (((ca,), (cb,)), ((), ())), preferred_element_type=F32)


def loop(n, step):
    def body(i, carry):
        step(i)
        return carry

    lax.fori_loop(0, n, body, 0)


def ds(i, n):
    return pl.ds(pl.multiple_of(i * n, n), n)


class Scan:
    GROUPS = 3

    def __init__(self, p, later, total, pair, up, down, got, sems):
        self.p, self.later, self.total, self.pair_ref, self.up_ref, self.down_ref = p, later, total, pair, up, down
        self.from_core, self.from_y, self.from_below, self.from_above = [got.at[i] for i in range(4)]
        self.sems = sems
        self.sent = []

    def rdma(self, src, dst, i, peer):
        return pltpu.make_async_remote_copy(
            src, dst, self.sems.at[0, i], self.sems.at[1, i], device_id=peer, device_id_type=MESH
        )

    def heads(self, g):
        n = self.total.shape[0] // self.GROUPS
        return pl.ds(g * n, n)

    def begin(self):
        t = self.p.t

        @pl.when(t == 0)
        def _():
            self.from_below[...] = jnp.zeros_like(self.from_below)

        @pl.when(t == 3)
        def _():
            self.from_above[...] = jnp.zeros_like(self.from_above)

        c = self.rdma(self.total, self.from_core, 0, self.p.core_nb)
        c.start()
        self.sent.append(c)

    def pair(self):
        self.rdma(self.total, self.from_core, 0, self.p.core_nb).wait_recv()
        self.pair_ref[...] = self.total[...] + self.from_core[...]
        c = self.rdma(self.pair_ref, self.from_y, 1, self.p.y_nb)
        c.start()
        self.sent.append(c)

    def column(self, g):
        p, h = self.p, self.heads(g)
        core, y = p.core.astype(F32), p.y.astype(F32)
        if self.later:
            core, y = 1.0 - core, 1.0 - y
        return core * self.from_core[h].astype(F32) + y * self.from_y[h].astype(F32)

    def wait_y(self):
        self.rdma(self.pair_ref, self.from_y, 1, self.p.y_nb).wait_recv()

    def hop(self, g, upward):
        p, h, t = self.p, self.heads(g), self.p.t
        got = self.from_below if upward else self.from_above
        out = self.up_ref if upward else self.down_ref
        peer = (p.d, p.c, t + 1 if upward else t - 1)
        has, sends = (t > 0, t < 3) if upward else (t < 3, t > 0)
        c = self.rdma(out.at[h], got.at[h], 2 + g + (0 if upward else self.GROUPS), peer)

        @pl.when(has)
        def _():
            c.wait_recv()

        @pl.when(sends)
        def _():
            value = self.column(g) + got[h].astype(F32)
            if upward != self.later:
                value = value + self.total[h].astype(F32)
            out[h] = value.astype(BF16)
            c.start()

    def chain(self, first):
        t = self.p.t

        @pl.when(t < 2)
        def _():
            for g in range(self.GROUPS):
                self.hop(g, first)

        @pl.when(t >= 2)
        def _():
            for g in range(self.GROUPS):
                self.hop(g, not first)

    def sum(self, g):
        h = self.heads(g)
        return self.column(g) + self.from_below[h].astype(F32) + self.from_above[h].astype(F32)

    def drain(self):
        p, t = self.p, self.p.t
        for c in self.sent:
            c.wait_send()
        for g in range(self.GROUPS):
            h = self.heads(g)
            for upward in (True, False):
                out = self.up_ref if upward else self.down_ref
                peer = (p.d, p.c, t + 1 if upward else t - 1)
                c = self.rdma(out.at[h], out.at[h], 2 + g + (0 if upward else self.GROUPS), peer)

                @pl.when(t < 3 if upward else t > 0)
                def _(c=c):
                    c.wait_send()


def layer_rows(v):
    c = v - jnp.mean(v, axis=-1, keepdims=True)
    r = lax.rsqrt(jnp.mean(c * c, axis=-1, keepdims=True) + EPSILON)
    return c * r, r


def fold(v):
    total = v[:8]
    for i in range(1, v.shape[0] // 8):
        total = total + v[8 * i : 8 * i + 8]
    return total


def layer_back(e, n, r, gain):
    m = e * gain
    return r * (
        m - jnp.mean(m, axis=-1, keepdims=True) - n * jnp.mean(m * n, axis=-1, keepdims=True)
    )


def block_kernel(m):
    p = place()
    t0 = p.t
    X, CT, S, WA, W1, W2 = m.X, m.CT, m.S, m.WA, m.W1, m.W2
    VEC, H1, H2, X2, ACC_O, ACC_E = m.vec, m.H1, m.H2, m.X2, m.ACC_O, m.ACC_E
    MIX, PH, VX, AT, PX, SL, OT, RD = m.MIX, m.PH, m.VX, m.AT, m.PX, m.SL, m.OT, m.RD
    A, DF, DNE, DU, GS = m.A, m.DF, m.DNE, m.DU, m.GS
    FW, BC, IB, SUMS = m.FW, m.BC, m.IB, m.SUMS
    ld = m.ld
    loads = [
        pltpu.make_async_copy(m.small, S.at[t0], ld.at[0]),
        pltpu.make_async_copy(m.wm, WA.at[t0, pl.ds(0, 576)], ld.at[1]),
        pltpu.make_async_copy(m.wo, WA.at[t0, pl.ds(576, 192)], ld.at[2]),
        pltpu.make_async_copy(m.w1, W1.at[t0], ld.at[3]),
        pltpu.make_async_copy(m.w2, W2.at[t0], ld.at[4]),
        pltpu.make_async_copy(m.x, X, ld.at[5]),
        pltpu.make_async_copy(m.g, CT, ld.at[6]),
    ]
    for c in loads:
        c.start()
    greet(p)
    gsems = m.gather_sems
    gs, gw, g1, g2 = gathers = [Gather(p, b, gsems, i) for i, b in enumerate((S, WA, W1, W2))]
    for n, (g, ws) in enumerate(zip(gathers, ([0], [1, 2], [3], [4]))):
        for i in ws:
            loads[i].wait()
        g.first() if n == 0 else g.first_hop()
    K = nearest(t0)
    shard = gs.shard

    loads[5].wait()
    loads[6].wait()

    def norm1(i):
        r = ds(i, 128)
        n, _ = layer_rows(X[r].astype(F32))
        H1[r] = (n * VEC[0:1] + VEC[1:2]).astype(BF16)

    loop(4, norm1)
    ones_row = jnp.where(lax.broadcasted_iota(jnp.int32, (16, 512), 0) == 0, 1.0, 0.0).astype(BF16)

    def init(h):
        VX[h, 64:80] = ones_row
        DNE[h, 64:80] = jnp.zeros((16, 512), BF16)

    loop(12, init)
    SUMS[...] = jnp.zeros_like(SUMS)

    def small(t):
        rows = S[t, 192:208].astype(F32)
        BC[t] = rows.T
        rows = S[t, 208:224].astype(F32)
        for i in range(6):
            IB[t, :, 128 * i : 128 * i + 128] = rows[i : i + 1]
        for h in range(3):
            w = S[t, 64 * h : 64 * h + 64].astype(F32)
            FW[0, t * 3 + h] = w[:, :64].astype(BF16)
            FW[1, t * 3 + h] = w[:, 64:].astype(BF16)

    def mix(t):
        value = dot(WA[t, 0:576], H1[...], 1, 1)
        for j in range(3):
            for h in range(3):
                n = j * 3 + h
                part = (value[64 * n : 64 * n + 64] + BC[t, 0:64, n : n + 1]).astype(BF16)
                if j < 2:
                    MIX[t, 64 * n : 64 * n + 64] = part
                else:
                    VX[t * 3 + h, 0:64] = part

    def features(t):
        for h in range(3):
            for i in range(2):
                u = dot(FW[i, t * 3 + h], MIX[t, 192 * i + 64 * h : 192 * i + 64 * h + 64], 0, 0)
                u = u + BC[t, 64 * i : 64 * i + 64, 9 + h : 10 + h]
                e = jnp.exp(u - jnp.max(u, axis=0, keepdims=True))
                PH[i, t * 3 + h, 0:64] = (e / jnp.sum(e, axis=0, keepdims=True)).astype(BF16)
                e = jnp.exp(jnp.min(u, axis=0, keepdims=True) - u)
                PH[i, t * 3 + h, 64:128] = (e / jnp.sum(e, axis=0, keepdims=True)).astype(BF16)

    def states(t):
        def one(i):
            h = t * 3 + i
            s0 = dot(VX[h, :, 0:256], PH[1, h, :, 0:256], 1, 1)
            s1 = dot(VX[h, :, 256:512], PH[1, h, :, 256:512], 1, 1)
            SL[h] = s0
            m.TOT[h] = (s0 + s1).astype(BF16)

        loop(3, one)

    small(t0)
    mix(t0)
    features(t0)
    states(t0)
    for k in K:
        gs.z(k)
        gw.zf(k)
    for k in K:
        gs.xy(k)
        gw.xy(k)
    for k in K:
        g1.zf(k)
    for k in K:
        gs.diag(k)
        gw.diag(k)
    for k in K:
        g1.xy(k)
    for n, k in enumerate(K):
        gs.done(k)
        gw.done(k)
        t = shard(k)
        small(t)
        mix(t)
        g2.zf(k)
        features(t)
        g1.diag(k)
        states(t)

    scan = Scan(p, False, m.TOT, m.PAIR, m.UP, m.DOWN, m.got_f, m.scan_f)
    scan.begin()
    causal = lax.broadcasted_iota(jnp.int32, (256, 256), 0) <= lax.broadcasted_iota(
        jnp.int32, (256, 256), 1
    )

    def scores(h):
        for j in range(2):
            c = slice(256 * j, 256 * j + 256)
            a = dot(PH[1, h, :, c], PH[0, h, :, c], 0, 0)
            AT[h, j] = jnp.where(causal, a, 0.0).astype(BF16)

    loop(3, scores)
    scan.pair()
    loop(3, lambda h: scores(h + 3))
    for k in K:
        g2.xy(k)
    scan.wait_y()
    scan.chain(True)
    loop(6, lambda h: scores(h + 6))
    scan.chain(False)
    for g in range(scan.GROUPS):
        value = scan.sum(g)
        h = scan.heads(g)
        PX[h, 0] = value.astype(BF16)
        PX[h, 1] = (value + SL[h]).astype(BF16)

    def attend(h):
        for j in range(2):
            c = slice(256 * j, 256 * j + 256)
            num = dot(PX[h, j], PH[0, h, :, c], 1, 0) + dot(VX[h, :, c], AT[h, j], 1, 0)
            r = 1.0 / num[64:65]
            RD[h, :, c] = r
            OT[ds(h, 64), c] = (num[0:64] * r).astype(BF16)

    loop(12, attend)
    for k in K:
        g2.diag(k)

    def norm2(i):
        r = ds(i, 256)
        total = X[r].astype(F32) + VEC[2:3]
        for t in range(4):
            total = total + dot(OT[192 * t : 192 * t + 192, r], WA[t, 576:768], 0, 0)
        X2[r] = total
        n, _ = layer_rows(total)
        H2[r] = (n * VEC[3:4] + VEC[4:5]).astype(BF16)
        ACC_O[r] = total + VEC[5:6]
        ACC_E[r] = jnp.zeros((256, 768), F32)

    loop(2, norm2)

    sems = m.reduce_sems
    land = (0, 1, 0, 3)
    R = [
        Reduce(p, i, m.G[i], *m.land[land[i]][1:], m.Z[i], m.F[i], m.outs[i], sems, m.own)
        for i in range(4)
    ]
    CORE, core_sems, STAGE = [m.land[j][0] for j in land], m.r_core, m.STAGE
    outgoing = []

    def hand(i, k, value, slot):
        t = shard(k)
        if len(outgoing) >= 2:
            outgoing[-2].wait_send()
        STAGE[slot] = value(1 - p.core).astype(BF16)
        c = pltpu.make_async_remote_copy(
            STAGE.at[slot],
            CORE[i].at[t],
            core_sems.at[0, i, k],
            core_sems.at[1, i, k],
            device_id=p.core_nb,
            device_id_type=MESH,
        )
        c.start()
        outgoing.append(c)
        R[i].G[t] = value(p.core).astype(BF16)

    def meet(i, k):
        t = shard(k)
        G, C = R[i].G, CORE[i]
        pltpu.make_async_remote_copy(
            C.at[t],
            C.at[t],
            core_sems.at[0, i, k],
            core_sems.at[1, i, k],
            device_id=p.core_nb,
            device_id_type=MESH,
        ).wait_recv()

        def add(j):
            r = ds(j, 64)
            G[t, r] = G[t, r] + C[t, r]

        loop(G.shape[1] // 64, add)
        R[i].one(k)

    def hidden(t):
        def rows(i):
            r = ds(i, 256)
            f = dot(H2[r], W1[t], 1, 0) + IB[t]
            th = jnp.tanh(0.7978845608028654 * (f + 0.044715 * f * f * f))
            a = (0.5 * f * (1.0 + th)).astype(BF16)
            A[r] = a
            slope = 0.5 * (1.0 + th) + 0.5 * f * (1.0 - th * th) * (
                0.7978845608028654 * (1.0 + 3.0 * 0.044715 * f * f)
            )
            df = (dot(CT[r], W2[t], 1, 1) * slope).astype(BF16)
            DF[r] = df
            m.DIB[t] += fold(df.astype(F32))
            ACC_O[r] += dot(a, W2[t], 1, 0)
            ACC_E[r] += dot(df, W1[t], 1, 1)

        loop(2, rows)

    def lanes(core):
        return pl.ds(pl.multiple_of(core * 384, 128), 384)

    m.DIB[...] = jnp.zeros_like(m.DIB)
    order = [0] + K
    for n, k in enumerate(order):
        t = shard(k)
        if n:
            g1.done(k)
            g2.done(k)
        hidden(t)
        hand(0, k, lambda core: dot(A[:, lanes(core)], CT[...], 0, 0), 0)
        hand(1, k, lambda core: dot(H2[:, lanes(core)], DF[...], 0, 0), 1)
        if n >= 1:
            R[0].two(order[n - 1])
        if n >= 2:
            R[0].three(order[n - 2])
        meet(0, k)
        if n >= 1:
            R[1].two(order[n - 1])
        if n >= 2:
            R[1].three(order[n - 2])
        meet(1, k)
    A[...] = ACC_O[...].astype(BF16)
    res_copy = pltpu.make_async_copy(A, m.result, ld.at[7])
    res_copy.start()

    def back2(i):
        r = ds(i, 128)
        n, s = layer_rows(X2[r])
        e = ACC_E[r]
        g = CT[r].astype(F32)
        dx = g + layer_back(e, n, s, VEC[3:4])
        SUMS[3] += fold(e * n)
        SUMS[4] += fold(e)
        SUMS[2] += fold(dx)
        SUMS[5] += fold(g)
        X2[r] = dx
        H2[r] = dx.astype(BF16)

    loop(4, back2)
    DX, GG = X2, H2

    for t in range(4):
        value = dot(WA[t, 576:768], GG[...], 1, 1).astype(BF16).astype(F32)
        for i in range(3):
            h = 3 * t + i
            do = value[64 * i : 64 * i + 64]
            r = RD[h]
            o = OT[64 * h : 64 * h + 64].astype(F32)
            DNE[h, 0:64] = (do * r).astype(BF16)
            dden = -jnp.sum(do * o, axis=0, keepdims=True) * r
            DNE[h, 64:80] = jnp.where(
                lax.broadcasted_iota(jnp.int32, (16, 512), 0) == 0, dden, 0.0
            ).astype(BF16)
    scan.drain()

    def states_back(h):
        s0 = dot(DNE[h, :, 0:256], PH[0, h, :, 0:256], 1, 1)
        s1 = dot(DNE[h, :, 256:512], PH[0, h, :, 256:512], 1, 1)
        SL[h] = s1
        m.TOT[h] = (s0 + s1).astype(BF16)

    loop(12, states_back)
    scan = Scan(p, True, m.TOT, m.PAIR, m.UP, m.DOWN, m.got_b, m.scan_b)
    scan.begin()
    for i in range(2):
        R[i].two(order[3])
        R[i].three(order[2])

    def feature_back(i, h, delta):
        delta = delta.astype(BF16).astype(F32)
        up, down = PH[i, h, 0:64].astype(F32), PH[i, h, 64:128].astype(F32)
        d, dd = delta[0:64], delta[64:128]
        du = up * (d - jnp.sum(up * d, axis=0, keepdims=True)) - down * (
            dd - jnp.sum(down * dd, axis=0, keepdims=True)
        )
        DU[h, 64 * i : 64 * i + 64] = du.astype(BF16)

    def query_back(h):
        parts = []
        for j in range(2):
            c = slice(256 * j, 256 * j + 256)
            dne = DNE[h, :, c]
            m.DV[ds(h, 64), c] = dot(DNE[h, 0:64, c], AT[h, j], 1, 1).astype(BF16)
            da = dot(VX[h, :, c], dne, 0, 0)
            da = jnp.where(causal, da, 0.0).astype(BF16)
            AT[h, j] = da
            parts.append(dot(PH[1, h, :, c], da, 1, 0) + dot(PX[h, j], dne, 0, 0))
        feature_back(0, h, jnp.concatenate(parts, axis=1))

    loop(3, query_back)
    scan.pair()
    loop(3, lambda h: query_back(h + 3))
    for i in range(2):
        R[i].three(order[3])
    for i in range(2):
        R[i].final()
    scan.wait_y()
    scan.chain(True)
    loop(6, lambda h: query_back(h + 6))
    for i in range(2):
        R[i].spread()
    scan.chain(False)
    for g in range(scan.GROUPS):
        value = scan.sum(g)
        h = scan.heads(g)
        PX[h, 1] = value.astype(BF16)
        PX[h, 0] = (value + SL[h]).astype(BF16)
    for i in range(2):
        R[i].corner()

    def key_back(t, i):
        h = t * 3 + i
        parts, values = [], []
        for j in range(2):
            c = slice(256 * j, 256 * j + 256)
            q = PX[h, j]
            parts.append(dot(PH[0, h, :, c], AT[h, j], 1, 1) + dot(q, VX[h, :, c], 0, 0))
            values.append(dot(q[0:64], PH[1, h, :, c], 1, 0))
        feature_back(1, h, jnp.concatenate(parts, axis=1))
        dv = jnp.concatenate(values, axis=1) + m.DV[ds(h, 64)].astype(F32)
        MIX[t, 384 + 64 * i : 448 + 64 * i] = dv.astype(BF16)

    ones8 = jnp.ones((8, 512), BF16)
    left = lax.broadcasted_iota(jnp.int32, (64, 128), 1) < 64

    def mixed_back(t, i):
        h = t * 3 + i
        du = DU[h]
        rows = [slice(192 * k + 64 * i, 192 * k + 64 * i + 64) for k in range(3)]
        GS[t, 64 * i : 64 * i + 64] = jnp.where(
            left, dot(MIX[t, rows[0]], du, 1, 1), dot(MIX[t, rows[1]], du, 1, 1)
        )
        GS[t, 201 + i : 202 + i] = dot(ones8, du, 1, 1)[0:1]
        for k in range(2):
            MIX[t, rows[k]] = dot(FW[k, h], du[64 * k : 64 * k + 64], 1, 0).astype(BF16)
        for k in range(3):
            GS[t, 192 + 3 * k + i : 193 + 3 * k + i, 0:64] = dot(ones8, MIX[t, rows[k]], 1, 1)[0:1]

    GS[:, 192:256] = jnp.zeros((4, 64, 128), F32)

    for i in range(2):
        R[i].end()
    for n, k in enumerate(order):
        t = shard(k)
        for i in range(3):
            key_back(t, i)
            mixed_back(t, i)
        for c in outgoing[-2:] if n == 0 else outgoing[-1:]:
            c.wait_send()
        STAGE[0] = dot(MIX[t, 0:384], H1[...], 1, 0).astype(BF16)
        STAGE[1, 0:192] = dot(MIX[t, 384:576], H1[...], 1, 0).astype(BF16)
        STAGE[1, 192:384] = dot(OT[ds(t, 192)], GG[...], 1, 0).astype(BF16)
        c = pltpu.make_async_remote_copy(
            STAGE.at[1 - p.core],
            CORE[2].at[t],
            core_sems.at[0, 2, k],
            core_sems.at[1, 2, k],
            device_id=p.core_nb,
            device_id_type=MESH,
        )
        c.start()
        outgoing.append(c)
        R[2].G[t] = STAGE[p.core]
        if n >= 1:
            R[2].two(order[n - 1])
        if n >= 2:
            R[2].three(order[n - 2])
        meet(2, k)

    def back1(i):
        r = ds(i, 256)
        e = dot(MIX[0, :, r], WA[0, 0:576], 0, 0)
        for t in range(1, 4):
            e = e + dot(MIX[t, :, r], WA[t, 0:576], 0, 0)
        n, s = layer_rows(X[r].astype(F32))
        SUMS[0] += fold(e * n)
        SUMS[1] += fold(e)
        ACC_E[r] = DX[r] + layer_back(e, n, s, VEC[0:1])

    loop(2, back1)
    tok_copy = pltpu.make_async_copy(ACC_E, m.tokens_gradient, ld.at[8])
    tok_copy.start()
    for k in range(6):
        row = jnp.sum(SUMS[k], axis=0, keepdims=True)
        for i in range(6):
            for t in range(4):
                GS[t, 216 + 6 * k + i : 217 + 6 * k + i] = row[:, 128 * i : 128 * i + 128]
    for t in range(4):
        row = jnp.sum(m.DIB[t], axis=0, keepdims=True)
        for i in range(6):
            GS[t, 208 + i : 209 + i] = row[:, 128 * i : 128 * i + 128]
    m.GB[...] = GS[...].astype(BF16)
    small_sent = []
    for k in order:
        t = shard(k)
        c = pltpu.make_async_remote_copy(
            m.GB.at[t, pl.ds(pl.multiple_of((1 - p.core) * 128, 128), 128)],
            CORE[3].at[t],
            core_sems.at[0, 3, k],
            core_sems.at[1, 3, k],
            device_id=p.core_nb,
            device_id_type=MESH,
        )
        c.start()
        small_sent.append(c)
        R[3].G[t] = m.GB[t, pl.ds(pl.multiple_of(p.core * 128, 128), 128)]
    for k in order:
        meet(3, k)
    R[2].two(order[3])
    R[2].three(order[2])
    for k in order:
        R[3].two(k)
    R[2].three(order[3])
    for k in order:
        R[3].three(k)
    for step in ("final", "spread", "corner", "end"):
        for i in (2, 3):
            getattr(R[i], step)()
    scan.drain()
    for c in outgoing[-1:] + small_sent:
        c.wait_send()
    for n, g in enumerate(gathers):
        g.drain()
        if n:
            g.drain_hops()
    res_copy.wait()
    tok_copy.wait()


def landing(rows, lanes):
    h = rows // 2
    q, r = h // 4, h // 8
    shapes = ((4, h), (4, 2, r), (4, 2, r), (4, r), (4, r))
    return [pltpu.VMEM((*shape, lanes), BF16) for shape in shapes]


def block_call(x, g, wm, wo, w1, w2, small, vec):
    rows, width = x.shape
    flat = pltpu.VMEM((rows, width), BF16)
    wide = pltpu.VMEM((rows, width), F32)
    weights = pltpu.VMEM((4, 768, 768), BF16)
    state = pltpu.VMEM((12, 80, 128), BF16)
    packs = ((768, 768), (768, 768), (768, 768), (256, 128))
    dma = pltpu.SemaphoreType.DMA
    scratch = dict(
        X=flat,
        CT=flat,
        S=pltpu.VMEM((4, 256, 128), BF16),
        WA=weights,
        W1=weights,
        W2=weights,
        H1=flat,
        H2=flat,
        X2=wide,
        ACC_O=wide,
        ACC_E=wide,
        MIX=pltpu.VMEM((4, 576, rows), BF16),
        PH=pltpu.VMEM((2, 12, 128, rows), BF16),
        VX=pltpu.VMEM((12, 80, rows), BF16),
        AT=pltpu.VMEM((12, 2, 256, 256), BF16),
        PX=pltpu.VMEM((12, 2, 80, 128), BF16),
        SL=pltpu.VMEM((12, 80, 128), F32),
        OT=pltpu.VMEM((768, rows), BF16),
        RD=pltpu.VMEM((12, 1, rows), F32),
        A=flat,
        DF=flat,
        DNE=pltpu.VMEM((12, 80, rows), BF16),
        DU=pltpu.VMEM((12, 128, rows), BF16),
        DV=pltpu.VMEM((768, rows), BF16),
        GS=pltpu.VMEM((4, 256, 128), F32),
        GB=pltpu.VMEM((4, 256, 128), BF16),
        FW=pltpu.VMEM((2, 12, 64, 64), BF16),
        BC=pltpu.VMEM((4, 128, 16), F32),
        IB=pltpu.VMEM((4, 1, 768), F32),
        SUMS=pltpu.VMEM((6, 8, 768), F32),
        DIB=pltpu.VMEM((4, 8, 768), F32),
        TOT=state,
        PAIR=state,
        UP=state,
        DOWN=state,
        got_f=pltpu.VMEM((4, 12, 80, 128), BF16),
        got_b=pltpu.VMEM((4, 12, 80, 128), BF16),
        STAGE=pltpu.VMEM((2, 384, 768), BF16),
        G=[pltpu.VMEM((4, n // 2, lanes), BF16) for n, lanes in packs],
        Z=[pltpu.VMEM((3, n // 8, lanes), BF16) for n, lanes in packs],
        F=[pltpu.VMEM((n // 8, lanes), BF16) for n, lanes in packs],
        land={i: landing(*packs[i]) for i in (0, 1, 3)},
        ld=dma((9,)),
        own=dma((4,)),
        r_core=dma((2, 4, 4)),
        gather_sems={k: dma((2, 4, 5)) for k in GATHER_SEMS},
        reduce_sems={k: dma((2, 4, 5)) for k in SEMS},
        scan_f=dma((2, 8)),
        scan_b=dma((2, 8)),
    )
    leaves, tree = jax.tree.flatten(scratch, is_leaf=lambda v: not isinstance(v, (dict, list)))
    results = [
        jax.ShapeDtypeStruct((rows, width), BF16),
        jax.ShapeDtypeStruct((rows, width), F32),
        *[jax.ShapeDtypeStruct(pack, BF16) for pack in packs],
    ]

    def body(x, g, wm, wo, w1, w2, small, vec, result, tokens_gradient, *rest):
        outs, refs = rest[:4], rest[4:]
        block_kernel(
            SimpleNamespace(
                x=x,
                g=g,
                wm=wm,
                wo=wo,
                w1=w1,
                w2=w2,
                small=small,
                vec=vec,
                result=result,
                tokens_gradient=tokens_gradient,
                outs=outs,
                **jax.tree.unflatten(tree, refs),
            )
        )

    anywhere = pl.BlockSpec(memory_space=pl.ANY)
    return pl.pallas_call(
        body,
        out_shape=results,
        in_specs=[anywhere] * 7 + [pl.BlockSpec(memory_space=pltpu.VMEM)],
        out_specs=[anywhere] * len(results),
        scratch_shapes=leaves,
        compiler_params=pltpu.CompilerParams(
            collective_id=0, has_side_effects=True, vmem_limit_bytes=67043328
        ),
        name="block",
    )(x, g, wm, wo, w1, w2, small, vec)


def small_pack(feature_weight, mixer_bias, feature_bias, inner_bias):
    rows = jnp.concatenate(
        [
            feature_weight.transpose(1, 2, 0, 3).reshape(192, 128),
            jnp.pad(mixer_bias.reshape(9, HD), ((0, 0), (0, HD))),
            feature_bias.transpose(1, 0, 2).reshape(3, 128),
            jnp.zeros((4, 128), feature_weight.dtype),
            inner_bias.reshape(6, 128),
        ]
    )
    return jnp.pad(rows, ((0, 42), (0, 0)))


def small_unpack(small):
    weights = small[:192].reshape(3, HD, 2, HD).transpose(2, 0, 1, 3)
    mixer_bias = small[192:201, :HD].reshape(3, 3 * HD)
    feature_bias = small[201:204].reshape(3, 2, HD).transpose(1, 0, 2)
    return weights, mixer_bias, feature_bias, small[208:214].reshape(768), small[216:252].reshape(6, 768)


def shards(
    fast,
    tokens,
    first_gain,
    first_bias,
    mixer_weight,
    mixer_bias,
    feature_weight,
    feature_bias,
    output_weight,
    output_bias,
    second_gain,
    second_bias,
    inner_weight,
    inner_bias,
    outer_weight,
    outer_bias,
    block_owner,
    cotangent,
):
    rows, width = tokens.shape
    n_tp, n_ctx = lax.axis_size("tp"), lax.axis_size("ctx")
    n_plane = lax.axis_size("dp") * n_ctx
    plane = lax.axis_index("dp") * n_ctx + lax.axis_index("ctx")
    heads_here = mixer_weight.shape[2] // HD
    heads = heads_here * n_tp
    mine = lax.axis_index("ctx") * n_tp + lax.axis_index("tp")

    mixer_t = mixer_weight.transpose(1, 2, 0).reshape(-1, width)
    if fast:
        vec = jnp.stack(
            [first_gain, first_bias, output_bias, second_gain, second_bias, outer_bias]
        )
        result, tokens_gradient, d_outer, d_inner, mixed, small = block_call(
            tokens,
            cotangent,
            mixer_t,
            output_weight,
            inner_weight,
            outer_weight,
            small_pack(feature_weight, mixer_bias, feature_bias, inner_bias),
            jnp.pad(vec.astype(F32), ((0, 2), (0, 0))),
        )
        d_feature, d_mixer_bias, d_feature_bias, d_inner_bias, shared = small_unpack(
            small.astype(F32)
        )
        mixed = mixed.astype(F32)
        return (
            result,
            tokens_gradient,
            shared[0],
            shared[1],
            mixed[:576].reshape(3, heads_here * HD, width).transpose(2, 0, 1),
            d_mixer_bias,
            d_feature,
            d_feature_bias,
            mixed[576:],
            shared[2],
            shared[3],
            shared[4],
            d_inner.astype(F32),
            d_inner_bias,
            d_outer.astype(F32),
            shared[5],
        )
    sizes = [w.shape[0] for w in (mixer_t, output_weight, inner_weight, outer_weight)]
    pack = jnp.concatenate([mixer_t, output_weight, inner_weight, outer_weight], axis=0)
    part = pack.shape[0] // n_plane
    piece = lax.dynamic_slice_in_dim(pack, plane * part, part, 0)
    full = lax.all_gather(piece, ALL, axis=0, tiled=True)
    full = full.reshape(n_plane, n_tp, part, width).transpose(1, 0, 2, 3).reshape(n_tp, -1, width)
    cuts = [0]
    for s in sizes:
        cuts.append(cuts[-1] + s)
    mixer_all, output_all, inner_all, outer_all = [
        full[:, a:b] for a, b in zip(cuts[:-1], cuts[1:])
    ]
    small = jnp.concatenate(
        [feature_weight.reshape(-1), mixer_bias.reshape(-1), feature_bias.reshape(-1), inner_bias]
    )
    small = lax.all_gather(small, "tp")
    cut = feature_weight.size
    feature_all = (
        small[:, :cut].reshape(n_tp, 2, heads_here, HD, HD).transpose(1, 0, 2, 3, 4)
    ).reshape(2, heads, HD, HD)
    mixer_bias_all = small[:, cut : cut + mixer_bias.size].astype(F32).reshape(n_tp, -1)
    cut += mixer_bias.size
    feature_bias_all = (
        small[:, cut : cut + feature_bias.size]
        .astype(F32)
        .reshape(n_tp, 2, heads_here, HD)
        .transpose(1, 0, 2, 3)
        .reshape(2, heads, HD)
    )
    cut += feature_bias.size
    inner_bias_all = small[:, cut:].astype(F32)

    x = tokens.astype(F32)
    gain1, gain2 = first_gain.astype(F32), second_gain.astype(F32)
    h1, n1, r1 = layer_norm(x, gain1, first_bias.astype(F32))
    h1 = h1.astype(BF16)
    mix = ein("td,skd->tsk", h1, mixer_all) + mixer_bias_all
    mix = mix.astype(BF16).reshape(rows, n_tp, 3, heads_here, HD).transpose(2, 0, 1, 3, 4)
    mix = mix.reshape(3, rows, heads, HD)
    q, k, v = mix[0], mix[1], mix[2]
    q_up, q_down, phi_q = feature_map(q, feature_all[0], feature_bias_all[0])
    k_up, k_down, phi_k = feature_map(k, feature_all[1], feature_bias_all[1])

    chunk = min(CHUNK, rows)
    chunks = rows // chunk
    pq = phi_q.reshape(chunks, chunk, heads, 2 * HD)
    pk = phi_k.reshape(chunks, chunk, heads, 2 * HD)
    vc = v.reshape(chunks, chunk, heads, HD)
    causal = jnp.arange(chunk)[:, None] >= jnp.arange(chunk)[None, :]
    state = ein("jthe,jthf->jhef", vc, pk)
    norm = jnp.sum(pk.astype(F32), axis=1)
    both = jnp.concatenate([state, norm[:, :, None]], axis=2)
    owners = block_owner[0].reshape(n_tp, -1)[:, 0]
    order = jnp.arange(n_ctx * n_tp)
    same = jnp.tile(owners, n_ctx) == jnp.tile(owners, n_ctx)[mine]

    def prefix(totals, reach):
        everything = lax.all_gather(totals.astype(BF16), ("ctx", "tp")).astype(F32)
        return jnp.einsum("s,shef->hef", reach.astype(F32), everything, precision="highest")

    def running(blocks, start, reverse):
        out = [None] * chunks
        acc = start
        for j in reversed(range(chunks)) if reverse else range(chunks):
            out[j] = acc
            acc = acc + blocks[j]
        return jnp.stack(out)

    before = running(both, prefix(jnp.sum(both, axis=0), same & (order < mine)), False)
    before = before.astype(BF16)
    scores = ein("jthf,jshf->jhts", pq, pk)
    a_low = jnp.where(causal, scores, 0.0).astype(BF16)
    v_one = jnp.concatenate([vc, jnp.ones(vc.shape[:-1] + (1,), BF16)], axis=-1)
    num = ein("jthf,jhef->jthe", pq, before) + ein("jhts,jshe->jthe", a_low, v_one)
    num, den = num[..., :HD], num[..., HD:]
    o = num / den
    o_low = o.astype(BF16)
    o_flat = o_low.reshape(rows, n_tp, heads_here * HD)
    x2 = x + ein("tsk,skd->td", o_flat, output_all) + output_bias.astype(F32)
    h2, n2, r2 = layer_norm(x2, gain2, second_bias.astype(F32))
    h2 = h2.astype(BF16)
    f = ein("td,sdf->tsf", h2, inner_all) + inner_bias_all
    a, slope = gelu_parts(f)
    a = a.astype(BF16)
    result = (x2 + ein("tsf,sfd->td", a, outer_all) + outer_bias.astype(F32)).astype(BF16)

    g = cotangent.astype(F32)
    d_outer = ein("tsf,td->sfd", a, cotangent)
    df = (ein("td,sfd->tsf", cotangent, outer_all) * slope).astype(BF16)
    d_inner_bias = jnp.sum(df.astype(F32), axis=0)
    d_inner = ein("td,tsf->sdf", h2, df)
    e2 = ein("tsf,sdf->td", df, inner_all)
    back2, d_gain2, d_bias2 = layer_norm_back(e2, n2, r2, gain2)
    dx2 = g + back2
    big_g = dx2.astype(BF16)
    d_output = ein("tsk,td->skd", o_flat, big_g)
    do = ein("td,skd->tsk", big_g, output_all).astype(BF16).astype(F32)
    do = do.reshape(chunks, chunk, heads, HD)
    dnum = do / den
    dden = -jnp.sum(do * o, axis=-1, keepdims=True) / den
    dne = jnp.concatenate([dnum, dden], axis=-1).astype(BF16)
    da = ein("jthe,jshe->jhts", dne, v_one)
    da_low = jnp.where(causal, da, 0.0).astype(BF16)
    d_both = ein("jthe,jthf->jhef", dne, pq)
    after = running(d_both, prefix(jnp.sum(d_both, axis=0), same & (order > mine)), True)
    after = after.astype(BF16)
    dphi_q = ein("jhts,jshf->jthf", da_low, pk) + ein("jthe,jhef->jthf", dne, before)
    dphi_k = ein("jhts,jthf->jshf", da_low, pq) + ein("jthe,jhef->jthf", v_one, after)
    dv = ein("jhts,jthe->jshe", a_low, dne[..., :HD]) + ein("jthf,jhef->jthe", pk, after[:, :, :HD])
    dphi_q = dphi_q.reshape(rows, heads, 2 * HD)
    dphi_k = dphi_k.reshape(rows, heads, 2 * HD)
    dq, d_fq, d_fbq = feature_back(dphi_q, q_up, q_down, q, feature_all[0])
    dk, d_fk, d_fbk = feature_back(dphi_k, k_up, k_down, k, feature_all[1])
    dmix = jnp.stack([dq, dk, dv.reshape(rows, heads, HD)], axis=1).astype(BF16)
    dmix = dmix.reshape(rows, 3, n_tp, heads_here * HD).transpose(0, 2, 1, 3)
    dmix = dmix.reshape(rows, n_tp, -1)
    d_mixer_bias = jnp.sum(dmix.astype(F32), axis=0)
    d_mixer = ein("tsk,td->skd", dmix, h1)
    e1 = ein("tsk,skd->td", dmix, mixer_all)
    back1, d_gain1, d_bias1 = layer_norm_back(e1, n1, r1, gain1)
    tokens_gradient = dx2 + back1

    big = jnp.concatenate([d_mixer, d_output, d_inner, d_outer], axis=1).astype(BF16)
    big = big.reshape(n_tp, n_plane, part, width).transpose(1, 0, 2, 3).reshape(-1, width)
    big = lax.psum_scatter(big, ("dp", "ctx"), scatter_dimension=0, tiled=True)
    big = lax.psum_scatter(big, "tp", scatter_dimension=0, tiled=True)
    big = lax.all_gather(big, ("dp", "ctx"), axis=0, tiled=True).astype(F32)
    d_mixer, d_output, d_inner, d_outer = [big[a:b] for a, b in zip(cuts[:-1], cuts[1:])]
    d_mixer = d_mixer.reshape(3, heads_here * HD, width).transpose(2, 0, 1)
    per_tp = jnp.concatenate(
        [
            jnp.stack([d_fq, d_fk]).reshape(2, n_tp, -1).transpose(1, 0, 2).reshape(n_tp, -1),
            d_mixer_bias,
            jnp.stack([d_fbq, d_fbk]).reshape(2, n_tp, -1).transpose(1, 0, 2).reshape(n_tp, -1),
            d_inner_bias,
        ],
        axis=1,
    )
    shared = jnp.stack(
        [d_gain1, d_bias1, jnp.sum(dx2, axis=0), d_gain2, d_bias2, jnp.sum(g, axis=0)]
    )
    total = lax.psum(jnp.concatenate([per_tp.reshape(-1), shared.reshape(-1)]), ALL)
    shared = total[per_tp.size :].reshape(6, width)
    own = lax.dynamic_slice_in_dim(
        total[: per_tp.size].reshape(n_tp, -1), lax.axis_index("tp"), 1, 0
    )[0]
    cut = feature_weight.size
    d_feature = own[:cut].reshape(feature_weight.shape)
    d_mixer_bias = own[cut : cut + mixer_bias.size].reshape(mixer_bias.shape)
    cut += mixer_bias.size
    d_feature_bias = own[cut : cut + feature_bias.size].reshape(feature_bias.shape)
    d_inner_bias = own[cut + feature_bias.size :]
    return (
        result,
        tokens_gradient,
        shared[0],
        shared[1],
        d_mixer,
        d_mixer_bias,
        d_feature,
        d_feature_bias,
        d_output,
        shared[2],
        shared[3],
        shared[4],
        d_inner,
        d_inner_bias,
        d_outer,
        shared[5],
    )


def solution(mesh):
    in_specs = (
        P(("dp", "ctx", "tp"), None),
        P(),
        P(),
        P(None, None, "tp"),
        P(None, "tp"),
        P(None, "tp", None, None),
        P(None, "tp", None),
        P("tp", None),
        P(),
        P(),
        P(),
        P(None, "tp"),
        P("tp"),
        P("tp", None),
        P(),
        P("dp", None),
        P(("dp", "ctx", "tp"), None),
    )
    out_specs = (
        P(("dp", "ctx", "tp"), None),
        P(("dp", "ctx", "tp"), None),
        P(),
        P(),
        P(None, None, "tp"),
        P(None, "tp"),
        P(None, "tp", None, None),
        P(None, "tp", None),
        P("tp", None),
        P(),
        P(),
        P(),
        P(None, "tp"),
        P("tp"),
        P("tp", None),
        P(),
    )
    fast = (mesh.shape["dp"], mesh.shape["ctx"], mesh.shape["tp"]) == (2, 4, 4)
    return jax.shard_map(functools.partial(shards, fast), mesh=mesh, in_specs=in_specs, out_specs=out_specs, check_vma=False)
```

```python
import functools
from types import SimpleNamespace

import jax
import jax.numpy as jnp
from jax import lax
from jax.experimental import pallas as pl
from jax.experimental.pallas import tpu as pltpu
from jax.sharding import PartitionSpec as P

MESH = pl.DeviceIdType.MESH

HD = 64
BLOCK = 64
CHUNK = 256
EPSILON = 1e-05
F32 = jnp.float32
BF16 = jnp.bfloat16
ALL = ("dp", "ctx", "tp")


def ein(spec, a, b):
    return jnp.einsum(spec, a, b, preferred_element_type=F32)


def layer_norm(v, gain, offset):
    c = v - jnp.mean(v, axis=-1, keepdims=True)
    r = lax.rsqrt(jnp.mean(c * c, axis=-1, keepdims=True) + EPSILON)
    n = c * r
    return n * gain + offset, n, r


def layer_norm_back(e, n, r, gain):
    m = e * gain
    back = r * (
        m - jnp.mean(m, axis=-1, keepdims=True) - n * jnp.mean(m * n, axis=-1, keepdims=True)
    )
    return back, jnp.sum(e * n, axis=0), jnp.sum(e, axis=0)


def gelu_parts(s):
    t = jnp.tanh(0.7978845608028654 * (s + 0.044715 * s * s * s))
    slope = 0.7978845608028654 * (1.0 + 3.0 * 0.044715 * s * s)
    return 0.5 * s * (1.0 + t), 0.5 * (1.0 + t) + 0.5 * s * (1.0 - t * t) * slope


def feature_map(q, weight, offset):
    u = ein("thd,hde->the", q, weight) + offset
    up, down = jax.nn.softmax(u, axis=-1), jax.nn.softmax(-u, axis=-1)
    return up, down, jnp.concatenate([up, down], axis=-1).astype(BF16)


def feature_back(delta, up, down, q, weight):
    d, dd = delta[..., :HD], delta[..., HD:]
    du = up * (d - jnp.sum(up * d, axis=-1, keepdims=True)) - down * (
        dd - jnp.sum(down * dd, axis=-1, keepdims=True)
    )
    low = du.astype(BF16)
    return ein("the,hde->thd", low, weight), ein("thd,the->hde", q, low), jnp.sum(du, axis=0)


HD = 64
BLOCK = 64
CHUNK = 256
EPSILON = 1e-05
F32 = jnp.float32
BF16 = jnp.bfloat16
ALL = ("dp", "ctx", "tp")


def ein(spec, a, b):
    return jnp.einsum(spec, a, b, preferred_element_type=F32)


def layer_norm(v, gain, offset):
    c = v - jnp.mean(v, axis=-1, keepdims=True)
    r = lax.rsqrt(jnp.mean(c * c, axis=-1, keepdims=True) + EPSILON)
    n = c * r
    return n * gain + offset, n, r


def layer_norm_back(e, n, r, gain):
    m = e * gain
    back = r * (
        m - jnp.mean(m, axis=-1, keepdims=True) - n * jnp.mean(m * n, axis=-1, keepdims=True)
    )
    return back, jnp.sum(e * n, axis=0), jnp.sum(e, axis=0)


def gelu_parts(s):
    t = jnp.tanh(0.7978845608028654 * (s + 0.044715 * s * s * s))
    slope = 0.7978845608028654 * (1.0 + 3.0 * 0.044715 * s * s)
    return 0.5 * s * (1.0 + t), 0.5 * (1.0 + t) + 0.5 * s * (1.0 - t * t) * slope


def feature_map(q, weight, offset):
    u = ein("thd,hde->the", q, weight) + offset
    up, down = jax.nn.softmax(u, axis=-1), jax.nn.softmax(-u, axis=-1)
    return up, down, jnp.concatenate([up, down], axis=-1).astype(BF16)


def feature_back(delta, up, down, q, weight):
    d, dd = delta[..., :HD], delta[..., HD:]
    du = up * (d - jnp.sum(up * d, axis=-1, keepdims=True)) - down * (
        dd - jnp.sum(down * dd, axis=-1, keepdims=True)
    )
    low = du.astype(BF16)
    return ein("the,hde->thd", low, weight), ein("thd,the->hde", q, low), jnp.sum(du, axis=0)


def place():
    d, c, t = lax.axis_index("dp"), lax.axis_index("ctx"), lax.axis_index("tp")
    y, core = c // 2, lax.rem(c, 2)
    return SimpleNamespace(d=d, c=c, t=t, y=y, core=core, q=d * 2 + y,
        x_nb=(1 - d, c, t), y_nb=(d, (1 - y) * 2 + core, t), core_nb=(d, y * 2 + 1 - core, t),
        qx=(1 - d) * 2 + y, qy=d * 2 + 1 - y, qd=(1 - d) * 2 + 1 - y)

def plane_peer(p, r):
    d = 1 - p.d if r & 4 else p.d
    y = 1 - p.y if r & 2 else p.y
    core = 1 - p.core if r & 1 else p.core
    return (d, y * 2 + core, p.t), d * 4 + y * 2 + core


def greet(p):
    bar = pltpu.get_barrier_semaphore()
    peers = [plane_peer(p, r)[0] for r in range(1, 8)]
    peers += [(p.d, p.c, lax.rem(p.t + k, 4)) for k in (1, 2, 3)]
    for peer in peers:
        pl.semaphore_signal(bar, inc=1, device_id=peer, device_id_type=MESH)


def met(p):
    pl.semaphore_wait(pltpu.get_barrier_semaphore(), 10)


def nearest(t):
    return [
        jnp.where(t < 2, 1, 3),
        jnp.where(t == 0, 2, jnp.where(t == 1, 3, jnp.where(t == 2, 1, 2))),
        jnp.where(t == 0, 3, jnp.where(t == 3, 1, 2)),
    ]


class Gather:
    def __init__(self, p, buf, sems, send, index):
        self.p, self.buf, self.sems, self.send, self.i = p, buf, sems, send.at[index], index
        self.rows = buf.shape[1]
        self.piece = self.rows // 8
        self.half = self.piece // 2
    def at(self, t, q, core, half=None):
        start = q * (2 * self.piece) + core * self.piece
        size = self.piece
        if half is not None:
            start, size = start + half * self.half, self.half
        return self.buf.at[t, pl.ds(pl.multiple_of(start, 16), size)]
    def shard(self, k): return lax.rem(self.p.t + k, 4)
    def copy(self, ref, kind, k, peer):
        n = 0 if kind == "z" else 2 if kind == "c" else 1
        recv = self.sems[kind].at[self.i, k - 1]
        return pltpu.make_async_remote_copy(
            ref, ref, self.send.at[n], recv, device_id=peer, device_id_type=MESH
        )

    def go(self, *a):
        self.copy(*a).start()

    def first(self):
        p = self.p
        ref = self.at(p.t, p.q, p.core)
        for k in (1, 2, 3):
            self.go(ref, "z", 4 - k, (p.d, p.c, lax.rem(p.t + k, 4)))

    def first_hop(self):
        p = self.p
        ref = self.at(p.t, p.q, p.core)
        pl.when(p.t < 3)(lambda: self.go(ref, "z", 3, (p.d, p.c, p.t + 1)))
        pl.when(p.t > 0)(lambda: self.go(ref, "z", 1, (p.d, p.c, p.t - 1)))

    def zf(self, k):
        p, t = self.p, self.shard(k)
        ref = self.at(t, p.q, p.core)
        self.copy(ref, "z", k, p.x_nb).wait_recv()
        up = jnp.logical_and(t < p.t, p.t < 3)
        down = jnp.logical_and(t > p.t, p.t > 0)
        pl.when(up)(lambda: self.go(ref, "z", k - 1, (p.d, p.c, p.t + 1)))
        pl.when(down)(lambda: self.go(ref, "z", k + 1, (p.d, p.c, p.t - 1)))
        self.go(ref, "x", k, p.x_nb)
        self.go(ref, "y", k, p.y_nb)

    def z(self, k):
        p, t = self.p, self.shard(k)
        ref = self.at(t, p.q, p.core)
        self.copy(ref, "z", k, p.x_nb).wait_recv()
        self.go(ref, "x", k, p.x_nb); self.go(ref, "y", k, p.y_nb)
    def xy(self, k):
        p, t = self.p, self.shard(k)
        self.copy(self.at(t, p.qx, p.core), "x", k, p.x_nb).wait_recv()
        self.go(self.at(t, p.qx, p.core, 0), "fy", k, p.y_nb)
        self.copy(self.at(t, p.qy, p.core), "y", k, p.y_nb).wait_recv()
        self.go(self.at(t, p.qy, p.core, 1), "fx", k, p.x_nb)
    def diag(self, k):
        p, t = self.p, self.shard(k)
        self.copy(self.at(t, p.qd, p.core, 0), "fy", k, p.y_nb).wait_recv()
        self.copy(self.at(t, p.qd, p.core, 1), "fx", k, p.x_nb).wait_recv()
        for q in range(4):
            self.go(self.at(t, q, p.core), "c", k, p.core_nb)
    def done(self, k):
        p, t = self.p, self.shard(k)
        self.copy(self.buf.at[t, pl.ds(0, 4 * self.piece)], "c", k, p.core_nb).wait_recv()

    def drain(self, hops):
        p = self.p

        def wait(kind, ref):
            self.copy(ref, kind, 1, p.core_nb).wait_send()

        line = lambda n: wait("z", self.buf.at[0, pl.ds(0, n * self.piece)])
        if hops:
            ends = jnp.logical_or(p.t == 0, p.t == 3)
            pl.when(ends)(lambda: line(1))
            pl.when(jnp.logical_not(ends))(lambda: line(5))
        else:
            line(3)
        wait("x", self.buf.at[pl.ds(0, 3), pl.ds(0, 3 * self.piece)])
        wait("c", self.buf.at[pl.ds(0, 3), pl.ds(0, 4 * self.piece)])


def lanes(core):
    return pl.ds(pl.multiple_of(core * 384, 128), 384)


class Reduce:
    def __init__(self, p, i, G, X1, Y1, X2, Y2, Z, OUT, sems, send, own):
        self.p, self.i, self.G, self.OUT, self.sems = p, i, G, OUT, sems
        self.X1, self.Y1, self.X2, self.Y2, self.Z = X1, Y1, X2, Y2, Z
        self.half = G.shape[1]; self.qr = self.half // 4; self.hr = self.qr // 2
        self.send = send
        self.own = own
    def t(self, k): return lax.rem(self.p.t + k, 4)
    def rows(self, q, h): return pl.ds(pl.multiple_of(q * self.qr + h * self.hr, 16), self.hr)
    def rdma(self, src, dst, kind, k, peer):
        n = 1 if kind == "z" else 0 if kind != "f" else 3 if k == 4 else 2
        return pltpu.make_async_remote_copy(
            src,
            dst,
            self.send.at[self.i, n],
            self.sems[kind].at[self.i, k],
            device_id=peer,
            device_id_type=MESH,
        )

    def go(self, *a):
        self.rdma(*a).start()

    def got(self, ref, kind, k):
        self.rdma(ref, ref, kind, k, self.p.x_nb).wait_recv()
    def one(self, k):
        p, t = self.p, self.t(k)
        for j in range(2):
            self.go(self.G.at[t, self.rows((1 - p.d) * 2 + j, 0)], self.X1.at[k, j], "x1", k, p.x_nb)
            self.go(self.G.at[t, self.rows(j * 2 + 1 - p.y, 1)], self.Y1.at[k, j], "y1", k, p.y_nb)
    def two(self, k):
        p, t, G = self.p, self.t(k), self.G
        self.got(self.X1.at[k], "x1", k)
        for j in range(2):
            r = self.rows(p.d * 2 + j, 0)
            G[t, r] = G[t, r] + self.X1[k, j]
        self.go(G.at[t, self.rows(p.qy, 0)], self.Y2.at[k], "y2", k, p.y_nb)
        self.got(self.Y1.at[k], "y1", k)
        for j in range(2):
            r = self.rows(j * 2 + p.y, 1)
            G[t, r] = G[t, r] + self.Y1[k, j]
        self.go(G.at[t, self.rows(p.qx, 1)], self.X2.at[k], "x2", k, p.x_nb)
    def three(self, k):
        p, t, G = self.p, self.t(k), self.G
        for h, (kind, R) in enumerate((("y2", self.Y2), ("x2", self.X2))):
            self.got(R.at[k], kind, k)
            r = self.rows(p.q, h)
            G[t, r] = G[t, r] + R[k]
        if not isinstance(k, int):
            whole = pl.ds(pl.multiple_of(p.q * self.qr, 16), self.qr)
            self.go(G.at[t, whole], self.Z.at[3 - k], "z", 3 - k, (p.d, p.c, t))
    def piece(self, q, core, h=None):
        start, size = q * self.qr, self.qr
        if h is not None:
            start, size = start + h * self.hr, self.hr
        return self.OUT.at[pl.ds(pl.multiple_of(start, 16), size), lanes(core)]

    def final(self):
        p = self.p
        whole = pl.ds(pl.multiple_of(p.q * self.qr, 16), self.qr)
        total = self.G[p.t, whole].astype(F32)
        for k in range(3):
            self.got(self.Z.at[k], "z", k)
            total = total + self.Z[k].astype(F32)
        ref = self.piece(p.q, p.core)
        mine = self.G.at[p.t, whole]
        mine[...] = total.astype(BF16)
        self.go(mine, ref, "f", 0, p.x_nb)
        self.go(mine, ref, "f", 1, p.y_nb)
        self.own_copy().start()

    def own_copy(self):
        p = self.p
        whole = pl.ds(pl.multiple_of(p.q * self.qr, 16), self.qr)
        return pltpu.make_async_copy(
            self.G.at[p.t, whole], self.piece(p.q, p.core), self.own.at[self.i]
        )

    def spread(self):
        p = self.p
        ref = self.piece(p.qx, p.core); self.got(ref, "f", 0)
        ref = self.piece(p.qx, p.core, 0); self.go(ref, ref, "f", 2, p.y_nb)
        ref = self.piece(p.qy, p.core); self.got(ref, "f", 1)
        ref = self.piece(p.qy, p.core, 1); self.go(ref, ref, "f", 3, p.x_nb)
    def corner(self):
        p = self.p
        self.own_copy().wait()
        self.got(self.piece(p.qd, p.core, 0), "f", 2); self.got(self.piece(p.qd, p.core, 1), "f", 3)
        ref = self.OUT.at[:, lanes(p.core)]
        self.go(ref, ref, "f", 4, p.core_nb)
    def end(self):
        p = self.p
        self.got(self.OUT.at[:, lanes(1 - p.core)], "f", 4)
        rows = 3 * self.half // 4
        sizes = (
            ("x1", 0, self.G.at[pl.ds(0, 3)]),
            ("z", 0, self.Z),
            ("f", 0, self.G.at[0, pl.ds(0, rows)]),
            ("f", 4, self.G.at[0]),
        )
        for kind, k, ref in sizes:
            self.rdma(ref, ref, kind, k, p.core_nb).wait_send()


GATHER_SEMS = ("z", "x", "y", "fx", "fy", "c")
SEMS = ("x1", "y1", "x2", "y2", "z", "f")


def dot(a, b, ca, cb):
    return lax.dot_general(a, b, (((ca,), (cb,)), ((), ())), preferred_element_type=F32)


def loop(n, step):
    def body(i, carry):
        step(i)
        return carry

    lax.fori_loop(0, n, body, 0)


def ds(i, n):
    return pl.ds(pl.multiple_of(i * n, n), n)


class Scan:
    def __init__(self, p, later, total, up, down, got, sems):
        self.p, self.later, self.total, self.up_ref, self.down_ref = p, later, total, up, down
        self.from_core, self.from_y, self.from_below, self.from_above = [got.at[i] for i in range(4)]
        self.sems = sems

    def rdma(self, src, dst, g, i, peer):
        h, i = self.heads(g), 4 * i + g
        return pltpu.make_async_remote_copy(
            src.at[h], dst.at[h], self.sems.at[0, i], self.sems.at[1, i], device_id=peer, device_id_type=MESH
        )

    def core_copy(self, g):
        return self.rdma(self.total, self.from_core, g, 0, self.p.core_nb)

    def y_copy(self, g):
        return self.rdma(self.up_ref, self.from_y, g, 1, self.p.y_nb)

    def line_copy(self, g, upward):
        p = self.p
        if upward:
            return self.rdma(self.up_ref, self.from_below, g, 2, (p.d, p.c, p.t + 1))
        return self.rdma(self.down_ref, self.from_above, g, 3, (p.d, p.c, p.t - 1))

    def heads(self, g):
        return pl.ds(3 * g, 3)

    def begin(self, g):
        h = self.heads(g)
        zero = jnp.zeros((3, 80, 128), BF16)

        @pl.when(self.p.t == 0)
        def _():
            self.from_below[h] = zero

        @pl.when(self.p.t == 3)
        def _():
            self.from_above[h] = zero

        self.core_copy(g).start()

    def pair(self, g):
        h = self.heads(g)
        self.core_copy(g).wait_recv()
        self.up_ref[h] = self.total[h] + self.from_core[h]
        self.y_copy(g).start()

    def column(self, g):
        p, h = self.p, self.heads(g)
        core, y = p.core.astype(F32), p.y.astype(F32)
        if self.later:
            core, y = 1.0 - core, 1.0 - y
        return core * self.from_core[h].astype(F32) + y * self.from_y[h].astype(F32)

    def hop(self, g, upward):
        h, t = self.heads(g), self.p.t
        has, sends = (t > 0, t < 3) if upward else (t < 3, t > 0)
        c = self.line_copy(g, upward)
        got = self.from_below if upward else self.from_above
        out = self.up_ref if upward else self.down_ref

        @pl.when(has)
        def _():
            c.wait_recv()

        @pl.when(sends)
        def _():
            value = self.column(g) + got[h].astype(F32)
            if upward != self.later:
                value = value + self.total[h].astype(F32)
            out[h] = value.astype(BF16)
            c.start()

    def chain(self, g):
        c = self.y_copy(g)
        c.wait_recv()
        c.wait_send()
        pl.when(self.p.t < 2)(lambda: self.hop(g, True))
        pl.when(self.p.t >= 2)(lambda: self.hop(g, False))

    def relay(self, g):
        pl.when(self.p.t == 1)(lambda: self.hop(g, False))
        pl.when(self.p.t == 2)(lambda: self.hop(g, True))

    def last(self, g):
        pl.when(self.p.t == 0)(lambda: self.hop(g, False))
        pl.when(self.p.t == 3)(lambda: self.hop(g, True))

    def sum(self, g):
        h = self.heads(g)
        return self.column(g) + self.from_below[h].astype(F32) + self.from_above[h].astype(F32)

    def drain(self):
        for g in range(4):
            self.core_copy(g).wait_send()
            pl.when(self.p.t < 3)(lambda g=g: self.line_copy(g, True).wait_send())
            pl.when(self.p.t > 0)(lambda g=g: self.line_copy(g, False).wait_send())


class Small:
    def __init__(self, p, low, full, plane, line, mid, out, sems, send, own):
        self.p, self.low, self.full, self.plane, self.line, self.mid, self.out = (
            p, low, full, plane, line, mid, out
        )
        self.sems, self.send, self.own = sems, send, own
        self.me = p.d * 4 + p.c

    def rdma(self, src, dst, i, peer):
        n = 0 if i < 7 else 1 if i < 10 else 2
        return pltpu.make_async_remote_copy(
            src, dst, self.send.at[n], self.sems.at[i], device_id=peer, device_id_type=MESH
        )

    def go(self, *a):
        self.rdma(*a).start()

    def begin(self):
        for r in range(1, 8):
            peer, j = plane_peer(self.p, r)
            self.go(self.low.at[ds(j, 32)], self.plane.at[r - 1], r - 1, peer)

    def across(self):
        p = self.p
        for r in range(1, 8):
            self.rdma(self.plane.at[r - 1], self.plane.at[r - 1], r - 1, p.x_nb).wait_recv()
        for t in range(4):
            total = self.full[t, ds(self.me, 32)]
            for r in range(7):
                total = total + self.plane[r, :, 128 * t : 128 * t + 128].astype(F32)
            self.full[t, ds(self.me, 32)] = total
            self.mid[t] = total.astype(BF16)
        for k in (1, 2, 3):
            t = lax.rem(p.t + k, 4)
            self.go(self.mid.at[t], self.line.at[3 - k], 10 - k, (p.d, p.c, t))

    def final(self):
        p = self.p
        total = self.full[p.t, ds(self.me, 32)]
        for k in range(3):
            self.rdma(self.line.at[k], self.line.at[k], 7 + k, p.x_nb).wait_recv()
            total = total + self.line[k].astype(F32)
        self.mid[4] = total.astype(BF16)
        ref = self.out.at[ds(self.me, 32)]
        for r in range(1, 8):
            self.go(self.mid.at[4], ref, 9 + r, plane_peer(p, r)[0])
        pltpu.make_async_copy(self.mid.at[4], ref, self.own).start()

    def end(self):
        pltpu.make_async_copy(self.mid.at[4], self.out.at[ds(self.me, 32)], self.own).wait()
        for r in range(1, 8):
            peer, j = plane_peer(self.p, r)
            ref = self.out.at[ds(j, 32)]
            self.rdma(ref, ref, 9 + r, peer).wait_recv()
        for i, ref in ((0, self.plane), (7, self.line), (10, self.plane.at[:, :, pl.ds(0, 128)])):
            self.rdma(ref, ref, i, self.p.core_nb).wait_send()


def layer_rows(v):
    c = v - jnp.mean(v, axis=-1, keepdims=True)
    r = lax.rsqrt(jnp.mean(c * c, axis=-1, keepdims=True) + EPSILON)
    return c * r, r


def fold(v):
    total = v[:8]
    for i in range(1, v.shape[0] // 8):
        total = total + v[8 * i : 8 * i + 8]
    return total


def layer_back(e, n, r, gain):
    m = e * gain
    return r * (
        m - jnp.mean(m, axis=-1, keepdims=True) - n * jnp.mean(m * n, axis=-1, keepdims=True)
    )


def block_kernel(m):
    p = place()
    t0 = p.t
    X, CT, S, WA, W1, W2 = m.X, m.CT, m.S, m.WA, m.W1, m.W2
    VEC, H1, H2, X2, ACC_O, ACC_E = m.VEC, m.H1, m.H2, m.X2, m.ACC_O, m.ACC_E
    MIX, PH, VX, AT, PX, SL, OT, RD = m.MIX, m.PH, m.VX, m.AT, m.PX, m.SL, m.OT, m.RD
    A, DF, GS, FW, BC, IB, SUMS = m.A, m.DF, m.GS, m.FW, m.BC, m.IB, m.SUMS
    ld = m.ld
    greet(p)
    loads = [
        pltpu.make_async_copy(m.wm, WA.at[t0, pl.ds(0, 576)], ld.at[0]),
        pltpu.make_async_copy(m.wo, WA.at[t0, pl.ds(576, 192)], ld.at[1]),
        pltpu.make_async_copy(m.x, X, ld.at[2]),
        pltpu.make_async_copy(m.w1, W1.at[t0], ld.at[3]),
        pltpu.make_async_copy(m.w2, W2.at[t0], ld.at[4]),
        pltpu.make_async_copy(m.g, CT, ld.at[5]),
    ]
    raw = [(m.fw, m.FWI), (m.mb, m.MBI), (m.fb, m.FBI)]
    raw += [(ref, m.VECI.at[i, pl.ds(0, 6)]) for i, ref in enumerate(m.vectors)]
    raw = [pltpu.make_async_copy(src, dst, ld.at[8 + i]) for i, (src, dst) in enumerate(raw)]
    for c in raw + loads:
        c.start()
    for c in raw:
        c.wait()

    for h in range(3):
        pair = [m.FWI[i, h].astype(F32) for i in range(2)]
        S[t0, 64 * h : 64 * h + 64] = jnp.concatenate(pair, axis=1).astype(BF16)
    zero = jnp.zeros((1, HD), F32)
    rows = []
    for j in range(3):
        row = m.MBI[j : j + 1].astype(F32)
        rows += [
            jnp.concatenate([row[:, HD * h : HD * h + HD], zero], axis=1) for h in range(3)
        ]
    for h in range(3):
        row = m.FBI[h].astype(F32)
        rows.append(jnp.concatenate([row[0:1], row[1:2]], axis=1))
    rows.append(jnp.zeros((4, 128), F32))
    S[t0, 192:208] = jnp.concatenate(rows, axis=0).astype(BF16)
    rows = [m.VECI[6].astype(F32)[0:6], jnp.zeros((42, 128), F32)]
    S[t0, 208:256] = jnp.concatenate(rows, axis=0).astype(BF16)
    for k in range(6):
        value = m.VECI[k].astype(F32)
        for i in range(6):
            VEC[k : k + 1, 128 * i : 128 * i + 128] = value[i : i + 1]

    gs, gw, g1, g2 = gathers = [
        Gather(p, b, m.gather_sems, m.gather_send, i) for i, b in enumerate((S, WA, W1, W2))
    ]
    K = nearest(t0)
    shard = gs.shard
    loads[0].wait()
    loads[1].wait()
    met(p)
    gw.first()
    gs.first()

    loads[2].wait()

    def norm1(i):
        r = ds(i, 128)
        n, _ = layer_rows(X[r].astype(F32))
        H1[r] = (n * VEC[0:1] + VEC[1:2]).astype(BF16)

    loop(4, norm1)
    ones_row = jnp.where(lax.broadcasted_iota(jnp.int32, (16, 512), 0) == 0, 1.0, 0.0).astype(BF16)

    def init(h):
        VX[h, 64:80] = ones_row

    loop(12, init)
    SUMS[...] = jnp.zeros_like(SUMS)

    def small(t):
        BC[...] = S[t, 192:208].astype(F32).T
        rows = S[t, 208:224].astype(F32)
        for i in range(6):
            IB[t, :, 128 * i : 128 * i + 128] = rows[i : i + 1]
        for h in range(3):
            w = S[t, 64 * h : 64 * h + 64].astype(F32)
            FW[0, t * 3 + h] = w[:, :64].astype(BF16)
            FW[1, t * 3 + h] = w[:, 64:].astype(BF16)

    def mix(t):
        value = dot(WA[t, 0:576], H1[...], 1, 1)
        for j in range(3):
            for h in range(3):
                n = j * 3 + h
                part = (value[64 * n : 64 * n + 64] + BC[0:64, n : n + 1]).astype(BF16)
                if j < 2:
                    MIX[t, 64 * n : 64 * n + 64] = part
                else:
                    VX[t * 3 + h, 0:64] = part

    def features(t):
        for h in range(3):
            for i in range(2):
                u = dot(FW[i, t * 3 + h], MIX[t, 192 * i + 64 * h : 192 * i + 64 * h + 64], 0, 0)
                u = u + BC[64 * i : 64 * i + 64, 9 + h : 10 + h]
                e = jnp.exp(u - jnp.max(u, axis=0, keepdims=True))
                PH[i, t * 3 + h, 0:64] = (e / jnp.sum(e, axis=0, keepdims=True)).astype(BF16)
                e = jnp.exp(jnp.min(u, axis=0, keepdims=True) - u)
                PH[i, t * 3 + h, 64:128] = (e / jnp.sum(e, axis=0, keepdims=True)).astype(BF16)

    def states(t):
        def one(i):
            h = t * 3 + i
            s0 = dot(VX[h, :, 0:256], PH[1, h, :, 0:256], 1, 1)
            s1 = dot(VX[h, :, 256:512], PH[1, h, :, 256:512], 1, 1)
            SL[h] = s0
            m.TOT[h] = (s0 + s1).astype(BF16)

        loop(3, one)

    small(t0)
    mix(t0)
    features(t0)
    states(t0)
    both = (g1, g2)
    for n, k in enumerate(K):
        gw.z(k)
        gs.z(k)
        if n == 1:
            loads[3].wait()
            loads[4].wait()
            for g in both:
                g.first_hop()
    for k in K:
        gw.xy(k)
        gs.xy(k)
    for k in K:
        gw.diag(k)
        gs.diag(k)
    middle = jnp.logical_or(t0 == 1, t0 == 2)
    for g in both:
        g.zf(K[0])
    for g in both:
        pl.when(middle)(lambda g=g: g.zf(K[1]))
    for n, k in enumerate(K):
        gs.done(k)
        gw.done(k)
        t = shard(k)
        small(t)
        mix(t)
        features(t)
        states(t)
    scan = Scan(p, False, m.TOT, m.UP, m.DOWN, m.got_f, m.scan_f)
    for g in range(4):
        scan.begin(g)
    causal = lax.broadcasted_iota(jnp.int32, (256, 256), 0) <= lax.broadcasted_iota(
        jnp.int32, (256, 256), 1
    )

    def scores(h):
        for j in range(2):
            c = slice(256 * j, 256 * j + 256)
            a = dot(PH[1, h, :, c], PH[0, h, :, c], 0, 0)
            AT[h, j] = jnp.where(causal, a, 0.0).astype(BF16)

    for g in both:
        g.zf(jnp.where(middle, K[2], K[1]))
    for g in range(4):
        scan.pair(g)
    loop(6, scores)
    for g in both:
        g.xy(K[0])
    loop(6, lambda h: scores(h + 6))
    for g in range(4):
        scan.chain(g)
    for g in both:
        pl.when(jnp.logical_not(middle))(lambda g=g: g.zf(K[2]))
    for g in range(4):
        scan.relay(g)
    for g in both:
        g.diag(K[0])

    def enter(first):
        for g in range(4):
            scan.last(g)
            value = scan.sum(g)
            h = scan.heads(g)
            PX[h, first] = value.astype(BF16)
            PX[h, 1 - first] = (value + SL[h]).astype(BF16)

    enter(0)

    def attend(h):
        for j in range(2):
            c = slice(256 * j, 256 * j + 256)
            num = dot(PX[h, j], PH[0, h, :, c], 1, 0) + dot(VX[h, :, c], AT[h, j], 1, 0)
            r = 1.0 / num[64:65]
            RD[h, :, c] = r
            OT[ds(h, 64), c] = (num[0:64] * r).astype(BF16)

    for g in both:
        g.xy(K[1])
    loop(12, attend)

    def norm2(i):
        r = ds(i, 256)
        total = X[r].astype(F32) + VEC[2:3]
        for t in range(4):
            total = total + dot(OT[192 * t : 192 * t + 192, r], WA[t, 576:768], 0, 0)
        X2[r] = total
        n, _ = layer_rows(total)
        H2[r] = (n * VEC[3:4] + VEC[4:5]).astype(BF16)
        ACC_O[r] = total + VEC[5:6]
        ACC_E[r] = jnp.zeros((256, 768), F32)

    loop(2, norm2)

    R = [
        Reduce(p, i, m.G[i], *m.land[i][1:], m.Z[i], m.outs[i], m.reduce_sems, m.reduce_send, m.own)
        for i in range(4)
    ]
    core_sems, STAGE = m.r_core, m.STAGE
    outgoing = []

    def core_copy(src, i, k):
        ref = m.land[i][0].at[shard(k)]
        return pltpu.make_async_remote_copy(
            ref if src is None else src,
            ref,
            core_sems.at[0, i, k],
            core_sems.at[1, i, k],
            device_id=p.core_nb,
            device_id_type=MESH,
        )

    def hand(i, k, value):
        slot = len(outgoing) % 2
        if len(outgoing) >= 2:
            outgoing[-2].wait_send()
        ref = STAGE.at[slot, pl.ds(0, R[i].half)]
        ref[...] = value(1 - p.core).astype(BF16)
        c = core_copy(ref, i, k)
        c.start()
        outgoing.append(c)
        R[i].G[shard(k)] = value(p.core).astype(BF16)

    def meet(i, k):
        t = shard(k)
        G, C = R[i].G, m.land[i][0]
        core_copy(None, i, k).wait_recv()

        def add(j):
            r = ds(j, 96)
            G[t, r] = G[t, r] + C[t, r]

        loop(R[i].half // 96, add)
        R[i].one(k)

    def hidden(t, slot):
        def rows(i):
            r = ds(i, 256)
            f = dot(H2[r], W1[t], 1, 0) + IB[t]
            th = jnp.tanh(0.7978845608028654 * (f + 0.044715 * f * f * f))
            a = (0.5 * f * (1.0 + th)).astype(BF16)
            A[slot, r] = a
            slope = 0.5 * (1.0 + th) + 0.5 * f * (1.0 - th * th) * (
                0.7978845608028654 * (1.0 + 3.0 * 0.044715 * f * f)
            )
            df = (dot(CT[r], W2[t], 1, 1) * slope).astype(BF16)
            DF[slot, r] = df
            m.DIB[t] += fold(df.astype(F32))
            ACC_O[r] += dot(a, W2[t], 1, 0)
            ACC_E[r] += dot(df, W1[t], 1, 1)

        loop(2, rows)

    def hand_hidden(k, slot):
        hand(0, k, lambda core: dot(A[slot], CT[:, lanes(core)], 0, 0))
        hand(1, k, lambda core: dot(H2[...], DF[slot, :, lanes(core)], 0, 0))

    m.DIB[...] = jnp.zeros_like(m.DIB)
    order = [0] + K
    loads[5].wait()
    for g in both:
        g.diag(K[1])
    hidden(t0, 0)
    for g in both:
        g.xy(K[2])
    hand_hidden(0, 0)
    for g in both:
        g.diag(K[2])
    for n, k in enumerate(K):
        g1.done(k)
        g2.done(k)
        hidden(shard(k), n // 2)
        if n < 2:
            for i in range(2):
                meet(i, order[n])
        if n < 1:
            hand_hidden(k, 0)
    for g in both:
        g.drain(True)
    RES, GG = W1.at[2, pl.ds(0, 512)], W1.at[3, pl.ds(0, 512)]

    def dne(h):
        start = pl.multiple_of(lax.rem(h, 9) * 80, 16)
        return W2.at[h // 9, pl.ds(start, 80), pl.ds(0, 512)]

    def du_of(h):
        return W1.at[h // 6, ds(lax.rem(h, 6), 128), pl.ds(0, 512)]

    def dv_of(h):
        return W2.at[2, ds(h, 64), pl.ds(0, 512)]

    def back2(i):
        r = ds(i, 128)
        n, s = layer_rows(X2[r])
        e = ACC_E[r]
        g = CT[r].astype(F32)
        dx = g + layer_back(e, n, s, VEC[3:4])
        SUMS[3] += fold(e * n)
        SUMS[4] += fold(e)
        SUMS[2] += fold(dx)
        SUMS[5] += fold(g)
        X2[r] = dx
        GG[r] = dx.astype(BF16)

    loop(4, back2)
    DX = X2
    first_row = lax.broadcasted_iota(jnp.int32, (16, 512), 0) == 0

    scan.drain()
    scan = Scan(p, True, m.TOT, m.UP, m.DOWN, m.got_b, m.scan_b)

    def states_back(t):
        value = dot(WA[t, 576:768], GG[...], 1, 1).astype(BF16).astype(F32)
        for i in range(3):
            h = 3 * t + i
            do = value[64 * i : 64 * i + 64]
            r = RD[h]
            o = OT[ds(h, 64)].astype(F32)
            ref = dne(h)
            ref[0:64] = (do * r).astype(BF16)
            dden = -jnp.sum(do * o, axis=0, keepdims=True) * r
            ref[64:80] = jnp.where(first_row, dden, 0.0).astype(BF16)
            s0 = dot(ref[:, 0:256], PH[0, h, :, 0:256], 1, 1)
            s1 = dot(ref[:, 256:512], PH[0, h, :, 256:512], 1, 1)
            SL[h] = s1
            m.TOT[h] = (s0 + s1).astype(BF16)

    for t in range(4):
        states_back(t)
        scan.begin(t)
    hand(0, order[2], lambda core: dot(A[0], CT[:, lanes(core)], 0, 0))
    for g in range(4):
        scan.pair(g)
    for i in range(2):
        R[i].two(order[0])
    hand(1, order[2], lambda core: dot(H2[...], DF[0, :, lanes(core)], 0, 0))
    for i in range(2):
        R[i].two(order[1])

    def feature_back(i, h, delta):
        delta = delta.astype(BF16).astype(F32)
        up, down = PH[i, h, 0:64].astype(F32), PH[i, h, 64:128].astype(F32)
        d, dd = delta[0:64], delta[64:128]
        du = up * (d - jnp.sum(up * d, axis=0, keepdims=True)) - down * (
            dd - jnp.sum(down * dd, axis=0, keepdims=True)
        )
        du_of(h)[64 * i : 64 * i + 64] = du.astype(BF16)

    def query_back(h):
        parts = []
        ref, dv = dne(h), dv_of(h)
        for j in range(2):
            c = slice(256 * j, 256 * j + 256)
            value = ref[:, c]
            dv[:, c] = dot(ref[0:64, c], AT[h, j], 1, 1).astype(BF16)
            da = dot(VX[h, :, c], value, 0, 0)
            da = jnp.where(causal, da, 0.0).astype(BF16)
            AT[h, j] = da
            parts.append(dot(PH[1, h, :, c], da, 1, 0) + dot(PX[h, j], value, 0, 0))
        feature_back(0, h, jnp.concatenate(parts, axis=1))

    ones8 = jnp.ones((8, 512), BF16)
    left = lax.broadcasted_iota(jnp.int32, (64, 128), 1) < 64
    GS[:, 192:256] = jnp.zeros((4, 64, 128), F32)

    def bias_row(t, j, i):
        ref = MIX[t, ds(3 * j + i, 64)]
        GS[t, pl.ds(192 + 3 * j + i, 1), 0:64] = dot(ones8, ref, 1, 1)[0:1]

    def early(k):
        t = shard(k)
        def one(i):
            h = t * 3 + i
            rows = ds(i, 64)
            du = du_of(h)[0:64]
            GS[t, rows, 0:64] = dot(MIX[t, rows], du, 1, 1)
            MIX[t, rows] = dot(FW[0, h], du, 1, 0).astype(BF16)
            bias_row(t, 0, i)

        loop(3, one)

        def value(core):
            both = [
                dot(MIX[t, 0:192], H1[:, lanes(core)], 1, 0),
                dot(OT[ds(t, 192)], GG[:, lanes(core)], 1, 0),
            ]
            return jnp.concatenate(both, axis=0)

        hand(2, k, value)

    def queries(g):
        loop(3, lambda i: query_back(3 * g + i))

    queries(0)
    scan.chain(0)
    for i in range(2):
        meet(i, order[2])
    queries(1)
    scan.chain(1)
    queries(2)
    scan.chain(2)
    scan.chain(3)
    for i in range(2):
        R[i].three(order[0])
        R[i].three(order[1])
    queries(3)
    for g in range(4):
        scan.relay(g)
    hand_hidden(order[3], 1)
    RES[...] = ACC_O[...].astype(BF16)
    res_copy = pltpu.make_async_copy(RES, m.result, ld.at[6])
    res_copy.start()
    for i in range(2):
        R[i].two(order[2])
        meet(i, order[3])
    early(order[0])
    early(order[1])
    meet(2, order[0])
    R[0].three(order[2])
    early(order[2])
    meet(2, order[1])
    R[1].three(order[2])
    for i in range(2):
        R[i].two(order[3])
    early(order[3])
    meet(2, order[2])
    enter(1)

    def key_back(t, i):
        h = t * 3 + i
        parts, values = [], []
        for j in range(2):
            c = slice(256 * j, 256 * j + 256)
            q = PX[h, j]
            parts.append(dot(PH[0, h, :, c], AT[h, j], 1, 1) + dot(q, VX[h, :, c], 0, 0))
            values.append(dot(q[0:64], PH[1, h, :, c], 1, 0))
        feature_back(1, h, jnp.concatenate(parts, axis=1))
        dv = jnp.concatenate(values, axis=1) + dv_of(h)[...].astype(F32)
        MIX[t, ds(6 + i, 64)] = dv.astype(BF16)
        du = du_of(h)
        rows = ds(3 + i, 64)
        ref = ds(i, 64)
        GS[t, ref] = jnp.where(left, GS[t, ref], dot(MIX[t, rows], du[...], 1, 1))
        GS[t, pl.ds(201 + i, 1)] = dot(ones8, du[...], 1, 1)[0:1]
        MIX[t, rows] = dot(FW[1, h], du[64:128], 1, 0).astype(BF16)
        bias_row(t, 1, i)
        bias_row(t, 2, i)

    for n, k in enumerate(order):
        t = shard(k)
        loop(3, lambda i: key_back(t, i))
        hand(3, k, lambda core: dot(MIX[t, 192:576], H1[:, lanes(core)], 1, 0))
        if n == 0:
            meet(2, order[3])
            R[2].two(order[0])
            R[2].two(order[1])
        else:
            meet(3, order[n - 1])
        if n == 1:
            R[0].three(order[3])
            R[1].three(order[3])
            R[2].two(order[2])
        if n == 2:
            R[2].two(order[3])
            R[2].three(order[0])
            R[2].three(order[1])
            R[2].three(order[2])
            R[3].two(order[0])
        if n == 3:
            R[0].final()
            R[2].three(order[3])
            R[3].two(order[1])
            R[3].three(order[0])

    def back1(i):
        r = ds(i, 256)
        e = dot(MIX[0, :, r], WA[0, 0:576], 0, 0)
        for t in range(1, 4):
            e = e + dot(MIX[t, :, r], WA[t, 0:576], 0, 0)
        n, s = layer_rows(X[r].astype(F32))
        SUMS[0] += fold(e * n)
        SUMS[1] += fold(e)
        ACC_E[r] = DX[r] + layer_back(e, n, s, VEC[0:1])

    back1(0)
    meet(3, order[3])
    R[1].final()
    R[3].two(order[2])
    R[3].three(order[1])
    back1(1)
    R[0].spread()
    tok_copy = pltpu.make_async_copy(ACC_E, m.tokens_gradient, ld.at[7])
    tok_copy.start()
    for k in range(6):
        row = jnp.sum(SUMS[k], axis=0, keepdims=True)
        for i in range(6):
            for t in range(4):
                GS[t, 216 + 6 * k + i : 217 + 6 * k + i] = row[:, 128 * i : 128 * i + 128]
    for t in range(4):
        row = jnp.sum(m.DIB[t], axis=0, keepdims=True)
        for i in range(6):
            GS[t, 208 + i : 209 + i] = row[:, 128 * i : 128 * i + 128]
    GB = W2.at[3, pl.ds(0, 256), pl.ds(0, 512)]
    for t in range(4):
        GB[:, 128 * t : 128 * t + 128] = GS[t].astype(BF16)
    tiny = Small(p, GB, GS, m.plane, m.line, m.mid, m.outs[4], m.small_sems, m.small_send, m.own.at[4])
    tiny.begin()
    R[3].two(order[3])
    R[3].three(order[2])
    R[1].spread()
    R[2].final()
    R[0].corner()
    R[3].three(order[3])
    tiny.across()
    R[2].spread()
    R[1].corner()
    tiny.final()
    R[3].final()
    R[2].corner()
    R[3].spread()
    R[3].corner()
    for r in R:
        r.end()
    tiny.end()
    scan.drain()
    for c in outgoing[-2:]:
        c.wait_send()
    gs.drain(False)
    gw.drain(False)
    res_copy.wait()
    tok_copy.wait()


PACKS = ((768, 768), (768, 768), (384, 768), (384, 768))


def landing(rows):
    q, r = rows // 4, rows // 8
    shapes = ((4, rows), (4, 2, r), (4, 2, r), (4, r), (4, r))
    return [pltpu.VMEM((*shape, 384), BF16) for shape in shapes]


def block_call(*args):
    rows, width = args[0].shape
    flat = pltpu.VMEM((rows, width), BF16)
    wide = pltpu.VMEM((rows, width), F32)
    weights = pltpu.VMEM((4, 768, 768), BF16)
    state = pltpu.VMEM((12, 80, 128), BF16)
    dma = pltpu.SemaphoreType.DMA
    scratch = dict(
        X=flat,
        CT=flat,
        S=pltpu.VMEM((4, 256, 128), BF16),
        WA=weights,
        W1=weights,
        W2=weights,
        VEC=pltpu.VMEM((8, 768), F32),
        VECI=pltpu.VMEM((7, 8, 128), BF16),
        FWI=pltpu.VMEM((2, 3, HD, HD), BF16),
        MBI=pltpu.VMEM((3, 192), BF16),
        FBI=pltpu.VMEM((3, 2, HD), BF16),
        H1=flat,
        H2=flat,
        X2=wide,
        ACC_O=wide,
        ACC_E=wide,
        MIX=pltpu.VMEM((4, 576, rows), BF16),
        PH=pltpu.VMEM((2, 12, 128, rows), BF16),
        VX=pltpu.VMEM((12, 80, rows), BF16),
        AT=pltpu.VMEM((12, 2, 256, 256), BF16),
        PX=pltpu.VMEM((12, 2, 80, 128), BF16),
        SL=pltpu.VMEM((12, 80, 128), F32),
        OT=pltpu.VMEM((768, rows), BF16),
        RD=pltpu.VMEM((12, 1, rows), F32),
        A=pltpu.VMEM((2, rows, width), BF16),
        DF=pltpu.VMEM((2, rows, width), BF16),
        GS=pltpu.VMEM((4, 256, 128), F32),
        FW=pltpu.VMEM((2, 12, 64, 64), BF16),
        BC=pltpu.VMEM((128, 16), F32),
        IB=pltpu.VMEM((4, 1, 768), F32),
        SUMS=pltpu.VMEM((6, 8, 768), F32),
        DIB=pltpu.VMEM((4, 8, 768), F32),
        TOT=state,
        UP=state,
        DOWN=state,
        got_f=pltpu.VMEM((4, 12, 80, 128), BF16),
        got_b=pltpu.VMEM((4, 12, 80, 128), BF16),
        plane=pltpu.VMEM((7, 32, 512), BF16),
        line=pltpu.VMEM((3, 32, 128), BF16),
        mid=pltpu.VMEM((5, 32, 128), BF16),
        STAGE=pltpu.VMEM((2, 768, 384), BF16),
        G=[pltpu.VMEM((4, n, 384), BF16) for n, _ in PACKS],
        Z=[pltpu.VMEM((3, n // 4, 384), BF16) for n, _ in PACKS],
        land=[landing(n) for n, _ in PACKS],
        ld=dma((18,)),
        own=dma((5,)),
        r_core=dma((2, 4, 4)),
        gather_sems={k: dma((4, 3)) for k in GATHER_SEMS},
        gather_send=dma((4, 3)),
        reduce_sems={k: dma((4, n)) for k, n in zip(SEMS, (4, 4, 4, 4, 3, 5))},
        reduce_send=dma((4, 4)),
        small_sems=dma((17,)),
        small_send=dma((3,)),
        scan_f=dma((2, 16)),
        scan_b=dma((2, 16)),
    )
    leaves, tree = jax.tree.flatten(scratch, is_leaf=lambda v: not isinstance(v, (dict, list)))
    results = [
        jax.ShapeDtypeStruct((rows, width), BF16),
        jax.ShapeDtypeStruct((rows, width), F32),
        *[jax.ShapeDtypeStruct(pack, BF16) for pack in PACKS],
        jax.ShapeDtypeStruct((256, 128), BF16),
    ]

    def body(x, g, wm, wo, w1, w2, fw, mb, fb, *rest):
        vectors, (result, tokens_gradient), rest = rest[:7], rest[7:9], rest[9:]
        given = dict(
            x=x, g=g, wm=wm, wo=wo, w1=w1, w2=w2, fw=fw, mb=mb, fb=fb, vectors=vectors
        )
        block_kernel(
            SimpleNamespace(
                **given,
                result=result,
                tokens_gradient=tokens_gradient,
                outs=rest[:5],
                **jax.tree.unflatten(tree, rest[5:]),
            )
        )

    anywhere = pl.BlockSpec(memory_space=pl.ANY)
    return pl.pallas_call(
        body,
        out_shape=results,
        in_specs=[anywhere] * len(args),
        out_specs=[anywhere] * len(results),
        scratch_shapes=leaves,
        compiler_params=pltpu.CompilerParams(
            collective_id=0, has_side_effects=True, vmem_limit_bytes=67043328
        ),
        name="block",
    )(*args)


def finish_kernel(
    res, tok, outer, inner, q, o, k, v, small,
    res_o, tok_o, outer_o, inner_o, mixer_o, output_o, feature_o, mixer_bias_o, feature_bias_o, *vec_o,
):
    res_o[...] = res[...]
    tok_o[...] = tok[...]
    outer_o[...] = outer[...].astype(F32)
    inner_o[...] = inner[...].astype(F32)
    for i, ref in enumerate((q, k, v)):
        mixer_o[i] = ref[...].astype(F32)
    output_o[...] = o[...].astype(F32)

    @pl.when(pl.program_id(0) == 0)
    def _():
        rows = small[192:256].astype(F32)
        for h in range(3):
            w = small[64 * h : 64 * h + 64].astype(F32)
            feature_o[0, h] = w[:, :64]
            feature_o[1, h] = w[:, 64:]
            pair = rows[9 + h : 10 + h]
            feature_bias_o[h] = jnp.concatenate([pair[:, :64], pair[:, 64:]], axis=0)
            parts = [rows[3 * h + i : 3 * h + i + 1, :64] for i in range(3)]
            mixer_bias_o[h : h + 1] = jnp.concatenate(parts, axis=1)
        for i in range(6):
            vec_o[i][...] = rows[24 + 6 * i : 30 + 6 * i]
        vec_o[6][...] = rows[16:22]


def finish_call(res, tok, outer, inner, early, late, small):
    rows, width = res.shape
    steps = 4

    def spec(n, shift=0):
        return pl.BlockSpec((n, width), lambda i: (i + shift, 0))

    def whole(*shape):
        return pl.BlockSpec(shape, lambda i: (0,) * len(shape))

    def out(*shape):
        return jax.ShapeDtypeStruct(shape, F32)

    vectors = [(6, 128)] * 7
    return pl.pallas_call(
        finish_kernel,
        grid=(steps,),
        in_specs=[
            spec(rows // steps),
            spec(rows // steps),
            spec(768 // steps),
            spec(768 // steps),
            spec(192 // steps),
            spec(192 // steps, steps),
            spec(192 // steps),
            spec(192 // steps, steps),
            whole(256, 128),
        ],
        out_specs=[
            spec(rows // steps),
            spec(rows // steps),
            spec(768 // steps),
            spec(768 // steps),
            pl.BlockSpec((3, 192 // steps, width), lambda i: (0, i, 0)),
            spec(192 // steps),
            whole(2, 3, HD, HD),
            whole(3, 192),
            whole(3, 2, HD),
            *[whole(*v) for v in vectors],
        ],
        out_shape=[
            jax.ShapeDtypeStruct((rows, width), BF16),
            out(rows, width),
            out(768, width),
            out(768, width),
            out(3, 192, width),
            out(192, width),
            out(2, 3, HD, HD),
            out(3, 192),
            out(3, 2, HD),
            *[out(*v) for v in vectors],
        ],
        name="finish",
    )(res, tok, outer, inner, early, early, late, late, small)


def shards(
    fast,
    tokens,
    first_gain,
    first_bias,
    mixer_weight,
    mixer_bias,
    feature_weight,
    feature_bias,
    output_weight,
    output_bias,
    second_gain,
    second_bias,
    inner_weight,
    inner_bias,
    outer_weight,
    outer_bias,
    block_owner,
    cotangent,
):
    rows, width = tokens.shape
    n_tp, n_ctx = lax.axis_size("tp"), lax.axis_size("ctx")
    n_plane = lax.axis_size("dp") * n_ctx
    plane = lax.axis_index("dp") * n_ctx + lax.axis_index("ctx")
    heads_here = mixer_weight.shape[2] // HD
    heads = heads_here * n_tp
    mine = lax.axis_index("ctx") * n_tp + lax.axis_index("tp")

    mixer_t = mixer_weight.transpose(1, 2, 0).reshape(-1, width)
    if fast:
        vectors = (
            first_gain, first_bias, output_bias, second_gain, second_bias, outer_bias, inner_bias
        )
        raw = block_call(
            tokens,
            cotangent,
            mixer_t,
            output_weight,
            inner_weight,
            outer_weight,
            feature_weight,
            mixer_bias,
            feature_bias.transpose(1, 0, 2),
            *[v.reshape(6, 128) for v in vectors],
        )
        (
            result, tokens_gradient, d_outer, d_inner, d_mixer, d_output,
            d_feature, d_mixer_bias, d_feature_bias, *shared
        ) = finish_call(*raw)
        shared = [v.reshape(width) for v in shared]
        return (
            result,
            tokens_gradient,
            shared[0],
            shared[1],
            d_mixer.transpose(2, 0, 1),
            d_mixer_bias,
            d_feature,
            d_feature_bias.transpose(1, 0, 2),
            d_output,
            shared[2],
            shared[3],
            shared[4],
            d_inner,
            shared[6],
            d_outer,
            shared[5],
        )
    sizes = [w.shape[0] for w in (mixer_t, output_weight, inner_weight, outer_weight)]
    pack = jnp.concatenate([mixer_t, output_weight, inner_weight, outer_weight], axis=0)
    part = pack.shape[0] // n_plane
    piece = lax.dynamic_slice_in_dim(pack, plane * part, part, 0)
    full = lax.all_gather(piece, ALL, axis=0, tiled=True)
    full = full.reshape(n_plane, n_tp, part, width).transpose(1, 0, 2, 3).reshape(n_tp, -1, width)
    cuts = [0]
    for s in sizes:
        cuts.append(cuts[-1] + s)
    mixer_all, output_all, inner_all, outer_all = [
        full[:, a:b] for a, b in zip(cuts[:-1], cuts[1:])
    ]
    small = jnp.concatenate(
        [feature_weight.reshape(-1), mixer_bias.reshape(-1), feature_bias.reshape(-1), inner_bias]
    )
    small = lax.all_gather(small, "tp")
    cut = feature_weight.size
    feature_all = (
        small[:, :cut].reshape(n_tp, 2, heads_here, HD, HD).transpose(1, 0, 2, 3, 4)
    ).reshape(2, heads, HD, HD)
    mixer_bias_all = small[:, cut : cut + mixer_bias.size].astype(F32).reshape(n_tp, -1)
    cut += mixer_bias.size
    feature_bias_all = (
        small[:, cut : cut + feature_bias.size]
        .astype(F32)
        .reshape(n_tp, 2, heads_here, HD)
        .transpose(1, 0, 2, 3)
        .reshape(2, heads, HD)
    )
    cut += feature_bias.size
    inner_bias_all = small[:, cut:].astype(F32)

    x = tokens.astype(F32)
    gain1, gain2 = first_gain.astype(F32), second_gain.astype(F32)
    h1, n1, r1 = layer_norm(x, gain1, first_bias.astype(F32))
    h1 = h1.astype(BF16)
    mix = ein("td,skd->tsk", h1, mixer_all) + mixer_bias_all
    mix = mix.astype(BF16).reshape(rows, n_tp, 3, heads_here, HD).transpose(2, 0, 1, 3, 4)
    mix = mix.reshape(3, rows, heads, HD)
    q, k, v = mix[0], mix[1], mix[2]
    q_up, q_down, phi_q = feature_map(q, feature_all[0], feature_bias_all[0])
    k_up, k_down, phi_k = feature_map(k, feature_all[1], feature_bias_all[1])

    chunk = min(CHUNK, rows)
    chunks = rows // chunk
    pq = phi_q.reshape(chunks, chunk, heads, 2 * HD)
    pk = phi_k.reshape(chunks, chunk, heads, 2 * HD)
    vc = v.reshape(chunks, chunk, heads, HD)
    causal = jnp.arange(chunk)[:, None] >= jnp.arange(chunk)[None, :]
    state = ein("jthe,jthf->jhef", vc, pk)
    norm = jnp.sum(pk.astype(F32), axis=1)
    both = jnp.concatenate([state, norm[:, :, None]], axis=2)
    owners = block_owner[0].reshape(n_tp, -1)[:, 0]
    order = jnp.arange(n_ctx * n_tp)
    same = jnp.tile(owners, n_ctx) == jnp.tile(owners, n_ctx)[mine]

    def prefix(totals, reach):
        everything = lax.all_gather(totals.astype(BF16), ("ctx", "tp")).astype(F32)
        return jnp.einsum("s,shef->hef", reach.astype(F32), everything, precision="highest")

    def running(blocks, start, reverse):
        out = [None] * chunks
        acc = start
        for j in reversed(range(chunks)) if reverse else range(chunks):
            out[j] = acc
            acc = acc + blocks[j]
        return jnp.stack(out)

    before = running(both, prefix(jnp.sum(both, axis=0), same & (order < mine)), False)
    before = before.astype(BF16)
    scores = ein("jthf,jshf->jhts", pq, pk)
    a_low = jnp.where(causal, scores, 0.0).astype(BF16)
    v_one = jnp.concatenate([vc, jnp.ones(vc.shape[:-1] + (1,), BF16)], axis=-1)
    num = ein("jthf,jhef->jthe", pq, before) + ein("jhts,jshe->jthe", a_low, v_one)
    num, den = num[..., :HD], num[..., HD:]
    o = num / den
    o_low = o.astype(BF16)
    o_flat = o_low.reshape(rows, n_tp, heads_here * HD)
    x2 = x + ein("tsk,skd->td", o_flat, output_all) + output_bias.astype(F32)
    h2, n2, r2 = layer_norm(x2, gain2, second_bias.astype(F32))
    h2 = h2.astype(BF16)
    f = ein("td,sdf->tsf", h2, inner_all) + inner_bias_all
    a, slope = gelu_parts(f)
    a = a.astype(BF16)
    result = (x2 + ein("tsf,sfd->td", a, outer_all) + outer_bias.astype(F32)).astype(BF16)

    g = cotangent.astype(F32)
    d_outer = ein("tsf,td->sfd", a, cotangent)
    df = (ein("td,sfd->tsf", cotangent, outer_all) * slope).astype(BF16)
    d_inner_bias = jnp.sum(df.astype(F32), axis=0)
    d_inner = ein("td,tsf->sdf", h2, df)
    e2 = ein("tsf,sdf->td", df, inner_all)
    back2, d_gain2, d_bias2 = layer_norm_back(e2, n2, r2, gain2)
    dx2 = g + back2
    big_g = dx2.astype(BF16)
    d_output = ein("tsk,td->skd", o_flat, big_g)
    do = ein("td,skd->tsk", big_g, output_all).astype(BF16).astype(F32)
    do = do.reshape(chunks, chunk, heads, HD)
    dnum = do / den
    dden = -jnp.sum(do * o, axis=-1, keepdims=True) / den
    dne = jnp.concatenate([dnum, dden], axis=-1).astype(BF16)
    da = ein("jthe,jshe->jhts", dne, v_one)
    da_low = jnp.where(causal, da, 0.0).astype(BF16)
    d_both = ein("jthe,jthf->jhef", dne, pq)
    after = running(d_both, prefix(jnp.sum(d_both, axis=0), same & (order > mine)), True)
    after = after.astype(BF16)
    dphi_q = ein("jhts,jshf->jthf", da_low, pk) + ein("jthe,jhef->jthf", dne, before)
    dphi_k = ein("jhts,jthf->jshf", da_low, pq) + ein("jthe,jhef->jthf", v_one, after)
    dv = ein("jhts,jthe->jshe", a_low, dne[..., :HD]) + ein("jthf,jhef->jthe", pk, after[:, :, :HD])
    dphi_q = dphi_q.reshape(rows, heads, 2 * HD)
    dphi_k = dphi_k.reshape(rows, heads, 2 * HD)
    dq, d_fq, d_fbq = feature_back(dphi_q, q_up, q_down, q, feature_all[0])
    dk, d_fk, d_fbk = feature_back(dphi_k, k_up, k_down, k, feature_all[1])
    dmix = jnp.stack([dq, dk, dv.reshape(rows, heads, HD)], axis=1).astype(BF16)
    dmix = dmix.reshape(rows, 3, n_tp, heads_here * HD).transpose(0, 2, 1, 3)
    dmix = dmix.reshape(rows, n_tp, -1)
    d_mixer_bias = jnp.sum(dmix.astype(F32), axis=0)
    d_mixer = ein("tsk,td->skd", dmix, h1)
    e1 = ein("tsk,skd->td", dmix, mixer_all)
    back1, d_gain1, d_bias1 = layer_norm_back(e1, n1, r1, gain1)
    tokens_gradient = dx2 + back1

    big = jnp.concatenate([d_mixer, d_output, d_inner, d_outer], axis=1).astype(BF16)
    big = big.reshape(n_tp, n_plane, part, width).transpose(1, 0, 2, 3).reshape(-1, width)
    big = lax.psum_scatter(big, ("dp", "ctx"), scatter_dimension=0, tiled=True)
    big = lax.psum_scatter(big, "tp", scatter_dimension=0, tiled=True)
    big = lax.all_gather(big, ("dp", "ctx"), axis=0, tiled=True).astype(F32)
    d_mixer, d_output, d_inner, d_outer = [big[a:b] for a, b in zip(cuts[:-1], cuts[1:])]
    d_mixer = d_mixer.reshape(3, heads_here * HD, width).transpose(2, 0, 1)
    per_tp = jnp.concatenate(
        [
            jnp.stack([d_fq, d_fk]).reshape(2, n_tp, -1).transpose(1, 0, 2).reshape(n_tp, -1),
            d_mixer_bias,
            jnp.stack([d_fbq, d_fbk]).reshape(2, n_tp, -1).transpose(1, 0, 2).reshape(n_tp, -1),
            d_inner_bias,
        ],
        axis=1,
    )
    shared = jnp.stack(
        [d_gain1, d_bias1, jnp.sum(dx2, axis=0), d_gain2, d_bias2, jnp.sum(g, axis=0)]
    )
    total = lax.psum(jnp.concatenate([per_tp.reshape(-1), shared.reshape(-1)]), ALL)
    shared = total[per_tp.size :].reshape(6, width)
    own = lax.dynamic_slice_in_dim(
        total[: per_tp.size].reshape(n_tp, -1), lax.axis_index("tp"), 1, 0
    )[0]
    cut = feature_weight.size
    d_feature = own[:cut].reshape(feature_weight.shape)
    d_mixer_bias = own[cut : cut + mixer_bias.size].reshape(mixer_bias.shape)
    cut += mixer_bias.size
    d_feature_bias = own[cut : cut + feature_bias.size].reshape(feature_bias.shape)
    d_inner_bias = own[cut + feature_bias.size :]
    return (
        result,
        tokens_gradient,
        shared[0],
        shared[1],
        d_mixer,
        d_mixer_bias,
        d_feature,
        d_feature_bias,
        d_output,
        shared[2],
        shared[3],
        shared[4],
        d_inner,
        d_inner_bias,
        d_outer,
        shared[5],
    )


def solution(mesh):
    in_specs = (
        P(("dp", "ctx", "tp"), None),
        P(),
        P(),
        P(None, None, "tp"),
        P(None, "tp"),
        P(None, "tp", None, None),
        P(None, "tp", None),
        P("tp", None),
        P(),
        P(),
        P(),
        P(None, "tp"),
        P("tp"),
        P("tp", None),
        P(),
        P("dp", None),
        P(("dp", "ctx", "tp"), None),
    )
    out_specs = (
        P(("dp", "ctx", "tp"), None),
        P(("dp", "ctx", "tp"), None),
        P(),
        P(),
        P(None, None, "tp"),
        P(None, "tp"),
        P(None, "tp", None, None),
        P(None, "tp", None),
        P("tp", None),
        P(),
        P(),
        P(),
        P(None, "tp"),
        P("tp"),
        P("tp", None),
        P(),
    )
    fast = (mesh.shape["dp"], mesh.shape["ctx"], mesh.shape["tp"]) == (2, 4, 4)
    return jax.shard_map(functools.partial(shards, fast), mesh=mesh, in_specs=in_specs, out_specs=out_specs, check_vma=False)
```

```python
import functools
from types import SimpleNamespace

import jax
import jax.numpy as jnp
from jax import lax
from jax.experimental import pallas as pl
from jax.experimental.pallas import tpu as pltpu
from jax.sharding import PartitionSpec as P

MESH = pl.DeviceIdType.MESH

HD = 64
BLOCK = 64
CHUNK = 256
EPSILON = 1e-05
F32 = jnp.float32
BF16 = jnp.bfloat16
ALL = ("dp", "ctx", "tp")


def ein(spec, a, b):
    return jnp.einsum(spec, a, b, preferred_element_type=F32)


def layer_norm(v, gain, offset):
    c = v - jnp.mean(v, axis=-1, keepdims=True)
    r = lax.rsqrt(jnp.mean(c * c, axis=-1, keepdims=True) + EPSILON)
    n = c * r
    return n * gain + offset, n, r


def layer_norm_back(e, n, r, gain):
    m = e * gain
    back = r * (
        m - jnp.mean(m, axis=-1, keepdims=True) - n * jnp.mean(m * n, axis=-1, keepdims=True)
    )
    return back, jnp.sum(e * n, axis=0), jnp.sum(e, axis=0)


def gelu_parts(s):
    t = jnp.tanh(0.7978845608028654 * (s + 0.044715 * s * s * s))
    slope = 0.7978845608028654 * (1.0 + 3.0 * 0.044715 * s * s)
    return 0.5 * s * (1.0 + t), 0.5 * (1.0 + t) + 0.5 * s * (1.0 - t * t) * slope


def feature_map(q, weight, offset):
    u = ein("thd,hde->the", q, weight) + offset
    up, down = jax.nn.softmax(u, axis=-1), jax.nn.softmax(-u, axis=-1)
    return up, down, jnp.concatenate([up, down], axis=-1).astype(BF16)


def feature_back(delta, up, down, q, weight):
    d, dd = delta[..., :HD], delta[..., HD:]
    du = up * (d - jnp.sum(up * d, axis=-1, keepdims=True)) - down * (
        dd - jnp.sum(down * dd, axis=-1, keepdims=True)
    )
    low = du.astype(BF16)
    return ein("the,hde->thd", low, weight), ein("thd,the->hde", q, low), jnp.sum(du, axis=0)


HD = 64
BLOCK = 64
CHUNK = 256
EPSILON = 1e-05
F32 = jnp.float32
BF16 = jnp.bfloat16
ALL = ("dp", "ctx", "tp")


def ein(spec, a, b):
    return jnp.einsum(spec, a, b, preferred_element_type=F32)


def layer_norm(v, gain, offset):
    c = v - jnp.mean(v, axis=-1, keepdims=True)
    r = lax.rsqrt(jnp.mean(c * c, axis=-1, keepdims=True) + EPSILON)
    n = c * r
    return n * gain + offset, n, r


def layer_norm_back(e, n, r, gain):
    m = e * gain
    back = r * (
        m - jnp.mean(m, axis=-1, keepdims=True) - n * jnp.mean(m * n, axis=-1, keepdims=True)
    )
    return back, jnp.sum(e * n, axis=0), jnp.sum(e, axis=0)


def gelu_parts(s):
    t = jnp.tanh(0.7978845608028654 * (s + 0.044715 * s * s * s))
    slope = 0.7978845608028654 * (1.0 + 3.0 * 0.044715 * s * s)
    return 0.5 * s * (1.0 + t), 0.5 * (1.0 + t) + 0.5 * s * (1.0 - t * t) * slope


def feature_map(q, weight, offset):
    u = ein("thd,hde->the", q, weight) + offset
    up, down = jax.nn.softmax(u, axis=-1), jax.nn.softmax(-u, axis=-1)
    return up, down, jnp.concatenate([up, down], axis=-1).astype(BF16)


def feature_back(delta, up, down, q, weight):
    d, dd = delta[..., :HD], delta[..., HD:]
    du = up * (d - jnp.sum(up * d, axis=-1, keepdims=True)) - down * (
        dd - jnp.sum(down * dd, axis=-1, keepdims=True)
    )
    low = du.astype(BF16)
    return ein("the,hde->thd", low, weight), ein("thd,the->hde", q, low), jnp.sum(du, axis=0)


def place():
    d, c, t = lax.axis_index("dp"), lax.axis_index("ctx"), lax.axis_index("tp")
    y, core = c // 2, lax.rem(c, 2)
    return SimpleNamespace(d=d, c=c, t=t, y=y, core=core, q=d * 2 + y,
        x_nb=(1 - d, c, t), y_nb=(d, (1 - y) * 2 + core, t), core_nb=(d, y * 2 + 1 - core, t),
        qx=(1 - d) * 2 + y, qy=d * 2 + 1 - y, qd=(1 - d) * 2 + 1 - y)

def plane_peer(p, r):
    d = 1 - p.d if r & 4 else p.d
    y = 1 - p.y if r & 2 else p.y
    core = 1 - p.core if r & 1 else p.core
    return (d, y * 2 + core, p.t), d * 4 + y * 2 + core


def greet(p):
    bar = pltpu.get_barrier_semaphore()
    peers = [plane_peer(p, r)[0] for r in range(1, 8)]
    peers += [(p.d, p.c, lax.rem(p.t + k, 4)) for k in (1, 2, 3)]
    for peer in peers:
        pl.semaphore_signal(bar, inc=1, device_id=peer, device_id_type=MESH)


def met(p):
    pl.semaphore_wait(pltpu.get_barrier_semaphore(), 10)


def nearest(t):
    return [
        jnp.where(t < 2, 1, 3),
        jnp.where(t == 0, 2, jnp.where(t == 1, 3, jnp.where(t == 2, 1, 2))),
        jnp.where(t == 0, 3, jnp.where(t == 3, 1, 2)),
    ]


class Gather:
    def __init__(self, p, buf, sems, send, index):
        self.p, self.buf, self.sems, self.send, self.i = p, buf, sems, send.at[index], index
        self.rows = buf.shape[1]
        self.piece = self.rows // 8
        self.half = self.piece // 2
    def at(self, t, q, core, half=None):
        start = q * (2 * self.piece) + core * self.piece
        size = self.piece
        if half is not None:
            start, size = start + half * self.half, self.half
        return self.buf.at[t, pl.ds(pl.multiple_of(start, 16), size)]
    def shard(self, k): return lax.rem(self.p.t + k, 4)
    def copy(self, ref, kind, k, peer):
        n = 0 if kind == "z" else 2 if kind == "c" else 1
        recv = self.sems[kind].at[self.i, k - 1]
        return pltpu.make_async_remote_copy(
            ref, ref, self.send.at[n], recv, device_id=peer, device_id_type=MESH
        )

    def go(self, *a):
        self.copy(*a).start()

    def first(self):
        p = self.p
        ref = self.at(p.t, p.q, p.core)
        for k in (1, 2, 3):
            self.go(ref, "z", 4 - k, (p.d, p.c, lax.rem(p.t + k, 4)))

    def first_hop(self):
        p = self.p
        ref = self.at(p.t, p.q, p.core)
        pl.when(p.t < 3)(lambda: self.go(ref, "z", 3, (p.d, p.c, p.t + 1)))
        pl.when(p.t > 0)(lambda: self.go(ref, "z", 1, (p.d, p.c, p.t - 1)))

    def zf(self, k):
        p, t = self.p, self.shard(k)
        ref = self.at(t, p.q, p.core)
        self.copy(ref, "z", k, p.x_nb).wait_recv()
        up = jnp.logical_and(t < p.t, p.t < 3)
        down = jnp.logical_and(t > p.t, p.t > 0)
        pl.when(up)(lambda: self.go(ref, "z", k - 1, (p.d, p.c, p.t + 1)))
        pl.when(down)(lambda: self.go(ref, "z", k + 1, (p.d, p.c, p.t - 1)))

    def spread(self, k):
        p = self.p
        ref = self.at(self.shard(k), p.q, p.core)
        self.go(ref, "x", k, p.x_nb)
        self.go(ref, "y", k, p.y_nb)

    def z(self, k):
        p, t = self.p, self.shard(k)
        ref = self.at(t, p.q, p.core)
        self.copy(ref, "z", k, p.x_nb).wait_recv()
        self.go(ref, "x", k, p.x_nb); self.go(ref, "y", k, p.y_nb)
    def xy(self, k):
        p, t = self.p, self.shard(k)
        self.copy(self.at(t, p.qx, p.core), "x", k, p.x_nb).wait_recv()
        self.go(self.at(t, p.qx, p.core, 0), "fy", k, p.y_nb)
        self.copy(self.at(t, p.qy, p.core), "y", k, p.y_nb).wait_recv()
        self.go(self.at(t, p.qy, p.core, 1), "fx", k, p.x_nb)
    def diag(self, k):
        p, t = self.p, self.shard(k)
        self.copy(self.at(t, p.qd, p.core, 0), "fy", k, p.y_nb).wait_recv()
        self.copy(self.at(t, p.qd, p.core, 1), "fx", k, p.x_nb).wait_recv()
        for q in range(4):
            self.go(self.at(t, q, p.core), "c", k, p.core_nb)
    def done(self, k):
        p, t = self.p, self.shard(k)
        self.copy(self.buf.at[t, pl.ds(0, 4 * self.piece)], "c", k, p.core_nb).wait_recv()

    def drain(self, hops):
        p = self.p

        def wait(kind, ref):
            self.copy(ref, kind, 1, p.core_nb).wait_send()

        line = lambda n: wait("z", self.buf.at[0, pl.ds(0, n * self.piece)])
        if hops:
            ends = jnp.logical_or(p.t == 0, p.t == 3)
            pl.when(ends)(lambda: line(1))
            pl.when(jnp.logical_not(ends))(lambda: line(5))
        else:
            line(3)
        wait("x", self.buf.at[pl.ds(0, 3), pl.ds(0, 3 * self.piece)])
        wait("c", self.buf.at[pl.ds(0, 3), pl.ds(0, 4 * self.piece)])


def lanes(core):
    return pl.ds(pl.multiple_of(core * 384, 128), 384)


class Reduce:
    def __init__(self, p, i, G, X1, Y1, X2, Y2, Z, OUT, sems, send, own):
        self.p, self.i, self.G, self.OUT, self.sems = p, i, G, OUT, sems
        self.X1, self.Y1, self.X2, self.Y2, self.Z = X1, Y1, X2, Y2, Z
        self.half = G.shape[1]; self.qr = self.half // 4; self.hr = self.qr // 2
        self.send = send
        self.own = own
    def t(self, k): return lax.rem(self.p.t + k, 4)
    def rows(self, q, h): return pl.ds(pl.multiple_of(q * self.qr + h * self.hr, 16), self.hr)
    def rdma(self, src, dst, kind, k, peer):
        n = 1 if kind == "z" else 0 if kind != "f" else 3 if k == 4 else 2
        return pltpu.make_async_remote_copy(
            src,
            dst,
            self.send.at[self.i, n],
            self.sems[kind].at[self.i, k],
            device_id=peer,
            device_id_type=MESH,
        )

    def go(self, *a):
        self.rdma(*a).start()

    def got(self, ref, kind, k):
        self.rdma(ref, ref, kind, k, self.p.x_nb).wait_recv()
    def one(self, k):
        p, t = self.p, self.t(k)
        for j in range(2):
            self.go(self.G.at[t, self.rows((1 - p.d) * 2 + j, 0)], self.X1.at[k, j], "x1", k, p.x_nb)
            self.go(self.G.at[t, self.rows(j * 2 + 1 - p.y, 1)], self.Y1.at[k, j], "y1", k, p.y_nb)
    def two(self, k):
        p, t, G = self.p, self.t(k), self.G
        self.got(self.X1.at[k], "x1", k)
        for j in range(2):
            r = self.rows(p.d * 2 + j, 0)
            G[t, r] = G[t, r] + self.X1[k, j]
        self.go(G.at[t, self.rows(p.qy, 0)], self.Y2.at[k], "y2", k, p.y_nb)
        self.got(self.Y1.at[k], "y1", k)
        for j in range(2):
            r = self.rows(j * 2 + p.y, 1)
            G[t, r] = G[t, r] + self.Y1[k, j]
        self.go(G.at[t, self.rows(p.qx, 1)], self.X2.at[k], "x2", k, p.x_nb)
    def three(self, k):
        p, t, G = self.p, self.t(k), self.G
        for h, (kind, R) in enumerate((("y2", self.Y2), ("x2", self.X2))):
            self.got(R.at[k], kind, k)
            r = self.rows(p.q, h)
            G[t, r] = G[t, r] + R[k]
        if not isinstance(k, int):
            whole = pl.ds(pl.multiple_of(p.q * self.qr, 16), self.qr)
            self.go(G.at[t, whole], self.Z.at[3 - k], "z", 3 - k, (p.d, p.c, t))
    def piece(self, q, core, h=None):
        start, size = q * self.qr, self.qr
        if h is not None:
            start, size = start + h * self.hr, self.hr
        return self.OUT.at[pl.ds(pl.multiple_of(start, 16), size), lanes(core)]

    def final(self):
        p = self.p
        whole = pl.ds(pl.multiple_of(p.q * self.qr, 16), self.qr)
        total = self.G[p.t, whole].astype(F32)
        for k in range(3):
            self.got(self.Z.at[k], "z", k)
            total = total + self.Z[k].astype(F32)
        ref = self.piece(p.q, p.core)
        mine = self.G.at[p.t, whole]
        mine[...] = total.astype(BF16)
        self.go(mine, ref, "f", 0, p.x_nb)
        self.go(mine, ref, "f", 1, p.y_nb)
        self.own_copy().start()

    def own_copy(self):
        p = self.p
        whole = pl.ds(pl.multiple_of(p.q * self.qr, 16), self.qr)
        return pltpu.make_async_copy(
            self.G.at[p.t, whole], self.piece(p.q, p.core), self.own.at[self.i]
        )

    def spread(self):
        p = self.p
        ref = self.piece(p.qx, p.core); self.got(ref, "f", 0)
        ref = self.piece(p.qx, p.core, 0); self.go(ref, ref, "f", 2, p.y_nb)
        ref = self.piece(p.qy, p.core); self.got(ref, "f", 1)
        ref = self.piece(p.qy, p.core, 1); self.go(ref, ref, "f", 3, p.x_nb)
    def corner(self):
        p = self.p
        self.own_copy().wait()
        self.got(self.piece(p.qd, p.core, 0), "f", 2); self.got(self.piece(p.qd, p.core, 1), "f", 3)
        ref = self.OUT.at[:, lanes(p.core)]
        self.go(ref, ref, "f", 4, p.core_nb)
    def end(self):
        p = self.p
        self.got(self.OUT.at[:, lanes(1 - p.core)], "f", 4)
        rows = 3 * self.half // 4
        sizes = (
            ("x1", 0, self.G.at[pl.ds(0, 3)]),
            ("z", 0, self.Z),
            ("f", 0, self.G.at[0, pl.ds(0, rows)]),
            ("f", 4, self.G.at[0]),
        )
        for kind, k, ref in sizes:
            self.rdma(ref, ref, kind, k, p.core_nb).wait_send()


GATHER_SEMS = ("z", "x", "y", "fx", "fy", "c")
SEMS = ("x1", "y1", "x2", "y2", "z", "f")


def dot(a, b, ca, cb):
    return lax.dot_general(a, b, (((ca,), (cb,)), ((), ())), preferred_element_type=F32)


def loop(n, step):
    def body(i, carry):
        step(i)
        return carry

    lax.fori_loop(0, n, body, 0)


def ds(i, n):
    return pl.ds(pl.multiple_of(i * n, n), n)


class Scan:
    def __init__(self, p, later, total, up, down, got, sems):
        self.p, self.later, self.total, self.up_ref, self.down_ref = p, later, total, up, down
        self.from_core, self.from_y, self.from_below, self.from_above = [got.at[i] for i in range(4)]
        self.sems = sems

    def rdma(self, src, dst, g, i, peer):
        h, i = self.heads(g), 4 * i + g
        return pltpu.make_async_remote_copy(
            src.at[h], dst.at[h], self.sems.at[0, i], self.sems.at[1, i], device_id=peer, device_id_type=MESH
        )

    def core_copy(self, g):
        return self.rdma(self.total, self.from_core, g, 0, self.p.core_nb)

    def y_copy(self, g):
        return self.rdma(self.up_ref, self.from_y, g, 1, self.p.y_nb)

    def line_copy(self, g, upward):
        p = self.p
        if upward:
            return self.rdma(self.up_ref, self.from_below, g, 2, (p.d, p.c, p.t + 1))
        return self.rdma(self.down_ref, self.from_above, g, 3, (p.d, p.c, p.t - 1))

    def heads(self, g):
        return pl.ds(3 * g, 3)

    def begin(self, g):
        h = self.heads(g)
        zero = jnp.zeros((3, 80, 128), BF16)

        @pl.when(self.p.t == 0)
        def _():
            self.from_below[h] = zero

        @pl.when(self.p.t == 3)
        def _():
            self.from_above[h] = zero

        self.core_copy(g).start()

    def pair(self, g):
        h = self.heads(g)
        self.core_copy(g).wait_recv()
        self.up_ref[h] = self.total[h] + self.from_core[h]
        self.y_copy(g).start()

    def column(self, g):
        p, h = self.p, self.heads(g)
        core, y = p.core.astype(F32), p.y.astype(F32)
        if self.later:
            core, y = 1.0 - core, 1.0 - y
        return core * self.from_core[h].astype(F32) + y * self.from_y[h].astype(F32)

    def hop(self, g, upward):
        h, t = self.heads(g), self.p.t
        has, sends = (t > 0, t < 3) if upward else (t < 3, t > 0)
        c = self.line_copy(g, upward)
        got = self.from_below if upward else self.from_above
        out = self.up_ref if upward else self.down_ref

        @pl.when(has)
        def _():
            c.wait_recv()

        @pl.when(sends)
        def _():
            value = self.column(g) + got[h].astype(F32)
            if upward != self.later:
                value = value + self.total[h].astype(F32)
            out[h] = value.astype(BF16)
            c.start()

    def chain(self, g):
        c = self.y_copy(g)
        c.wait_recv()
        c.wait_send()
        pl.when(self.p.t < 2)(lambda: self.hop(g, True))
        pl.when(self.p.t >= 2)(lambda: self.hop(g, False))

    def relay(self, g):
        pl.when(self.p.t == 1)(lambda: self.hop(g, False))
        pl.when(self.p.t == 2)(lambda: self.hop(g, True))

    def last(self, g):
        pl.when(self.p.t == 0)(lambda: self.hop(g, False))
        pl.when(self.p.t == 3)(lambda: self.hop(g, True))

    def sum(self, g):
        h = self.heads(g)
        return self.column(g) + self.from_below[h].astype(F32) + self.from_above[h].astype(F32)

    def drain(self):
        for g in range(4):
            self.core_copy(g).wait_send()
            pl.when(self.p.t < 3)(lambda g=g: self.line_copy(g, True).wait_send())
            pl.when(self.p.t > 0)(lambda g=g: self.line_copy(g, False).wait_send())


class Small:
    def __init__(self, p, low, full, plane, line, mid, out, sems, send, own):
        self.p, self.low, self.full, self.plane, self.line, self.mid, self.out = (
            p, low, full, plane, line, mid, out
        )
        self.sems, self.send, self.own = sems, send, own
        self.me = p.d * 4 + p.c

    def rdma(self, src, dst, i, peer):
        n = 0 if i < 7 else 1 if i < 10 else 2
        return pltpu.make_async_remote_copy(
            src, dst, self.send.at[n], self.sems.at[i], device_id=peer, device_id_type=MESH
        )

    def go(self, *a):
        self.rdma(*a).start()

    def begin(self):
        for r in range(1, 8):
            peer, j = plane_peer(self.p, r)
            self.go(self.low.at[ds(j, 32)], self.plane.at[r - 1], r - 1, peer)

    def across(self):
        p = self.p
        for r in range(1, 8):
            self.rdma(self.plane.at[r - 1], self.plane.at[r - 1], r - 1, p.x_nb).wait_recv()
        for t in range(4):
            total = self.full[t, ds(self.me, 32)]
            for r in range(7):
                total = total + self.plane[r, :, 128 * t : 128 * t + 128].astype(F32)
            self.full[t, ds(self.me, 32)] = total
            self.mid[t] = total.astype(BF16)
        for k in (1, 2, 3):
            t = lax.rem(p.t + k, 4)
            self.go(self.mid.at[t], self.line.at[3 - k], 10 - k, (p.d, p.c, t))

    def final(self):
        p = self.p
        total = self.full[p.t, ds(self.me, 32)]
        for k in range(3):
            self.rdma(self.line.at[k], self.line.at[k], 7 + k, p.x_nb).wait_recv()
            total = total + self.line[k].astype(F32)
        self.mid[4] = total.astype(BF16)
        ref = self.out.at[ds(self.me, 32)]
        for r in range(1, 8):
            self.go(self.mid.at[4], ref, 9 + r, plane_peer(p, r)[0])
        pltpu.make_async_copy(self.mid.at[4], ref, self.own).start()

    def end(self):
        pltpu.make_async_copy(self.mid.at[4], self.out.at[ds(self.me, 32)], self.own).wait()
        for r in range(1, 8):
            peer, j = plane_peer(self.p, r)
            ref = self.out.at[ds(j, 32)]
            self.rdma(ref, ref, 9 + r, peer).wait_recv()
        for i, ref in ((0, self.plane), (7, self.line), (10, self.plane.at[:, :, pl.ds(0, 128)])):
            self.rdma(ref, ref, i, self.p.core_nb).wait_send()


def layer_rows(v):
    c = v - jnp.mean(v, axis=-1, keepdims=True)
    r = lax.rsqrt(jnp.mean(c * c, axis=-1, keepdims=True) + EPSILON)
    return c * r, r


def fold(v):
    total = v[:8]
    for i in range(1, v.shape[0] // 8):
        total = total + v[8 * i : 8 * i + 8]
    return total


def layer_back(e, n, r, gain):
    m = e * gain
    return r * (
        m - jnp.mean(m, axis=-1, keepdims=True) - n * jnp.mean(m * n, axis=-1, keepdims=True)
    )


def block_kernel(m):
    p = place()
    t0 = p.t
    X, CT, S, WA, W1, W2 = m.X, m.CT, m.S, m.WA, m.W1, m.W2
    VEC, H1, H2, X2, ACC_O, ACC_E = m.VEC, m.H1, m.H2, m.X2, m.ACC_O, m.ACC_E
    MIX, PH, VX, AT, PX, SL, OT, RD = m.MIX, m.PH, m.VX, m.AT, m.PX, m.SL, m.OT, m.RD
    A, DF, GS, FW, BC, IB, SUMS = m.A, m.DF, m.GS, m.FW, m.BC, m.IB, m.SUMS
    ld = m.ld
    greet(p)
    loads = [
        pltpu.make_async_copy(m.wm, WA.at[t0, pl.ds(0, 576)], ld.at[0]),
        pltpu.make_async_copy(m.wo, WA.at[t0, pl.ds(576, 192)], ld.at[1]),
        pltpu.make_async_copy(m.x, X, ld.at[2]),
        pltpu.make_async_copy(m.w1, W1.at[t0], ld.at[3]),
        pltpu.make_async_copy(m.w2, W2.at[t0], ld.at[4]),
        pltpu.make_async_copy(m.g, CT, ld.at[5]),
    ]
    raw = [(m.fw, m.FWI), (m.mb, m.MBI), (m.fb, m.FBI)]
    raw += [(ref, m.VECI.at[i, pl.ds(0, 6)]) for i, ref in enumerate(m.vectors)]
    raw = [pltpu.make_async_copy(src, dst, ld.at[8 + i]) for i, (src, dst) in enumerate(raw)]
    for c in raw + loads:
        c.start()
    for c in raw:
        c.wait()

    for h in range(3):
        pair = [m.FWI[i, h].astype(F32) for i in range(2)]
        S[t0, 64 * h : 64 * h + 64] = jnp.concatenate(pair, axis=1).astype(BF16)
    zero = jnp.zeros((1, HD), F32)
    rows = []
    for j in range(3):
        row = m.MBI[j : j + 1].astype(F32)
        rows += [
            jnp.concatenate([row[:, HD * h : HD * h + HD], zero], axis=1) for h in range(3)
        ]
    for h in range(3):
        row = m.FBI[h].astype(F32)
        rows.append(jnp.concatenate([row[0:1], row[1:2]], axis=1))
    rows.append(jnp.zeros((4, 128), F32))
    S[t0, 192:208] = jnp.concatenate(rows, axis=0).astype(BF16)
    rows = [m.VECI[6].astype(F32)[0:6], jnp.zeros((42, 128), F32)]
    S[t0, 208:256] = jnp.concatenate(rows, axis=0).astype(BF16)
    for k in range(6):
        value = m.VECI[k].astype(F32)
        for i in range(6):
            VEC[k : k + 1, 128 * i : 128 * i + 128] = value[i : i + 1]

    gs, gw, g1, g2 = gathers = [
        Gather(p, b, m.gather_sems, m.gather_send, i) for i, b in enumerate((S, WA, W1, W2))
    ]
    K = nearest(t0)
    shard = gs.shard
    loads[0].wait()
    loads[1].wait()
    met(p)
    gw.first()
    gs.first()

    loads[2].wait()

    def norm1(i):
        r = ds(i, 128)
        n, _ = layer_rows(X[r].astype(F32))
        H1[r] = (n * VEC[0:1] + VEC[1:2]).astype(BF16)

    loop(4, norm1)
    ones_row = jnp.where(lax.broadcasted_iota(jnp.int32, (16, 512), 0) == 0, 1.0, 0.0).astype(BF16)

    def init(h):
        VX[h, 64:80] = ones_row

    loop(12, init)
    SUMS[...] = jnp.zeros_like(SUMS)

    def small(t):
        BC[...] = S[t, 192:208].astype(F32).T
        rows = S[t, 208:224].astype(F32)
        for i in range(6):
            IB[t, :, 128 * i : 128 * i + 128] = rows[i : i + 1]
        for h in range(3):
            w = S[t, 64 * h : 64 * h + 64].astype(F32)
            FW[0, t * 3 + h] = w[:, :64].astype(BF16)
            FW[1, t * 3 + h] = w[:, 64:].astype(BF16)

    def mix(t):
        value = dot(WA[t, 0:576], H1[...], 1, 1)
        for j in range(3):
            for h in range(3):
                n = j * 3 + h
                part = (value[64 * n : 64 * n + 64] + BC[0:64, n : n + 1]).astype(BF16)
                if j < 2:
                    MIX[t, 64 * n : 64 * n + 64] = part
                else:
                    VX[t * 3 + h, 0:64] = part

    def features(t):
        for h in range(3):
            for i in range(2):
                u = dot(FW[i, t * 3 + h], MIX[t, 192 * i + 64 * h : 192 * i + 64 * h + 64], 0, 0)
                u = u + BC[64 * i : 64 * i + 64, 9 + h : 10 + h]
                e = jnp.exp(u - jnp.max(u, axis=0, keepdims=True))
                PH[i, t * 3 + h, 0:64] = (e / jnp.sum(e, axis=0, keepdims=True)).astype(BF16)
                e = jnp.exp(jnp.min(u, axis=0, keepdims=True) - u)
                PH[i, t * 3 + h, 64:128] = (e / jnp.sum(e, axis=0, keepdims=True)).astype(BF16)

    def states(t):
        def one(i):
            h = t * 3 + i
            s0 = dot(VX[h, :, 0:256], PH[1, h, :, 0:256], 1, 1)
            s1 = dot(VX[h, :, 256:512], PH[1, h, :, 256:512], 1, 1)
            SL[h] = s0
            m.TOT[h] = (s0 + s1).astype(BF16)

        loop(3, one)

    small(t0)
    mix(t0)
    features(t0)
    states(t0)
    both = (g1, g2)
    for n, k in enumerate(K):
        gw.z(k)
        gs.z(k)
        if n == 1:
            loads[3].wait()
            loads[4].wait()
            for g in both:
                g.first_hop()
    for k in K:
        gw.xy(k)
        gs.xy(k)
    for k in K:
        gw.diag(k)
        gs.diag(k)
    middle = jnp.logical_or(t0 == 1, t0 == 2)
    for g in both:
        g.zf(K[0])
        g.spread(K[0])
    for g in both:
        pl.when(middle)(lambda g=g: g.zf(K[1]))
    def arrived(n):
        k = jnp.where(n == 0, K[0], jnp.where(n == 1, K[1], K[2]))
        gs.done(k)
        gw.done(k)
        t = shard(k)
        small(t)
        mix(t)
        features(t)
        states(t)

    loop(3, arrived)
    scan = Scan(p, False, m.TOT, m.UP, m.DOWN, m.got_f, m.scan_f)
    for g in range(4):
        scan.begin(g)
    causal = lax.broadcasted_iota(jnp.int32, (256, 256), 0) <= lax.broadcasted_iota(
        jnp.int32, (256, 256), 1
    )

    def scores(h):
        for j in range(2):
            c = slice(256 * j, 256 * j + 256)
            a = dot(PH[1, h, :, c], PH[0, h, :, c], 0, 0)
            AT[h, j] = jnp.where(causal, a, 0.0).astype(BF16)

    for g in both:
        g.zf(jnp.where(middle, K[2], K[1]))
    for g in range(4):
        scan.pair(g)
    loop(12, scores)
    for g in range(4):
        scan.chain(g)
    for g in both:
        g.xy(K[0])
        g.spread(K[1])
    for g in both:
        pl.when(jnp.logical_not(middle))(lambda g=g: g.zf(K[2]))
    for g in range(4):
        scan.relay(g)
    for g in both:
        g.spread(K[2])

    def enter(first):
        for g in range(4):
            scan.last(g)
            value = scan.sum(g)
            h = scan.heads(g)
            PX[h, first] = value.astype(BF16)
            PX[h, 1 - first] = (value + SL[h]).astype(BF16)

    enter(0)

    def attend(h):
        for j in range(2):
            c = slice(256 * j, 256 * j + 256)
            num = dot(PX[h, j], PH[0, h, :, c], 1, 0) + dot(VX[h, :, c], AT[h, j], 1, 0)
            r = 1.0 / num[64:65]
            RD[h, :, c] = r
            OT[ds(h, 64), c] = (num[0:64] * r).astype(BF16)

    loop(12, attend)

    def norm2(i):
        r = ds(i, 256)
        total = X[r].astype(F32) + VEC[2:3]
        for t in range(4):
            total = total + dot(OT[192 * t : 192 * t + 192, r], WA[t, 576:768], 0, 0)
        X2[r] = total
        n, _ = layer_rows(total)
        H2[r] = (n * VEC[3:4] + VEC[4:5]).astype(BF16)
        ACC_O[r] = total + VEC[5:6]
        ACC_E[r] = jnp.zeros((256, 768), F32)

    loop(2, norm2)

    R = [
        Reduce(p, i, m.G[i], *m.land[i][1:], m.Z[i], m.outs[i], m.reduce_sems, m.reduce_send, m.own)
        for i in range(4)
    ]
    core_sems, STAGE = m.r_core, m.STAGE
    outgoing = []

    def core_copy(src, i, k):
        ref = m.land[i][0].at[shard(k)]
        return pltpu.make_async_remote_copy(
            ref if src is None else src,
            ref,
            core_sems.at[0, i, k],
            core_sems.at[1, i, k],
            device_id=p.core_nb,
            device_id_type=MESH,
        )

    def hand(i, k, value):
        slot = len(outgoing) % 2
        if len(outgoing) >= 2:
            outgoing[-2].wait_send()
        ref = STAGE.at[slot, pl.ds(0, R[i].half)]
        ref[...] = value(1 - p.core).astype(BF16)
        c = core_copy(ref, i, k)
        c.start()
        outgoing.append(c)
        R[i].G[shard(k)] = value(p.core).astype(BF16)

    def meet(i, k):
        t = shard(k)
        G, C = R[i].G, m.land[i][0]
        core_copy(None, i, k).wait_recv()

        def add(j):
            r = ds(j, 96)
            G[t, r] = G[t, r] + C[t, r]

        loop(R[i].half // 96, add)
        R[i].one(k)

    def hidden(t, slot):
        def rows(i):
            r = ds(i, 256)
            f = dot(H2[r], W1[t], 1, 0) + IB[t]
            th = jnp.tanh(0.7978845608028654 * (f + 0.044715 * f * f * f))
            a = (0.5 * f * (1.0 + th)).astype(BF16)
            A[slot, r] = a
            slope = 0.5 * (1.0 + th) + 0.5 * f * (1.0 - th * th) * (
                0.7978845608028654 * (1.0 + 3.0 * 0.044715 * f * f)
            )
            df = (dot(CT[r], W2[t], 1, 1) * slope).astype(BF16)
            DF[slot, r] = df
            m.DIB[t] += fold(df.astype(F32))
            ACC_O[r] += dot(a, W2[t], 1, 0)
            ACC_E[r] += dot(df, W1[t], 1, 1)

        loop(2, rows)

    def hand_hidden(k, slot):
        hand(0, k, lambda core: dot(A[slot], CT[:, lanes(core)], 0, 0))
        hand(1, k, lambda core: dot(H2[...], DF[slot, :, lanes(core)], 0, 0))

    m.DIB[...] = jnp.zeros_like(m.DIB)
    order = [0] + K
    loads[5].wait()
    for g in both:
        g.diag(K[0])
        g.xy(K[1])
    hidden(t0, 0)
    for g in both:
        g.xy(K[2])
        g.diag(K[1])
    hand_hidden(0, 0)
    for n, k in enumerate(K):
        g1.done(k)
        g2.done(k)
        hidden(shard(k), n // 2)
        if n == 0:
            for g in both:
                g.diag(K[2])
        if n < 2:
            for i in range(2):
                meet(i, order[n])
        if n < 1:
            hand_hidden(k, 0)
    for g in both:
        g.drain(True)
    RES, GG = W1.at[2, pl.ds(0, 512)], W1.at[3, pl.ds(0, 512)]

    def dne(h):
        start = pl.multiple_of(lax.rem(h, 9) * 80, 16)
        return W2.at[h // 9, pl.ds(start, 80), pl.ds(0, 512)]

    def du_of(h):
        return W1.at[h // 6, ds(lax.rem(h, 6), 128), pl.ds(0, 512)]

    def dv_of(h):
        return W2.at[2, ds(h, 64), pl.ds(0, 512)]

    def back2(i):
        r = ds(i, 128)
        n, s = layer_rows(X2[r])
        e = ACC_E[r]
        g = CT[r].astype(F32)
        dx = g + layer_back(e, n, s, VEC[3:4])
        SUMS[3] += fold(e * n)
        SUMS[4] += fold(e)
        SUMS[2] += fold(dx)
        SUMS[5] += fold(g)
        X2[r] = dx
        GG[r] = dx.astype(BF16)

    loop(4, back2)
    DX = X2
    first_row = lax.broadcasted_iota(jnp.int32, (16, 512), 0) == 0

    scan.drain()
    scan = Scan(p, True, m.TOT, m.UP, m.DOWN, m.got_b, m.scan_b)

    def states_back(t):
        value = dot(WA[t, 576:768], GG[...], 1, 1).astype(BF16).astype(F32)
        for i in range(3):
            h = 3 * t + i
            do = value[64 * i : 64 * i + 64]
            r = RD[h]
            o = OT[ds(h, 64)].astype(F32)
            ref = dne(h)
            ref[0:64] = (do * r).astype(BF16)
            dden = -jnp.sum(do * o, axis=0, keepdims=True) * r
            ref[64:80] = jnp.where(first_row, dden, 0.0).astype(BF16)
            s0 = dot(ref[:, 0:256], PH[0, h, :, 0:256], 1, 1)
            s1 = dot(ref[:, 256:512], PH[0, h, :, 256:512], 1, 1)
            SL[h] = s1
            m.TOT[h] = (s0 + s1).astype(BF16)

    def give(t):
        states_back(t)
        scan.begin(t)

    loop(4, give)
    hand(0, order[2], lambda core: dot(A[0], CT[:, lanes(core)], 0, 0))
    for g in range(4):
        scan.pair(g)
    for i in range(2):
        R[i].two(order[0])
    hand(1, order[2], lambda core: dot(H2[...], DF[0, :, lanes(core)], 0, 0))
    for i in range(2):
        R[i].two(order[1])

    def feature_back(i, h, delta):
        delta = delta.astype(BF16).astype(F32)
        up, down = PH[i, h, 0:64].astype(F32), PH[i, h, 64:128].astype(F32)
        d, dd = delta[0:64], delta[64:128]
        du = up * (d - jnp.sum(up * d, axis=0, keepdims=True)) - down * (
            dd - jnp.sum(down * dd, axis=0, keepdims=True)
        )
        du_of(h)[64 * i : 64 * i + 64] = du.astype(BF16)

    def query_back(h):
        parts = []
        ref, dv = dne(h), dv_of(h)
        for j in range(2):
            c = slice(256 * j, 256 * j + 256)
            value = ref[:, c]
            dv[:, c] = dot(ref[0:64, c], AT[h, j], 1, 1).astype(BF16)
            da = dot(VX[h, :, c], value, 0, 0)
            da = jnp.where(causal, da, 0.0).astype(BF16)
            AT[h, j] = da
            parts.append(dot(PH[1, h, :, c], da, 1, 0) + dot(PX[h, j], value, 0, 0))
        feature_back(0, h, jnp.concatenate(parts, axis=1))

    ones8 = jnp.ones((8, 512), BF16)
    left = lax.broadcasted_iota(jnp.int32, (64, 128), 1) < 64
    GS[:, 192:256] = jnp.zeros((4, 64, 128), F32)

    def bias_row(t, j, i):
        ref = MIX[t, ds(3 * j + i, 64)]
        GS[t, pl.ds(192 + 3 * j + i, 1), 0:64] = dot(ones8, ref, 1, 1)[0:1]

    def early(k):
        t = shard(k)
        def one(i):
            h = t * 3 + i
            rows = ds(i, 64)
            du = du_of(h)[0:64]
            GS[t, rows, 0:64] = dot(MIX[t, rows], du, 1, 1)
            MIX[t, rows] = dot(FW[0, h], du, 1, 0).astype(BF16)
            bias_row(t, 0, i)

        loop(3, one)

        def value(core):
            both = [
                dot(MIX[t, 0:192], H1[:, lanes(core)], 1, 0),
                dot(OT[ds(t, 192)], GG[:, lanes(core)], 1, 0),
            ]
            return jnp.concatenate(both, axis=0)

        hand(2, k, value)

    def queries(g):
        loop(3, lambda i: query_back(3 * g + i))

    def ask(g):
        queries(g)
        scan.chain(g)

    loop(2, ask)
    for i in range(2):
        meet(i, order[2])
    loop(2, lambda g: ask(g + 2))
    for i in range(2):
        R[i].three(order[0])
        R[i].three(order[1])
    for g in range(4):
        scan.relay(g)
    hand_hidden(order[3], 1)
    RES[...] = ACC_O[...].astype(BF16)
    res_copy = pltpu.make_async_copy(RES, m.result, ld.at[6])
    res_copy.start()
    for i in range(2):
        R[i].two(order[2])
        meet(i, order[3])
    early(order[0])
    early(order[1])
    meet(2, order[0])
    R[0].three(order[2])
    early(order[2])
    meet(2, order[1])
    R[1].three(order[2])
    for i in range(2):
        R[i].two(order[3])
    early(order[3])
    meet(2, order[2])
    enter(1)

    def key_back(t, i):
        h = t * 3 + i
        parts, values = [], []
        for j in range(2):
            c = slice(256 * j, 256 * j + 256)
            q = PX[h, j]
            parts.append(dot(PH[0, h, :, c], AT[h, j], 1, 1) + dot(q, VX[h, :, c], 0, 0))
            values.append(dot(q[0:64], PH[1, h, :, c], 1, 0))
        feature_back(1, h, jnp.concatenate(parts, axis=1))
        dv = jnp.concatenate(values, axis=1) + dv_of(h)[...].astype(F32)
        MIX[t, ds(6 + i, 64)] = dv.astype(BF16)
        du = du_of(h)
        rows = ds(3 + i, 64)
        ref = ds(i, 64)
        GS[t, ref] = jnp.where(left, GS[t, ref], dot(MIX[t, rows], du[...], 1, 1))
        GS[t, pl.ds(201 + i, 1)] = dot(ones8, du[...], 1, 1)[0:1]
        MIX[t, rows] = dot(FW[1, h], du[64:128], 1, 0).astype(BF16)
        bias_row(t, 1, i)
        bias_row(t, 2, i)

    for n, k in enumerate(order):
        t = shard(k)
        loop(3, lambda i: key_back(t, i))
        hand(3, k, lambda core: dot(MIX[t, 192:576], H1[:, lanes(core)], 1, 0))
        if n == 0:
            meet(2, order[3])
            R[2].two(order[0])
            R[2].two(order[1])
        else:
            meet(3, order[n - 1])
        if n == 1:
            R[0].three(order[3])
            R[1].three(order[3])
            R[2].two(order[2])
        if n == 2:
            R[2].two(order[3])
            R[2].three(order[0])
            R[2].three(order[1])
            R[2].three(order[2])
            R[3].two(order[0])
        if n == 3:
            R[2].three(order[3])
            R[3].two(order[1])
            R[3].three(order[0])

    def back1(i):
        r = ds(i, 256)
        e = dot(MIX[0, :, r], WA[0, 0:576], 0, 0)
        for t in range(1, 4):
            e = e + dot(MIX[t, :, r], WA[t, 0:576], 0, 0)
        n, s = layer_rows(X[r].astype(F32))
        SUMS[0] += fold(e * n)
        SUMS[1] += fold(e)
        ACC_E[r] = DX[r] + layer_back(e, n, s, VEC[0:1])

    back1(0)
    meet(3, order[3])
    R[3].two(order[2])
    R[0].final()
    R[3].three(order[1])
    R[1].final()
    back1(1)
    R[0].spread()
    tok_copy = pltpu.make_async_copy(ACC_E, m.tokens_gradient, ld.at[7])
    tok_copy.start()
    for k in range(6):
        row = jnp.sum(SUMS[k], axis=0, keepdims=True)
        for i in range(6):
            for t in range(4):
                GS[t, 216 + 6 * k + i : 217 + 6 * k + i] = row[:, 128 * i : 128 * i + 128]
    for t in range(4):
        row = jnp.sum(m.DIB[t], axis=0, keepdims=True)
        for i in range(6):
            GS[t, 208 + i : 209 + i] = row[:, 128 * i : 128 * i + 128]
    GB = W2.at[3, pl.ds(0, 256), pl.ds(0, 512)]
    for t in range(4):
        GB[:, 128 * t : 128 * t + 128] = GS[t].astype(BF16)
    tiny = Small(p, GB, GS, m.plane, m.line, m.mid, m.outs[4], m.small_sems, m.small_send, m.own.at[4])
    tiny.begin()
    R[3].two(order[3])
    R[1].spread()
    R[3].three(order[2])
    R[2].final()
    R[0].corner()
    R[3].three(order[3])
    R[1].corner()
    tiny.across()
    R[2].spread()
    R[3].final()
    tiny.final()
    R[2].corner()
    R[3].spread()
    R[3].corner()
    for r in R:
        r.end()
    tiny.end()
    scan.drain()
    for c in outgoing[-2:]:
        c.wait_send()
    gs.drain(False)
    gw.drain(False)
    res_copy.wait()
    tok_copy.wait()


PACKS = ((768, 768), (768, 768), (384, 768), (384, 768))


def landing(rows):
    q, r = rows // 4, rows // 8
    shapes = ((4, rows), (4, 2, r), (4, 2, r), (4, r), (4, r))
    return [pltpu.VMEM((*shape, 384), BF16) for shape in shapes]


def block_call(*args):
    rows, width = args[0].shape
    flat = pltpu.VMEM((rows, width), BF16)
    wide = pltpu.VMEM((rows, width), F32)
    weights = pltpu.VMEM((4, 768, 768), BF16)
    state = pltpu.VMEM((12, 80, 128), BF16)
    dma = pltpu.SemaphoreType.DMA
    scratch = dict(
        X=flat,
        CT=flat,
        S=pltpu.VMEM((4, 256, 128), BF16),
        WA=weights,
        W1=weights,
        W2=weights,
        VEC=pltpu.VMEM((8, 768), F32),
        VECI=pltpu.VMEM((7, 8, 128), BF16),
        FWI=pltpu.VMEM((2, 3, HD, HD), BF16),
        MBI=pltpu.VMEM((3, 192), BF16),
        FBI=pltpu.VMEM((3, 2, HD), BF16),
        H1=flat,
        H2=flat,
        X2=wide,
        ACC_O=wide,
        ACC_E=wide,
        MIX=pltpu.VMEM((4, 576, rows), BF16),
        PH=pltpu.VMEM((2, 12, 128, rows), BF16),
        VX=pltpu.VMEM((12, 80, rows), BF16),
        AT=pltpu.VMEM((12, 2, 256, 256), BF16),
        PX=pltpu.VMEM((12, 2, 80, 128), BF16),
        SL=pltpu.VMEM((12, 80, 128), F32),
        OT=pltpu.VMEM((768, rows), BF16),
        RD=pltpu.VMEM((12, 1, rows), F32),
        A=pltpu.VMEM((2, rows, width), BF16),
        DF=pltpu.VMEM((2, rows, width), BF16),
        GS=pltpu.VMEM((4, 256, 128), F32),
        FW=pltpu.VMEM((2, 12, 64, 64), BF16),
        BC=pltpu.VMEM((128, 16), F32),
        IB=pltpu.VMEM((4, 1, 768), F32),
        SUMS=pltpu.VMEM((6, 8, 768), F32),
        DIB=pltpu.VMEM((4, 8, 768), F32),
        TOT=state,
        UP=state,
        DOWN=state,
        got_f=pltpu.VMEM((4, 12, 80, 128), BF16),
        got_b=pltpu.VMEM((4, 12, 80, 128), BF16),
        plane=pltpu.VMEM((7, 32, 512), BF16),
        line=pltpu.VMEM((3, 32, 128), BF16),
        mid=pltpu.VMEM((5, 32, 128), BF16),
        STAGE=pltpu.VMEM((2, 768, 384), BF16),
        G=[pltpu.VMEM((4, n, 384), BF16) for n, _ in PACKS],
        Z=[pltpu.VMEM((3, n // 4, 384), BF16) for n, _ in PACKS],
        land=[landing(n) for n, _ in PACKS],
        ld=dma((18,)),
        own=dma((5,)),
        r_core=dma((2, 4, 4)),
        gather_sems={k: dma((4, 3)) for k in GATHER_SEMS},
        gather_send=dma((4, 3)),
        reduce_sems={k: dma((4, n)) for k, n in zip(SEMS, (4, 4, 4, 4, 3, 5))},
        reduce_send=dma((4, 4)),
        small_sems=dma((17,)),
        small_send=dma((3,)),
        scan_f=dma((2, 16)),
        scan_b=dma((2, 16)),
    )
    leaves, tree = jax.tree.flatten(scratch, is_leaf=lambda v: not isinstance(v, (dict, list)))
    results = [
        jax.ShapeDtypeStruct((rows, width), BF16),
        jax.ShapeDtypeStruct((rows, width), F32),
        *[jax.ShapeDtypeStruct(pack, BF16) for pack in PACKS],
        jax.ShapeDtypeStruct((256, 128), BF16),
    ]

    def body(x, g, wm, wo, w1, w2, fw, mb, fb, *rest):
        vectors, (result, tokens_gradient), rest = rest[:7], rest[7:9], rest[9:]
        given = dict(
            x=x, g=g, wm=wm, wo=wo, w1=w1, w2=w2, fw=fw, mb=mb, fb=fb, vectors=vectors
        )
        block_kernel(
            SimpleNamespace(
                **given,
                result=result,
                tokens_gradient=tokens_gradient,
                outs=rest[:5],
                **jax.tree.unflatten(tree, rest[5:]),
            )
        )

    anywhere = pl.BlockSpec(memory_space=pl.ANY)
    return pl.pallas_call(
        body,
        out_shape=results,
        in_specs=[anywhere] * len(args),
        out_specs=[anywhere] * len(results),
        scratch_shapes=leaves,
        compiler_params=pltpu.CompilerParams(
            collective_id=0, has_side_effects=True, vmem_limit_bytes=67043328
        ),
        name="block",
    )(*args)


def finish_kernel(
    res, tok, outer, inner, q, o, k, v, small,
    res_o, tok_o, outer_o, inner_o, mixer_o, output_o, feature_o, mixer_bias_o, feature_bias_o, *vec_o,
):
    res_o[...] = res[...]
    tok_o[...] = tok[...]
    outer_o[...] = outer[...].astype(F32)
    inner_o[...] = inner[...].astype(F32)
    for i, ref in enumerate((q, k, v)):
        mixer_o[i] = ref[...].astype(F32)
    output_o[...] = o[...].astype(F32)

    @pl.when(pl.program_id(0) == 0)
    def _():
        rows = small[192:256].astype(F32)
        for h in range(3):
            w = small[64 * h : 64 * h + 64].astype(F32)
            feature_o[0, h] = w[:, :64]
            feature_o[1, h] = w[:, 64:]
            pair = rows[9 + h : 10 + h]
            feature_bias_o[h] = jnp.concatenate([pair[:, :64], pair[:, 64:]], axis=0)
            parts = [rows[3 * h + i : 3 * h + i + 1, :64] for i in range(3)]
            mixer_bias_o[h : h + 1] = jnp.concatenate(parts, axis=1)
        for i in range(6):
            vec_o[i][...] = rows[24 + 6 * i : 30 + 6 * i]
        vec_o[6][...] = rows[16:22]


def finish_call(res, tok, outer, inner, early, late, small):
    rows, width = res.shape
    steps = 4

    def spec(n, shift=0):
        return pl.BlockSpec((n, width), lambda i: (i + shift, 0))

    def whole(*shape):
        return pl.BlockSpec(shape, lambda i: (0,) * len(shape))

    def out(*shape):
        return jax.ShapeDtypeStruct(shape, F32)

    vectors = [(6, 128)] * 7
    return pl.pallas_call(
        finish_kernel,
        grid=(steps,),
        in_specs=[
            spec(rows // steps),
            spec(rows // steps),
            spec(768 // steps),
            spec(768 // steps),
            spec(192 // steps),
            spec(192 // steps, steps),
            spec(192 // steps),
            spec(192 // steps, steps),
            whole(256, 128),
        ],
        out_specs=[
            spec(rows // steps),
            spec(rows // steps),
            spec(768 // steps),
            spec(768 // steps),
            pl.BlockSpec((3, 192 // steps, width), lambda i: (0, i, 0)),
            spec(192 // steps),
            whole(2, 3, HD, HD),
            whole(3, 192),
            whole(3, 2, HD),
            *[whole(*v) for v in vectors],
        ],
        out_shape=[
            jax.ShapeDtypeStruct((rows, width), BF16),
            out(rows, width),
            out(768, width),
            out(768, width),
            out(3, 192, width),
            out(192, width),
            out(2, 3, HD, HD),
            out(3, 192),
            out(3, 2, HD),
            *[out(*v) for v in vectors],
        ],
        name="finish",
    )(res, tok, outer, inner, early, early, late, late, small)


def shards(
    fast,
    tokens,
    first_gain,
    first_bias,
    mixer_weight,
    mixer_bias,
    feature_weight,
    feature_bias,
    output_weight,
    output_bias,
    second_gain,
    second_bias,
    inner_weight,
    inner_bias,
    outer_weight,
    outer_bias,
    block_owner,
    cotangent,
):
    rows, width = tokens.shape
    n_tp, n_ctx = lax.axis_size("tp"), lax.axis_size("ctx")
    n_plane = lax.axis_size("dp") * n_ctx
    plane = lax.axis_index("dp") * n_ctx + lax.axis_index("ctx")
    heads_here = mixer_weight.shape[2] // HD
    heads = heads_here * n_tp
    mine = lax.axis_index("ctx") * n_tp + lax.axis_index("tp")

    mixer_t = mixer_weight.transpose(1, 2, 0).reshape(-1, width)
    if fast:
        vectors = (
            first_gain, first_bias, output_bias, second_gain, second_bias, outer_bias, inner_bias
        )
        raw = block_call(
            tokens,
            cotangent,
            mixer_t,
            output_weight,
            inner_weight,
            outer_weight,
            feature_weight,
            mixer_bias,
            feature_bias.transpose(1, 0, 2),
            *[v.reshape(6, 128) for v in vectors],
        )
        (
            result, tokens_gradient, d_outer, d_inner, d_mixer, d_output,
            d_feature, d_mixer_bias, d_feature_bias, *shared
        ) = finish_call(*raw)
        shared = [v.reshape(width) for v in shared]
        return (
            result,
            tokens_gradient,
            shared[0],
            shared[1],
            d_mixer.transpose(2, 0, 1),
            d_mixer_bias,
            d_feature,
            d_feature_bias.transpose(1, 0, 2),
            d_output,
            shared[2],
            shared[3],
            shared[4],
            d_inner,
            shared[6],
            d_outer,
            shared[5],
        )
    sizes = [w.shape[0] for w in (mixer_t, output_weight, inner_weight, outer_weight)]
    pack = jnp.concatenate([mixer_t, output_weight, inner_weight, outer_weight], axis=0)
    part = pack.shape[0] // n_plane
    piece = lax.dynamic_slice_in_dim(pack, plane * part, part, 0)
    full = lax.all_gather(piece, ALL, axis=0, tiled=True)
    full = full.reshape(n_plane, n_tp, part, width).transpose(1, 0, 2, 3).reshape(n_tp, -1, width)
    cuts = [0]
    for s in sizes:
        cuts.append(cuts[-1] + s)
    mixer_all, output_all, inner_all, outer_all = [
        full[:, a:b] for a, b in zip(cuts[:-1], cuts[1:])
    ]
    small = jnp.concatenate(
        [feature_weight.reshape(-1), mixer_bias.reshape(-1), feature_bias.reshape(-1), inner_bias]
    )
    small = lax.all_gather(small, "tp")
    cut = feature_weight.size
    feature_all = (
        small[:, :cut].reshape(n_tp, 2, heads_here, HD, HD).transpose(1, 0, 2, 3, 4)
    ).reshape(2, heads, HD, HD)
    mixer_bias_all = small[:, cut : cut + mixer_bias.size].astype(F32).reshape(n_tp, -1)
    cut += mixer_bias.size
    feature_bias_all = (
        small[:, cut : cut + feature_bias.size]
        .astype(F32)
        .reshape(n_tp, 2, heads_here, HD)
        .transpose(1, 0, 2, 3)
        .reshape(2, heads, HD)
    )
    cut += feature_bias.size
    inner_bias_all = small[:, cut:].astype(F32)

    x = tokens.astype(F32)
    gain1, gain2 = first_gain.astype(F32), second_gain.astype(F32)
    h1, n1, r1 = layer_norm(x, gain1, first_bias.astype(F32))
    h1 = h1.astype(BF16)
    mix = ein("td,skd->tsk", h1, mixer_all) + mixer_bias_all
    mix = mix.astype(BF16).reshape(rows, n_tp, 3, heads_here, HD).transpose(2, 0, 1, 3, 4)
    mix = mix.reshape(3, rows, heads, HD)
    q, k, v = mix[0], mix[1], mix[2]
    q_up, q_down, phi_q = feature_map(q, feature_all[0], feature_bias_all[0])
    k_up, k_down, phi_k = feature_map(k, feature_all[1], feature_bias_all[1])

    chunk = min(CHUNK, rows)
    chunks = rows // chunk
    pq = phi_q.reshape(chunks, chunk, heads, 2 * HD)
    pk = phi_k.reshape(chunks, chunk, heads, 2 * HD)
    vc = v.reshape(chunks, chunk, heads, HD)
    causal = jnp.arange(chunk)[:, None] >= jnp.arange(chunk)[None, :]
    state = ein("jthe,jthf->jhef", vc, pk)
    norm = jnp.sum(pk.astype(F32), axis=1)
    both = jnp.concatenate([state, norm[:, :, None]], axis=2)
    owners = block_owner[0].reshape(n_tp, -1)[:, 0]
    order = jnp.arange(n_ctx * n_tp)
    same = jnp.tile(owners, n_ctx) == jnp.tile(owners, n_ctx)[mine]

    def prefix(totals, reach):
        everything = lax.all_gather(totals.astype(BF16), ("ctx", "tp")).astype(F32)
        return jnp.einsum("s,shef->hef", reach.astype(F32), everything, precision="highest")

    def running(blocks, start, reverse):
        out = [None] * chunks
        acc = start
        for j in reversed(range(chunks)) if reverse else range(chunks):
            out[j] = acc
            acc = acc + blocks[j]
        return jnp.stack(out)

    before = running(both, prefix(jnp.sum(both, axis=0), same & (order < mine)), False)
    before = before.astype(BF16)
    scores = ein("jthf,jshf->jhts", pq, pk)
    a_low = jnp.where(causal, scores, 0.0).astype(BF16)
    v_one = jnp.concatenate([vc, jnp.ones(vc.shape[:-1] + (1,), BF16)], axis=-1)
    num = ein("jthf,jhef->jthe", pq, before) + ein("jhts,jshe->jthe", a_low, v_one)
    num, den = num[..., :HD], num[..., HD:]
    o = num / den
    o_low = o.astype(BF16)
    o_flat = o_low.reshape(rows, n_tp, heads_here * HD)
    x2 = x + ein("tsk,skd->td", o_flat, output_all) + output_bias.astype(F32)
    h2, n2, r2 = layer_norm(x2, gain2, second_bias.astype(F32))
    h2 = h2.astype(BF16)
    f = ein("td,sdf->tsf", h2, inner_all) + inner_bias_all
    a, slope = gelu_parts(f)
    a = a.astype(BF16)
    result = (x2 + ein("tsf,sfd->td", a, outer_all) + outer_bias.astype(F32)).astype(BF16)

    g = cotangent.astype(F32)
    d_outer = ein("tsf,td->sfd", a, cotangent)
    df = (ein("td,sfd->tsf", cotangent, outer_all) * slope).astype(BF16)
    d_inner_bias = jnp.sum(df.astype(F32), axis=0)
    d_inner = ein("td,tsf->sdf", h2, df)
    e2 = ein("tsf,sdf->td", df, inner_all)
    back2, d_gain2, d_bias2 = layer_norm_back(e2, n2, r2, gain2)
    dx2 = g + back2
    big_g = dx2.astype(BF16)
    d_output = ein("tsk,td->skd", o_flat, big_g)
    do = ein("td,skd->tsk", big_g, output_all).astype(BF16).astype(F32)
    do = do.reshape(chunks, chunk, heads, HD)
    dnum = do / den
    dden = -jnp.sum(do * o, axis=-1, keepdims=True) / den
    dne = jnp.concatenate([dnum, dden], axis=-1).astype(BF16)
    da = ein("jthe,jshe->jhts", dne, v_one)
    da_low = jnp.where(causal, da, 0.0).astype(BF16)
    d_both = ein("jthe,jthf->jhef", dne, pq)
    after = running(d_both, prefix(jnp.sum(d_both, axis=0), same & (order > mine)), True)
    after = after.astype(BF16)
    dphi_q = ein("jhts,jshf->jthf", da_low, pk) + ein("jthe,jhef->jthf", dne, before)
    dphi_k = ein("jhts,jthf->jshf", da_low, pq) + ein("jthe,jhef->jthf", v_one, after)
    dv = ein("jhts,jthe->jshe", a_low, dne[..., :HD]) + ein("jthf,jhef->jthe", pk, after[:, :, :HD])
    dphi_q = dphi_q.reshape(rows, heads, 2 * HD)
    dphi_k = dphi_k.reshape(rows, heads, 2 * HD)
    dq, d_fq, d_fbq = feature_back(dphi_q, q_up, q_down, q, feature_all[0])
    dk, d_fk, d_fbk = feature_back(dphi_k, k_up, k_down, k, feature_all[1])
    dmix = jnp.stack([dq, dk, dv.reshape(rows, heads, HD)], axis=1).astype(BF16)
    dmix = dmix.reshape(rows, 3, n_tp, heads_here * HD).transpose(0, 2, 1, 3)
    dmix = dmix.reshape(rows, n_tp, -1)
    d_mixer_bias = jnp.sum(dmix.astype(F32), axis=0)
    d_mixer = ein("tsk,td->skd", dmix, h1)
    e1 = ein("tsk,skd->td", dmix, mixer_all)
    back1, d_gain1, d_bias1 = layer_norm_back(e1, n1, r1, gain1)
    tokens_gradient = dx2 + back1

    big = jnp.concatenate([d_mixer, d_output, d_inner, d_outer], axis=1).astype(BF16)
    big = big.reshape(n_tp, n_plane, part, width).transpose(1, 0, 2, 3).reshape(-1, width)
    big = lax.psum_scatter(big, ("dp", "ctx"), scatter_dimension=0, tiled=True)
    big = lax.psum_scatter(big, "tp", scatter_dimension=0, tiled=True)
    big = lax.all_gather(big, ("dp", "ctx"), axis=0, tiled=True).astype(F32)
    d_mixer, d_output, d_inner, d_outer = [big[a:b] for a, b in zip(cuts[:-1], cuts[1:])]
    d_mixer = d_mixer.reshape(3, heads_here * HD, width).transpose(2, 0, 1)
    per_tp = jnp.concatenate(
        [
            jnp.stack([d_fq, d_fk]).reshape(2, n_tp, -1).transpose(1, 0, 2).reshape(n_tp, -1),
            d_mixer_bias,
            jnp.stack([d_fbq, d_fbk]).reshape(2, n_tp, -1).transpose(1, 0, 2).reshape(n_tp, -1),
            d_inner_bias,
        ],
        axis=1,
    )
    shared = jnp.stack(
        [d_gain1, d_bias1, jnp.sum(dx2, axis=0), d_gain2, d_bias2, jnp.sum(g, axis=0)]
    )
    total = lax.psum(jnp.concatenate([per_tp.reshape(-1), shared.reshape(-1)]), ALL)
    shared = total[per_tp.size :].reshape(6, width)
    own = lax.dynamic_slice_in_dim(
        total[: per_tp.size].reshape(n_tp, -1), lax.axis_index("tp"), 1, 0
    )[0]
    cut = feature_weight.size
    d_feature = own[:cut].reshape(feature_weight.shape)
    d_mixer_bias = own[cut : cut + mixer_bias.size].reshape(mixer_bias.shape)
    cut += mixer_bias.size
    d_feature_bias = own[cut : cut + feature_bias.size].reshape(feature_bias.shape)
    d_inner_bias = own[cut + feature_bias.size :]
    return (
        result,
        tokens_gradient,
        shared[0],
        shared[1],
        d_mixer,
        d_mixer_bias,
        d_feature,
        d_feature_bias,
        d_output,
        shared[2],
        shared[3],
        shared[4],
        d_inner,
        d_inner_bias,
        d_outer,
        shared[5],
    )


def solution(mesh):
    in_specs = (
        P(("dp", "ctx", "tp"), None),
        P(),
        P(),
        P(None, None, "tp"),
        P(None, "tp"),
        P(None, "tp", None, None),
        P(None, "tp", None),
        P("tp", None),
        P(),
        P(),
        P(),
        P(None, "tp"),
        P("tp"),
        P("tp", None),
        P(),
        P("dp", None),
        P(("dp", "ctx", "tp"), None),
    )
    out_specs = (
        P(("dp", "ctx", "tp"), None),
        P(("dp", "ctx", "tp"), None),
        P(),
        P(),
        P(None, None, "tp"),
        P(None, "tp"),
        P(None, "tp", None, None),
        P(None, "tp", None),
        P("tp", None),
        P(),
        P(),
        P(),
        P(None, "tp"),
        P("tp"),
        P("tp", None),
        P(),
    )
    fast = (mesh.shape["dp"], mesh.shape["ctx"], mesh.shape["tp"]) == (2, 4, 4)
    return jax.shard_map(functools.partial(shards, fast), mesh=mesh, in_specs=in_specs, out_specs=out_specs, check_vma=False)
```

```python
import functools
from types import SimpleNamespace

import jax
import jax.numpy as jnp
from jax import lax
from jax.experimental import pallas as pl
from jax.experimental.pallas import tpu as pltpu
from jax.sharding import PartitionSpec as P

MESH = pl.DeviceIdType.MESH

HD = 64
BLOCK = 64
CHUNK = 256
EPSILON = 1e-05
F32 = jnp.float32
BF16 = jnp.bfloat16
ALL = ("dp", "ctx", "tp")


def ein(spec, a, b):
    return jnp.einsum(spec, a, b, preferred_element_type=F32)


def layer_norm(v, gain, offset):
    c = v - jnp.mean(v, axis=-1, keepdims=True)
    r = lax.rsqrt(jnp.mean(c * c, axis=-1, keepdims=True) + EPSILON)
    n = c * r
    return n * gain + offset, n, r


def layer_norm_back(e, n, r, gain):
    m = e * gain
    back = r * (
        m - jnp.mean(m, axis=-1, keepdims=True) - n * jnp.mean(m * n, axis=-1, keepdims=True)
    )
    return back, jnp.sum(e * n, axis=0), jnp.sum(e, axis=0)


def gelu_parts(s):
    t = jnp.tanh(0.7978845608028654 * (s + 0.044715 * s * s * s))
    slope = 0.7978845608028654 * (1.0 + 3.0 * 0.044715 * s * s)
    return 0.5 * s * (1.0 + t), 0.5 * (1.0 + t) + 0.5 * s * (1.0 - t * t) * slope


def feature_map(q, weight, offset):
    u = ein("thd,hde->the", q, weight) + offset
    up, down = jax.nn.softmax(u, axis=-1), jax.nn.softmax(-u, axis=-1)
    return up, down, jnp.concatenate([up, down], axis=-1).astype(BF16)


def feature_back(delta, up, down, q, weight):
    d, dd = delta[..., :HD], delta[..., HD:]
    du = up * (d - jnp.sum(up * d, axis=-1, keepdims=True)) - down * (
        dd - jnp.sum(down * dd, axis=-1, keepdims=True)
    )
    low = du.astype(BF16)
    return ein("the,hde->thd", low, weight), ein("thd,the->hde", q, low), jnp.sum(du, axis=0)


HD = 64
BLOCK = 64
CHUNK = 256
EPSILON = 1e-05
F32 = jnp.float32
BF16 = jnp.bfloat16
ALL = ("dp", "ctx", "tp")


def ein(spec, a, b):
    return jnp.einsum(spec, a, b, preferred_element_type=F32)


def layer_norm(v, gain, offset):
    c = v - jnp.mean(v, axis=-1, keepdims=True)
    r = lax.rsqrt(jnp.mean(c * c, axis=-1, keepdims=True) + EPSILON)
    n = c * r
    return n * gain + offset, n, r


def layer_norm_back(e, n, r, gain):
    m = e * gain
    back = r * (
        m - jnp.mean(m, axis=-1, keepdims=True) - n * jnp.mean(m * n, axis=-1, keepdims=True)
    )
    return back, jnp.sum(e * n, axis=0), jnp.sum(e, axis=0)


def gelu_parts(s):
    t = jnp.tanh(0.7978845608028654 * (s + 0.044715 * s * s * s))
    slope = 0.7978845608028654 * (1.0 + 3.0 * 0.044715 * s * s)
    return 0.5 * s * (1.0 + t), 0.5 * (1.0 + t) + 0.5 * s * (1.0 - t * t) * slope


def feature_map(q, weight, offset):
    u = ein("thd,hde->the", q, weight) + offset
    up, down = jax.nn.softmax(u, axis=-1), jax.nn.softmax(-u, axis=-1)
    return up, down, jnp.concatenate([up, down], axis=-1).astype(BF16)


def feature_back(delta, up, down, q, weight):
    d, dd = delta[..., :HD], delta[..., HD:]
    du = up * (d - jnp.sum(up * d, axis=-1, keepdims=True)) - down * (
        dd - jnp.sum(down * dd, axis=-1, keepdims=True)
    )
    low = du.astype(BF16)
    return ein("the,hde->thd", low, weight), ein("thd,the->hde", q, low), jnp.sum(du, axis=0)


def place():
    d, c, t = lax.axis_index("dp"), lax.axis_index("ctx"), lax.axis_index("tp")
    y, core = c // 2, lax.rem(c, 2)
    return SimpleNamespace(d=d, c=c, t=t, y=y, core=core, q=d * 2 + y,
        x_nb=(1 - d, c, t), y_nb=(d, (1 - y) * 2 + core, t), core_nb=(d, y * 2 + 1 - core, t),
        qx=(1 - d) * 2 + y, qy=d * 2 + 1 - y, qd=(1 - d) * 2 + 1 - y)

def plane_peer(p, r):
    d = 1 - p.d if r & 4 else p.d
    y = 1 - p.y if r & 2 else p.y
    core = 1 - p.core if r & 1 else p.core
    return (d, y * 2 + core, p.t), d * 4 + y * 2 + core


def greet(p):
    bar = pltpu.get_barrier_semaphore()
    peers = [plane_peer(p, r)[0] for r in range(1, 8)]
    peers += [(p.d, p.c, lax.rem(p.t + k, 4)) for k in (1, 2, 3)]
    for peer in peers:
        pl.semaphore_signal(bar, inc=1, device_id=peer, device_id_type=MESH)


def met(p):
    pl.semaphore_wait(pltpu.get_barrier_semaphore(), 10)


def nearest(t):
    return [
        jnp.where(t < 2, 1, 3),
        jnp.where(t == 0, 2, jnp.where(t == 1, 3, jnp.where(t == 2, 1, 2))),
        jnp.where(t == 0, 3, jnp.where(t == 3, 1, 2)),
    ]


class Gather:
    def __init__(self, p, buf, sems, send, index):
        self.p, self.buf, self.sems, self.send, self.i = p, buf, sems, send.at[index], index
        self.rows = buf.shape[1]
        self.piece = self.rows // 8
        self.half = self.piece // 2
    def at(self, t, q, core, half=None):
        start = q * (2 * self.piece) + core * self.piece
        size = self.piece
        if half is not None:
            start, size = start + half * self.half, self.half
        return self.buf.at[t, pl.ds(pl.multiple_of(start, 16), size)]
    def shard(self, k): return lax.rem(self.p.t + k, 4)
    def copy(self, ref, kind, k, peer):
        n = 0 if kind == "z" else 2 if kind == "c" else 1
        recv = self.sems[kind].at[self.i, k - 1]
        return pltpu.make_async_remote_copy(
            ref, ref, self.send.at[n], recv, device_id=peer, device_id_type=MESH
        )

    def go(self, *a):
        self.copy(*a).start()

    def first(self):
        p = self.p
        ref = self.at(p.t, p.q, p.core)
        for k in (1, 2, 3):
            self.go(ref, "z", 4 - k, (p.d, p.c, lax.rem(p.t + k, 4)))

    def first_hop(self):
        p = self.p
        ref = self.at(p.t, p.q, p.core)
        pl.when(p.t < 3)(lambda: self.go(ref, "z", 3, (p.d, p.c, p.t + 1)))
        pl.when(p.t > 0)(lambda: self.go(ref, "z", 1, (p.d, p.c, p.t - 1)))

    def zf(self, k):
        p, t = self.p, self.shard(k)
        ref = self.at(t, p.q, p.core)
        self.copy(ref, "z", k, p.x_nb).wait_recv()
        up = jnp.logical_and(t < p.t, p.t < 3)
        down = jnp.logical_and(t > p.t, p.t > 0)
        pl.when(up)(lambda: self.go(ref, "z", k - 1, (p.d, p.c, p.t + 1)))
        pl.when(down)(lambda: self.go(ref, "z", k + 1, (p.d, p.c, p.t - 1)))

    def spread(self, k):
        p = self.p
        ref = self.at(self.shard(k), p.q, p.core)
        self.go(ref, "x", k, p.x_nb)
        self.go(ref, "y", k, p.y_nb)

    def z(self, k):
        p, t = self.p, self.shard(k)
        ref = self.at(t, p.q, p.core)
        self.copy(ref, "z", k, p.x_nb).wait_recv()
        self.go(ref, "x", k, p.x_nb); self.go(ref, "y", k, p.y_nb)
    def xy(self, k):
        p, t = self.p, self.shard(k)
        self.copy(self.at(t, p.qx, p.core), "x", k, p.x_nb).wait_recv()
        self.go(self.at(t, p.qx, p.core, 0), "fy", k, p.y_nb)
        self.copy(self.at(t, p.qy, p.core), "y", k, p.y_nb).wait_recv()
        self.go(self.at(t, p.qy, p.core, 1), "fx", k, p.x_nb)
    def diag(self, k):
        p, t = self.p, self.shard(k)
        self.copy(self.at(t, p.qd, p.core, 0), "fy", k, p.y_nb).wait_recv()
        self.copy(self.at(t, p.qd, p.core, 1), "fx", k, p.x_nb).wait_recv()
        for q in range(4):
            self.go(self.at(t, q, p.core), "c", k, p.core_nb)
    def done(self, k):
        p, t = self.p, self.shard(k)
        self.copy(self.buf.at[t, pl.ds(0, 4 * self.piece)], "c", k, p.core_nb).wait_recv()

    def drain(self, hops):
        p = self.p

        def wait(kind, ref):
            self.copy(ref, kind, 1, p.core_nb).wait_send()

        line = lambda n: wait("z", self.buf.at[0, pl.ds(0, n * self.piece)])
        if hops:
            ends = jnp.logical_or(p.t == 0, p.t == 3)
            pl.when(ends)(lambda: line(1))
            pl.when(jnp.logical_not(ends))(lambda: line(5))
        else:
            line(3)
        wait("x", self.buf.at[pl.ds(0, 3), pl.ds(0, 3 * self.piece)])
        wait("c", self.buf.at[pl.ds(0, 3), pl.ds(0, 4 * self.piece)])


def lanes(core):
    return pl.ds(pl.multiple_of(core * 384, 128), 384)


class Reduce:
    def __init__(self, p, i, G, X1, Y1, X2, Y2, Z, OUT, sems, send, own):
        self.p, self.i, self.G, self.OUT, self.sems = p, i, G, OUT, sems
        self.X1, self.Y1, self.X2, self.Y2, self.Z = X1, Y1, X2, Y2, Z
        self.half = G.shape[1]; self.qr = self.half // 4; self.hr = self.qr // 2
        self.send = send
        self.own = own
    def t(self, k): return lax.rem(self.p.t + k, 4)
    def rows(self, q, h): return pl.ds(pl.multiple_of(q * self.qr + h * self.hr, 16), self.hr)
    def rdma(self, src, dst, kind, k, peer):
        n = 1 if kind == "z" else 0 if kind != "f" else 3 if k == 4 else 2
        return pltpu.make_async_remote_copy(
            src,
            dst,
            self.send.at[self.i, n],
            self.sems[kind].at[self.i, k],
            device_id=peer,
            device_id_type=MESH,
        )

    def go(self, *a):
        self.rdma(*a).start()

    def got(self, ref, kind, k):
        self.rdma(ref, ref, kind, k, self.p.x_nb).wait_recv()
    def one(self, k):
        p, t = self.p, self.t(k)
        for j in range(2):
            self.go(self.G.at[t, self.rows((1 - p.d) * 2 + j, 0)], self.X1.at[k, j], "x1", k, p.x_nb)
            self.go(self.G.at[t, self.rows(j * 2 + 1 - p.y, 1)], self.Y1.at[k, j], "y1", k, p.y_nb)
    def two(self, k):
        p, t, G = self.p, self.t(k), self.G
        self.got(self.X1.at[k], "x1", k)
        for j in range(2):
            r = self.rows(p.d * 2 + j, 0)
            G[t, r] = G[t, r] + self.X1[k, j]
        self.go(G.at[t, self.rows(p.qy, 0)], self.Y2.at[k], "y2", k, p.y_nb)
        self.got(self.Y1.at[k], "y1", k)
        for j in range(2):
            r = self.rows(j * 2 + p.y, 1)
            G[t, r] = G[t, r] + self.Y1[k, j]
        self.go(G.at[t, self.rows(p.qx, 1)], self.X2.at[k], "x2", k, p.x_nb)
    def three(self, k):
        p, t, G = self.p, self.t(k), self.G
        for h, (kind, R) in enumerate((("y2", self.Y2), ("x2", self.X2))):
            self.got(R.at[k], kind, k)
            r = self.rows(p.q, h)
            G[t, r] = G[t, r] + R[k]
        if not isinstance(k, int):
            whole = pl.ds(pl.multiple_of(p.q * self.qr, 16), self.qr)
            self.go(G.at[t, whole], self.Z.at[3 - k], "z", 3 - k, (p.d, p.c, t))
    def piece(self, q, core, h=None):
        start, size = q * self.qr, self.qr
        if h is not None:
            start, size = start + h * self.hr, self.hr
        return self.OUT.at[pl.ds(pl.multiple_of(start, 16), size), lanes(core)]

    def final(self):
        p = self.p
        whole = pl.ds(pl.multiple_of(p.q * self.qr, 16), self.qr)
        total = self.G[p.t, whole].astype(F32)
        for k in range(3):
            self.got(self.Z.at[k], "z", k)
            total = total + self.Z[k].astype(F32)
        ref = self.piece(p.q, p.core)
        mine = self.G.at[p.t, whole]
        mine[...] = total.astype(BF16)
        self.go(mine, ref, "f", 0, p.x_nb)
        self.go(mine, ref, "f", 1, p.y_nb)
        self.own_copy().start()

    def own_copy(self):
        p = self.p
        whole = pl.ds(pl.multiple_of(p.q * self.qr, 16), self.qr)
        return pltpu.make_async_copy(
            self.G.at[p.t, whole], self.piece(p.q, p.core), self.own.at[self.i]
        )

    def spread(self):
        p = self.p
        ref = self.piece(p.qx, p.core); self.got(ref, "f", 0)
        ref = self.piece(p.qx, p.core, 0); self.go(ref, ref, "f", 2, p.y_nb)
        ref = self.piece(p.qy, p.core); self.got(ref, "f", 1)
        ref = self.piece(p.qy, p.core, 1); self.go(ref, ref, "f", 3, p.x_nb)
    def corner(self):
        p = self.p
        self.own_copy().wait()
        self.got(self.piece(p.qd, p.core, 0), "f", 2); self.got(self.piece(p.qd, p.core, 1), "f", 3)
        ref = self.OUT.at[:, lanes(p.core)]
        self.go(ref, ref, "f", 4, p.core_nb)
    def end(self):
        p = self.p
        self.got(self.OUT.at[:, lanes(1 - p.core)], "f", 4)
        rows = 3 * self.half // 4
        sizes = (
            ("x1", 0, self.G.at[pl.ds(0, 3)]),
            ("z", 0, self.Z),
            ("f", 0, self.G.at[0, pl.ds(0, rows)]),
            ("f", 4, self.G.at[0]),
        )
        for kind, k, ref in sizes:
            self.rdma(ref, ref, kind, k, p.core_nb).wait_send()


GATHER_SEMS = ("z", "x", "y", "fx", "fy", "c")
SEMS = ("x1", "y1", "x2", "y2", "z", "f")


def dot(a, b, ca, cb):
    return lax.dot_general(a, b, (((ca,), (cb,)), ((), ())), preferred_element_type=F32)


def loop(n, step):
    def body(i, carry):
        step(i)
        return carry

    lax.fori_loop(0, n, body, 0)


def ds(i, n):
    return pl.ds(pl.multiple_of(i * n, n), n)


class Scan:
    def __init__(self, p, later, total, up, down, got, sems):
        self.p, self.later, self.total, self.up_ref, self.down_ref = p, later, total, up, down
        self.from_core, self.from_y, self.from_below, self.from_above = [got.at[i] for i in range(4)]
        self.sems = sems

    def rdma(self, src, dst, g, i, peer):
        h, i = self.heads(g), 4 * i + g
        return pltpu.make_async_remote_copy(
            src.at[h], dst.at[h], self.sems.at[0, i], self.sems.at[1, i], device_id=peer, device_id_type=MESH
        )

    def core_copy(self, g):
        return self.rdma(self.total, self.from_core, g, 0, self.p.core_nb)

    def y_copy(self, g):
        return self.rdma(self.up_ref, self.from_y, g, 1, self.p.y_nb)

    def line_copy(self, g, upward):
        p = self.p
        if upward:
            return self.rdma(self.up_ref, self.from_below, g, 2, (p.d, p.c, p.t + 1))
        return self.rdma(self.down_ref, self.from_above, g, 3, (p.d, p.c, p.t - 1))

    def heads(self, g):
        return pl.ds(3 * g, 3)

    def begin(self, g):
        h = self.heads(g)
        zero = jnp.zeros((3, 80, 128), BF16)

        @pl.when(self.p.t == 0)
        def _():
            self.from_below[h] = zero

        @pl.when(self.p.t == 3)
        def _():
            self.from_above[h] = zero

        self.core_copy(g).start()

    def pair(self, g):
        h = self.heads(g)
        self.core_copy(g).wait_recv()
        self.up_ref[h] = self.total[h] + self.from_core[h]
        self.y_copy(g).start()

    def column(self, g):
        p, h = self.p, self.heads(g)
        core, y = p.core.astype(F32), p.y.astype(F32)
        if self.later:
            core, y = 1.0 - core, 1.0 - y
        return core * self.from_core[h].astype(F32) + y * self.from_y[h].astype(F32)

    def hop(self, g, upward):
        h, t = self.heads(g), self.p.t
        has, sends = (t > 0, t < 3) if upward else (t < 3, t > 0)
        c = self.line_copy(g, upward)
        got = self.from_below if upward else self.from_above
        out = self.up_ref if upward else self.down_ref

        @pl.when(has)
        def _():
            c.wait_recv()

        @pl.when(sends)
        def _():
            value = self.column(g) + got[h].astype(F32)
            if upward != self.later:
                value = value + self.total[h].astype(F32)
            out[h] = value.astype(BF16)
            c.start()

    def chain(self, g):
        c = self.y_copy(g)
        c.wait_recv()
        c.wait_send()
        pl.when(self.p.t < 2)(lambda: self.hop(g, True))
        pl.when(self.p.t >= 2)(lambda: self.hop(g, False))

    def relay(self, g):
        pl.when(self.p.t == 1)(lambda: self.hop(g, False))
        pl.when(self.p.t == 2)(lambda: self.hop(g, True))

    def last(self, g):
        pl.when(self.p.t == 0)(lambda: self.hop(g, False))
        pl.when(self.p.t == 3)(lambda: self.hop(g, True))

    def sum(self, g):
        h = self.heads(g)
        return self.column(g) + self.from_below[h].astype(F32) + self.from_above[h].astype(F32)

    def drain(self):
        for g in range(4):
            self.core_copy(g).wait_send()
            pl.when(self.p.t < 3)(lambda g=g: self.line_copy(g, True).wait_send())
            pl.when(self.p.t > 0)(lambda g=g: self.line_copy(g, False).wait_send())


class Small:
    def __init__(self, p, low, full, plane, line, mid, out, sems, send, own):
        self.p, self.low, self.full, self.plane, self.line, self.mid, self.out = (
            p, low, full, plane, line, mid, out
        )
        self.sems, self.send, self.own = sems, send, own
        self.me = p.d * 4 + p.c

    def rdma(self, src, dst, i, peer):
        n = 0 if i < 7 else 1 if i < 10 else 2
        return pltpu.make_async_remote_copy(
            src, dst, self.send.at[n], self.sems.at[i], device_id=peer, device_id_type=MESH
        )

    def go(self, *a):
        self.rdma(*a).start()

    def begin(self):
        for r in range(1, 8):
            peer, j = plane_peer(self.p, r)
            self.go(self.low.at[ds(j, 32)], self.plane.at[r - 1], r - 1, peer)

    def across(self):
        p = self.p
        for r in range(1, 8):
            self.rdma(self.plane.at[r - 1], self.plane.at[r - 1], r - 1, p.x_nb).wait_recv()
        for t in range(4):
            total = self.full[t, ds(self.me, 32)]
            for r in range(7):
                total = total + self.plane[r, :, 128 * t : 128 * t + 128].astype(F32)
            self.full[t, ds(self.me, 32)] = total
            self.mid[t] = total.astype(BF16)
        for k in (1, 2, 3):
            t = lax.rem(p.t + k, 4)
            self.go(self.mid.at[t], self.line.at[3 - k], 10 - k, (p.d, p.c, t))

    def final(self):
        p = self.p
        total = self.full[p.t, ds(self.me, 32)]
        for k in range(3):
            self.rdma(self.line.at[k], self.line.at[k], 7 + k, p.x_nb).wait_recv()
            total = total + self.line[k].astype(F32)
        self.mid[4] = total.astype(BF16)
        ref = self.out.at[ds(self.me, 32)]
        for r in range(1, 8):
            self.go(self.mid.at[4], ref, 9 + r, plane_peer(p, r)[0])
        pltpu.make_async_copy(self.mid.at[4], ref, self.own).start()

    def end(self):
        pltpu.make_async_copy(self.mid.at[4], self.out.at[ds(self.me, 32)], self.own).wait()
        for r in range(1, 8):
            peer, j = plane_peer(self.p, r)
            ref = self.out.at[ds(j, 32)]
            self.rdma(ref, ref, 9 + r, peer).wait_recv()
        for i, ref in ((0, self.plane), (7, self.line), (10, self.plane.at[:, :, pl.ds(0, 128)])):
            self.rdma(ref, ref, i, self.p.core_nb).wait_send()


def layer_rows(v):
    c = v - jnp.mean(v, axis=-1, keepdims=True)
    r = lax.rsqrt(jnp.mean(c * c, axis=-1, keepdims=True) + EPSILON)
    return c * r, r


def fold(v):
    total = v[:8]
    for i in range(1, v.shape[0] // 8):
        total = total + v[8 * i : 8 * i + 8]
    return total


def layer_back(e, n, r, gain):
    m = e * gain
    return r * (
        m - jnp.mean(m, axis=-1, keepdims=True) - n * jnp.mean(m * n, axis=-1, keepdims=True)
    )


def block_kernel(m):
    p = place()
    t0 = p.t
    X, CT, S, WA, W1, W2 = m.X, m.CT, m.S, m.WA, m.W1, m.W2
    VEC, H1, H2, X2, ACC_O, ACC_E = m.VEC, m.H1, m.H2, m.X2, m.ACC_O, m.ACC_E
    MIX, PH, VX, AT, PX, SL, OT, RD = m.MIX, m.PH, m.VX, m.AT, m.PX, m.SL, m.OT, m.RD
    A, DF, GS, FW, BC, IB, SUMS = m.A, m.DF, m.GS, m.FW, m.BC, m.IB, m.SUMS
    ld = m.ld
    greet(p)
    loads = [
        pltpu.make_async_copy(m.wm, WA.at[t0, pl.ds(0, 576)], ld.at[0]),
        pltpu.make_async_copy(m.wo, WA.at[t0, pl.ds(576, 192)], ld.at[1]),
        pltpu.make_async_copy(m.x, X, ld.at[2]),
        pltpu.make_async_copy(m.w1, W1.at[t0], ld.at[3]),
        pltpu.make_async_copy(m.w2, W2.at[t0], ld.at[4]),
        pltpu.make_async_copy(m.g, CT, ld.at[5]),
    ]
    raw = [(m.fw, m.FWI), (m.mb, m.MBI), (m.fb, m.FBI)]
    raw += [(ref, m.VECI.at[i, pl.ds(0, 6)]) for i, ref in enumerate(m.vectors)]
    raw = [pltpu.make_async_copy(src, dst, ld.at[8 + i]) for i, (src, dst) in enumerate(raw)]
    for c in raw + loads:
        c.start()
    for c in raw:
        c.wait()

    for h in range(3):
        pair = [m.FWI[i, h].astype(F32) for i in range(2)]
        S[t0, 64 * h : 64 * h + 64] = jnp.concatenate(pair, axis=1).astype(BF16)
    zero = jnp.zeros((1, HD), F32)
    rows = []
    for j in range(3):
        row = m.MBI[j : j + 1].astype(F32)
        rows += [
            jnp.concatenate([row[:, HD * h : HD * h + HD], zero], axis=1) for h in range(3)
        ]
    for h in range(3):
        row = m.FBI[h].astype(F32)
        rows.append(jnp.concatenate([row[0:1], row[1:2]], axis=1))
    rows.append(jnp.zeros((4, 128), F32))
    S[t0, 192:208] = jnp.concatenate(rows, axis=0).astype(BF16)
    rows = [m.VECI[6].astype(F32)[0:6], jnp.zeros((42, 128), F32)]
    S[t0, 208:256] = jnp.concatenate(rows, axis=0).astype(BF16)
    for k in range(6):
        value = m.VECI[k].astype(F32)
        for i in range(6):
            VEC[k : k + 1, 128 * i : 128 * i + 128] = value[i : i + 1]

    gs, gw, g1, g2 = gathers = [
        Gather(p, b, m.gather_sems, m.gather_send, i) for i, b in enumerate((S, WA, W1, W2))
    ]
    K = nearest(t0)
    shard = gs.shard
    loads[0].wait()
    loads[1].wait()
    met(p)
    gw.first()
    gs.first()

    loads[2].wait()

    def norm1(i):
        r = ds(i, 128)
        n, _ = layer_rows(X[r].astype(F32))
        H1[r] = (n * VEC[0:1] + VEC[1:2]).astype(BF16)

    loop(4, norm1)
    ones_row = jnp.where(lax.broadcasted_iota(jnp.int32, (16, 512), 0) == 0, 1.0, 0.0).astype(BF16)

    def init(h):
        VX[h, 64:80] = ones_row

    loop(12, init)
    SUMS[...] = jnp.zeros_like(SUMS)

    def small(t):
        BC[...] = S[t, 192:208].astype(F32).T
        rows = S[t, 208:224].astype(F32)
        for i in range(6):
            IB[t, :, 128 * i : 128 * i + 128] = rows[i : i + 1]
        for h in range(3):
            w = S[t, 64 * h : 64 * h + 64].astype(F32)
            FW[0, t * 3 + h] = w[:, :64].astype(BF16)
            FW[1, t * 3 + h] = w[:, 64:].astype(BF16)

    def mix(t):
        value = dot(WA[t, 0:576], H1[...], 1, 1)
        for j in range(3):
            for h in range(3):
                n = j * 3 + h
                part = (value[64 * n : 64 * n + 64] + BC[0:64, n : n + 1]).astype(BF16)
                if j < 2:
                    MIX[t, 64 * n : 64 * n + 64] = part
                else:
                    VX[t * 3 + h, 0:64] = part

    def features(t):
        for h in range(3):
            for i in range(2):
                u = dot(FW[i, t * 3 + h], MIX[t, 192 * i + 64 * h : 192 * i + 64 * h + 64], 0, 0)
                u = u + BC[64 * i : 64 * i + 64, 9 + h : 10 + h]
                e = jnp.exp(u - jnp.max(u, axis=0, keepdims=True))
                PH[i, t * 3 + h, 0:64] = (e / jnp.sum(e, axis=0, keepdims=True)).astype(BF16)
                e = jnp.exp(jnp.min(u, axis=0, keepdims=True) - u)
                PH[i, t * 3 + h, 64:128] = (e / jnp.sum(e, axis=0, keepdims=True)).astype(BF16)

    def states(t):
        def one(i):
            h = t * 3 + i
            s0 = dot(VX[h, :, 0:256], PH[1, h, :, 0:256], 1, 1)
            s1 = dot(VX[h, :, 256:512], PH[1, h, :, 256:512], 1, 1)
            SL[h] = s0
            m.TOT[h] = (s0 + s1).astype(BF16)

        loop(3, one)

    small(t0)
    mix(t0)
    features(t0)
    states(t0)
    both = (g1, g2)
    for n, k in enumerate(K):
        gw.z(k)
        gs.z(k)
        if n == 1:
            loads[3].wait()
            loads[4].wait()
            for g in both:
                g.first_hop()
    for k in K:
        gw.xy(k)
        gs.xy(k)
    for k in K:
        gw.diag(k)
        gs.diag(k)
    middle = jnp.logical_or(t0 == 1, t0 == 2)
    for g in both:
        g.zf(K[0])
        g.spread(K[0])
    for g in both:
        pl.when(middle)(lambda g=g: g.zf(K[1]))
    def arrived(n):
        k = jnp.where(n == 0, K[0], jnp.where(n == 1, K[1], K[2]))
        gs.done(k)
        gw.done(k)
        t = shard(k)
        small(t)
        mix(t)
        features(t)
        states(t)

    loop(3, arrived)
    scan = Scan(p, False, m.TOT, m.UP, m.DOWN, m.got_f, m.scan_f)
    for g in range(4):
        scan.begin(g)
    causal = lax.broadcasted_iota(jnp.int32, (256, 256), 0) <= lax.broadcasted_iota(
        jnp.int32, (256, 256), 1
    )

    def scores(h):
        for j in range(2):
            c = slice(256 * j, 256 * j + 256)
            a = dot(PH[1, h, :, c], PH[0, h, :, c], 0, 0)
            AT[h, j] = jnp.where(causal, a, 0.0).astype(BF16)

    for g in both:
        g.zf(jnp.where(middle, K[2], K[1]))
    for g in range(4):
        scan.pair(g)
    loop(12, scores)
    for g in range(4):
        scan.chain(g)
    for g in both:
        g.xy(K[0])
        g.spread(K[1])
    for g in both:
        pl.when(jnp.logical_not(middle))(lambda g=g: g.zf(K[2]))
    for g in range(4):
        scan.relay(g)
    for g in both:
        g.spread(K[2])

    def enter(first):
        for g in range(4):
            scan.last(g)
            value = scan.sum(g)
            h = scan.heads(g)
            PX[h, first] = value.astype(BF16)
            PX[h, 1 - first] = (value + SL[h]).astype(BF16)

    enter(0)

    def attend(h):
        for j in range(2):
            c = slice(256 * j, 256 * j + 256)
            num = dot(PX[h, j], PH[0, h, :, c], 1, 0) + dot(VX[h, :, c], AT[h, j], 1, 0)
            r = 1.0 / num[64:65]
            RD[h, :, c] = r
            OT[ds(h, 64), c] = (num[0:64] * r).astype(BF16)

    loop(12, attend)

    def norm2(i):
        r = ds(i, 256)
        total = X[r].astype(F32) + VEC[2:3]
        for t in range(4):
            total = total + dot(OT[192 * t : 192 * t + 192, r], WA[t, 576:768], 0, 0)
        X2[r] = total
        n, _ = layer_rows(total)
        H2[r] = (n * VEC[3:4] + VEC[4:5]).astype(BF16)
        ACC_O[r] = total + VEC[5:6]
        ACC_E[r] = jnp.zeros((256, 768), F32)

    loop(2, norm2)

    R = [
        Reduce(p, i, m.G[i], *m.land[i][1:], m.Z[i], m.outs[i], m.reduce_sems, m.reduce_send, m.own)
        for i in range(4)
    ]
    core_sems, STAGE = m.r_core, m.STAGE
    outgoing = []

    def core_copy(src, i, k):
        ref = m.land[i][0].at[shard(k)]
        return pltpu.make_async_remote_copy(
            ref if src is None else src,
            ref,
            core_sems.at[0, i, k],
            core_sems.at[1, i, k],
            device_id=p.core_nb,
            device_id_type=MESH,
        )

    def hand(i, k, value):
        slot = len(outgoing) % 2
        if len(outgoing) >= 2:
            outgoing[-2].wait_send()
        ref = STAGE.at[slot, pl.ds(0, R[i].half)]
        ref[...] = value(1 - p.core).astype(BF16)
        c = core_copy(ref, i, k)
        c.start()
        outgoing.append(c)
        R[i].G[shard(k)] = value(p.core).astype(BF16)

    def meet(i, k):
        t = shard(k)
        G, C = R[i].G, m.land[i][0]
        core_copy(None, i, k).wait_recv()

        def add(j):
            r = ds(j, 96)
            G[t, r] = G[t, r] + C[t, r]

        loop(R[i].half // 96, add)
        R[i].one(k)

    def hidden(t, slot):
        def rows(i):
            r = ds(i, 256)
            f = dot(H2[r], W1[t], 1, 0) + IB[t]
            th = jnp.tanh(0.7978845608028654 * (f + 0.044715 * f * f * f))
            a = (0.5 * f * (1.0 + th)).astype(BF16)
            A[slot, r] = a
            slope = 0.5 * (1.0 + th) + 0.5 * f * (1.0 - th * th) * (
                0.7978845608028654 * (1.0 + 3.0 * 0.044715 * f * f)
            )
            df = (dot(CT[r], W2[t], 1, 1) * slope).astype(BF16)
            DF[slot, r] = df
            m.DIB[t] += fold(df.astype(F32))
            ACC_O[r] += dot(a, W2[t], 1, 0)
            ACC_E[r] += dot(df, W1[t], 1, 1)

        loop(2, rows)

    def hand_hidden(k, slot):
        hand(0, k, lambda core: dot(A[slot], CT[:, lanes(core)], 0, 0))
        hand(1, k, lambda core: dot(H2[...], DF[slot, :, lanes(core)], 0, 0))

    m.DIB[...] = jnp.zeros_like(m.DIB)
    order = K + [0]
    loads[5].wait()
    for g in both:
        g.diag(K[0])
    hidden(t0, 0)
    for g in both:
        g.xy(K[1])
    for n, k in enumerate(K):
        g1.done(k)
        g2.done(k)
        hidden(shard(k), 1)
        for g in both:
            if n == 0:
                g.xy(K[2])
                g.diag(K[1])
            if n == 1:
                g.diag(K[2])
        if n:
            meet(1, K[n - 1])
        if n < 2:
            hand_hidden(k, 1)
            meet(0, k)
    for g in both:
        g.drain(True)
    RES, GG = W1.at[2, pl.ds(0, 512)], W1.at[3, pl.ds(0, 512)]

    def dne(h):
        start = pl.multiple_of(lax.rem(h, 9) * 80, 16)
        return W2.at[h // 9, pl.ds(start, 80), pl.ds(0, 512)]

    def du_of(h):
        return W1.at[h // 6, ds(lax.rem(h, 6), 128), pl.ds(0, 512)]

    def dv_of(h):
        return W2.at[2, ds(h, 64), pl.ds(0, 512)]

    def back2(i):
        r = ds(i, 128)
        n, s = layer_rows(X2[r])
        e = ACC_E[r]
        g = CT[r].astype(F32)
        dx = g + layer_back(e, n, s, VEC[3:4])
        SUMS[3] += fold(e * n)
        SUMS[4] += fold(e)
        SUMS[2] += fold(dx)
        SUMS[5] += fold(g)
        X2[r] = dx
        GG[r] = dx.astype(BF16)

    loop(4, back2)
    DX = X2
    first_row = lax.broadcasted_iota(jnp.int32, (16, 512), 0) == 0

    scan.drain()
    scan = Scan(p, True, m.TOT, m.UP, m.DOWN, m.got_b, m.scan_b)

    def states_back(t):
        value = dot(WA[t, 576:768], GG[...], 1, 1).astype(BF16).astype(F32)
        for i in range(3):
            h = 3 * t + i
            do = value[64 * i : 64 * i + 64]
            r = RD[h]
            o = OT[ds(h, 64)].astype(F32)
            ref = dne(h)
            ref[0:64] = (do * r).astype(BF16)
            dden = -jnp.sum(do * o, axis=0, keepdims=True) * r
            ref[64:80] = jnp.where(first_row, dden, 0.0).astype(BF16)
            s0 = dot(ref[:, 0:256], PH[0, h, :, 0:256], 1, 1)
            s1 = dot(ref[:, 256:512], PH[0, h, :, 256:512], 1, 1)
            SL[h] = s1
            m.TOT[h] = (s0 + s1).astype(BF16)

    def give(t):
        states_back(t)
        scan.begin(t)

    loop(4, give)
    hand(0, order[2], lambda core: dot(A[1], CT[:, lanes(core)], 0, 0))
    for g in range(4):
        scan.pair(g)
    for i in range(2):
        R[i].two(order[0])
    hand(1, order[2], lambda core: dot(H2[...], DF[1, :, lanes(core)], 0, 0))
    for i in range(2):
        R[i].two(order[1])

    def feature_back(i, h, delta):
        delta = delta.astype(BF16).astype(F32)
        up, down = PH[i, h, 0:64].astype(F32), PH[i, h, 64:128].astype(F32)
        d, dd = delta[0:64], delta[64:128]
        du = up * (d - jnp.sum(up * d, axis=0, keepdims=True)) - down * (
            dd - jnp.sum(down * dd, axis=0, keepdims=True)
        )
        du_of(h)[64 * i : 64 * i + 64] = du.astype(BF16)

    def query_back(h):
        parts = []
        ref, dv = dne(h), dv_of(h)
        for j in range(2):
            c = slice(256 * j, 256 * j + 256)
            value = ref[:, c]
            dv[:, c] = dot(ref[0:64, c], AT[h, j], 1, 1).astype(BF16)
            da = dot(VX[h, :, c], value, 0, 0)
            da = jnp.where(causal, da, 0.0).astype(BF16)
            AT[h, j] = da
            parts.append(dot(PH[1, h, :, c], da, 1, 0) + dot(PX[h, j], value, 0, 0))
        feature_back(0, h, jnp.concatenate(parts, axis=1))

    ones8 = jnp.ones((8, 512), BF16)
    left = lax.broadcasted_iota(jnp.int32, (64, 128), 1) < 64
    GS[:, 192:256] = jnp.zeros((4, 64, 128), F32)

    def bias_row(t, j, i):
        ref = MIX[t, ds(3 * j + i, 64)]
        GS[t, pl.ds(192 + 3 * j + i, 1), 0:64] = dot(ones8, ref, 1, 1)[0:1]

    def early(k):
        t = shard(k)
        def one(i):
            h = t * 3 + i
            rows = ds(i, 64)
            du = du_of(h)[0:64]
            GS[t, rows, 0:64] = dot(MIX[t, rows], du, 1, 1)
            MIX[t, rows] = dot(FW[0, h], du, 1, 0).astype(BF16)
            bias_row(t, 0, i)

        loop(3, one)

        def value(core):
            both = [
                dot(MIX[t, 0:192], H1[:, lanes(core)], 1, 0),
                dot(OT[ds(t, 192)], GG[:, lanes(core)], 1, 0),
            ]
            return jnp.concatenate(both, axis=0)

        hand(2, k, value)

    def queries(g):
        loop(3, lambda i: query_back(3 * g + i))

    def ask(g):
        queries(g)
        scan.chain(g)

    loop(2, ask)
    for i in range(2):
        meet(i, order[2])
    loop(2, lambda g: ask(g + 2))
    hand_hidden(0, 0)
    for g in range(4):
        scan.relay(g)
    for i in range(2):
        R[i].three(order[0])
        R[i].three(order[1])
    RES[...] = ACC_O[...].astype(BF16)
    res_copy = pltpu.make_async_copy(RES, m.result, ld.at[6])
    res_copy.start()
    early(order[0])
    for i in range(2):
        meet(i, order[3])
    early(order[1])
    meet(2, order[0])
    for i in range(2):
        R[i].two(order[2])
    early(order[2])
    meet(2, order[1])
    early(order[3])
    meet(2, order[2])
    for i in range(2):
        R[i].two(order[3])
    enter(1)

    def key_back(t, i):
        h = t * 3 + i
        parts, values = [], []
        for j in range(2):
            c = slice(256 * j, 256 * j + 256)
            q = PX[h, j]
            parts.append(dot(PH[0, h, :, c], AT[h, j], 1, 1) + dot(q, VX[h, :, c], 0, 0))
            values.append(dot(q[0:64], PH[1, h, :, c], 1, 0))
        feature_back(1, h, jnp.concatenate(parts, axis=1))
        dv = jnp.concatenate(values, axis=1) + dv_of(h)[...].astype(F32)
        MIX[t, ds(6 + i, 64)] = dv.astype(BF16)
        du = du_of(h)
        rows = ds(3 + i, 64)
        ref = ds(i, 64)
        GS[t, ref] = jnp.where(left, GS[t, ref], dot(MIX[t, rows], du[...], 1, 1))
        GS[t, pl.ds(201 + i, 1)] = dot(ones8, du[...], 1, 1)[0:1]
        MIX[t, rows] = dot(FW[1, h], du[64:128], 1, 0).astype(BF16)
        bias_row(t, 1, i)
        bias_row(t, 2, i)

    for n, k in enumerate(order):
        t = shard(k)
        loop(3, lambda i: key_back(t, i))
        hand(3, k, lambda core: dot(MIX[t, 192:576], H1[:, lanes(core)], 1, 0))
        if n == 0:
            for i in range(2):
                R[i].three(order[2])
            meet(2, order[3])
            R[2].two(order[0])
            R[2].two(order[1])
        else:
            meet(3, order[n - 1])
        if n == 1:
            R[0].three(order[3])
            R[1].three(order[3])
            R[2].two(order[2])
        if n == 2:
            R[2].two(order[3])
            R[2].three(order[0])
            R[2].three(order[1])
            R[3].two(order[0])
            R[0].final()
            R[1].final()
        if n == 3:
            R[2].three(order[2])
            R[2].three(order[3])
            R[3].two(order[1])
            R[3].three(order[0])

    def back1(i):
        r = ds(i, 256)
        e = dot(MIX[0, :, r], WA[0, 0:576], 0, 0)
        for t in range(1, 4):
            e = e + dot(MIX[t, :, r], WA[t, 0:576], 0, 0)
        n, s = layer_rows(X[r].astype(F32))
        SUMS[0] += fold(e * n)
        SUMS[1] += fold(e)
        ACC_E[r] = DX[r] + layer_back(e, n, s, VEC[0:1])

    back1(0)
    meet(3, order[3])
    R[0].spread()
    R[3].two(order[2])
    R[1].spread()
    R[3].three(order[1])
    back1(1)
    R[3].two(order[3])
    R[0].corner()
    tok_copy = pltpu.make_async_copy(ACC_E, m.tokens_gradient, ld.at[7])
    tok_copy.start()
    for k in range(6):
        row = jnp.sum(SUMS[k], axis=0, keepdims=True)
        for i in range(6):
            for t in range(4):
                GS[t, 216 + 6 * k + i : 217 + 6 * k + i] = row[:, 128 * i : 128 * i + 128]
    for t in range(4):
        row = jnp.sum(m.DIB[t], axis=0, keepdims=True)
        for i in range(6):
            GS[t, 208 + i : 209 + i] = row[:, 128 * i : 128 * i + 128]
    GB = W2.at[3, pl.ds(0, 256), pl.ds(0, 512)]
    for t in range(4):
        GB[:, 128 * t : 128 * t + 128] = GS[t].astype(BF16)
    tiny = Small(p, GB, GS, m.plane, m.line, m.mid, m.outs[4], m.small_sems, m.small_send, m.own.at[4])
    tiny.begin()
    R[2].final()
    R[3].three(order[2])
    R[1].corner()
    R[3].three(order[3])
    tiny.across()
    R[2].spread()
    R[3].final()
    tiny.final()
    R[2].corner()
    R[3].spread()
    R[3].corner()
    for r in R:
        r.end()
    tiny.end()
    scan.drain()
    for c in outgoing[-2:]:
        c.wait_send()
    gs.drain(False)
    gw.drain(False)
    res_copy.wait()
    tok_copy.wait()


PACKS = ((768, 768), (768, 768), (384, 768), (384, 768))


def landing(rows):
    q, r = rows // 4, rows // 8
    shapes = ((4, rows), (4, 2, r), (4, 2, r), (4, r), (4, r))
    return [pltpu.VMEM((*shape, 384), BF16) for shape in shapes]


def block_call(*args):
    rows, width = args[0].shape
    flat = pltpu.VMEM((rows, width), BF16)
    wide = pltpu.VMEM((rows, width), F32)
    weights = pltpu.VMEM((4, 768, 768), BF16)
    state = pltpu.VMEM((12, 80, 128), BF16)
    dma = pltpu.SemaphoreType.DMA
    scratch = dict(
        X=flat,
        CT=flat,
        S=pltpu.VMEM((4, 256, 128), BF16),
        WA=weights,
        W1=weights,
        W2=weights,
        VEC=pltpu.VMEM((8, 768), F32),
        VECI=pltpu.VMEM((7, 8, 128), BF16),
        FWI=pltpu.VMEM((2, 3, HD, HD), BF16),
        MBI=pltpu.VMEM((3, 192), BF16),
        FBI=pltpu.VMEM((3, 2, HD), BF16),
        H1=flat,
        H2=flat,
        X2=wide,
        ACC_O=wide,
        ACC_E=wide,
        MIX=pltpu.VMEM((4, 576, rows), BF16),
        PH=pltpu.VMEM((2, 12, 128, rows), BF16),
        VX=pltpu.VMEM((12, 80, rows), BF16),
        AT=pltpu.VMEM((12, 2, 256, 256), BF16),
        PX=pltpu.VMEM((12, 2, 80, 128), BF16),
        SL=pltpu.VMEM((12, 80, 128), F32),
        OT=pltpu.VMEM((768, rows), BF16),
        RD=pltpu.VMEM((12, 1, rows), F32),
        A=pltpu.VMEM((2, rows, width), BF16),
        DF=pltpu.VMEM((2, rows, width), BF16),
        GS=pltpu.VMEM((4, 256, 128), F32),
        FW=pltpu.VMEM((2, 12, 64, 64), BF16),
        BC=pltpu.VMEM((128, 16), F32),
        IB=pltpu.VMEM((4, 1, 768), F32),
        SUMS=pltpu.VMEM((6, 8, 768), F32),
        DIB=pltpu.VMEM((4, 8, 768), F32),
        TOT=state,
        UP=state,
        DOWN=state,
        got_f=pltpu.VMEM((4, 12, 80, 128), BF16),
        got_b=pltpu.VMEM((4, 12, 80, 128), BF16),
        plane=pltpu.VMEM((7, 32, 512), BF16),
        line=pltpu.VMEM((3, 32, 128), BF16),
        mid=pltpu.VMEM((5, 32, 128), BF16),
        STAGE=pltpu.VMEM((2, 768, 384), BF16),
        G=[pltpu.VMEM((4, n, 384), BF16) for n, _ in PACKS],
        Z=[pltpu.VMEM((3, n // 4, 384), BF16) for n, _ in PACKS],
        land=[landing(n) for n, _ in PACKS],
        ld=dma((18,)),
        own=dma((5,)),
        r_core=dma((2, 4, 4)),
        gather_sems={k: dma((4, 3)) for k in GATHER_SEMS},
        gather_send=dma((4, 3)),
        reduce_sems={k: dma((4, n)) for k, n in zip(SEMS, (4, 4, 4, 4, 3, 5))},
        reduce_send=dma((4, 4)),
        small_sems=dma((17,)),
        small_send=dma((3,)),
        scan_f=dma((2, 16)),
        scan_b=dma((2, 16)),
    )
    leaves, tree = jax.tree.flatten(scratch, is_leaf=lambda v: not isinstance(v, (dict, list)))
    results = [
        jax.ShapeDtypeStruct((rows, width), BF16),
        jax.ShapeDtypeStruct((rows, width), F32),
        *[jax.ShapeDtypeStruct(pack, BF16) for pack in PACKS],
        jax.ShapeDtypeStruct((256, 128), BF16),
    ]

    def body(x, g, wm, wo, w1, w2, fw, mb, fb, *rest):
        vectors, (result, tokens_gradient), rest = rest[:7], rest[7:9], rest[9:]
        given = dict(
            x=x, g=g, wm=wm, wo=wo, w1=w1, w2=w2, fw=fw, mb=mb, fb=fb, vectors=vectors
        )
        block_kernel(
            SimpleNamespace(
                **given,
                result=result,
                tokens_gradient=tokens_gradient,
                outs=rest[:5],
                **jax.tree.unflatten(tree, rest[5:]),
            )
        )

    anywhere = pl.BlockSpec(memory_space=pl.ANY)
    return pl.pallas_call(
        body,
        out_shape=results,
        in_specs=[anywhere] * len(args),
        out_specs=[anywhere] * len(results),
        scratch_shapes=leaves,
        compiler_params=pltpu.CompilerParams(
            collective_id=0, has_side_effects=True, vmem_limit_bytes=67043328
        ),
        name="block",
    )(*args)


def finish_kernel(
    res, tok, outer, inner, q, o, k, v, small,
    res_o, tok_o, outer_o, inner_o, mixer_o, output_o, feature_o, mixer_bias_o, feature_bias_o, *vec_o,
):
    res_o[...] = res[...]
    tok_o[...] = tok[...]
    outer_o[...] = outer[...].astype(F32)
    inner_o[...] = inner[...].astype(F32)
    for i, ref in enumerate((q, k, v)):
        mixer_o[i] = ref[...].astype(F32)
    output_o[...] = o[...].astype(F32)

    @pl.when(pl.program_id(0) == 0)
    def _():
        rows = small[192:256].astype(F32)
        for h in range(3):
            w = small[64 * h : 64 * h + 64].astype(F32)
            feature_o[0, h] = w[:, :64]
            feature_o[1, h] = w[:, 64:]
            pair = rows[9 + h : 10 + h]
            feature_bias_o[h] = jnp.concatenate([pair[:, :64], pair[:, 64:]], axis=0)
            parts = [rows[3 * h + i : 3 * h + i + 1, :64] for i in range(3)]
            mixer_bias_o[h : h + 1] = jnp.concatenate(parts, axis=1)
        for i in range(6):
            vec_o[i][...] = rows[24 + 6 * i : 30 + 6 * i]
        vec_o[6][...] = rows[16:22]


def finish_call(res, tok, outer, inner, early, late, small):
    rows, width = res.shape
    steps = 4

    def spec(n, shift=0):
        return pl.BlockSpec((n, width), lambda i: (i + shift, 0))

    def whole(*shape):
        return pl.BlockSpec(shape, lambda i: (0,) * len(shape))

    def out(*shape):
        return jax.ShapeDtypeStruct(shape, F32)

    vectors = [(6, 128)] * 7
    return pl.pallas_call(
        finish_kernel,
        grid=(steps,),
        in_specs=[
            spec(rows // steps),
            spec(rows // steps),
            spec(768 // steps),
            spec(768 // steps),
            spec(192 // steps),
            spec(192 // steps, steps),
            spec(192 // steps),
            spec(192 // steps, steps),
            whole(256, 128),
        ],
        out_specs=[
            spec(rows // steps),
            spec(rows // steps),
            spec(768 // steps),
            spec(768 // steps),
            pl.BlockSpec((3, 192 // steps, width), lambda i: (0, i, 0)),
            spec(192 // steps),
            whole(2, 3, HD, HD),
            whole(3, 192),
            whole(3, 2, HD),
            *[whole(*v) for v in vectors],
        ],
        out_shape=[
            jax.ShapeDtypeStruct((rows, width), BF16),
            out(rows, width),
            out(768, width),
            out(768, width),
            out(3, 192, width),
            out(192, width),
            out(2, 3, HD, HD),
            out(3, 192),
            out(3, 2, HD),
            *[out(*v) for v in vectors],
        ],
        name="finish",
    )(res, tok, outer, inner, early, early, late, late, small)


def shards(
    fast,
    tokens,
    first_gain,
    first_bias,
    mixer_weight,
    mixer_bias,
    feature_weight,
    feature_bias,
    output_weight,
    output_bias,
    second_gain,
    second_bias,
    inner_weight,
    inner_bias,
    outer_weight,
    outer_bias,
    block_owner,
    cotangent,
):
    rows, width = tokens.shape
    n_tp, n_ctx = lax.axis_size("tp"), lax.axis_size("ctx")
    n_plane = lax.axis_size("dp") * n_ctx
    plane = lax.axis_index("dp") * n_ctx + lax.axis_index("ctx")
    heads_here = mixer_weight.shape[2] // HD
    heads = heads_here * n_tp
    mine = lax.axis_index("ctx") * n_tp + lax.axis_index("tp")

    mixer_t = mixer_weight.transpose(1, 2, 0).reshape(-1, width)
    if fast:
        vectors = (
            first_gain, first_bias, output_bias, second_gain, second_bias, outer_bias, inner_bias
        )
        raw = block_call(
            tokens,
            cotangent,
            mixer_t,
            output_weight,
            inner_weight,
            outer_weight,
            feature_weight,
            mixer_bias,
            feature_bias.transpose(1, 0, 2),
            *[v.reshape(6, 128) for v in vectors],
        )
        (
            result, tokens_gradient, d_outer, d_inner, d_mixer, d_output,
            d_feature, d_mixer_bias, d_feature_bias, *shared
        ) = finish_call(*raw)
        shared = [v.reshape(width) for v in shared]
        return (
            result,
            tokens_gradient,
            shared[0],
            shared[1],
            d_mixer.transpose(2, 0, 1),
            d_mixer_bias,
            d_feature,
            d_feature_bias.transpose(1, 0, 2),
            d_output,
            shared[2],
            shared[3],
            shared[4],
            d_inner,
            shared[6],
            d_outer,
            shared[5],
        )
    sizes = [w.shape[0] for w in (mixer_t, output_weight, inner_weight, outer_weight)]
    pack = jnp.concatenate([mixer_t, output_weight, inner_weight, outer_weight], axis=0)
    part = pack.shape[0] // n_plane
    piece = lax.dynamic_slice_in_dim(pack, plane * part, part, 0)
    full = lax.all_gather(piece, ALL, axis=0, tiled=True)
    full = full.reshape(n_plane, n_tp, part, width).transpose(1, 0, 2, 3).reshape(n_tp, -1, width)
    cuts = [0]
    for s in sizes:
        cuts.append(cuts[-1] + s)
    mixer_all, output_all, inner_all, outer_all = [
        full[:, a:b] for a, b in zip(cuts[:-1], cuts[1:])
    ]
    small = jnp.concatenate(
        [feature_weight.reshape(-1), mixer_bias.reshape(-1), feature_bias.reshape(-1), inner_bias]
    )
    small = lax.all_gather(small, "tp")
    cut = feature_weight.size
    feature_all = (
        small[:, :cut].reshape(n_tp, 2, heads_here, HD, HD).transpose(1, 0, 2, 3, 4)
    ).reshape(2, heads, HD, HD)
    mixer_bias_all = small[:, cut : cut + mixer_bias.size].astype(F32).reshape(n_tp, -1)
    cut += mixer_bias.size
    feature_bias_all = (
        small[:, cut : cut + feature_bias.size]
        .astype(F32)
        .reshape(n_tp, 2, heads_here, HD)
        .transpose(1, 0, 2, 3)
        .reshape(2, heads, HD)
    )
    cut += feature_bias.size
    inner_bias_all = small[:, cut:].astype(F32)

    x = tokens.astype(F32)
    gain1, gain2 = first_gain.astype(F32), second_gain.astype(F32)
    h1, n1, r1 = layer_norm(x, gain1, first_bias.astype(F32))
    h1 = h1.astype(BF16)
    mix = ein("td,skd->tsk", h1, mixer_all) + mixer_bias_all
    mix = mix.astype(BF16).reshape(rows, n_tp, 3, heads_here, HD).transpose(2, 0, 1, 3, 4)
    mix = mix.reshape(3, rows, heads, HD)
    q, k, v = mix[0], mix[1], mix[2]
    q_up, q_down, phi_q = feature_map(q, feature_all[0], feature_bias_all[0])
    k_up, k_down, phi_k = feature_map(k, feature_all[1], feature_bias_all[1])

    chunk = min(CHUNK, rows)
    chunks = rows // chunk
    pq = phi_q.reshape(chunks, chunk, heads, 2 * HD)
    pk = phi_k.reshape(chunks, chunk, heads, 2 * HD)
    vc = v.reshape(chunks, chunk, heads, HD)
    causal = jnp.arange(chunk)[:, None] >= jnp.arange(chunk)[None, :]
    state = ein("jthe,jthf->jhef", vc, pk)
    norm = jnp.sum(pk.astype(F32), axis=1)
    both = jnp.concatenate([state, norm[:, :, None]], axis=2)
    owners = block_owner[0].reshape(n_tp, -1)[:, 0]
    order = jnp.arange(n_ctx * n_tp)
    same = jnp.tile(owners, n_ctx) == jnp.tile(owners, n_ctx)[mine]

    def prefix(totals, reach):
        everything = lax.all_gather(totals.astype(BF16), ("ctx", "tp")).astype(F32)
        return jnp.einsum("s,shef->hef", reach.astype(F32), everything, precision="highest")

    def running(blocks, start, reverse):
        out = [None] * chunks
        acc = start
        for j in reversed(range(chunks)) if reverse else range(chunks):
            out[j] = acc
            acc = acc + blocks[j]
        return jnp.stack(out)

    before = running(both, prefix(jnp.sum(both, axis=0), same & (order < mine)), False)
    before = before.astype(BF16)
    scores = ein("jthf,jshf->jhts", pq, pk)
    a_low = jnp.where(causal, scores, 0.0).astype(BF16)
    v_one = jnp.concatenate([vc, jnp.ones(vc.shape[:-1] + (1,), BF16)], axis=-1)
    num = ein("jthf,jhef->jthe", pq, before) + ein("jhts,jshe->jthe", a_low, v_one)
    num, den = num[..., :HD], num[..., HD:]
    o = num / den
    o_low = o.astype(BF16)
    o_flat = o_low.reshape(rows, n_tp, heads_here * HD)
    x2 = x + ein("tsk,skd->td", o_flat, output_all) + output_bias.astype(F32)
    h2, n2, r2 = layer_norm(x2, gain2, second_bias.astype(F32))
    h2 = h2.astype(BF16)
    f = ein("td,sdf->tsf", h2, inner_all) + inner_bias_all
    a, slope = gelu_parts(f)
    a = a.astype(BF16)
    result = (x2 + ein("tsf,sfd->td", a, outer_all) + outer_bias.astype(F32)).astype(BF16)

    g = cotangent.astype(F32)
    d_outer = ein("tsf,td->sfd", a, cotangent)
    df = (ein("td,sfd->tsf", cotangent, outer_all) * slope).astype(BF16)
    d_inner_bias = jnp.sum(df.astype(F32), axis=0)
    d_inner = ein("td,tsf->sdf", h2, df)
    e2 = ein("tsf,sdf->td", df, inner_all)
    back2, d_gain2, d_bias2 = layer_norm_back(e2, n2, r2, gain2)
    dx2 = g + back2
    big_g = dx2.astype(BF16)
    d_output = ein("tsk,td->skd", o_flat, big_g)
    do = ein("td,skd->tsk", big_g, output_all).astype(BF16).astype(F32)
    do = do.reshape(chunks, chunk, heads, HD)
    dnum = do / den
    dden = -jnp.sum(do * o, axis=-1, keepdims=True) / den
    dne = jnp.concatenate([dnum, dden], axis=-1).astype(BF16)
    da = ein("jthe,jshe->jhts", dne, v_one)
    da_low = jnp.where(causal, da, 0.0).astype(BF16)
    d_both = ein("jthe,jthf->jhef", dne, pq)
    after = running(d_both, prefix(jnp.sum(d_both, axis=0), same & (order > mine)), True)
    after = after.astype(BF16)
    dphi_q = ein("jhts,jshf->jthf", da_low, pk) + ein("jthe,jhef->jthf", dne, before)
    dphi_k = ein("jhts,jthf->jshf", da_low, pq) + ein("jthe,jhef->jthf", v_one, after)
    dv = ein("jhts,jthe->jshe", a_low, dne[..., :HD]) + ein("jthf,jhef->jthe", pk, after[:, :, :HD])
    dphi_q = dphi_q.reshape(rows, heads, 2 * HD)
    dphi_k = dphi_k.reshape(rows, heads, 2 * HD)
    dq, d_fq, d_fbq = feature_back(dphi_q, q_up, q_down, q, feature_all[0])
    dk, d_fk, d_fbk = feature_back(dphi_k, k_up, k_down, k, feature_all[1])
    dmix = jnp.stack([dq, dk, dv.reshape(rows, heads, HD)], axis=1).astype(BF16)
    dmix = dmix.reshape(rows, 3, n_tp, heads_here * HD).transpose(0, 2, 1, 3)
    dmix = dmix.reshape(rows, n_tp, -1)
    d_mixer_bias = jnp.sum(dmix.astype(F32), axis=0)
    d_mixer = ein("tsk,td->skd", dmix, h1)
    e1 = ein("tsk,skd->td", dmix, mixer_all)
    back1, d_gain1, d_bias1 = layer_norm_back(e1, n1, r1, gain1)
    tokens_gradient = dx2 + back1

    big = jnp.concatenate([d_mixer, d_output, d_inner, d_outer], axis=1).astype(BF16)
    big = big.reshape(n_tp, n_plane, part, width).transpose(1, 0, 2, 3).reshape(-1, width)
    big = lax.psum_scatter(big, ("dp", "ctx"), scatter_dimension=0, tiled=True)
    big = lax.psum_scatter(big, "tp", scatter_dimension=0, tiled=True)
    big = lax.all_gather(big, ("dp", "ctx"), axis=0, tiled=True).astype(F32)
    d_mixer, d_output, d_inner, d_outer = [big[a:b] for a, b in zip(cuts[:-1], cuts[1:])]
    d_mixer = d_mixer.reshape(3, heads_here * HD, width).transpose(2, 0, 1)
    per_tp = jnp.concatenate(
        [
            jnp.stack([d_fq, d_fk]).reshape(2, n_tp, -1).transpose(1, 0, 2).reshape(n_tp, -1),
            d_mixer_bias,
            jnp.stack([d_fbq, d_fbk]).reshape(2, n_tp, -1).transpose(1, 0, 2).reshape(n_tp, -1),
            d_inner_bias,
        ],
        axis=1,
    )
    shared = jnp.stack(
        [d_gain1, d_bias1, jnp.sum(dx2, axis=0), d_gain2, d_bias2, jnp.sum(g, axis=0)]
    )
    total = lax.psum(jnp.concatenate([per_tp.reshape(-1), shared.reshape(-1)]), ALL)
    shared = total[per_tp.size :].reshape(6, width)
    own = lax.dynamic_slice_in_dim(
        total[: per_tp.size].reshape(n_tp, -1), lax.axis_index("tp"), 1, 0
    )[0]
    cut = feature_weight.size
    d_feature = own[:cut].reshape(feature_weight.shape)
    d_mixer_bias = own[cut : cut + mixer_bias.size].reshape(mixer_bias.shape)
    cut += mixer_bias.size
    d_feature_bias = own[cut : cut + feature_bias.size].reshape(feature_bias.shape)
    d_inner_bias = own[cut + feature_bias.size :]
    return (
        result,
        tokens_gradient,
        shared[0],
        shared[1],
        d_mixer,
        d_mixer_bias,
        d_feature,
        d_feature_bias,
        d_output,
        shared[2],
        shared[3],
        shared[4],
        d_inner,
        d_inner_bias,
        d_outer,
        shared[5],
    )


def solution(mesh):
    in_specs = (
        P(("dp", "ctx", "tp"), None),
        P(),
        P(),
        P(None, None, "tp"),
        P(None, "tp"),
        P(None, "tp", None, None),
        P(None, "tp", None),
        P("tp", None),
        P(),
        P(),
        P(),
        P(None, "tp"),
        P("tp"),
        P("tp", None),
        P(),
        P("dp", None),
        P(("dp", "ctx", "tp"), None),
    )
    out_specs = (
        P(("dp", "ctx", "tp"), None),
        P(("dp", "ctx", "tp"), None),
        P(),
        P(),
        P(None, None, "tp"),
        P(None, "tp"),
        P(None, "tp", None, None),
        P(None, "tp", None),
        P("tp", None),
        P(),
        P(),
        P(),
        P(None, "tp"),
        P("tp"),
        P("tp", None),
        P(),
    )
    fast = (mesh.shape["dp"], mesh.shape["ctx"], mesh.shape["tp"]) == (2, 4, 4)
    return jax.shard_map(functools.partial(shards, fast), mesh=mesh, in_specs=in_specs, out_specs=out_specs, check_vma=False)
```

```python
import functools
from types import SimpleNamespace

import jax
import jax.numpy as jnp
from jax import lax
from jax.experimental import pallas as pl
from jax.experimental.pallas import tpu as pltpu
from jax.sharding import PartitionSpec as P

MESH = pl.DeviceIdType.MESH

HD = 64
BLOCK = 64
CHUNK = 256
EPSILON = 1e-05
F32 = jnp.float32
BF16 = jnp.bfloat16
ALL = ("dp", "ctx", "tp")


def ein(spec, a, b):
    return jnp.einsum(spec, a, b, preferred_element_type=F32)


def layer_norm(v, gain, offset):
    c = v - jnp.mean(v, axis=-1, keepdims=True)
    r = lax.rsqrt(jnp.mean(c * c, axis=-1, keepdims=True) + EPSILON)
    n = c * r
    return n * gain + offset, n, r


def layer_norm_back(e, n, r, gain):
    m = e * gain
    back = r * (
        m - jnp.mean(m, axis=-1, keepdims=True) - n * jnp.mean(m * n, axis=-1, keepdims=True)
    )
    return back, jnp.sum(e * n, axis=0), jnp.sum(e, axis=0)


def gelu_parts(s):
    t = jnp.tanh(0.7978845608028654 * (s + 0.044715 * s * s * s))
    slope = 0.7978845608028654 * (1.0 + 3.0 * 0.044715 * s * s)
    return 0.5 * s * (1.0 + t), 0.5 * (1.0 + t) + 0.5 * s * (1.0 - t * t) * slope


def feature_map(q, weight, offset):
    u = ein("thd,hde->the", q, weight) + offset
    up, down = jax.nn.softmax(u, axis=-1), jax.nn.softmax(-u, axis=-1)
    return up, down, jnp.concatenate([up, down], axis=-1).astype(BF16)


def feature_back(delta, up, down, q, weight):
    d, dd = delta[..., :HD], delta[..., HD:]
    du = up * (d - jnp.sum(up * d, axis=-1, keepdims=True)) - down * (
        dd - jnp.sum(down * dd, axis=-1, keepdims=True)
    )
    low = du.astype(BF16)
    return ein("the,hde->thd", low, weight), ein("thd,the->hde", q, low), jnp.sum(du, axis=0)


HD = 64
BLOCK = 64
CHUNK = 256
EPSILON = 1e-05
F32 = jnp.float32
BF16 = jnp.bfloat16
ALL = ("dp", "ctx", "tp")


def ein(spec, a, b):
    return jnp.einsum(spec, a, b, preferred_element_type=F32)


def layer_norm(v, gain, offset):
    c = v - jnp.mean(v, axis=-1, keepdims=True)
    r = lax.rsqrt(jnp.mean(c * c, axis=-1, keepdims=True) + EPSILON)
    n = c * r
    return n * gain + offset, n, r


def layer_norm_back(e, n, r, gain):
    m = e * gain
    back = r * (
        m - jnp.mean(m, axis=-1, keepdims=True) - n * jnp.mean(m * n, axis=-1, keepdims=True)
    )
    return back, jnp.sum(e * n, axis=0), jnp.sum(e, axis=0)


def gelu_parts(s):
    t = jnp.tanh(0.7978845608028654 * (s + 0.044715 * s * s * s))
    slope = 0.7978845608028654 * (1.0 + 3.0 * 0.044715 * s * s)
    return 0.5 * s * (1.0 + t), 0.5 * (1.0 + t) + 0.5 * s * (1.0 - t * t) * slope


def feature_map(q, weight, offset):
    u = ein("thd,hde->the", q, weight) + offset
    up, down = jax.nn.softmax(u, axis=-1), jax.nn.softmax(-u, axis=-1)
    return up, down, jnp.concatenate([up, down], axis=-1).astype(BF16)


def feature_back(delta, up, down, q, weight):
    d, dd = delta[..., :HD], delta[..., HD:]
    du = up * (d - jnp.sum(up * d, axis=-1, keepdims=True)) - down * (
        dd - jnp.sum(down * dd, axis=-1, keepdims=True)
    )
    low = du.astype(BF16)
    return ein("the,hde->thd", low, weight), ein("thd,the->hde", q, low), jnp.sum(du, axis=0)


def place():
    d, c, t = lax.axis_index("dp"), lax.axis_index("ctx"), lax.axis_index("tp")
    y, core = c // 2, lax.rem(c, 2)
    return SimpleNamespace(d=d, c=c, t=t, y=y, core=core, q=d * 2 + y,
        x_nb=(1 - d, c, t), y_nb=(d, (1 - y) * 2 + core, t), core_nb=(d, y * 2 + 1 - core, t),
        qx=(1 - d) * 2 + y, qy=d * 2 + 1 - y, qd=(1 - d) * 2 + 1 - y)

def plane_peer(p, r):
    d = 1 - p.d if r & 4 else p.d
    y = 1 - p.y if r & 2 else p.y
    core = 1 - p.core if r & 1 else p.core
    return (d, y * 2 + core, p.t), d * 4 + y * 2 + core


def greet(p):
    bar = pltpu.get_barrier_semaphore()
    peers = [plane_peer(p, r)[0] for r in range(1, 8)]
    peers += [(p.d, p.c, lax.rem(p.t + k, 4)) for k in (1, 2, 3)]
    for peer in peers:
        pl.semaphore_signal(bar, inc=1, device_id=peer, device_id_type=MESH)


def met(p):
    pl.semaphore_wait(pltpu.get_barrier_semaphore(), 10)


def nearest(t):
    return [
        jnp.where(t < 2, 1, 3),
        jnp.where(t == 0, 2, jnp.where(t == 1, 3, jnp.where(t == 2, 1, 2))),
        jnp.where(t == 0, 3, jnp.where(t == 3, 1, 2)),
    ]


class Gather:
    def __init__(self, p, buf, sems, send, index, base=0, rows=None):
        self.p, self.buf, self.sems, self.send, self.i = p, buf, sems, send.at[index], index
        self.base, self.rows = base, rows or buf.shape[1]
        self.wide = buf.shape[2] == 768
        self.piece = self.rows // (4 if self.wide else 8)
        self.lanes = lanes(0) if self.wide else slice(None)

    def at(self, t, q, core, half=None):
        start = q * (self.rows // 4) + (0 if self.wide else core * self.piece)
        size = self.piece
        if half is not None:
            first = (size + 16) // 32 * 16
            start, size = start + half * first, size - first if half else first
        rows = pl.ds(pl.multiple_of(self.base + start, 16), size)
        return self.buf.at[t, rows, lanes(core)] if self.wide else self.buf.at[t, rows]

    def shard(self, k): return lax.rem(self.p.t + k, 4)
    def copy(self, ref, kind, k, peer):
        n = 0 if kind == "z" else 2 if kind == "c" else 1
        recv = self.sems[kind].at[self.i, k - 1]
        return pltpu.make_async_remote_copy(
            ref, ref, self.send.at[n], recv, device_id=peer, device_id_type=MESH
        )

    def go(self, *a):
        self.copy(*a).start()

    def first(self):
        p = self.p
        ref = self.at(p.t, p.q, p.core)
        for k in (1, 2, 3):
            self.go(ref, "z", 4 - k, (p.d, p.c, lax.rem(p.t + k, 4)))

    def first_hop(self):
        p = self.p
        ref = self.at(p.t, p.q, p.core)
        pl.when(p.t < 3)(lambda: self.go(ref, "z", 3, (p.d, p.c, p.t + 1)))
        pl.when(p.t > 0)(lambda: self.go(ref, "z", 1, (p.d, p.c, p.t - 1)))

    def zf(self, k):
        p, t = self.p, self.shard(k)
        ref = self.at(t, p.q, p.core)
        self.copy(ref, "z", k, p.x_nb).wait_recv()
        up = jnp.logical_and(t < p.t, p.t < 3)
        down = jnp.logical_and(t > p.t, p.t > 0)
        pl.when(up)(lambda: self.go(ref, "z", k - 1, (p.d, p.c, p.t + 1)))
        pl.when(down)(lambda: self.go(ref, "z", k + 1, (p.d, p.c, p.t - 1)))

    def spread(self, k):
        p = self.p
        ref = self.at(self.shard(k), p.q, p.core)
        self.go(ref, "x", k, p.x_nb)
        self.go(ref, "y", k, p.y_nb)

    def z(self, k):
        p, t = self.p, self.shard(k)
        ref = self.at(t, p.q, p.core)
        self.copy(ref, "z", k, p.x_nb).wait_recv()
        self.go(ref, "x", k, p.x_nb); self.go(ref, "y", k, p.y_nb)
    def xy(self, k):
        p, t = self.p, self.shard(k)
        self.copy(self.at(t, p.qx, p.core), "x", k, p.x_nb).wait_recv()
        self.go(self.at(t, p.qx, p.core, 0), "fy", k, p.y_nb)
        self.copy(self.at(t, p.qy, p.core), "y", k, p.y_nb).wait_recv()
        self.go(self.at(t, p.qy, p.core, 1), "fx", k, p.x_nb)
    def diag(self, k):
        p, t = self.p, self.shard(k)
        self.copy(self.at(t, p.qd, p.core, 0), "fy", k, p.y_nb).wait_recv()
        self.copy(self.at(t, p.qd, p.core, 1), "fx", k, p.x_nb).wait_recv()
        if self.wide:
            self.go(self.buf.at[t, pl.ds(self.base, self.rows), lanes(p.core)], "c", k, p.core_nb)
        else:
            for q in range(4):
                self.go(self.at(t, q, p.core), "c", k, p.core_nb)

    def done(self, k):
        p, t = self.p, self.shard(k)
        if self.wide:
            ref = self.buf.at[t, pl.ds(self.base, self.rows), lanes(1 - p.core)]
        else:
            ref = self.buf.at[t, pl.ds(0, 4 * self.piece)]
        self.copy(ref, "c", k, p.core_nb).wait_recv()

    def drain(self, hops):
        p, n = self.p, self.piece

        def wait(kind, ref):
            self.copy(ref, kind, 1, p.core_nb).wait_send()

        if hops:
            ends = jnp.logical_or(p.t == 0, p.t == 3)
            pl.when(ends)(lambda: wait("z", self.buf.at[0, pl.ds(0, n // 2)]))
            pl.when(jnp.logical_not(ends))(lambda: wait("z", self.buf.at[0, pl.ds(0, 5 * n // 2)]))
        else:
            wait("z", self.buf.at[0, pl.ds(0, 3 * n), self.lanes])
        wait("x", self.buf.at[pl.ds(0, 3), pl.ds(0, 3 * n), self.lanes])
        wait("c", self.buf.at[pl.ds(0, 3), pl.ds(0, 4 * n), self.lanes])


def lanes(core):
    return pl.ds(pl.multiple_of(core * 384, 128), 384)


class Reduce:
    def __init__(self, p, i, G, X1, Y1, X2, Y2, Z, OUT, sems, send, own):
        self.p, self.i, self.G, self.OUT, self.sems = p, i, G, OUT, sems
        self.X1, self.Y1, self.X2, self.Y2, self.Z = X1, Y1, X2, Y2, Z
        self.half = G.shape[1]; self.qr = self.half // 4; self.hr = self.qr // 2
        self.send = send
        self.own = own
    def t(self, k): return lax.rem(self.p.t + k, 4)
    def rows(self, q, h): return pl.ds(pl.multiple_of(q * self.qr + h * self.hr, 16), self.hr)
    def rdma(self, src, dst, kind, k, peer):
        n = 1 if kind == "z" else 0 if kind != "f" else 3 if k == 4 else 2
        return pltpu.make_async_remote_copy(
            src,
            dst,
            self.send.at[self.i, n],
            self.sems[kind].at[self.i, k],
            device_id=peer,
            device_id_type=MESH,
        )

    def go(self, *a):
        self.rdma(*a).start()

    def got(self, ref, kind, k):
        self.rdma(ref, ref, kind, k, self.p.x_nb).wait_recv()
    def one(self, k):
        p, t = self.p, self.t(k)
        for j in range(2):
            self.go(self.G.at[t, self.rows((1 - p.d) * 2 + j, 0)], self.X1.at[k, j], "x1", k, p.x_nb)
            self.go(self.G.at[t, self.rows(j * 2 + 1 - p.y, 1)], self.Y1.at[k, j], "y1", k, p.y_nb)
    def two(self, k):
        p, t, G = self.p, self.t(k), self.G
        self.got(self.X1.at[k], "x1", k)
        for j in range(2):
            r = self.rows(p.d * 2 + j, 0)
            G[t, r] = G[t, r] + self.X1[k, j]
        self.go(G.at[t, self.rows(p.qy, 0)], self.Y2.at[k], "y2", k, p.y_nb)
        self.got(self.Y1.at[k], "y1", k)
        for j in range(2):
            r = self.rows(j * 2 + p.y, 1)
            G[t, r] = G[t, r] + self.Y1[k, j]
        self.go(G.at[t, self.rows(p.qx, 1)], self.X2.at[k], "x2", k, p.x_nb)
    def three(self, k):
        p, t, G = self.p, self.t(k), self.G
        for h, (kind, R) in enumerate((("y2", self.Y2), ("x2", self.X2))):
            self.got(R.at[k], kind, k)
            r = self.rows(p.q, h)
            G[t, r] = G[t, r] + R[k]
        if not isinstance(k, int):
            whole = pl.ds(pl.multiple_of(p.q * self.qr, 16), self.qr)
            self.go(G.at[t, whole], self.Z.at[3 - k], "z", 3 - k, (p.d, p.c, t))
    def piece(self, q, core, h=None):
        start, size = q * self.qr, self.qr
        if h is not None:
            start, size = start + h * self.hr, self.hr
        return self.OUT.at[pl.ds(pl.multiple_of(start, 16), size), lanes(core)]

    def final(self):
        p = self.p
        whole = pl.ds(pl.multiple_of(p.q * self.qr, 16), self.qr)
        total = self.G[p.t, whole].astype(F32)
        for k in range(3):
            self.got(self.Z.at[k], "z", k)
            total = total + self.Z[k].astype(F32)
        ref = self.piece(p.q, p.core)
        mine = self.G.at[p.t, whole]
        mine[...] = total.astype(BF16)
        self.go(mine, ref, "f", 0, p.x_nb)
        self.go(mine, ref, "f", 1, p.y_nb)
        self.own_copy().start()

    def own_copy(self):
        p = self.p
        whole = pl.ds(pl.multiple_of(p.q * self.qr, 16), self.qr)
        return pltpu.make_async_copy(
            self.G.at[p.t, whole], self.piece(p.q, p.core), self.own.at[self.i]
        )

    def spread(self):
        p = self.p
        ref = self.piece(p.qx, p.core); self.got(ref, "f", 0)
        ref = self.piece(p.qx, p.core, 0); self.go(ref, ref, "f", 2, p.y_nb)
        ref = self.piece(p.qy, p.core); self.got(ref, "f", 1)
        ref = self.piece(p.qy, p.core, 1); self.go(ref, ref, "f", 3, p.x_nb)
    def corner(self):
        p = self.p
        self.own_copy().wait()
        self.got(self.piece(p.qd, p.core, 0), "f", 2); self.got(self.piece(p.qd, p.core, 1), "f", 3)
        ref = self.OUT.at[:, lanes(p.core)]
        self.go(ref, ref, "f", 4, p.core_nb)
    def end(self):
        p = self.p
        self.got(self.OUT.at[:, lanes(1 - p.core)], "f", 4)
        rows = 3 * self.half // 4
        sizes = (
            ("x1", 0, self.G.at[pl.ds(0, 3)]),
            ("z", 0, self.Z),
            ("f", 0, self.G.at[0, pl.ds(0, rows)]),
            ("f", 4, self.G.at[0]),
        )
        for kind, k, ref in sizes:
            self.rdma(ref, ref, kind, k, p.core_nb).wait_send()


GATHER_SEMS = ("z", "x", "y", "fx", "fy", "c")
SEMS = ("x1", "y1", "x2", "y2", "z", "f")


def dot(a, b, ca, cb):
    return lax.dot_general(a, b, (((ca,), (cb,)), ((), ())), preferred_element_type=F32)


def loop(n, step):
    def body(i, carry):
        step(i)
        return carry

    lax.fori_loop(0, n, body, 0)


def ds(i, n):
    return pl.ds(pl.multiple_of(i * n, n), n)


class Scan:
    def __init__(self, p, later, total, up, down, got, sems):
        self.p, self.later, self.total, self.up_ref, self.down_ref = p, later, total, up, down
        self.from_core, self.from_y, self.from_below, self.from_above = [got.at[i] for i in range(4)]
        self.sems = sems

    def rdma(self, src, dst, g, i, peer):
        h, i = self.heads(g), 4 * i + g
        return pltpu.make_async_remote_copy(
            src.at[h], dst.at[h], self.sems.at[0, i], self.sems.at[1, i], device_id=peer, device_id_type=MESH
        )

    def core_copy(self, g):
        return self.rdma(self.total, self.from_core, g, 0, self.p.core_nb)

    def y_copy(self, g):
        return self.rdma(self.up_ref, self.from_y, g, 1, self.p.y_nb)

    def line_copy(self, g, upward):
        p = self.p
        if upward:
            return self.rdma(self.up_ref, self.from_below, g, 2, (p.d, p.c, p.t + 1))
        return self.rdma(self.down_ref, self.from_above, g, 3, (p.d, p.c, p.t - 1))

    def heads(self, g):
        return pl.ds(3 * g, 3)

    def begin(self, g):
        h = self.heads(g)
        zero = jnp.zeros((3, 80, 128), BF16)

        @pl.when(self.p.t == 0)
        def _():
            self.from_below[h] = zero

        @pl.when(self.p.t == 3)
        def _():
            self.from_above[h] = zero

        self.core_copy(g).start()

    def pair(self, g):
        h = self.heads(g)
        self.core_copy(g).wait_recv()
        self.up_ref[h] = self.total[h] + self.from_core[h]
        self.y_copy(g).start()

    def column(self, g):
        p, h = self.p, self.heads(g)
        core, y = p.core.astype(F32), p.y.astype(F32)
        if self.later:
            core, y = 1.0 - core, 1.0 - y
        return core * self.from_core[h].astype(F32) + y * self.from_y[h].astype(F32)

    def hop(self, g, upward):
        h, t = self.heads(g), self.p.t
        has, sends = (t > 0, t < 3) if upward else (t < 3, t > 0)
        c = self.line_copy(g, upward)
        got = self.from_below if upward else self.from_above
        out = self.up_ref if upward else self.down_ref

        @pl.when(has)
        def _():
            c.wait_recv()

        @pl.when(sends)
        def _():
            value = self.column(g) + got[h].astype(F32)
            if upward != self.later:
                value = value + self.total[h].astype(F32)
            out[h] = value.astype(BF16)
            c.start()

    def chain(self, g):
        c = self.y_copy(g)
        c.wait_recv()
        c.wait_send()
        pl.when(self.p.t < 2)(lambda: self.hop(g, True))
        pl.when(self.p.t >= 2)(lambda: self.hop(g, False))

    def relay(self, g):
        pl.when(self.p.t == 1)(lambda: self.hop(g, False))
        pl.when(self.p.t == 2)(lambda: self.hop(g, True))

    def last(self, g):
        pl.when(self.p.t == 0)(lambda: self.hop(g, False))
        pl.when(self.p.t == 3)(lambda: self.hop(g, True))

    def sum(self, g):
        h = self.heads(g)
        return self.column(g) + self.from_below[h].astype(F32) + self.from_above[h].astype(F32)

    def drain(self):
        for g in range(4):
            self.core_copy(g).wait_send()
            pl.when(self.p.t < 3)(lambda g=g: self.line_copy(g, True).wait_send())
            pl.when(self.p.t > 0)(lambda g=g: self.line_copy(g, False).wait_send())


class Small:
    def __init__(self, p, low, full, plane, line, mid, out, sems, send, own):
        self.p, self.low, self.full, self.plane, self.line, self.mid, self.out = (
            p, low, full, plane, line, mid, out
        )
        self.sems, self.send, self.own = sems, send, own
        self.me = p.d * 4 + p.c

    def rdma(self, src, dst, i, peer):
        n = 0 if i < 7 else 1 if i < 10 else 2
        return pltpu.make_async_remote_copy(
            src, dst, self.send.at[n], self.sems.at[i], device_id=peer, device_id_type=MESH
        )

    def go(self, *a):
        self.rdma(*a).start()

    def begin(self):
        for r in range(1, 8):
            peer, j = plane_peer(self.p, r)
            self.go(self.low.at[ds(j, 32)], self.plane.at[r - 1], r - 1, peer)

    def across(self):
        p = self.p
        for r in range(1, 8):
            self.rdma(self.plane.at[r - 1], self.plane.at[r - 1], r - 1, p.x_nb).wait_recv()
        for t in range(4):
            total = self.full[t, ds(self.me, 32)]
            for r in range(7):
                total = total + self.plane[r, :, 128 * t : 128 * t + 128].astype(F32)
            self.full[t, ds(self.me, 32)] = total
            self.mid[t] = total.astype(BF16)
        for k in (1, 2, 3):
            t = lax.rem(p.t + k, 4)
            self.go(self.mid.at[t], self.line.at[3 - k], 10 - k, (p.d, p.c, t))

    def final(self):
        p = self.p
        total = self.full[p.t, ds(self.me, 32)]
        for k in range(3):
            self.rdma(self.line.at[k], self.line.at[k], 7 + k, p.x_nb).wait_recv()
            total = total + self.line[k].astype(F32)
        self.mid[4] = total.astype(BF16)
        ref = self.out.at[ds(self.me, 32)]
        for r in range(1, 8):
            self.go(self.mid.at[4], ref, 9 + r, plane_peer(p, r)[0])
        pltpu.make_async_copy(self.mid.at[4], ref, self.own).start()

    def end(self):
        pltpu.make_async_copy(self.mid.at[4], self.out.at[ds(self.me, 32)], self.own).wait()
        for r in range(1, 8):
            peer, j = plane_peer(self.p, r)
            ref = self.out.at[ds(j, 32)]
            self.rdma(ref, ref, 9 + r, peer).wait_recv()
        for i, ref in ((0, self.plane), (7, self.line), (10, self.plane.at[:, :, pl.ds(0, 128)])):
            self.rdma(ref, ref, i, self.p.core_nb).wait_send()


def layer_rows(v):
    c = v - jnp.mean(v, axis=-1, keepdims=True)
    r = lax.rsqrt(jnp.mean(c * c, axis=-1, keepdims=True) + EPSILON)
    return c * r, r


def fold(v):
    total = v[:8]
    for i in range(1, v.shape[0] // 8):
        total = total + v[8 * i : 8 * i + 8]
    return total


def layer_back(e, n, r, gain):
    m = e * gain
    return r * (
        m - jnp.mean(m, axis=-1, keepdims=True) - n * jnp.mean(m * n, axis=-1, keepdims=True)
    )


def block_kernel(m):
    p = place()
    t0 = p.t
    X, CT, S, WA, W1, W2 = m.X, m.CT, m.S, m.WA, m.W1, m.W2
    VEC, H1, H2, X2, ACC_O, ACC_E = m.VEC, m.H1, m.H2, m.X2, m.ACC_O, m.ACC_E
    MIX, PH, VX, AT, PX, SL, OT, RD = m.MIX, m.PH, m.VX, m.AT, m.PX, m.SL, m.OT, m.RD
    A, DF, GS, FW, BC, IB, SUMS = m.A, m.DF, m.GS, m.FW, m.BC, m.IB, m.SUMS
    ld = m.ld
    greet(p)
    loads = [
        pltpu.make_async_copy(m.wm, WA.at[t0, pl.ds(0, 576)], ld.at[0]),
        pltpu.make_async_copy(m.wo, WA.at[t0, pl.ds(576, 192)], ld.at[1]),
        pltpu.make_async_copy(m.x, X, ld.at[2]),
        pltpu.make_async_copy(m.w1, W1.at[t0], ld.at[3]),
        pltpu.make_async_copy(m.w2, W2.at[t0], ld.at[4]),
        pltpu.make_async_copy(m.g, CT, ld.at[5]),
    ]
    raw = [(m.fw, m.FWI), (m.mb, m.MBI), (m.fb, m.FBI)]
    raw += [(ref, m.VECI.at[i, pl.ds(0, 6)]) for i, ref in enumerate(m.vectors)]
    raw = [pltpu.make_async_copy(src, dst, ld.at[8 + i]) for i, (src, dst) in enumerate(raw)]
    for c in raw + loads:
        c.start()
    for c in raw:
        c.wait()

    for h in range(3):
        pair = [m.FWI[i, h].astype(F32) for i in range(2)]
        S[t0, 64 * h : 64 * h + 64] = jnp.concatenate(pair, axis=1).astype(BF16)
    zero = jnp.zeros((1, HD), F32)
    rows = []
    for j in range(3):
        row = m.MBI[j : j + 1].astype(F32)
        rows += [
            jnp.concatenate([row[:, HD * h : HD * h + HD], zero], axis=1) for h in range(3)
        ]
    for h in range(3):
        row = m.FBI[h].astype(F32)
        rows.append(jnp.concatenate([row[0:1], row[1:2]], axis=1))
    rows.append(jnp.zeros((4, 128), F32))
    S[t0, 192:208] = jnp.concatenate(rows, axis=0).astype(BF16)
    rows = [m.VECI[6].astype(F32)[0:6], jnp.zeros((42, 128), F32)]
    S[t0, 208:256] = jnp.concatenate(rows, axis=0).astype(BF16)
    for k in range(6):
        value = m.VECI[k].astype(F32)
        for i in range(6):
            VEC[k : k + 1, 128 * i : 128 * i + 128] = value[i : i + 1]

    packs = ((S, 0, 256), (WA, 0, 576), (W1, 0, 768), (W2, 0, 768), (WA, 576, 192))
    gs, gw, g1, g2, go = [
        Gather(p, buf, m.gather_sems, m.gather_send, i, base, rows)
        for i, (buf, base, rows) in enumerate(packs)
    ]
    K = nearest(t0)
    shard = gs.shard
    loads[0].wait()
    met(p)
    gw.first()
    gs.first()

    loads[2].wait()

    def norm1(i):
        r = ds(i, 128)
        n, _ = layer_rows(X[r].astype(F32))
        H1[r] = (n * VEC[0:1] + VEC[1:2]).astype(BF16)

    loop(4, norm1)
    ones_row = jnp.where(lax.broadcasted_iota(jnp.int32, (16, 512), 0) == 0, 1.0, 0.0).astype(BF16)

    def init(h):
        VX[h, 64:80] = ones_row

    loop(12, init)
    SUMS[...] = jnp.zeros_like(SUMS)

    def small(t):
        BC[...] = S[t, 192:208].astype(F32).T
        rows = S[t, 208:224].astype(F32)
        for i in range(6):
            IB[t, :, 128 * i : 128 * i + 128] = rows[i : i + 1]
        for h in range(3):
            w = S[t, 64 * h : 64 * h + 64].astype(F32)
            FW[0, t * 3 + h] = w[:, :64].astype(BF16)
            FW[1, t * 3 + h] = w[:, 64:].astype(BF16)

    def mix(t):
        value = dot(WA[t, 0:576], H1[...], 1, 1)
        for j in range(3):
            for h in range(3):
                n = j * 3 + h
                part = (value[64 * n : 64 * n + 64] + BC[0:64, n : n + 1]).astype(BF16)
                if j < 2:
                    MIX[t, 64 * n : 64 * n + 64] = part
                else:
                    VX[t * 3 + h, 0:64] = part

    def features(t):
        for h in range(3):
            for i in range(2):
                u = dot(FW[i, t * 3 + h], MIX[t, 192 * i + 64 * h : 192 * i + 64 * h + 64], 0, 0)
                u = u + BC[64 * i : 64 * i + 64, 9 + h : 10 + h]
                e = jnp.exp(u - jnp.max(u, axis=0, keepdims=True))
                PH[i, t * 3 + h, 0:64] = (e / jnp.sum(e, axis=0, keepdims=True)).astype(BF16)
                e = jnp.exp(jnp.min(u, axis=0, keepdims=True) - u)
                PH[i, t * 3 + h, 64:128] = (e / jnp.sum(e, axis=0, keepdims=True)).astype(BF16)

    def states(t):
        def one(i):
            h = t * 3 + i
            s0 = dot(VX[h, :, 0:256], PH[1, h, :, 0:256], 1, 1)
            s1 = dot(VX[h, :, 256:512], PH[1, h, :, 256:512], 1, 1)
            SL[h] = s0
            m.TOT[h] = (s0 + s1).astype(BF16)

        loop(3, one)

    small(t0)
    mix(t0)
    features(t0)
    states(t0)
    both = (g1, g2)
    for n, k in enumerate(K):
        gw.z(k)
        gs.z(k)
        if n == 1:
            for c in (loads[1], loads[3], loads[4]):
                c.wait()
            go.first()
            for g in both:
                g.first_hop()
    for k in K:
        gw.xy(k)
        gs.xy(k)
    for k in K:
        gw.diag(k)
        gs.diag(k)
    middle = jnp.logical_or(t0 == 1, t0 == 2)
    for k in K:
        go.z(k)
    for g in both:
        g.zf(K[0])
        g.spread(K[0])
    for g in both:
        pl.when(middle)(lambda g=g: g.zf(K[1]))
    def arrived(n):
        k = jnp.where(n == 0, K[0], jnp.where(n == 1, K[1], K[2]))
        gs.done(k)
        gw.done(k)
        t = shard(k)
        small(t)
        mix(t)
        features(t)
        states(t)

    loop(3, arrived)
    scan = Scan(p, False, m.TOT, m.UP, m.DOWN, m.got_f, m.scan_f)
    for g in range(4):
        scan.begin(g)
    causal = lax.broadcasted_iota(jnp.int32, (256, 256), 0) <= lax.broadcasted_iota(
        jnp.int32, (256, 256), 1
    )

    def scores(h):
        for j in range(2):
            c = slice(256 * j, 256 * j + 256)
            a = dot(PH[1, h, :, c], PH[0, h, :, c], 0, 0)
            AT[h, j] = jnp.where(causal, a, 0.0).astype(BF16)

    for k in K:
        go.xy(k)
    for g in both:
        g.zf(jnp.where(middle, K[2], K[1]))
    for g in range(4):
        scan.pair(g)
    loop(12, scores)
    for g in range(4):
        scan.chain(g)
    for k in K:
        go.diag(k)
    for g in both:
        g.xy(K[0])
        g.spread(K[1])
    for g in both:
        pl.when(jnp.logical_not(middle))(lambda g=g: g.zf(K[2]))
    for g in range(4):
        scan.relay(g)
    for g in both:
        g.spread(K[2])

    def enter(first):
        for g in range(4):
            scan.last(g)
            value = scan.sum(g)
            h = scan.heads(g)
            PX[h, first] = value.astype(BF16)
            PX[h, 1 - first] = (value + SL[h]).astype(BF16)

    enter(0)

    def attend(h):
        for j in range(2):
            c = slice(256 * j, 256 * j + 256)
            num = dot(PX[h, j], PH[0, h, :, c], 1, 0) + dot(VX[h, :, c], AT[h, j], 1, 0)
            r = 1.0 / num[64:65]
            RD[h, :, c] = r
            OT[ds(h, 64), c] = (num[0:64] * r).astype(BF16)

    loop(12, attend)
    for k in K:
        go.done(k)

    def norm2(i):
        r = ds(i, 256)
        total = X[r].astype(F32) + VEC[2:3]
        for t in range(4):
            total = total + dot(OT[192 * t : 192 * t + 192, r], WA[t, 576:768], 0, 0)
        X2[r] = total
        n, _ = layer_rows(total)
        H2[r] = (n * VEC[3:4] + VEC[4:5]).astype(BF16)
        ACC_O[r] = total + VEC[5:6]
        ACC_E[r] = jnp.zeros((256, 768), F32)

    loop(2, norm2)

    R = [
        Reduce(p, i, m.G[i], *m.land[i][1:], m.Z[i], m.outs[i], m.reduce_sems, m.reduce_send, m.own)
        for i in range(4)
    ]
    core_sems, STAGE = m.r_core, m.STAGE
    outgoing = []

    def core_copy(src, i, k):
        ref = m.land[i][0].at[shard(k)]
        return pltpu.make_async_remote_copy(
            ref if src is None else src,
            ref,
            core_sems.at[0, i, k],
            core_sems.at[1, i, k],
            device_id=p.core_nb,
            device_id_type=MESH,
        )

    def hand(i, k, value):
        slot = len(outgoing) % 2
        if len(outgoing) >= 2:
            outgoing[-2].wait_send()
        ref = STAGE.at[slot, pl.ds(0, R[i].half)]
        ref[...] = value(1 - p.core).astype(BF16)
        c = core_copy(ref, i, k)
        c.start()
        outgoing.append(c)
        R[i].G[shard(k)] = value(p.core).astype(BF16)

    def meet(i, k):
        t = shard(k)
        G, C = R[i].G, m.land[i][0]
        core_copy(None, i, k).wait_recv()

        def add(j):
            r = ds(j, 96)
            G[t, r] = G[t, r] + C[t, r]

        loop(R[i].half // 96, add)
        R[i].one(k)

    def hidden(t, slot):
        def rows(i):
            r = ds(i, 256)
            f = dot(H2[r], W1[t], 1, 0) + IB[t]
            th = jnp.tanh(0.7978845608028654 * (f + 0.044715 * f * f * f))
            a = (0.5 * f * (1.0 + th)).astype(BF16)
            A[slot, r] = a
            slope = 0.5 * (1.0 + th) + 0.5 * f * (1.0 - th * th) * (
                0.7978845608028654 * (1.0 + 3.0 * 0.044715 * f * f)
            )
            df = (dot(CT[r], W2[t], 1, 1) * slope).astype(BF16)
            DF[slot, r] = df
            m.DIB[t] += fold(df.astype(F32))
            ACC_O[r] += dot(a, W2[t], 1, 0)
            ACC_E[r] += dot(df, W1[t], 1, 1)

        loop(2, rows)

    def hand_hidden(k, slot):
        hand(0, k, lambda core: dot(A[slot], CT[:, lanes(core)], 0, 0))
        hand(1, k, lambda core: dot(H2[...], DF[slot, :, lanes(core)], 0, 0))

    m.DIB[...] = jnp.zeros_like(m.DIB)
    order = K + [0]
    loads[5].wait()
    for g in both:
        g.diag(K[0])
    hidden(t0, 0)
    for g in both:
        g.xy(K[1])
    for n, k in enumerate(K):
        g1.done(k)
        g2.done(k)
        hidden(shard(k), 1)
        for g in both:
            if n == 0:
                g.xy(K[2])
                g.diag(K[1])
            if n == 1:
                g.diag(K[2])
        if n:
            meet(1, K[n - 1])
        if n < 2:
            hand_hidden(k, 1)
            meet(0, k)
    for g in both:
        g.drain(True)
    RES, GG = W1.at[2, pl.ds(0, 512)], W1.at[3, pl.ds(0, 512)]

    def dne(h):
        start = pl.multiple_of(lax.rem(h, 9) * 80, 16)
        return W2.at[h // 9, pl.ds(start, 80), pl.ds(0, 512)]

    def du_of(h):
        return W1.at[h // 6, ds(lax.rem(h, 6), 128), pl.ds(0, 512)]

    def dv_of(h):
        return W2.at[2, ds(h, 64), pl.ds(0, 512)]

    def back2(i):
        r = ds(i, 128)
        n, s = layer_rows(X2[r])
        e = ACC_E[r]
        g = CT[r].astype(F32)
        dx = g + layer_back(e, n, s, VEC[3:4])
        SUMS[3] += fold(e * n)
        SUMS[4] += fold(e)
        SUMS[2] += fold(dx)
        SUMS[5] += fold(g)
        X2[r] = dx
        GG[r] = dx.astype(BF16)

    loop(4, back2)
    DX = X2
    first_row = lax.broadcasted_iota(jnp.int32, (16, 512), 0) == 0

    scan.drain()
    scan = Scan(p, True, m.TOT, m.UP, m.DOWN, m.got_b, m.scan_b)

    def states_back(t):
        value = dot(WA[t, 576:768], GG[...], 1, 1).astype(BF16).astype(F32)
        for i in range(3):
            h = 3 * t + i
            do = value[64 * i : 64 * i + 64]
            r = RD[h]
            o = OT[ds(h, 64)].astype(F32)
            ref = dne(h)
            ref[0:64] = (do * r).astype(BF16)
            dden = -jnp.sum(do * o, axis=0, keepdims=True) * r
            ref[64:80] = jnp.where(first_row, dden, 0.0).astype(BF16)
            s0 = dot(ref[:, 0:256], PH[0, h, :, 0:256], 1, 1)
            s1 = dot(ref[:, 256:512], PH[0, h, :, 256:512], 1, 1)
            SL[h] = s1
            m.TOT[h] = (s0 + s1).astype(BF16)

    def give(t):
        states_back(t)
        scan.begin(t)

    loop(4, give)
    hand(0, order[2], lambda core: dot(A[1], CT[:, lanes(core)], 0, 0))
    for g in range(4):
        scan.pair(g)
    for i in range(2):
        R[i].two(order[0])
    hand(1, order[2], lambda core: dot(H2[...], DF[1, :, lanes(core)], 0, 0))
    for i in range(2):
        R[i].two(order[1])

    def feature_back(i, h, delta):
        delta = delta.astype(BF16).astype(F32)
        up, down = PH[i, h, 0:64].astype(F32), PH[i, h, 64:128].astype(F32)
        d, dd = delta[0:64], delta[64:128]
        du = up * (d - jnp.sum(up * d, axis=0, keepdims=True)) - down * (
            dd - jnp.sum(down * dd, axis=0, keepdims=True)
        )
        du_of(h)[64 * i : 64 * i + 64] = du.astype(BF16)

    def query_back(h):
        parts = []
        ref, dv = dne(h), dv_of(h)
        for j in range(2):
            c = slice(256 * j, 256 * j + 256)
            value = ref[:, c]
            dv[:, c] = dot(ref[0:64, c], AT[h, j], 1, 1).astype(BF16)
            da = dot(VX[h, :, c], value, 0, 0)
            da = jnp.where(causal, da, 0.0).astype(BF16)
            AT[h, j] = da
            parts.append(dot(PH[1, h, :, c], da, 1, 0) + dot(PX[h, j], value, 0, 0))
        feature_back(0, h, jnp.concatenate(parts, axis=1))

    ones8 = jnp.ones((8, 512), BF16)
    left = lax.broadcasted_iota(jnp.int32, (64, 128), 1) < 64
    GS[:, 192:256] = jnp.zeros((4, 64, 128), F32)

    def bias_row(t, j, i):
        ref = MIX[t, ds(3 * j + i, 64)]
        GS[t, pl.ds(192 + 3 * j + i, 1), 0:64] = dot(ones8, ref, 1, 1)[0:1]

    def early(k):
        t = shard(k)
        def one(i):
            h = t * 3 + i
            rows = ds(i, 64)
            du = du_of(h)[0:64]
            GS[t, rows, 0:64] = dot(MIX[t, rows], du, 1, 1)
            MIX[t, rows] = dot(FW[0, h], du, 1, 0).astype(BF16)
            bias_row(t, 0, i)

        loop(3, one)

        def value(core):
            both = [
                dot(MIX[t, 0:192], H1[:, lanes(core)], 1, 0),
                dot(OT[ds(t, 192)], GG[:, lanes(core)], 1, 0),
            ]
            return jnp.concatenate(both, axis=0)

        hand(2, k, value)

    def queries(g):
        loop(3, lambda i: query_back(3 * g + i))

    def ask(g):
        queries(g)
        scan.chain(g)

    loop(2, ask)
    for i in range(2):
        meet(i, order[2])
    loop(2, lambda g: ask(g + 2))
    hand_hidden(0, 0)
    for g in range(4):
        scan.relay(g)
    for i in range(2):
        R[i].three(order[0])
        R[i].three(order[1])
    RES[...] = ACC_O[...].astype(BF16)
    res_copy = pltpu.make_async_copy(RES, m.result, ld.at[6])
    res_copy.start()
    early(order[0])
    for i in range(2):
        meet(i, order[3])
    early(order[1])
    meet(2, order[0])
    for i in range(2):
        R[i].two(order[2])
    early(order[2])
    meet(2, order[1])
    early(order[3])
    meet(2, order[2])
    for i in range(2):
        R[i].two(order[3])
    enter(1)

    def key_back(t, i):
        h = t * 3 + i
        parts, values = [], []
        for j in range(2):
            c = slice(256 * j, 256 * j + 256)
            q = PX[h, j]
            parts.append(dot(PH[0, h, :, c], AT[h, j], 1, 1) + dot(q, VX[h, :, c], 0, 0))
            values.append(dot(q[0:64], PH[1, h, :, c], 1, 0))
        feature_back(1, h, jnp.concatenate(parts, axis=1))
        dv = jnp.concatenate(values, axis=1) + dv_of(h)[...].astype(F32)
        MIX[t, ds(6 + i, 64)] = dv.astype(BF16)
        du = du_of(h)
        rows = ds(3 + i, 64)
        ref = ds(i, 64)
        GS[t, ref] = jnp.where(left, GS[t, ref], dot(MIX[t, rows], du[...], 1, 1))
        GS[t, pl.ds(201 + i, 1)] = dot(ones8, du[...], 1, 1)[0:1]
        MIX[t, rows] = dot(FW[1, h], du[64:128], 1, 0).astype(BF16)
        bias_row(t, 1, i)
        bias_row(t, 2, i)

    for n, k in enumerate(order):
        t = shard(k)
        loop(3, lambda i: key_back(t, i))
        hand(3, k, lambda core: dot(MIX[t, 192:576], H1[:, lanes(core)], 1, 0))
        if n == 0:
            for i in range(2):
                R[i].three(order[2])
            meet(2, order[3])
            R[2].two(order[0])
            R[2].two(order[1])
        else:
            meet(3, order[n - 1])
        if n == 1:
            R[0].three(order[3])
            R[1].three(order[3])
            R[2].two(order[2])
        if n == 2:
            R[2].two(order[3])
            R[2].three(order[0])
            R[2].three(order[1])
            R[3].two(order[0])
            R[0].final()
            R[1].final()
        if n == 3:
            R[2].three(order[2])
            R[2].three(order[3])
            R[3].two(order[1])
            R[3].three(order[0])

    def back1(i):
        r = ds(i, 256)
        e = dot(MIX[0, :, r], WA[0, 0:576], 0, 0)
        for t in range(1, 4):
            e = e + dot(MIX[t, :, r], WA[t, 0:576], 0, 0)
        n, s = layer_rows(X[r].astype(F32))
        SUMS[0] += fold(e * n)
        SUMS[1] += fold(e)
        ACC_E[r] = DX[r] + layer_back(e, n, s, VEC[0:1])

    back1(0)
    meet(3, order[3])
    R[0].spread()
    R[3].two(order[2])
    R[1].spread()
    R[3].three(order[1])
    back1(1)
    R[3].two(order[3])
    R[0].corner()
    tok_copy = pltpu.make_async_copy(ACC_E, m.tokens_gradient, ld.at[7])
    tok_copy.start()
    for k in range(6):
        row = jnp.sum(SUMS[k], axis=0, keepdims=True)
        for i in range(6):
            for t in range(4):
                GS[t, 216 + 6 * k + i : 217 + 6 * k + i] = row[:, 128 * i : 128 * i + 128]
    for t in range(4):
        row = jnp.sum(m.DIB[t], axis=0, keepdims=True)
        for i in range(6):
            GS[t, 208 + i : 209 + i] = row[:, 128 * i : 128 * i + 128]
    GB = W2.at[3, pl.ds(0, 256), pl.ds(0, 512)]
    for t in range(4):
        GB[:, 128 * t : 128 * t + 128] = GS[t].astype(BF16)
    tiny = Small(p, GB, GS, m.plane, m.line, m.mid, m.outs[4], m.small_sems, m.small_send, m.own.at[4])
    tiny.begin()
    R[2].final()
    R[3].three(order[2])
    R[1].corner()
    R[3].three(order[3])
    tiny.across()
    R[2].spread()
    R[3].final()
    tiny.final()
    R[2].corner()
    R[3].spread()
    R[3].corner()
    for r in R:
        r.end()
    tiny.end()
    scan.drain()
    for c in outgoing[-2:]:
        c.wait_send()
    gs.drain(False)
    gw.drain(False)
    go.drain(False)
    res_copy.wait()
    tok_copy.wait()


PACKS = ((768, 768), (768, 768), (384, 768), (384, 768))


def landing(rows):
    q, r = rows // 4, rows // 8
    shapes = ((4, rows), (4, 2, r), (4, 2, r), (4, r), (4, r))
    return [pltpu.VMEM((*shape, 384), BF16) for shape in shapes]


def block_call(*args):
    rows, width = args[0].shape
    flat = pltpu.VMEM((rows, width), BF16)
    wide = pltpu.VMEM((rows, width), F32)
    weights = pltpu.VMEM((4, 768, 768), BF16)
    state = pltpu.VMEM((12, 80, 128), BF16)
    dma = pltpu.SemaphoreType.DMA
    scratch = dict(
        X=flat,
        CT=flat,
        S=pltpu.VMEM((4, 256, 128), BF16),
        WA=weights,
        W1=weights,
        W2=weights,
        VEC=pltpu.VMEM((8, 768), F32),
        VECI=pltpu.VMEM((7, 8, 128), BF16),
        FWI=pltpu.VMEM((2, 3, HD, HD), BF16),
        MBI=pltpu.VMEM((3, 192), BF16),
        FBI=pltpu.VMEM((3, 2, HD), BF16),
        H1=flat,
        H2=flat,
        X2=wide,
        ACC_O=wide,
        ACC_E=wide,
        MIX=pltpu.VMEM((4, 576, rows), BF16),
        PH=pltpu.VMEM((2, 12, 128, rows), BF16),
        VX=pltpu.VMEM((12, 80, rows), BF16),
        AT=pltpu.VMEM((12, 2, 256, 256), BF16),
        PX=pltpu.VMEM((12, 2, 80, 128), BF16),
        SL=pltpu.VMEM((12, 80, 128), F32),
        OT=pltpu.VMEM((768, rows), BF16),
        RD=pltpu.VMEM((12, 1, rows), F32),
        A=pltpu.VMEM((2, rows, width), BF16),
        DF=pltpu.VMEM((2, rows, width), BF16),
        GS=pltpu.VMEM((4, 256, 128), F32),
        FW=pltpu.VMEM((2, 12, 64, 64), BF16),
        BC=pltpu.VMEM((128, 16), F32),
        IB=pltpu.VMEM((4, 1, 768), F32),
        SUMS=pltpu.VMEM((6, 8, 768), F32),
        DIB=pltpu.VMEM((4, 8, 768), F32),
        TOT=state,
        UP=state,
        DOWN=state,
        got_f=pltpu.VMEM((4, 12, 80, 128), BF16),
        got_b=pltpu.VMEM((4, 12, 80, 128), BF16),
        plane=pltpu.VMEM((7, 32, 512), BF16),
        line=pltpu.VMEM((3, 32, 128), BF16),
        mid=pltpu.VMEM((5, 32, 128), BF16),
        STAGE=pltpu.VMEM((2, 768, 384), BF16),
        G=[pltpu.VMEM((4, n, 384), BF16) for n, _ in PACKS],
        Z=[pltpu.VMEM((3, n // 4, 384), BF16) for n, _ in PACKS],
        land=[landing(n) for n, _ in PACKS],
        ld=dma((18,)),
        own=dma((5,)),
        r_core=dma((2, 4, 4)),
        gather_sems={k: dma((5, 3)) for k in GATHER_SEMS},
        gather_send=dma((5, 3)),
        reduce_sems={k: dma((4, n)) for k, n in zip(SEMS, (4, 4, 4, 4, 3, 5))},
        reduce_send=dma((4, 4)),
        small_sems=dma((17,)),
        small_send=dma((3,)),
        scan_f=dma((2, 16)),
        scan_b=dma((2, 16)),
    )
    leaves, tree = jax.tree.flatten(scratch, is_leaf=lambda v: not isinstance(v, (dict, list)))
    results = [
        jax.ShapeDtypeStruct((rows, width), BF16),
        jax.ShapeDtypeStruct((rows, width), F32),
        *[jax.ShapeDtypeStruct(pack, BF16) for pack in PACKS],
        jax.ShapeDtypeStruct((256, 128), BF16),
    ]

    def body(x, g, wm, wo, w1, w2, fw, mb, fb, *rest):
        vectors, (result, tokens_gradient), rest = rest[:7], rest[7:9], rest[9:]
        given = dict(
            x=x, g=g, wm=wm, wo=wo, w1=w1, w2=w2, fw=fw, mb=mb, fb=fb, vectors=vectors
        )
        block_kernel(
            SimpleNamespace(
                **given,
                result=result,
                tokens_gradient=tokens_gradient,
                outs=rest[:5],
                **jax.tree.unflatten(tree, rest[5:]),
            )
        )

    anywhere = pl.BlockSpec(memory_space=pl.ANY)
    return pl.pallas_call(
        body,
        out_shape=results,
        in_specs=[anywhere] * len(args),
        out_specs=[anywhere] * len(results),
        scratch_shapes=leaves,
        compiler_params=pltpu.CompilerParams(
            collective_id=0, has_side_effects=True, vmem_limit_bytes=67043328
        ),
        name="block",
    )(*args)


def finish_kernel(
    res, tok, outer, inner, q, o, k, v, small,
    res_o, tok_o, outer_o, inner_o, mixer_o, output_o, feature_o, mixer_bias_o, feature_bias_o, *vec_o,
):
    res_o[...] = res[...]
    tok_o[...] = tok[...]
    outer_o[...] = outer[...].astype(F32)
    inner_o[...] = inner[...].astype(F32)
    for i, ref in enumerate((q, k, v)):
        mixer_o[i] = ref[...].astype(F32)
    output_o[...] = o[...].astype(F32)

    @pl.when(pl.program_id(0) == 0)
    def _():
        rows = small[192:256].astype(F32)
        for h in range(3):
            w = small[64 * h : 64 * h + 64].astype(F32)
            feature_o[0, h] = w[:, :64]
            feature_o[1, h] = w[:, 64:]
            pair = rows[9 + h : 10 + h]
            feature_bias_o[h] = jnp.concatenate([pair[:, :64], pair[:, 64:]], axis=0)
            parts = [rows[3 * h + i : 3 * h + i + 1, :64] for i in range(3)]
            mixer_bias_o[h : h + 1] = jnp.concatenate(parts, axis=1)
        for i in range(6):
            vec_o[i][...] = rows[24 + 6 * i : 30 + 6 * i]
        vec_o[6][...] = rows[16:22]


def finish_call(res, tok, outer, inner, early, late, small):
    rows, width = res.shape
    steps = 4

    def spec(n, shift=0):
        return pl.BlockSpec((n, width), lambda i: (i + shift, 0))

    def whole(*shape):
        return pl.BlockSpec(shape, lambda i: (0,) * len(shape))

    def out(*shape):
        return jax.ShapeDtypeStruct(shape, F32)

    vectors = [(6, 128)] * 7
    return pl.pallas_call(
        finish_kernel,
        grid=(steps,),
        in_specs=[
            spec(rows // steps),
            spec(rows // steps),
            spec(768 // steps),
            spec(768 // steps),
            spec(192 // steps),
            spec(192 // steps, steps),
            spec(192 // steps),
            spec(192 // steps, steps),
            whole(256, 128),
        ],
        out_specs=[
            spec(rows // steps),
            spec(rows // steps),
            spec(768 // steps),
            spec(768 // steps),
            pl.BlockSpec((3, 192 // steps, width), lambda i: (0, i, 0)),
            spec(192 // steps),
            whole(2, 3, HD, HD),
            whole(3, 192),
            whole(3, 2, HD),
            *[whole(*v) for v in vectors],
        ],
        out_shape=[
            jax.ShapeDtypeStruct((rows, width), BF16),
            out(rows, width),
            out(768, width),
            out(768, width),
            out(3, 192, width),
            out(192, width),
            out(2, 3, HD, HD),
            out(3, 192),
            out(3, 2, HD),
            *[out(*v) for v in vectors],
        ],
        name="finish",
    )(res, tok, outer, inner, early, early, late, late, small)


def shards(
    fast,
    tokens,
    first_gain,
    first_bias,
    mixer_weight,
    mixer_bias,
    feature_weight,
    feature_bias,
    output_weight,
    output_bias,
    second_gain,
    second_bias,
    inner_weight,
    inner_bias,
    outer_weight,
    outer_bias,
    block_owner,
    cotangent,
):
    rows, width = tokens.shape
    n_tp, n_ctx = lax.axis_size("tp"), lax.axis_size("ctx")
    n_plane = lax.axis_size("dp") * n_ctx
    plane = lax.axis_index("dp") * n_ctx + lax.axis_index("ctx")
    heads_here = mixer_weight.shape[2] // HD
    heads = heads_here * n_tp
    mine = lax.axis_index("ctx") * n_tp + lax.axis_index("tp")

    mixer_t = mixer_weight.transpose(1, 2, 0).reshape(-1, width)
    if fast:
        vectors = (
            first_gain, first_bias, output_bias, second_gain, second_bias, outer_bias, inner_bias
        )
        raw = block_call(
            tokens,
            cotangent,
            mixer_t,
            output_weight,
            inner_weight,
            outer_weight,
            feature_weight,
            mixer_bias,
            feature_bias.transpose(1, 0, 2),
            *[v.reshape(6, 128) for v in vectors],
        )
        (
            result, tokens_gradient, d_outer, d_inner, d_mixer, d_output,
            d_feature, d_mixer_bias, d_feature_bias, *shared
        ) = finish_call(*raw)
        shared = [v.reshape(width) for v in shared]
        return (
            result,
            tokens_gradient,
            shared[0],
            shared[1],
            d_mixer.transpose(2, 0, 1),
            d_mixer_bias,
            d_feature,
            d_feature_bias.transpose(1, 0, 2),
            d_output,
            shared[2],
            shared[3],
            shared[4],
            d_inner,
            shared[6],
            d_outer,
            shared[5],
        )
    sizes = [w.shape[0] for w in (mixer_t, output_weight, inner_weight, outer_weight)]
    pack = jnp.concatenate([mixer_t, output_weight, inner_weight, outer_weight], axis=0)
    part = pack.shape[0] // n_plane
    piece = lax.dynamic_slice_in_dim(pack, plane * part, part, 0)
    full = lax.all_gather(piece, ALL, axis=0, tiled=True)
    full = full.reshape(n_plane, n_tp, part, width).transpose(1, 0, 2, 3).reshape(n_tp, -1, width)
    cuts = [0]
    for s in sizes:
        cuts.append(cuts[-1] + s)
    mixer_all, output_all, inner_all, outer_all = [
        full[:, a:b] for a, b in zip(cuts[:-1], cuts[1:])
    ]
    small = jnp.concatenate(
        [feature_weight.reshape(-1), mixer_bias.reshape(-1), feature_bias.reshape(-1), inner_bias]
    )
    small = lax.all_gather(small, "tp")
    cut = feature_weight.size
    feature_all = (
        small[:, :cut].reshape(n_tp, 2, heads_here, HD, HD).transpose(1, 0, 2, 3, 4)
    ).reshape(2, heads, HD, HD)
    mixer_bias_all = small[:, cut : cut + mixer_bias.size].astype(F32).reshape(n_tp, -1)
    cut += mixer_bias.size
    feature_bias_all = (
        small[:, cut : cut + feature_bias.size]
        .astype(F32)
        .reshape(n_tp, 2, heads_here, HD)
        .transpose(1, 0, 2, 3)
        .reshape(2, heads, HD)
    )
    cut += feature_bias.size
    inner_bias_all = small[:, cut:].astype(F32)

    x = tokens.astype(F32)
    gain1, gain2 = first_gain.astype(F32), second_gain.astype(F32)
    h1, n1, r1 = layer_norm(x, gain1, first_bias.astype(F32))
    h1 = h1.astype(BF16)
    mix = ein("td,skd->tsk", h1, mixer_all) + mixer_bias_all
    mix = mix.astype(BF16).reshape(rows, n_tp, 3, heads_here, HD).transpose(2, 0, 1, 3, 4)
    mix = mix.reshape(3, rows, heads, HD)
    q, k, v = mix[0], mix[1], mix[2]
    q_up, q_down, phi_q = feature_map(q, feature_all[0], feature_bias_all[0])
    k_up, k_down, phi_k = feature_map(k, feature_all[1], feature_bias_all[1])

    chunk = min(CHUNK, rows)
    chunks = rows // chunk
    pq = phi_q.reshape(chunks, chunk, heads, 2 * HD)
    pk = phi_k.reshape(chunks, chunk, heads, 2 * HD)
    vc = v.reshape(chunks, chunk, heads, HD)
    causal = jnp.arange(chunk)[:, None] >= jnp.arange(chunk)[None, :]
    state = ein("jthe,jthf->jhef", vc, pk)
    norm = jnp.sum(pk.astype(F32), axis=1)
    both = jnp.concatenate([state, norm[:, :, None]], axis=2)
    owners = block_owner[0].reshape(n_tp, -1)[:, 0]
    order = jnp.arange(n_ctx * n_tp)
    same = jnp.tile(owners, n_ctx) == jnp.tile(owners, n_ctx)[mine]

    def prefix(totals, reach):
        everything = lax.all_gather(totals.astype(BF16), ("ctx", "tp")).astype(F32)
        return jnp.einsum("s,shef->hef", reach.astype(F32), everything, precision="highest")

    def running(blocks, start, reverse):
        out = [None] * chunks
        acc = start
        for j in reversed(range(chunks)) if reverse else range(chunks):
            out[j] = acc
            acc = acc + blocks[j]
        return jnp.stack(out)

    before = running(both, prefix(jnp.sum(both, axis=0), same & (order < mine)), False)
    before = before.astype(BF16)
    scores = ein("jthf,jshf->jhts", pq, pk)
    a_low = jnp.where(causal, scores, 0.0).astype(BF16)
    v_one = jnp.concatenate([vc, jnp.ones(vc.shape[:-1] + (1,), BF16)], axis=-1)
    num = ein("jthf,jhef->jthe", pq, before) + ein("jhts,jshe->jthe", a_low, v_one)
    num, den = num[..., :HD], num[..., HD:]
    o = num / den
    o_low = o.astype(BF16)
    o_flat = o_low.reshape(rows, n_tp, heads_here * HD)
    x2 = x + ein("tsk,skd->td", o_flat, output_all) + output_bias.astype(F32)
    h2, n2, r2 = layer_norm(x2, gain2, second_bias.astype(F32))
    h2 = h2.astype(BF16)
    f = ein("td,sdf->tsf", h2, inner_all) + inner_bias_all
    a, slope = gelu_parts(f)
    a = a.astype(BF16)
    result = (x2 + ein("tsf,sfd->td", a, outer_all) + outer_bias.astype(F32)).astype(BF16)

    g = cotangent.astype(F32)
    d_outer = ein("tsf,td->sfd", a, cotangent)
    df = (ein("td,sfd->tsf", cotangent, outer_all) * slope).astype(BF16)
    d_inner_bias = jnp.sum(df.astype(F32), axis=0)
    d_inner = ein("td,tsf->sdf", h2, df)
    e2 = ein("tsf,sdf->td", df, inner_all)
    back2, d_gain2, d_bias2 = layer_norm_back(e2, n2, r2, gain2)
    dx2 = g + back2
    big_g = dx2.astype(BF16)
    d_output = ein("tsk,td->skd", o_flat, big_g)
    do = ein("td,skd->tsk", big_g, output_all).astype(BF16).astype(F32)
    do = do.reshape(chunks, chunk, heads, HD)
    dnum = do / den
    dden = -jnp.sum(do * o, axis=-1, keepdims=True) / den
    dne = jnp.concatenate([dnum, dden], axis=-1).astype(BF16)
    da = ein("jthe,jshe->jhts", dne, v_one)
    da_low = jnp.where(causal, da, 0.0).astype(BF16)
    d_both = ein("jthe,jthf->jhef", dne, pq)
    after = running(d_both, prefix(jnp.sum(d_both, axis=0), same & (order > mine)), True)
    after = after.astype(BF16)
    dphi_q = ein("jhts,jshf->jthf", da_low, pk) + ein("jthe,jhef->jthf", dne, before)
    dphi_k = ein("jhts,jthf->jshf", da_low, pq) + ein("jthe,jhef->jthf", v_one, after)
    dv = ein("jhts,jthe->jshe", a_low, dne[..., :HD]) + ein("jthf,jhef->jthe", pk, after[:, :, :HD])
    dphi_q = dphi_q.reshape(rows, heads, 2 * HD)
    dphi_k = dphi_k.reshape(rows, heads, 2 * HD)
    dq, d_fq, d_fbq = feature_back(dphi_q, q_up, q_down, q, feature_all[0])
    dk, d_fk, d_fbk = feature_back(dphi_k, k_up, k_down, k, feature_all[1])
    dmix = jnp.stack([dq, dk, dv.reshape(rows, heads, HD)], axis=1).astype(BF16)
    dmix = dmix.reshape(rows, 3, n_tp, heads_here * HD).transpose(0, 2, 1, 3)
    dmix = dmix.reshape(rows, n_tp, -1)
    d_mixer_bias = jnp.sum(dmix.astype(F32), axis=0)
    d_mixer = ein("tsk,td->skd", dmix, h1)
    e1 = ein("tsk,skd->td", dmix, mixer_all)
    back1, d_gain1, d_bias1 = layer_norm_back(e1, n1, r1, gain1)
    tokens_gradient = dx2 + back1

    big = jnp.concatenate([d_mixer, d_output, d_inner, d_outer], axis=1).astype(BF16)
    big = big.reshape(n_tp, n_plane, part, width).transpose(1, 0, 2, 3).reshape(-1, width)
    big = lax.psum_scatter(big, ("dp", "ctx"), scatter_dimension=0, tiled=True)
    big = lax.psum_scatter(big, "tp", scatter_dimension=0, tiled=True)
    big = lax.all_gather(big, ("dp", "ctx"), axis=0, tiled=True).astype(F32)
    d_mixer, d_output, d_inner, d_outer = [big[a:b] for a, b in zip(cuts[:-1], cuts[1:])]
    d_mixer = d_mixer.reshape(3, heads_here * HD, width).transpose(2, 0, 1)
    per_tp = jnp.concatenate(
        [
            jnp.stack([d_fq, d_fk]).reshape(2, n_tp, -1).transpose(1, 0, 2).reshape(n_tp, -1),
            d_mixer_bias,
            jnp.stack([d_fbq, d_fbk]).reshape(2, n_tp, -1).transpose(1, 0, 2).reshape(n_tp, -1),
            d_inner_bias,
        ],
        axis=1,
    )
    shared = jnp.stack(
        [d_gain1, d_bias1, jnp.sum(dx2, axis=0), d_gain2, d_bias2, jnp.sum(g, axis=0)]
    )
    total = lax.psum(jnp.concatenate([per_tp.reshape(-1), shared.reshape(-1)]), ALL)
    shared = total[per_tp.size :].reshape(6, width)
    own = lax.dynamic_slice_in_dim(
        total[: per_tp.size].reshape(n_tp, -1), lax.axis_index("tp"), 1, 0
    )[0]
    cut = feature_weight.size
    d_feature = own[:cut].reshape(feature_weight.shape)
    d_mixer_bias = own[cut : cut + mixer_bias.size].reshape(mixer_bias.shape)
    cut += mixer_bias.size
    d_feature_bias = own[cut : cut + feature_bias.size].reshape(feature_bias.shape)
    d_inner_bias = own[cut + feature_bias.size :]
    return (
        result,
        tokens_gradient,
        shared[0],
        shared[1],
        d_mixer,
        d_mixer_bias,
        d_feature,
        d_feature_bias,
        d_output,
        shared[2],
        shared[3],
        shared[4],
        d_inner,
        d_inner_bias,
        d_outer,
        shared[5],
    )


def solution(mesh):
    in_specs = (
        P(("dp", "ctx", "tp"), None),
        P(),
        P(),
        P(None, None, "tp"),
        P(None, "tp"),
        P(None, "tp", None, None),
        P(None, "tp", None),
        P("tp", None),
        P(),
        P(),
        P(),
        P(None, "tp"),
        P("tp"),
        P("tp", None),
        P(),
        P("dp", None),
        P(("dp", "ctx", "tp"), None),
    )
    out_specs = (
        P(("dp", "ctx", "tp"), None),
        P(("dp", "ctx", "tp"), None),
        P(),
        P(),
        P(None, None, "tp"),
        P(None, "tp"),
        P(None, "tp", None, None),
        P(None, "tp", None),
        P("tp", None),
        P(),
        P(),
        P(),
        P(None, "tp"),
        P("tp"),
        P("tp", None),
        P(),
    )
    fast = (mesh.shape["dp"], mesh.shape["ctx"], mesh.shape["tp"]) == (2, 4, 4)
    return jax.shard_map(functools.partial(shards, fast), mesh=mesh, in_specs=in_specs, out_specs=out_specs, check_vma=False)
```

```python
import functools
from types import SimpleNamespace

import jax
import jax.numpy as jnp
from jax import lax
from jax.experimental import pallas as pl
from jax.experimental.pallas import tpu as pltpu
from jax.sharding import PartitionSpec as P

MESH = pl.DeviceIdType.MESH

HD = 64
BLOCK = 64
CHUNK = 256
EPSILON = 1e-05
F32 = jnp.float32
BF16 = jnp.bfloat16
ALL = ("dp", "ctx", "tp")


def ein(spec, a, b):
    return jnp.einsum(spec, a, b, preferred_element_type=F32)


def layer_norm(v, gain, offset):
    c = v - jnp.mean(v, axis=-1, keepdims=True)
    r = lax.rsqrt(jnp.mean(c * c, axis=-1, keepdims=True) + EPSILON)
    n = c * r
    return n * gain + offset, n, r


def layer_norm_back(e, n, r, gain):
    m = e * gain
    back = r * (
        m - jnp.mean(m, axis=-1, keepdims=True) - n * jnp.mean(m * n, axis=-1, keepdims=True)
    )
    return back, jnp.sum(e * n, axis=0), jnp.sum(e, axis=0)


def gelu_parts(s):
    t = jnp.tanh(0.7978845608028654 * (s + 0.044715 * s * s * s))
    slope = 0.7978845608028654 * (1.0 + 3.0 * 0.044715 * s * s)
    return 0.5 * s * (1.0 + t), 0.5 * (1.0 + t) + 0.5 * s * (1.0 - t * t) * slope


def feature_map(q, weight, offset):
    u = ein("thd,hde->the", q, weight) + offset
    up, down = jax.nn.softmax(u, axis=-1), jax.nn.softmax(-u, axis=-1)
    return up, down, jnp.concatenate([up, down], axis=-1).astype(BF16)


def feature_back(delta, up, down, q, weight):
    d, dd = delta[..., :HD], delta[..., HD:]
    du = up * (d - jnp.sum(up * d, axis=-1, keepdims=True)) - down * (
        dd - jnp.sum(down * dd, axis=-1, keepdims=True)
    )
    low = du.astype(BF16)
    return ein("the,hde->thd", low, weight), ein("thd,the->hde", q, low), jnp.sum(du, axis=0)


HD = 64
BLOCK = 64
CHUNK = 256
EPSILON = 1e-05
F32 = jnp.float32
BF16 = jnp.bfloat16
ALL = ("dp", "ctx", "tp")


def ein(spec, a, b):
    return jnp.einsum(spec, a, b, preferred_element_type=F32)


def layer_norm(v, gain, offset):
    c = v - jnp.mean(v, axis=-1, keepdims=True)
    r = lax.rsqrt(jnp.mean(c * c, axis=-1, keepdims=True) + EPSILON)
    n = c * r
    return n * gain + offset, n, r


def layer_norm_back(e, n, r, gain):
    m = e * gain
    back = r * (
        m - jnp.mean(m, axis=-1, keepdims=True) - n * jnp.mean(m * n, axis=-1, keepdims=True)
    )
    return back, jnp.sum(e * n, axis=0), jnp.sum(e, axis=0)


def gelu_parts(s):
    t = jnp.tanh(0.7978845608028654 * (s + 0.044715 * s * s * s))
    slope = 0.7978845608028654 * (1.0 + 3.0 * 0.044715 * s * s)
    return 0.5 * s * (1.0 + t), 0.5 * (1.0 + t) + 0.5 * s * (1.0 - t * t) * slope


def feature_map(q, weight, offset):
    u = ein("thd,hde->the", q, weight) + offset
    up, down = jax.nn.softmax(u, axis=-1), jax.nn.softmax(-u, axis=-1)
    return up, down, jnp.concatenate([up, down], axis=-1).astype(BF16)


def feature_back(delta, up, down, q, weight):
    d, dd = delta[..., :HD], delta[..., HD:]
    du = up * (d - jnp.sum(up * d, axis=-1, keepdims=True)) - down * (
        dd - jnp.sum(down * dd, axis=-1, keepdims=True)
    )
    low = du.astype(BF16)
    return ein("the,hde->thd", low, weight), ein("thd,the->hde", q, low), jnp.sum(du, axis=0)


def place():
    d, c, t = lax.axis_index("dp"), lax.axis_index("ctx"), lax.axis_index("tp")
    y, core = c // 2, lax.rem(c, 2)
    return SimpleNamespace(d=d, c=c, t=t, y=y, core=core, q=d * 2 + y,
        x_nb=(1 - d, c, t), y_nb=(d, (1 - y) * 2 + core, t), core_nb=(d, y * 2 + 1 - core, t),
        qx=(1 - d) * 2 + y, qy=d * 2 + 1 - y, qd=(1 - d) * 2 + 1 - y)

def plane_peer(p, r):
    d = 1 - p.d if r & 4 else p.d
    y = 1 - p.y if r & 2 else p.y
    core = 1 - p.core if r & 1 else p.core
    return (d, y * 2 + core, p.t), d * 4 + y * 2 + core


def greet(p):
    bar = pltpu.get_barrier_semaphore()
    peers = [plane_peer(p, r)[0] for r in range(1, 8)]
    peers += [(p.d, p.c, lax.rem(p.t + k, 4)) for k in (1, 2, 3)]
    for peer in peers:
        pl.semaphore_signal(bar, inc=1, device_id=peer, device_id_type=MESH)


def met(p):
    pl.semaphore_wait(pltpu.get_barrier_semaphore(), 10)


def nearest(t):
    return [
        jnp.where(t < 2, 1, 3),
        jnp.where(t == 0, 2, jnp.where(t == 1, 3, jnp.where(t == 2, 1, 2))),
        jnp.where(t == 0, 3, jnp.where(t == 3, 1, 2)),
    ]


class Gather:
    def __init__(self, p, buf, sems, send, index, base=0, rows=None):
        self.p, self.buf, self.sems, self.send, self.i = p, buf, sems, send.at[index], index
        self.base, self.rows = base, rows or buf.shape[1]
        self.wide = buf.shape[2] == 768
        self.piece = self.rows // (4 if self.wide else 8)
        self.lanes = lanes(0) if self.wide else slice(None)

    def at(self, t, q, core, half=None):
        start = q * (self.rows // 4) + (0 if self.wide else core * self.piece)
        size = self.piece
        if half is not None:
            first = (size + 16) // 32 * 16
            start, size = start + half * first, size - first if half else first
        rows = pl.ds(pl.multiple_of(self.base + start, 16), size)
        return self.buf.at[t, rows, lanes(core)] if self.wide else self.buf.at[t, rows]

    def shard(self, k): return lax.rem(self.p.t + k, 4)
    def copy(self, ref, kind, k, peer):
        n = 0 if kind == "z" else 2 if kind == "c" else 1
        recv = self.sems[kind].at[self.i, k - 1]
        return pltpu.make_async_remote_copy(
            ref, ref, self.send.at[n], recv, device_id=peer, device_id_type=MESH
        )

    def go(self, *a):
        self.copy(*a).start()

    def first(self):
        p = self.p
        ref = self.at(p.t, p.q, p.core)
        for k in (1, 2, 3):
            self.go(ref, "z", 4 - k, (p.d, p.c, lax.rem(p.t + k, 4)))

    def first_hop(self):
        p = self.p
        ref = self.at(p.t, p.q, p.core)
        pl.when(p.t < 3)(lambda: self.go(ref, "z", 3, (p.d, p.c, p.t + 1)))
        pl.when(p.t > 0)(lambda: self.go(ref, "z", 1, (p.d, p.c, p.t - 1)))

    def zf(self, k):
        p, t = self.p, self.shard(k)
        ref = self.at(t, p.q, p.core)
        self.copy(ref, "z", k, p.x_nb).wait_recv()
        up = jnp.logical_and(t < p.t, p.t < 3)
        down = jnp.logical_and(t > p.t, p.t > 0)
        pl.when(up)(lambda: self.go(ref, "z", k - 1, (p.d, p.c, p.t + 1)))
        pl.when(down)(lambda: self.go(ref, "z", k + 1, (p.d, p.c, p.t - 1)))

    def spread(self, k):
        p = self.p
        ref = self.at(self.shard(k), p.q, p.core)
        self.go(ref, "x", k, p.x_nb)
        self.go(ref, "y", k, p.y_nb)

    def z(self, k):
        p, t = self.p, self.shard(k)
        ref = self.at(t, p.q, p.core)
        self.copy(ref, "z", k, p.x_nb).wait_recv()
        self.go(ref, "x", k, p.x_nb); self.go(ref, "y", k, p.y_nb)
    def xy(self, k):
        p, t = self.p, self.shard(k)
        self.copy(self.at(t, p.qx, p.core), "x", k, p.x_nb).wait_recv()
        self.go(self.at(t, p.qx, p.core, 0), "fy", k, p.y_nb)
        self.copy(self.at(t, p.qy, p.core), "y", k, p.y_nb).wait_recv()
        self.go(self.at(t, p.qy, p.core, 1), "fx", k, p.x_nb)
    def diag(self, k):
        p, t = self.p, self.shard(k)
        self.copy(self.at(t, p.qd, p.core, 0), "fy", k, p.y_nb).wait_recv()
        self.copy(self.at(t, p.qd, p.core, 1), "fx", k, p.x_nb).wait_recv()
        if self.wide:
            self.go(self.buf.at[t, pl.ds(self.base, self.rows), lanes(p.core)], "c", k, p.core_nb)
        else:
            for q in range(4):
                self.go(self.at(t, q, p.core), "c", k, p.core_nb)

    def done(self, k):
        p, t = self.p, self.shard(k)
        if self.wide:
            ref = self.buf.at[t, pl.ds(self.base, self.rows), lanes(1 - p.core)]
        else:
            ref = self.buf.at[t, pl.ds(0, 4 * self.piece)]
        self.copy(ref, "c", k, p.core_nb).wait_recv()

    def drain(self, hops):
        p, n = self.p, self.piece

        def wait(kind, ref):
            self.copy(ref, kind, 1, p.core_nb).wait_send()

        if hops:
            ends = jnp.logical_or(p.t == 0, p.t == 3)
            pl.when(ends)(lambda: wait("z", self.buf.at[0, pl.ds(0, n // 2)]))
            pl.when(jnp.logical_not(ends))(lambda: wait("z", self.buf.at[0, pl.ds(0, 5 * n // 2)]))
        else:
            wait("z", self.buf.at[0, pl.ds(0, 3 * n), self.lanes])
        wait("x", self.buf.at[pl.ds(0, 3), pl.ds(0, 3 * n), self.lanes])
        wait("c", self.buf.at[pl.ds(0, 3), pl.ds(0, 4 * n), self.lanes])


def lanes(core):
    return pl.ds(pl.multiple_of(core * 384, 128), 384)


class Reduce:
    def __init__(self, p, i, G, X1, Y1, X2, Y2, Z, OUT, sems, send, own):
        self.p, self.i, self.G, self.OUT, self.sems = p, i, G, OUT, sems
        self.X1, self.Y1, self.X2, self.Y2, self.Z = X1, Y1, X2, Y2, Z
        self.half = G.shape[1]; self.qr = self.half // 4; self.hr = self.qr // 2
        self.send = send
        self.own = own
    def t(self, k): return lax.rem(self.p.t + k, 4)
    def rows(self, q, h): return pl.ds(pl.multiple_of(q * self.qr + h * self.hr, 16), self.hr)
    def rdma(self, src, dst, kind, k, peer):
        n = 1 if kind == "z" else 0 if kind != "f" else 3 if k == 4 else 2
        return pltpu.make_async_remote_copy(
            src,
            dst,
            self.send.at[self.i, n],
            self.sems[kind].at[self.i, k],
            device_id=peer,
            device_id_type=MESH,
        )

    def go(self, *a):
        self.rdma(*a).start()

    def got(self, ref, kind, k):
        self.rdma(ref, ref, kind, k, self.p.x_nb).wait_recv()
    def one(self, k):
        p, t = self.p, self.t(k)
        for j in range(2):
            self.go(self.G.at[t, self.rows((1 - p.d) * 2 + j, 0)], self.X1.at[k, j], "x1", k, p.x_nb)
            self.go(self.G.at[t, self.rows(j * 2 + 1 - p.y, 1)], self.Y1.at[k, j], "y1", k, p.y_nb)
    def two(self, k):
        p, t, G = self.p, self.t(k), self.G
        self.got(self.X1.at[k], "x1", k)
        for j in range(2):
            r = self.rows(p.d * 2 + j, 0)
            G[t, r] = G[t, r] + self.X1[k, j]
        self.go(G.at[t, self.rows(p.qy, 0)], self.Y2.at[k], "y2", k, p.y_nb)
        self.got(self.Y1.at[k], "y1", k)
        for j in range(2):
            r = self.rows(j * 2 + p.y, 1)
            G[t, r] = G[t, r] + self.Y1[k, j]
        self.go(G.at[t, self.rows(p.qx, 1)], self.X2.at[k], "x2", k, p.x_nb)
    def three(self, k):
        p, t, G = self.p, self.t(k), self.G
        for h, (kind, R) in enumerate((("y2", self.Y2), ("x2", self.X2))):
            self.got(R.at[k], kind, k)
            r = self.rows(p.q, h)
            G[t, r] = G[t, r] + R[k]
        if not isinstance(k, int):
            whole = pl.ds(pl.multiple_of(p.q * self.qr, 16), self.qr)
            self.go(G.at[t, whole], self.Z.at[3 - k], "z", 3 - k, (p.d, p.c, t))
    def piece(self, q, core, h=None):
        start, size = q * self.qr, self.qr
        if h is not None:
            start, size = start + h * self.hr, self.hr
        return self.OUT.at[pl.ds(pl.multiple_of(start, 16), size), lanes(core)]

    def final(self):
        p = self.p
        whole = pl.ds(pl.multiple_of(p.q * self.qr, 16), self.qr)
        total = self.G[p.t, whole].astype(F32)
        for k in range(3):
            self.got(self.Z.at[k], "z", k)
            total = total + self.Z[k].astype(F32)
        ref = self.piece(p.q, p.core)
        mine = self.G.at[p.t, whole]
        mine[...] = total.astype(BF16)
        self.go(mine, ref, "f", 0, p.x_nb)
        self.go(mine, ref, "f", 1, p.y_nb)
        self.own_copy().start()

    def own_copy(self):
        p = self.p
        whole = pl.ds(pl.multiple_of(p.q * self.qr, 16), self.qr)
        return pltpu.make_async_copy(
            self.G.at[p.t, whole], self.piece(p.q, p.core), self.own.at[self.i]
        )

    def spread(self):
        p = self.p
        ref = self.piece(p.qx, p.core); self.got(ref, "f", 0)
        ref = self.piece(p.qx, p.core, 0); self.go(ref, ref, "f", 2, p.y_nb)
        ref = self.piece(p.qy, p.core); self.got(ref, "f", 1)
        ref = self.piece(p.qy, p.core, 1); self.go(ref, ref, "f", 3, p.x_nb)
    def corner(self):
        p = self.p
        self.own_copy().wait()
        self.got(self.piece(p.qd, p.core, 0), "f", 2); self.got(self.piece(p.qd, p.core, 1), "f", 3)
        ref = self.OUT.at[:, lanes(p.core)]
        self.go(ref, ref, "f", 4, p.core_nb)
    def end(self):
        p = self.p
        self.got(self.OUT.at[:, lanes(1 - p.core)], "f", 4)
        rows = 3 * self.half // 4
        sizes = (
            ("x1", 0, self.G.at[pl.ds(0, 3)]),
            ("z", 0, self.Z),
            ("f", 0, self.G.at[0, pl.ds(0, rows)]),
            ("f", 4, self.G.at[0]),
        )
        for kind, k, ref in sizes:
            self.rdma(ref, ref, kind, k, p.core_nb).wait_send()


GATHER_SEMS = ("z", "x", "y", "fx", "fy", "c")
SEMS = ("x1", "y1", "x2", "y2", "z", "f")


def dot(a, b, ca, cb):
    return lax.dot_general(a, b, (((ca,), (cb,)), ((), ())), preferred_element_type=F32)


def loop(n, step):
    def body(i, carry):
        step(i)
        return carry

    lax.fori_loop(0, n, body, 0)


def ds(i, n):
    return pl.ds(pl.multiple_of(i * n, n), n)


class Scan:
    def __init__(self, p, later, total, up, down, got, sems):
        self.p, self.later, self.total, self.up_ref, self.down_ref = p, later, total, up, down
        self.from_core, self.from_y, self.from_below, self.from_above = [got.at[i] for i in range(4)]
        self.sems = sems

    def rdma(self, src, dst, g, i, peer):
        h, i = self.heads(g), 4 * i + g
        return pltpu.make_async_remote_copy(
            src.at[h], dst.at[h], self.sems.at[0, i], self.sems.at[1, i], device_id=peer, device_id_type=MESH
        )

    def core_copy(self, g):
        return self.rdma(self.total, self.from_core, g, 0, self.p.core_nb)

    def y_copy(self, g):
        return self.rdma(self.up_ref, self.from_y, g, 1, self.p.y_nb)

    def line_copy(self, g, upward):
        p = self.p
        if upward:
            return self.rdma(self.up_ref, self.from_below, g, 2, (p.d, p.c, p.t + 1))
        return self.rdma(self.down_ref, self.from_above, g, 3, (p.d, p.c, p.t - 1))

    def heads(self, g):
        return pl.ds(3 * g, 3)

    def begin(self, g):
        h = self.heads(g)
        zero = jnp.zeros((3, 80, 128), BF16)

        @pl.when(self.p.t == 0)
        def _():
            self.from_below[h] = zero

        @pl.when(self.p.t == 3)
        def _():
            self.from_above[h] = zero

        self.core_copy(g).start()

    def pair(self, g):
        h = self.heads(g)
        self.core_copy(g).wait_recv()
        self.up_ref[h] = self.total[h] + self.from_core[h]
        self.y_copy(g).start()

    def column(self, g):
        p, h = self.p, self.heads(g)
        core, y = p.core.astype(F32), p.y.astype(F32)
        if self.later:
            core, y = 1.0 - core, 1.0 - y
        return core * self.from_core[h].astype(F32) + y * self.from_y[h].astype(F32)

    def hop(self, g, upward):
        h, t = self.heads(g), self.p.t
        has, sends = (t > 0, t < 3) if upward else (t < 3, t > 0)
        c = self.line_copy(g, upward)
        got = self.from_below if upward else self.from_above
        out = self.up_ref if upward else self.down_ref

        @pl.when(has)
        def _():
            c.wait_recv()

        @pl.when(sends)
        def _():
            value = self.column(g) + got[h].astype(F32)
            if upward != self.later:
                value = value + self.total[h].astype(F32)
            out[h] = value.astype(BF16)
            c.start()

    def chain(self, g):
        c = self.y_copy(g)
        c.wait_recv()
        c.wait_send()
        pl.when(self.p.t < 2)(lambda: self.hop(g, True))
        pl.when(self.p.t >= 2)(lambda: self.hop(g, False))

    def relay(self, g):
        pl.when(self.p.t == 1)(lambda: self.hop(g, False))
        pl.when(self.p.t == 2)(lambda: self.hop(g, True))

    def last(self, g):
        pl.when(self.p.t == 0)(lambda: self.hop(g, False))
        pl.when(self.p.t == 3)(lambda: self.hop(g, True))

    def sum(self, g):
        h = self.heads(g)
        return self.column(g) + self.from_below[h].astype(F32) + self.from_above[h].astype(F32)

    def drain(self):
        for g in range(4):
            self.core_copy(g).wait_send()
            pl.when(self.p.t < 3)(lambda g=g: self.line_copy(g, True).wait_send())
            pl.when(self.p.t > 0)(lambda g=g: self.line_copy(g, False).wait_send())


class Small:
    def __init__(self, p, low, full, plane, line, mid, out, sems, send, own):
        self.p, self.low, self.full, self.plane, self.line, self.mid, self.out = (
            p, low, full, plane, line, mid, out
        )
        self.sems, self.send, self.own = sems, send, own
        self.me = p.d * 4 + p.c

    def rdma(self, src, dst, i, peer):
        n = 0 if i < 7 else 1 if i < 10 else 2
        return pltpu.make_async_remote_copy(
            src, dst, self.send.at[n], self.sems.at[i], device_id=peer, device_id_type=MESH
        )

    def go(self, *a):
        self.rdma(*a).start()

    def begin(self):
        for r in range(1, 8):
            peer, j = plane_peer(self.p, r)
            self.go(self.low.at[ds(j, 32)], self.plane.at[r - 1], r - 1, peer)

    def across(self):
        p = self.p
        for r in range(1, 8):
            self.rdma(self.plane.at[r - 1], self.plane.at[r - 1], r - 1, p.x_nb).wait_recv()
        for t in range(4):
            total = self.full[t, ds(self.me, 32)]
            for r in range(7):
                total = total + self.plane[r, :, 128 * t : 128 * t + 128].astype(F32)
            self.full[t, ds(self.me, 32)] = total
            self.mid[t] = total.astype(BF16)
        for k in (1, 2, 3):
            t = lax.rem(p.t + k, 4)
            self.go(self.mid.at[t], self.line.at[3 - k], 10 - k, (p.d, p.c, t))

    def final(self):
        p = self.p
        total = self.full[p.t, ds(self.me, 32)]
        for k in range(3):
            self.rdma(self.line.at[k], self.line.at[k], 7 + k, p.x_nb).wait_recv()
            total = total + self.line[k].astype(F32)
        self.mid[4] = total.astype(BF16)
        ref = self.out.at[ds(self.me, 32)]
        for r in range(1, 8):
            self.go(self.mid.at[4], ref, 9 + r, plane_peer(p, r)[0])
        pltpu.make_async_copy(self.mid.at[4], ref, self.own).start()

    def end(self):
        pltpu.make_async_copy(self.mid.at[4], self.out.at[ds(self.me, 32)], self.own).wait()
        for r in range(1, 8):
            peer, j = plane_peer(self.p, r)
            ref = self.out.at[ds(j, 32)]
            self.rdma(ref, ref, 9 + r, peer).wait_recv()
        for i, ref in ((0, self.plane), (7, self.line), (10, self.plane.at[:, :, pl.ds(0, 128)])):
            self.rdma(ref, ref, i, self.p.core_nb).wait_send()


def layer_rows(v):
    c = v - jnp.mean(v, axis=-1, keepdims=True)
    r = lax.rsqrt(jnp.mean(c * c, axis=-1, keepdims=True) + EPSILON)
    return c * r, r


def fold(v):
    total = v[:8]
    for i in range(1, v.shape[0] // 8):
        total = total + v[8 * i : 8 * i + 8]
    return total


def layer_back(e, n, r, gain):
    m = e * gain
    return r * (
        m - jnp.mean(m, axis=-1, keepdims=True) - n * jnp.mean(m * n, axis=-1, keepdims=True)
    )


def block_kernel(m):
    p = place()
    t0 = p.t
    X, CT, S, WA, W1, W2 = m.X, m.CT, m.S, m.WA, m.W1, m.W2
    VEC, H1, H2, X2, ACC_O, ACC_E = m.VEC, m.H1, m.H2, m.X2, m.ACC_O, m.ACC_E
    MIX, PH, VX, AT, PX, SL, OT, RD = m.MIX, m.PH, m.VX, m.AT, m.PX, m.SL, m.OT, m.RD
    A, DF, GS, FW, BC, IB, SUMS = m.A, m.DF, m.GS, m.FW, m.BC, m.IB, m.SUMS
    ld = m.ld
    greet(p)
    loads = [
        pltpu.make_async_copy(m.wm, WA.at[t0, pl.ds(0, 576)], ld.at[0]),
        pltpu.make_async_copy(m.wo, WA.at[t0, pl.ds(576, 192)], ld.at[1]),
        pltpu.make_async_copy(m.x, X, ld.at[2]),
        pltpu.make_async_copy(m.w1, W1.at[t0], ld.at[3]),
        pltpu.make_async_copy(m.w2, W2.at[t0], ld.at[4]),
        pltpu.make_async_copy(m.g, CT, ld.at[5]),
    ]
    raw = [(m.fw, m.FWI), (m.mb, m.MBI), (m.fb, m.FBI)]
    raw += [(ref, m.VECI.at[i, pl.ds(0, 6)]) for i, ref in enumerate(m.vectors)]
    raw = [pltpu.make_async_copy(src, dst, ld.at[8 + i]) for i, (src, dst) in enumerate(raw)]
    for c in raw + loads:
        c.start()
    for c in raw:
        c.wait()

    for h in range(3):
        pair = [m.FWI[i, h].astype(F32) for i in range(2)]
        S[t0, 64 * h : 64 * h + 64] = jnp.concatenate(pair, axis=1).astype(BF16)
    zero = jnp.zeros((1, HD), F32)
    rows = []
    for j in range(3):
        row = m.MBI[j : j + 1].astype(F32)
        rows += [
            jnp.concatenate([row[:, HD * h : HD * h + HD], zero], axis=1) for h in range(3)
        ]
    for h in range(3):
        row = m.FBI[h].astype(F32)
        rows.append(jnp.concatenate([row[0:1], row[1:2]], axis=1))
    rows.append(jnp.zeros((4, 128), F32))
    S[t0, 192:208] = jnp.concatenate(rows, axis=0).astype(BF16)
    rows = [m.VECI[6].astype(F32)[0:6], jnp.zeros((42, 128), F32)]
    S[t0, 208:256] = jnp.concatenate(rows, axis=0).astype(BF16)
    for k in range(6):
        value = m.VECI[k].astype(F32)
        for i in range(6):
            VEC[k : k + 1, 128 * i : 128 * i + 128] = value[i : i + 1]

    packs = ((S, 0, 256), (WA, 0, 576), (W1, 0, 768), (W2, 0, 768), (WA, 576, 192))
    gs, gw, g1, g2, go = [
        Gather(p, buf, m.gather_sems, m.gather_send, i, base, rows)
        for i, (buf, base, rows) in enumerate(packs)
    ]
    K = nearest(t0)
    shard = gs.shard
    loads[0].wait()
    met(p)
    gw.first()
    gs.first()

    loads[2].wait()

    def norm1(i):
        r = ds(i, 128)
        n, _ = layer_rows(X[r].astype(F32))
        H1[r] = (n * VEC[0:1] + VEC[1:2]).astype(BF16)

    loop(4, norm1)
    ones_row = jnp.where(lax.broadcasted_iota(jnp.int32, (16, 512), 0) == 0, 1.0, 0.0).astype(BF16)

    def init(h):
        VX[h, 64:80] = ones_row

    loop(12, init)
    SUMS[...] = jnp.zeros_like(SUMS)

    def small(t):
        BC[...] = S[t, 192:208].astype(F32).T
        rows = S[t, 208:224].astype(F32)
        for i in range(6):
            IB[t, :, 128 * i : 128 * i + 128] = rows[i : i + 1]
        for h in range(3):
            w = S[t, 64 * h : 64 * h + 64].astype(F32)
            FW[0, t * 3 + h] = w[:, :64].astype(BF16)
            FW[1, t * 3 + h] = w[:, 64:].astype(BF16)

    def mix(t):
        value = dot(WA[t, 0:576], H1[...], 1, 1)
        for j in range(3):
            for h in range(3):
                n = j * 3 + h
                part = (value[64 * n : 64 * n + 64] + BC[0:64, n : n + 1]).astype(BF16)
                if j < 2:
                    MIX[t, 64 * n : 64 * n + 64] = part
                else:
                    VX[t * 3 + h, 0:64] = part

    def features(t):
        for h in range(3):
            for i in range(2):
                u = dot(FW[i, t * 3 + h], MIX[t, 192 * i + 64 * h : 192 * i + 64 * h + 64], 0, 0)
                u = u + BC[64 * i : 64 * i + 64, 9 + h : 10 + h]
                e = jnp.exp(u - jnp.max(u, axis=0, keepdims=True))
                PH[i, t * 3 + h, 0:64] = (e / jnp.sum(e, axis=0, keepdims=True)).astype(BF16)
                e = jnp.exp(jnp.min(u, axis=0, keepdims=True) - u)
                PH[i, t * 3 + h, 64:128] = (e / jnp.sum(e, axis=0, keepdims=True)).astype(BF16)

    def states(t):
        def one(i):
            h = t * 3 + i
            s0 = dot(VX[h, :, 0:256], PH[1, h, :, 0:256], 1, 1)
            s1 = dot(VX[h, :, 256:512], PH[1, h, :, 256:512], 1, 1)
            SL[h] = s0
            m.TOT[h] = (s0 + s1).astype(BF16)

        loop(3, one)

    small(t0)
    mix(t0)
    features(t0)
    states(t0)
    both = (g1, g2)
    for n, k in enumerate(K):
        gw.z(k)
        gs.z(k)
        if n == 1:
            for c in (loads[1], loads[3], loads[4]):
                c.wait()
            go.first()
            for g in both:
                g.first_hop()
    for k in K:
        gw.xy(k)
        gs.xy(k)
    for k in K:
        gw.diag(k)
        gs.diag(k)
    middle = jnp.logical_or(t0 == 1, t0 == 2)
    for k in K:
        go.z(k)
    for g in both:
        g.zf(K[0])
        g.spread(K[0])
    for g in both:
        pl.when(middle)(lambda g=g: g.zf(K[1]))
    def arrived(n):
        k = jnp.where(n == 0, K[0], jnp.where(n == 1, K[1], K[2]))
        gs.done(k)
        gw.done(k)
        t = shard(k)
        small(t)
        mix(t)
        features(t)
        states(t)

    loop(3, arrived)
    scan = Scan(p, False, m.TOT, m.UP, m.DOWN, m.got_f, m.scan_f)
    for g in range(4):
        scan.begin(g)
    causal = lax.broadcasted_iota(jnp.int32, (256, 256), 0) <= lax.broadcasted_iota(
        jnp.int32, (256, 256), 1
    )

    def scores(h):
        for j in range(2):
            c = slice(256 * j, 256 * j + 256)
            a = dot(PH[1, h, :, c], PH[0, h, :, c], 0, 0)
            AT[h, j] = jnp.where(causal, a, 0.0).astype(BF16)

    for k in K:
        go.xy(k)
    for g in both:
        g.zf(jnp.where(middle, K[2], K[1]))
    for g in range(4):
        scan.pair(g)
    loop(12, scores)
    for g in range(4):
        scan.chain(g)
    for k in K:
        go.diag(k)
    for g in both:
        g.xy(K[0])
        g.spread(K[1])
    for g in both:
        pl.when(jnp.logical_not(middle))(lambda g=g: g.zf(K[2]))
    for g in range(4):
        scan.relay(g)
    for g in both:
        g.spread(K[2])

    def enter(first):
        for g in range(4):
            scan.last(g)
            value = scan.sum(g)
            h = scan.heads(g)
            PX[h, first] = value.astype(BF16)
            PX[h, 1 - first] = (value + SL[h]).astype(BF16)

    enter(0)

    def attend(h):
        for j in range(2):
            c = slice(256 * j, 256 * j + 256)
            num = dot(PX[h, j], PH[0, h, :, c], 1, 0) + dot(VX[h, :, c], AT[h, j], 1, 0)
            r = 1.0 / num[64:65]
            RD[h, :, c] = r
            OT[ds(h, 64), c] = (num[0:64] * r).astype(BF16)

    loop(12, attend)
    for k in K:
        go.done(k)

    def norm2(i):
        r = ds(i, 256)
        total = X[r].astype(F32) + VEC[2:3]
        for t in range(4):
            total = total + dot(OT[192 * t : 192 * t + 192, r], WA[t, 576:768], 0, 0)
        X2[r] = total
        n, _ = layer_rows(total)
        H2[r] = (n * VEC[3:4] + VEC[4:5]).astype(BF16)
        ACC_O[r] = total + VEC[5:6]
        ACC_E[r] = jnp.zeros((256, 768), F32)

    loop(2, norm2)

    R = [
        Reduce(p, i, m.G[i], *m.land[i][1:], m.Z[i], m.outs[i], m.reduce_sems, m.reduce_send, m.own)
        for i in range(4)
    ]
    core_sems, STAGE = m.r_core, m.STAGE
    outgoing = []

    def core_copy(src, i, k):
        ref = m.land[i][0].at[shard(k)]
        return pltpu.make_async_remote_copy(
            ref if src is None else src,
            ref,
            core_sems.at[0, i, k],
            core_sems.at[1, i, k],
            device_id=p.core_nb,
            device_id_type=MESH,
        )

    def hand(i, k, value):
        slot = len(outgoing) % 2
        if len(outgoing) >= 2:
            outgoing[-2].wait_send()
        ref = STAGE.at[slot, pl.ds(0, R[i].half)]
        ref[...] = value(1 - p.core).astype(BF16)
        c = core_copy(ref, i, k)
        c.start()
        outgoing.append(c)
        R[i].G[shard(k)] = value(p.core).astype(BF16)

    def meet(i, k):
        t = shard(k)
        G, C = R[i].G, m.land[i][0]
        core_copy(None, i, k).wait_recv()

        def add(j):
            r = ds(j, 96)
            G[t, r] = G[t, r] + C[t, r]

        loop(R[i].half // 96, add)
        R[i].one(k)

    def hidden(t, slot):
        def rows(i):
            r = ds(i, 256)
            f = dot(H2[r], W1[t], 1, 0) + IB[t]
            th = jnp.tanh(0.7978845608028654 * (f + 0.044715 * f * f * f))
            a = (0.5 * f * (1.0 + th)).astype(BF16)
            A[slot, r] = a
            slope = 0.5 * (1.0 + th) + 0.5 * f * (1.0 - th * th) * (
                0.7978845608028654 * (1.0 + 3.0 * 0.044715 * f * f)
            )
            df = (dot(CT[r], W2[t], 1, 1) * slope).astype(BF16)
            DF[slot, r] = df
            m.DIB[t] += fold(df.astype(F32))
            ACC_O[r] += dot(a, W2[t], 1, 0)
            ACC_E[r] += dot(df, W1[t], 1, 1)

        loop(2, rows)

    def hand_hidden(k, slot):
        hand(0, k, lambda core: dot(A[slot], CT[:, lanes(core)], 0, 0))
        hand(1, k, lambda core: dot(H2[...], DF[slot, :, lanes(core)], 0, 0))

    m.DIB[...] = jnp.zeros_like(m.DIB)
    order = K + [0]
    loads[5].wait()
    for g in both:
        g.diag(K[0])
    hidden(t0, 0)
    for g in both:
        g.xy(K[1])
    hand(0, 0, lambda core: dot(A[0], CT[:, lanes(core)], 0, 0))
    for n, k in enumerate(K):
        g1.done(k)
        g2.done(k)
        hidden(shard(k), 1)
        for g in both:
            if n == 0:
                g.xy(K[2])
                g.diag(K[1])
            if n == 1:
                g.diag(K[2])
        if n:
            meet(1, K[n - 1])
        else:
            meet(0, 0)
        if n < 2:
            hand_hidden(k, 1)
            meet(0, k)
    for g in both:
        g.drain(True)
    RES, GG = W1.at[2, pl.ds(0, 512)], W1.at[3, pl.ds(0, 512)]

    def dne(h):
        start = pl.multiple_of(lax.rem(h, 9) * 80, 16)
        return W2.at[h // 9, pl.ds(start, 80), pl.ds(0, 512)]

    def du_of(h):
        return W1.at[h // 6, ds(lax.rem(h, 6), 128), pl.ds(0, 512)]

    def dv_of(h):
        return W2.at[2, ds(h, 64), pl.ds(0, 512)]

    def back2(i):
        r = ds(i, 128)
        n, s = layer_rows(X2[r])
        e = ACC_E[r]
        g = CT[r].astype(F32)
        dx = g + layer_back(e, n, s, VEC[3:4])
        SUMS[3] += fold(e * n)
        SUMS[4] += fold(e)
        SUMS[2] += fold(dx)
        SUMS[5] += fold(g)
        X2[r] = dx
        GG[r] = dx.astype(BF16)

    loop(4, back2)
    DX = X2
    first_row = lax.broadcasted_iota(jnp.int32, (16, 512), 0) == 0

    scan.drain()
    scan = Scan(p, True, m.TOT, m.UP, m.DOWN, m.got_b, m.scan_b)

    def states_back(t):
        value = dot(WA[t, 576:768], GG[...], 1, 1).astype(BF16).astype(F32)
        for i in range(3):
            h = 3 * t + i
            do = value[64 * i : 64 * i + 64]
            r = RD[h]
            o = OT[ds(h, 64)].astype(F32)
            ref = dne(h)
            ref[0:64] = (do * r).astype(BF16)
            dden = -jnp.sum(do * o, axis=0, keepdims=True) * r
            ref[64:80] = jnp.where(first_row, dden, 0.0).astype(BF16)
            s0 = dot(ref[:, 0:256], PH[0, h, :, 0:256], 1, 1)
            s1 = dot(ref[:, 256:512], PH[0, h, :, 256:512], 1, 1)
            SL[h] = s1
            m.TOT[h] = (s0 + s1).astype(BF16)

    def give(t):
        states_back(t)
        scan.begin(t)

    loop(4, give)
    hand(0, order[2], lambda core: dot(A[1], CT[:, lanes(core)], 0, 0))
    for g in range(4):
        scan.pair(g)
    R[0].two(0)
    for i in range(2):
        R[i].two(order[0])
    hand(1, order[2], lambda core: dot(H2[...], DF[1, :, lanes(core)], 0, 0))
    for i in range(2):
        R[i].two(order[1])

    def feature_back(i, h, delta):
        delta = delta.astype(BF16).astype(F32)
        up, down = PH[i, h, 0:64].astype(F32), PH[i, h, 64:128].astype(F32)
        d, dd = delta[0:64], delta[64:128]
        du = up * (d - jnp.sum(up * d, axis=0, keepdims=True)) - down * (
            dd - jnp.sum(down * dd, axis=0, keepdims=True)
        )
        du_of(h)[64 * i : 64 * i + 64] = du.astype(BF16)

    def query_back(h):
        parts = []
        ref, dv = dne(h), dv_of(h)
        for j in range(2):
            c = slice(256 * j, 256 * j + 256)
            value = ref[:, c]
            dv[:, c] = dot(ref[0:64, c], AT[h, j], 1, 1).astype(BF16)
            da = dot(VX[h, :, c], value, 0, 0)
            da = jnp.where(causal, da, 0.0).astype(BF16)
            AT[h, j] = da
            parts.append(dot(PH[1, h, :, c], da, 1, 0) + dot(PX[h, j], value, 0, 0))
        feature_back(0, h, jnp.concatenate(parts, axis=1))

    ones8 = jnp.ones((8, 512), BF16)
    left = lax.broadcasted_iota(jnp.int32, (64, 128), 1) < 64
    GS[:, 192:256] = jnp.zeros((4, 64, 128), F32)

    def bias_row(t, j, i):
        ref = MIX[t, ds(3 * j + i, 64)]
        GS[t, pl.ds(192 + 3 * j + i, 1), 0:64] = dot(ones8, ref, 1, 1)[0:1]

    def early(k):
        t = shard(k)
        def one(i):
            h = t * 3 + i
            rows = ds(i, 64)
            du = du_of(h)[0:64]
            GS[t, rows, 0:64] = dot(MIX[t, rows], du, 1, 1)
            MIX[t, rows] = dot(FW[0, h], du, 1, 0).astype(BF16)
            bias_row(t, 0, i)

        loop(3, one)

        def value(core):
            both = [
                dot(MIX[t, 0:192], H1[:, lanes(core)], 1, 0),
                dot(OT[ds(t, 192)], GG[:, lanes(core)], 1, 0),
            ]
            return jnp.concatenate(both, axis=0)

        hand(2, k, value)

    def queries(g):
        loop(3, lambda i: query_back(3 * g + i))

    def ask(g):
        queries(g)
        scan.chain(g)

    loop(2, ask)
    for i in range(2):
        meet(i, order[2])
    loop(2, lambda g: ask(g + 2))
    hand(1, 0, lambda core: dot(H2[...], DF[0, :, lanes(core)], 0, 0))
    for g in range(4):
        scan.relay(g)
    R[0].three(0)
    for i in range(2):
        R[i].three(order[0])
        R[i].three(order[1])
    RES[...] = ACC_O[...].astype(BF16)
    res_copy = pltpu.make_async_copy(RES, m.result, ld.at[6])
    res_copy.start()
    early(order[0])
    meet(1, order[3])
    early(order[1])
    meet(2, order[0])
    for i in range(2):
        R[i].two(order[2])
    early(order[2])
    meet(2, order[1])
    early(order[3])
    meet(2, order[2])
    R[1].two(order[3])
    enter(1)

    def key_back(t, i):
        h = t * 3 + i
        parts, values = [], []
        for j in range(2):
            c = slice(256 * j, 256 * j + 256)
            q = PX[h, j]
            parts.append(dot(PH[0, h, :, c], AT[h, j], 1, 1) + dot(q, VX[h, :, c], 0, 0))
            values.append(dot(q[0:64], PH[1, h, :, c], 1, 0))
        feature_back(1, h, jnp.concatenate(parts, axis=1))
        dv = jnp.concatenate(values, axis=1) + dv_of(h)[...].astype(F32)
        MIX[t, ds(6 + i, 64)] = dv.astype(BF16)
        du = du_of(h)
        rows = ds(3 + i, 64)
        ref = ds(i, 64)
        GS[t, ref] = jnp.where(left, GS[t, ref], dot(MIX[t, rows], du[...], 1, 1))
        GS[t, pl.ds(201 + i, 1)] = dot(ones8, du[...], 1, 1)[0:1]
        MIX[t, rows] = dot(FW[1, h], du[64:128], 1, 0).astype(BF16)
        bias_row(t, 1, i)
        bias_row(t, 2, i)

    for n, k in enumerate(order):
        t = shard(k)
        loop(3, lambda i: key_back(t, i))
        hand(3, k, lambda core: dot(MIX[t, 192:576], H1[:, lanes(core)], 1, 0))
        if n == 0:
            for i in range(2):
                R[i].three(order[2])
            meet(2, order[3])
            R[2].two(order[0])
            R[2].two(order[1])
        else:
            meet(3, order[n - 1])
        if n == 1:
            R[1].three(order[3])
            R[2].two(order[2])
        if n == 2:
            R[2].two(order[3])
            R[2].three(order[0])
            R[2].three(order[1])
            R[3].two(order[0])
            R[0].final()
            R[1].final()
        if n == 3:
            R[2].three(order[2])
            R[2].three(order[3])
            R[3].two(order[1])
            R[3].three(order[0])

    def back1(i):
        r = ds(i, 256)
        e = dot(MIX[0, :, r], WA[0, 0:576], 0, 0)
        for t in range(1, 4):
            e = e + dot(MIX[t, :, r], WA[t, 0:576], 0, 0)
        n, s = layer_rows(X[r].astype(F32))
        SUMS[0] += fold(e * n)
        SUMS[1] += fold(e)
        ACC_E[r] = DX[r] + layer_back(e, n, s, VEC[0:1])

    back1(0)
    meet(3, order[3])
    R[0].spread()
    R[3].two(order[2])
    R[1].spread()
    R[3].three(order[1])
    back1(1)
    R[3].two(order[3])
    R[0].corner()
    tok_copy = pltpu.make_async_copy(ACC_E, m.tokens_gradient, ld.at[7])
    tok_copy.start()
    for k in range(6):
        row = jnp.sum(SUMS[k], axis=0, keepdims=True)
        for i in range(6):
            for t in range(4):
                GS[t, 216 + 6 * k + i : 217 + 6 * k + i] = row[:, 128 * i : 128 * i + 128]
    for t in range(4):
        row = jnp.sum(m.DIB[t], axis=0, keepdims=True)
        for i in range(6):
            GS[t, 208 + i : 209 + i] = row[:, 128 * i : 128 * i + 128]
    GB = W2.at[3, pl.ds(0, 256), pl.ds(0, 512)]
    for t in range(4):
        GB[:, 128 * t : 128 * t + 128] = GS[t].astype(BF16)
    tiny = Small(p, GB, GS, m.plane, m.line, m.mid, m.outs[4], m.small_sems, m.small_send, m.own.at[4])
    tiny.begin()
    R[2].final()
    R[3].three(order[2])
    R[1].corner()
    R[3].three(order[3])
    tiny.across()
    R[2].spread()
    R[3].final()
    tiny.final()
    R[2].corner()
    R[3].spread()
    R[3].corner()
    for r in R:
        r.end()
    tiny.end()
    scan.drain()
    for c in outgoing[-2:]:
        c.wait_send()
    gs.drain(False)
    gw.drain(False)
    go.drain(False)
    res_copy.wait()
    tok_copy.wait()


PACKS = ((768, 768), (768, 768), (384, 768), (384, 768))


def landing(rows):
    q, r = rows // 4, rows // 8
    shapes = ((4, rows), (4, 2, r), (4, 2, r), (4, r), (4, r))
    return [pltpu.VMEM((*shape, 384), BF16) for shape in shapes]


def block_call(*args):
    rows, width = args[0].shape
    flat = pltpu.VMEM((rows, width), BF16)
    wide = pltpu.VMEM((rows, width), F32)
    weights = pltpu.VMEM((4, 768, 768), BF16)
    state = pltpu.VMEM((12, 80, 128), BF16)
    dma = pltpu.SemaphoreType.DMA
    scratch = dict(
        X=flat,
        CT=flat,
        S=pltpu.VMEM((4, 256, 128), BF16),
        WA=weights,
        W1=weights,
        W2=weights,
        VEC=pltpu.VMEM((8, 768), F32),
        VECI=pltpu.VMEM((7, 8, 128), BF16),
        FWI=pltpu.VMEM((2, 3, HD, HD), BF16),
        MBI=pltpu.VMEM((3, 192), BF16),
        FBI=pltpu.VMEM((3, 2, HD), BF16),
        H1=flat,
        H2=flat,
        X2=wide,
        ACC_O=wide,
        ACC_E=wide,
        MIX=pltpu.VMEM((4, 576, rows), BF16),
        PH=pltpu.VMEM((2, 12, 128, rows), BF16),
        VX=pltpu.VMEM((12, 80, rows), BF16),
        AT=pltpu.VMEM((12, 2, 256, 256), BF16),
        PX=pltpu.VMEM((12, 2, 80, 128), BF16),
        SL=pltpu.VMEM((12, 80, 128), F32),
        OT=pltpu.VMEM((768, rows), BF16),
        RD=pltpu.VMEM((12, 1, rows), F32),
        A=pltpu.VMEM((2, rows, width), BF16),
        DF=pltpu.VMEM((2, rows, width), BF16),
        GS=pltpu.VMEM((4, 256, 128), F32),
        FW=pltpu.VMEM((2, 12, 64, 64), BF16),
        BC=pltpu.VMEM((128, 16), F32),
        IB=pltpu.VMEM((4, 1, 768), F32),
        SUMS=pltpu.VMEM((6, 8, 768), F32),
        DIB=pltpu.VMEM((4, 8, 768), F32),
        TOT=state,
        UP=state,
        DOWN=state,
        got_f=pltpu.VMEM((4, 12, 80, 128), BF16),
        got_b=pltpu.VMEM((4, 12, 80, 128), BF16),
        plane=pltpu.VMEM((7, 32, 512), BF16),
        line=pltpu.VMEM((3, 32, 128), BF16),
        mid=pltpu.VMEM((5, 32, 128), BF16),
        STAGE=pltpu.VMEM((2, 768, 384), BF16),
        G=[pltpu.VMEM((4, n, 384), BF16) for n, _ in PACKS],
        Z=[pltpu.VMEM((3, n // 4, 384), BF16) for n, _ in PACKS],
        land=[landing(n) for n, _ in PACKS],
        ld=dma((18,)),
        own=dma((5,)),
        r_core=dma((2, 4, 4)),
        gather_sems={k: dma((5, 3)) for k in GATHER_SEMS},
        gather_send=dma((5, 3)),
        reduce_sems={k: dma((4, n)) for k, n in zip(SEMS, (4, 4, 4, 4, 3, 5))},
        reduce_send=dma((4, 4)),
        small_sems=dma((17,)),
        small_send=dma((3,)),
        scan_f=dma((2, 16)),
        scan_b=dma((2, 16)),
    )
    leaves, tree = jax.tree.flatten(scratch, is_leaf=lambda v: not isinstance(v, (dict, list)))
    results = [
        jax.ShapeDtypeStruct((rows, width), BF16),
        jax.ShapeDtypeStruct((rows, width), F32),
        *[jax.ShapeDtypeStruct(pack, BF16) for pack in PACKS],
        jax.ShapeDtypeStruct((256, 128), BF16),
    ]

    def body(x, g, wm, wo, w1, w2, fw, mb, fb, *rest):
        vectors, (result, tokens_gradient), rest = rest[:7], rest[7:9], rest[9:]
        given = dict(
            x=x, g=g, wm=wm, wo=wo, w1=w1, w2=w2, fw=fw, mb=mb, fb=fb, vectors=vectors
        )
        block_kernel(
            SimpleNamespace(
                **given,
                result=result,
                tokens_gradient=tokens_gradient,
                outs=rest[:5],
                **jax.tree.unflatten(tree, rest[5:]),
            )
        )

    anywhere = pl.BlockSpec(memory_space=pl.ANY)
    return pl.pallas_call(
        body,
        out_shape=results,
        in_specs=[anywhere] * len(args),
        out_specs=[anywhere] * len(results),
        scratch_shapes=leaves,
        compiler_params=pltpu.CompilerParams(
            collective_id=0, has_side_effects=True, vmem_limit_bytes=67043328
        ),
        name="block",
    )(*args)


def finish_kernel(
    res, tok, outer, inner, q, o, k, v, small,
    res_o, tok_o, outer_o, inner_o, mixer_o, output_o, feature_o, mixer_bias_o, feature_bias_o, *vec_o,
):
    res_o[...] = res[...]
    tok_o[...] = tok[...]
    outer_o[...] = outer[...].astype(F32)
    inner_o[...] = inner[...].astype(F32)
    for i, ref in enumerate((q, k, v)):
        mixer_o[i] = ref[...].astype(F32)
    output_o[...] = o[...].astype(F32)

    @pl.when(pl.program_id(0) == 0)
    def _():
        rows = small[192:256].astype(F32)
        for h in range(3):
            w = small[64 * h : 64 * h + 64].astype(F32)
            feature_o[0, h] = w[:, :64]
            feature_o[1, h] = w[:, 64:]
            pair = rows[9 + h : 10 + h]
            feature_bias_o[h] = jnp.concatenate([pair[:, :64], pair[:, 64:]], axis=0)
            parts = [rows[3 * h + i : 3 * h + i + 1, :64] for i in range(3)]
            mixer_bias_o[h : h + 1] = jnp.concatenate(parts, axis=1)
        for i in range(6):
            vec_o[i][...] = rows[24 + 6 * i : 30 + 6 * i]
        vec_o[6][...] = rows[16:22]


def finish_call(res, tok, outer, inner, early, late, small):
    rows, width = res.shape
    steps = 4

    def spec(n, shift=0):
        return pl.BlockSpec((n, width), lambda i: (i + shift, 0))

    def whole(*shape):
        return pl.BlockSpec(shape, lambda i: (0,) * len(shape))

    def out(*shape):
        return jax.ShapeDtypeStruct(shape, F32)

    vectors = [(6, 128)] * 7
    return pl.pallas_call(
        finish_kernel,
        grid=(steps,),
        in_specs=[
            spec(rows // steps),
            spec(rows // steps),
            spec(768 // steps),
            spec(768 // steps),
            spec(192 // steps),
            spec(192 // steps, steps),
            spec(192 // steps),
            spec(192 // steps, steps),
            whole(256, 128),
        ],
        out_specs=[
            spec(rows // steps),
            spec(rows // steps),
            spec(768 // steps),
            spec(768 // steps),
            pl.BlockSpec((3, 192 // steps, width), lambda i: (0, i, 0)),
            spec(192 // steps),
            whole(2, 3, HD, HD),
            whole(3, 192),
            whole(3, 2, HD),
            *[whole(*v) for v in vectors],
        ],
        out_shape=[
            jax.ShapeDtypeStruct((rows, width), BF16),
            out(rows, width),
            out(768, width),
            out(768, width),
            out(3, 192, width),
            out(192, width),
            out(2, 3, HD, HD),
            out(3, 192),
            out(3, 2, HD),
            *[out(*v) for v in vectors],
        ],
        name="finish",
    )(res, tok, outer, inner, early, early, late, late, small)


def shards(
    fast,
    tokens,
    first_gain,
    first_bias,
    mixer_weight,
    mixer_bias,
    feature_weight,
    feature_bias,
    output_weight,
    output_bias,
    second_gain,
    second_bias,
    inner_weight,
    inner_bias,
    outer_weight,
    outer_bias,
    block_owner,
    cotangent,
):
    rows, width = tokens.shape
    n_tp, n_ctx = lax.axis_size("tp"), lax.axis_size("ctx")
    n_plane = lax.axis_size("dp") * n_ctx
    plane = lax.axis_index("dp") * n_ctx + lax.axis_index("ctx")
    heads_here = mixer_weight.shape[2] // HD
    heads = heads_here * n_tp
    mine = lax.axis_index("ctx") * n_tp + lax.axis_index("tp")

    mixer_t = mixer_weight.transpose(1, 2, 0).reshape(-1, width)
    if fast:
        vectors = (
            first_gain, first_bias, output_bias, second_gain, second_bias, outer_bias, inner_bias
        )
        raw = block_call(
            tokens,
            cotangent,
            mixer_t,
            output_weight,
            inner_weight,
            outer_weight,
            feature_weight,
            mixer_bias,
            feature_bias.transpose(1, 0, 2),
            *[v.reshape(6, 128) for v in vectors],
        )
        (
            result, tokens_gradient, d_outer, d_inner, d_mixer, d_output,
            d_feature, d_mixer_bias, d_feature_bias, *shared
        ) = finish_call(*raw)
        shared = [v.reshape(width) for v in shared]
        return (
            result,
            tokens_gradient,
            shared[0],
            shared[1],
            d_mixer.transpose(2, 0, 1),
            d_mixer_bias,
            d_feature,
            d_feature_bias.transpose(1, 0, 2),
            d_output,
            shared[2],
            shared[3],
            shared[4],
            d_inner,
            shared[6],
            d_outer,
            shared[5],
        )
    sizes = [w.shape[0] for w in (mixer_t, output_weight, inner_weight, outer_weight)]
    pack = jnp.concatenate([mixer_t, output_weight, inner_weight, outer_weight], axis=0)
    part = pack.shape[0] // n_plane
    piece = lax.dynamic_slice_in_dim(pack, plane * part, part, 0)
    full = lax.all_gather(piece, ALL, axis=0, tiled=True)
    full = full.reshape(n_plane, n_tp, part, width).transpose(1, 0, 2, 3).reshape(n_tp, -1, width)
    cuts = [0]
    for s in sizes:
        cuts.append(cuts[-1] + s)
    mixer_all, output_all, inner_all, outer_all = [
        full[:, a:b] for a, b in zip(cuts[:-1], cuts[1:])
    ]
    small = jnp.concatenate(
        [feature_weight.reshape(-1), mixer_bias.reshape(-1), feature_bias.reshape(-1), inner_bias]
    )
    small = lax.all_gather(small, "tp")
    cut = feature_weight.size
    feature_all = (
        small[:, :cut].reshape(n_tp, 2, heads_here, HD, HD).transpose(1, 0, 2, 3, 4)
    ).reshape(2, heads, HD, HD)
    mixer_bias_all = small[:, cut : cut + mixer_bias.size].astype(F32).reshape(n_tp, -1)
    cut += mixer_bias.size
    feature_bias_all = (
        small[:, cut : cut + feature_bias.size]
        .astype(F32)
        .reshape(n_tp, 2, heads_here, HD)
        .transpose(1, 0, 2, 3)
        .reshape(2, heads, HD)
    )
    cut += feature_bias.size
    inner_bias_all = small[:, cut:].astype(F32)

    x = tokens.astype(F32)
    gain1, gain2 = first_gain.astype(F32), second_gain.astype(F32)
    h1, n1, r1 = layer_norm(x, gain1, first_bias.astype(F32))
    h1 = h1.astype(BF16)
    mix = ein("td,skd->tsk", h1, mixer_all) + mixer_bias_all
    mix = mix.astype(BF16).reshape(rows, n_tp, 3, heads_here, HD).transpose(2, 0, 1, 3, 4)
    mix = mix.reshape(3, rows, heads, HD)
    q, k, v = mix[0], mix[1], mix[2]
    q_up, q_down, phi_q = feature_map(q, feature_all[0], feature_bias_all[0])
    k_up, k_down, phi_k = feature_map(k, feature_all[1], feature_bias_all[1])

    chunk = min(CHUNK, rows)
    chunks = rows // chunk
    pq = phi_q.reshape(chunks, chunk, heads, 2 * HD)
    pk = phi_k.reshape(chunks, chunk, heads, 2 * HD)
    vc = v.reshape(chunks, chunk, heads, HD)
    causal = jnp.arange(chunk)[:, None] >= jnp.arange(chunk)[None, :]
    state = ein("jthe,jthf->jhef", vc, pk)
    norm = jnp.sum(pk.astype(F32), axis=1)
    both = jnp.concatenate([state, norm[:, :, None]], axis=2)
    owners = block_owner[0].reshape(n_tp, -1)[:, 0]
    order = jnp.arange(n_ctx * n_tp)
    same = jnp.tile(owners, n_ctx) == jnp.tile(owners, n_ctx)[mine]

    def prefix(totals, reach):
        everything = lax.all_gather(totals.astype(BF16), ("ctx", "tp")).astype(F32)
        return jnp.einsum("s,shef->hef", reach.astype(F32), everything, precision="highest")

    def running(blocks, start, reverse):
        out = [None] * chunks
        acc = start
        for j in reversed(range(chunks)) if reverse else range(chunks):
            out[j] = acc
            acc = acc + blocks[j]
        return jnp.stack(out)

    before = running(both, prefix(jnp.sum(both, axis=0), same & (order < mine)), False)
    before = before.astype(BF16)
    scores = ein("jthf,jshf->jhts", pq, pk)
    a_low = jnp.where(causal, scores, 0.0).astype(BF16)
    v_one = jnp.concatenate([vc, jnp.ones(vc.shape[:-1] + (1,), BF16)], axis=-1)
    num = ein("jthf,jhef->jthe", pq, before) + ein("jhts,jshe->jthe", a_low, v_one)
    num, den = num[..., :HD], num[..., HD:]
    o = num / den
    o_low = o.astype(BF16)
    o_flat = o_low.reshape(rows, n_tp, heads_here * HD)
    x2 = x + ein("tsk,skd->td", o_flat, output_all) + output_bias.astype(F32)
    h2, n2, r2 = layer_norm(x2, gain2, second_bias.astype(F32))
    h2 = h2.astype(BF16)
    f = ein("td,sdf->tsf", h2, inner_all) + inner_bias_all
    a, slope = gelu_parts(f)
    a = a.astype(BF16)
    result = (x2 + ein("tsf,sfd->td", a, outer_all) + outer_bias.astype(F32)).astype(BF16)

    g = cotangent.astype(F32)
    d_outer = ein("tsf,td->sfd", a, cotangent)
    df = (ein("td,sfd->tsf", cotangent, outer_all) * slope).astype(BF16)
    d_inner_bias = jnp.sum(df.astype(F32), axis=0)
    d_inner = ein("td,tsf->sdf", h2, df)
    e2 = ein("tsf,sdf->td", df, inner_all)
    back2, d_gain2, d_bias2 = layer_norm_back(e2, n2, r2, gain2)
    dx2 = g + back2
    big_g = dx2.astype(BF16)
    d_output = ein("tsk,td->skd", o_flat, big_g)
    do = ein("td,skd->tsk", big_g, output_all).astype(BF16).astype(F32)
    do = do.reshape(chunks, chunk, heads, HD)
    dnum = do / den
    dden = -jnp.sum(do * o, axis=-1, keepdims=True) / den
    dne = jnp.concatenate([dnum, dden], axis=-1).astype(BF16)
    da = ein("jthe,jshe->jhts", dne, v_one)
    da_low = jnp.where(causal, da, 0.0).astype(BF16)
    d_both = ein("jthe,jthf->jhef", dne, pq)
    after = running(d_both, prefix(jnp.sum(d_both, axis=0), same & (order > mine)), True)
    after = after.astype(BF16)
    dphi_q = ein("jhts,jshf->jthf", da_low, pk) + ein("jthe,jhef->jthf", dne, before)
    dphi_k = ein("jhts,jthf->jshf", da_low, pq) + ein("jthe,jhef->jthf", v_one, after)
    dv = ein("jhts,jthe->jshe", a_low, dne[..., :HD]) + ein("jthf,jhef->jthe", pk, after[:, :, :HD])
    dphi_q = dphi_q.reshape(rows, heads, 2 * HD)
    dphi_k = dphi_k.reshape(rows, heads, 2 * HD)
    dq, d_fq, d_fbq = feature_back(dphi_q, q_up, q_down, q, feature_all[0])
    dk, d_fk, d_fbk = feature_back(dphi_k, k_up, k_down, k, feature_all[1])
    dmix = jnp.stack([dq, dk, dv.reshape(rows, heads, HD)], axis=1).astype(BF16)
    dmix = dmix.reshape(rows, 3, n_tp, heads_here * HD).transpose(0, 2, 1, 3)
    dmix = dmix.reshape(rows, n_tp, -1)
    d_mixer_bias = jnp.sum(dmix.astype(F32), axis=0)
    d_mixer = ein("tsk,td->skd", dmix, h1)
    e1 = ein("tsk,skd->td", dmix, mixer_all)
    back1, d_gain1, d_bias1 = layer_norm_back(e1, n1, r1, gain1)
    tokens_gradient = dx2 + back1

    big = jnp.concatenate([d_mixer, d_output, d_inner, d_outer], axis=1).astype(BF16)
    big = big.reshape(n_tp, n_plane, part, width).transpose(1, 0, 2, 3).reshape(-1, width)
    big = lax.psum_scatter(big, ("dp", "ctx"), scatter_dimension=0, tiled=True)
    big = lax.psum_scatter(big, "tp", scatter_dimension=0, tiled=True)
    big = lax.all_gather(big, ("dp", "ctx"), axis=0, tiled=True).astype(F32)
    d_mixer, d_output, d_inner, d_outer = [big[a:b] for a, b in zip(cuts[:-1], cuts[1:])]
    d_mixer = d_mixer.reshape(3, heads_here * HD, width).transpose(2, 0, 1)
    per_tp = jnp.concatenate(
        [
            jnp.stack([d_fq, d_fk]).reshape(2, n_tp, -1).transpose(1, 0, 2).reshape(n_tp, -1),
            d_mixer_bias,
            jnp.stack([d_fbq, d_fbk]).reshape(2, n_tp, -1).transpose(1, 0, 2).reshape(n_tp, -1),
            d_inner_bias,
        ],
        axis=1,
    )
    shared = jnp.stack(
        [d_gain1, d_bias1, jnp.sum(dx2, axis=0), d_gain2, d_bias2, jnp.sum(g, axis=0)]
    )
    total = lax.psum(jnp.concatenate([per_tp.reshape(-1), shared.reshape(-1)]), ALL)
    shared = total[per_tp.size :].reshape(6, width)
    own = lax.dynamic_slice_in_dim(
        total[: per_tp.size].reshape(n_tp, -1), lax.axis_index("tp"), 1, 0
    )[0]
    cut = feature_weight.size
    d_feature = own[:cut].reshape(feature_weight.shape)
    d_mixer_bias = own[cut : cut + mixer_bias.size].reshape(mixer_bias.shape)
    cut += mixer_bias.size
    d_feature_bias = own[cut : cut + feature_bias.size].reshape(feature_bias.shape)
    d_inner_bias = own[cut + feature_bias.size :]
    return (
        result,
        tokens_gradient,
        shared[0],
        shared[1],
        d_mixer,
        d_mixer_bias,
        d_feature,
        d_feature_bias,
        d_output,
        shared[2],
        shared[3],
        shared[4],
        d_inner,
        d_inner_bias,
        d_outer,
        shared[5],
    )


def solution(mesh):
    in_specs = (
        P(("dp", "ctx", "tp"), None),
        P(),
        P(),
        P(None, None, "tp"),
        P(None, "tp"),
        P(None, "tp", None, None),
        P(None, "tp", None),
        P("tp", None),
        P(),
        P(),
        P(),
        P(None, "tp"),
        P("tp"),
        P("tp", None),
        P(),
        P("dp", None),
        P(("dp", "ctx", "tp"), None),
    )
    out_specs = (
        P(("dp", "ctx", "tp"), None),
        P(("dp", "ctx", "tp"), None),
        P(),
        P(),
        P(None, None, "tp"),
        P(None, "tp"),
        P(None, "tp", None, None),
        P(None, "tp", None),
        P("tp", None),
        P(),
        P(),
        P(),
        P(None, "tp"),
        P("tp"),
        P("tp", None),
        P(),
    )
    fast = (mesh.shape["dp"], mesh.shape["ctx"], mesh.shape["tp"]) == (2, 4, 4)
    return jax.shard_map(functools.partial(shards, fast), mesh=mesh, in_specs=in_specs, out_specs=out_specs, check_vma=False)
```
